32 devices in a mesh: seg: 8 (over z, y), pos: 4 (over x, core).
Axes of the slice: x: 2, y: 2, z: 4, core: 2. Of those that a mesh axis runs over, the one named last changes fastest.
Arguments:
- block_input: bfloat16 [16, 1024, 1024], P('seg', 'pos'), may hold values from -6 to 6
- memory_rows: bfloat16 [16, 1024, 1024], P('seg', 'pos'), may hold values from -6 to 6
- memory_length: int32 [16], P('seg'), may hold values from 0 to 1024, as said below
- value_routes: int32 [16, 2, 1024, 4, 2], P('seg', None, 'pos'), may hold values from 0 to 4, all different within a row
- output_routes: int32 [16, 1024, 4, 2], P('seg', 'pos'), may hold values from 0 to 4, all different within a row
- first_gain: bfloat16 [1024], replicated, may hold values from 0.5 to 1.5
- first_shift: bfloat16 [1024], replicated, may hold values from -1.25 to 1.25
- query_weight: bfloat16 [1024, 448], replicated, may hold values from -0.1875 to 0.1875
- key_weight: bfloat16 [1024, 448], replicated, may hold values from -0.1875 to 0.1875
- position_weight: bfloat16 [1024, 448], replicated, may hold values from -0.25 to 0.25
- value_experts: bfloat16 [1024, 2240], replicated, may hold values from -0.1875 to 0.1875
- value_router: bfloat16 [1024, 20], replicated, may hold values from -0.125 to 0.125
- content_bias: bfloat16 [448], replicated, may hold values from -3 to 3
- position_bias: bfloat16 [448], replicated, may hold values from -3 to 3
- output_experts: bfloat16 [2240, 1024], replicated, may hold values from -6 to 6
- output_gate_matrix: bfloat16 [1024, 20], replicated, may hold values from -0.125 to 0.125
- second_gain: bfloat16 [1024], replicated, may hold values from 0.5 to 1.5
- second_shift: bfloat16 [1024], replicated, may hold values from -1.25 to 1.25
- up_projection_weight: bfloat16 [1024, 4096], replicated, may hold values from -0.1875 to 0.1875
- expand_bias: bfloat16 [4096], replicated, may hold values from -1.25 to 1.25
- down_projection_weight: bfloat16 [4096, 1024], replicated, may hold values from -0.125 to 0.125
- contract_bias: bfloat16 [1024], replicated, may hold values from -1.25 to 1.25
- output_cotangent: bfloat16 [16, 1024, 1024], P('seg', 'pos'), may hold values from -6 to 6
Outputs:
- block_output: bfloat16 [16, 1024, 1024], P('seg', 'pos')
- input_grad: bfloat16 [16, 1024, 1024], P('seg', 'pos')
- first_gain_grad: float32 [1024], P('seg')
- first_shift_grad: float32 [1024], P('seg')
- query_weight_grad: float32 [1024, 448], P('seg')
- key_weight_grad: float32 [1024, 448], P('seg')
- position_weight_grad: float32 [1024, 448], P('seg')
- value_experts_grad: float32 [1024, 2240], P('seg')
- value_router_grad: float32 [1024, 20], P('seg')
- content_bias_grad: float32 [448], P('seg')
- position_bias_grad: float32 [448], P('seg')
- output_experts_grad: float32 [2240, 1024], P('seg')
- output_router_grad: float32 [1024, 20], P('seg')
- second_gain_grad: float32 [1024], P('seg')
- second_shift_grad: float32 [1024], P('seg')
- expand_weight_grad: float32 [1024, 4096], P('seg')
- expand_bias_grad: float32 [4096], P('seg')
- contract_weight_grad: float32 [4096, 1024], P('seg')
- contract_bias_grad: float32 [1024], P('seg')
The draws below stay inside these ranges and needn't reach their ends.
Inputs may be any that keep to these rules, and one draw needn't show every extreme that they name: A segment attends to the last memory_length of its 1024 memory rows; some segments have none and some have all 1024. `value_routes`: the two value experts that a row names for a head differ. `output_routes`: the two output experts that a row names for a head differ.
All inputs are finite; a program needn't handle non-finite values.
Results may differ from the reference program's by a relative error of at most 0.017.
Values may be sent and summed in bfloat16 or wider, within the bound.
A program may use at most 256 MiB of HBM per device.

```python
import jax
import jax.numpy as jnp
from jax import lax

D = 1024
HEADS = 4
DH = 112
EXPERTS = 5
FF = 4096
SEQ = 1024
SEGS = 16


def draw_memory_length(key, part):
    key_kind, key_ragged, key_shuffle = jax.random.split(key, 3)
    length_kind = jax.random.randint(key_kind, (SEGS,), 0, 3)
    ragged = jax.random.randint(key_ragged, (SEGS,), 1, SEQ + 1)
    shuffled = jax.random.permutation(key_shuffle, SEGS)
    length_kind = jnp.where(shuffled == 0, 0, jnp.where(shuffled == 1, 1, length_kind))
    return jnp.where(length_kind == 0, 0, jnp.where(length_kind == 1, SEQ, ragged)).astype(jnp.int32)


def strengthened(drawn, stream_key, source, target, parts, factor):
    def block_of(position):
        return (jnp.arange(drawn.shape[position]) // (drawn.shape[position] // parts)).reshape((-1,) + (1,) * (drawn.ndim - 1 - position))

    one_side = jax.random.permutation(stream_key, parts)[block_of(target)]
    second = (block_of(target) + parts // 2) % parts
    return jnp.where((block_of(source) == one_side) | (block_of(source) == second), factor * drawn, drawn)


def level_of(stream_key, extent, cuts, least, high):
    def one(dim, shards_of):
        steps = jax.random.uniform(jax.random.fold_in(jax.random.fold_in(stream_key, 6), dim), (shards_of,), jnp.float32, least / len(cuts), high / len(cuts))
        return jnp.repeat(jnp.exp(steps), extent[dim] // shards_of).reshape((-1,) + (1,) * (len(extent) - dim - 1))

    level = one(*cuts[0])
    for cut in cuts[1:]:
        level = level * one(*cut)
    return level


def different_ones(own_key, rows, amount, top, lift):
    ranking = jax.random.permutation(jax.random.fold_in(own_key, 1), amount)
    boost = ranking
    for power in range(3):
        boost = boost * boost // amount
    boost = boost * lift // amount
    lots = jax.random.randint(jax.random.fold_in(own_key, 2), (rows, amount), 0, 4096) + boost
    holders = jax.random.permutation(jax.random.fold_in(own_key, 3), rows)[jnp.arange(amount) % rows]
    lots = jnp.where(jnp.arange(rows)[:, None] == holders[None, :], 1 << 14, lots)
    merit = lots * amount + jnp.arange(amount)
    return lax.top_k(merit.astype(jnp.int32), top)[1].astype(jnp.int32)


def noise(stream_key, shape, scale, reach, pieces=(), held_as=jnp.bfloat16):
    values = jax.random.normal(stream_key, shape, jnp.float32) * scale
    if len(pieces) > 0:
        values = level_of(stream_key, shape, pieces, -0.22, 0.18) * values
    return jnp.clip(values, min=-reach, max=reach).astype(held_as)


def noise_with(rng, dims, scale, limit, cuts, heavy, dtype=jnp.bfloat16):
    array = scale * jax.random.normal(rng, dims, jnp.float32)
    if cuts:
        array = array * level_of(rng, dims, cuts, -0.22, 0.18)
    return jnp.clip(strengthened(array, jax.random.fold_in(rng, 3), *heavy), -limit, limit).astype(dtype)


def setup_inputs(seed: int = 0) -> dict:
    key_list = jax.random.split(jax.random.key(seed), 24)
    return {
        "block_input": noise_with(key_list[0], (SEGS, SEQ, D), 1.0, 6.0, ((0, 8), (1, 4)), (0, 2, 8, 2.0)),
        "memory_rows": noise(key_list[1], (SEGS, SEQ, D), 1.0, 6.0, ((0, 8), (1, 4))),
        "memory_length": draw_memory_length(jax.random.fold_in(key_list[23], 71), 0),
        "value_routes": different_ones(key_list[3], SEGS * 2 * SEQ * HEADS, EXPERTS, 2, 3276).reshape((SEGS, 2, SEQ, HEADS, 2)),
        "output_routes": different_ones(key_list[4], SEGS * SEQ * HEADS, EXPERTS, 2, 3276).reshape((SEGS, SEQ, HEADS, 2)),
        "first_gain": jnp.clip(1.0 + 0.1 * jax.random.normal(key_list[5], (D,), jnp.float32), 0.5, 1.5).astype(jnp.bfloat16),
        "first_shift": noise(key_list[6], (D,), 0.2, 1.25),
        "query_weight": noise(key_list[7], (D, HEADS * DH), D ** -0.5, 0.1875),
        "key_weight": noise(key_list[8], (D, HEADS * DH), D ** -0.5, 0.1875),
        "position_weight": noise(key_list[9], (D, HEADS * DH), (D // 2) ** -0.5, 0.25),
        "value_experts": noise(key_list[10], (D, HEADS * EXPERTS * DH), D ** -0.5, 0.1875),
        "value_router": noise(key_list[11], (D, HEADS * EXPERTS), (2 * D) ** -0.5, 0.125),
        "content_bias": noise(key_list[12], (HEADS * DH,), 0.5, 3.0),
        "position_bias": noise(key_list[13], (HEADS * DH,), 0.5, 3.0),
        "output_experts": noise(key_list[14], (HEADS * EXPERTS * DH, D), 1.5, 6.0),
        "output_gate_matrix": noise(key_list[15], (D, HEADS * EXPERTS), (2 * D) ** -0.5, 0.125),
        "second_gain": jnp.clip(1.0 + 0.1 * jax.random.normal(key_list[16], (D,), jnp.float32), 0.5, 1.5).astype(jnp.bfloat16),
        "second_shift": noise(key_list[17], (D,), 0.2, 1.25),
        "up_projection_weight": noise(key_list[18], (D, FF), D ** -0.5, 0.1875),
        "expand_bias": noise(key_list[19], (FF,), 0.2, 1.25),
        "down_projection_weight": noise(key_list[20], (FF, D), (FF // 2) ** -0.5, 0.125),
        "contract_bias": noise(key_list[21], (D,), 0.2, 1.25),
        "output_cotangent": noise(key_list[22], (SEGS, SEQ, D), 1.0, 6.0, ((0, 8), (1, 4))),
    }


@jax.custom_vjp
def low(v):
    return lax.optimization_barrier(v.astype(jnp.bfloat16)).astype(jnp.float32)

@jax.custom_vjp
def low_back(v):
    return v

def low_keep(v):
    return (low(v), None)

def low_pass(kept, grad):
    return (grad,)

def back_keep(v):
    return (v, None)

def back_low(kept, grad):
    return (low(grad),)
low.defvjp(low_keep, low_pass)
low_back.defvjp(back_keep, back_low)
norm_eps = 1e-05
highest = lax.Precision.HIGHEST

def layer_norm(row_data, gain_vec, shift_vec):
    center = row_data - lax.optimization_barrier(jnp.mean(row_data, axis=-1, keepdims=True))
    spread = lax.optimization_barrier(jnp.mean(center * center, axis=-1, keepdims=True))
    return center * lax.rsqrt(spread + norm_eps) * gain_vec + shift_vec

def position_table(row_count, width_count):
    distance = (row_count - 1 - jnp.arange(row_count)).astype(jnp.float32)
    inverse_freq = 10000.0 ** (-jnp.arange(0, width_count, 2).astype(jnp.float32) / width_count)
    angles = distance[:, None] * inverse_freq[None, :]
    return jnp.concatenate([jnp.sin(angles), jnp.cos(angles)], axis=1)

def skew_rows(table_in):
    row_count = table_in.shape[-2]
    col_count = table_in.shape[-1]
    padded = jnp.pad(table_in, [(0, 0)] * (table_in.ndim - 2) + [(0, 0), (0, row_count)])
    flat_rows = padded.reshape(table_in.shape[:-2] + (row_count * (col_count + row_count),))
    shifted = flat_rows[..., row_count - 1:row_count - 1 + row_count * (col_count + row_count - 1)]
    return shifted.reshape(table_in.shape[:-2] + (row_count, col_count + row_count - 1))[..., :col_count]

def key_mask(mem_count):
    query_pos = jnp.arange(SEQ)[:, None]
    key_pos = jnp.arange(2 * SEQ)[None, :]
    return (key_pos <= query_pos + SEQ) & (key_pos >= SEQ - mem_count)

def route_mask(routes, expert_count):
    return lax.optimization_barrier(jnp.sum((routes[..., None] == jnp.arange(expert_count)).astype(jnp.float32), axis=-2))

def segment_forward(params, seg_rows, mem_rows, mem_count, value_pick, out_pick, table_low):
    first_gain, first_shift, query_weight, key_weight, position_weight, value_experts, value_router, content_bias, position_bias, output_experts, output_gate_matrix, second_gain, second_shift, up_projection_weight, expand_bias, down_projection_weight, contract_bias = params
    all_rows = jnp.concatenate([mem_rows, seg_rows], axis=0)
    normed = low(layer_norm(all_rows, first_gain, first_shift))
    segment_normalized = normed[SEQ:]
    query_rows = low_back(jnp.dot(segment_normalized, query_weight, precision=highest))
    key_rows = low_back(low(jnp.dot(normed, key_weight, precision=highest)))
    value_all = low_back(jnp.dot(normed, value_experts, precision=highest)).reshape(2 * SEQ, HEADS, EXPERTS, DH)
    value_logit = low_back(jnp.dot(normed, value_router, precision=highest)).reshape(2 * SEQ, HEADS, EXPERTS)
    value_gate = jax.nn.sigmoid(value_logit) * value_pick
    values = low_back(low(lax.optimization_barrier(jnp.sum(value_gate[..., None] * value_all, axis=2))))
    positions = low_back(low(jnp.dot(table_low, position_weight, precision=highest))).reshape(2 * SEQ, HEADS, DH)
    score_scale = DH ** (-0.5)
    content_query = low((query_rows + content_bias) * score_scale).reshape(SEQ, HEADS, DH)
    position_query = low((query_rows + position_bias) * score_scale).reshape(SEQ, HEADS, DH)
    allowed = key_mask(mem_count)

    def one_head(operands):
        content_head, position_head, keys_head, values_head, rel_head = operands
        content_part = jnp.dot(content_head, keys_head.T, precision=highest)
        rel_part = skew_rows(jnp.dot(position_head, rel_head.T, precision=highest))
        scores = low_back(content_part + rel_part)
        masked = jnp.where(allowed, scores, -1e+30)
        row_max = lax.optimization_barrier(jnp.max(masked, axis=1, keepdims=True))
        weights = jnp.where(allowed, jnp.exp(masked - row_max), 0.0)
        softmax_out = weights / lax.optimization_barrier(jnp.sum(weights, axis=1, keepdims=True))
        return jnp.dot(low(softmax_out), values_head, precision=highest)
    per_head = lax.map(jax.checkpoint(one_head), (jnp.transpose(content_query, (1, 0, 2)), jnp.transpose(position_query, (1, 0, 2)), jnp.transpose(key_rows.reshape(2 * SEQ, HEADS, DH), (1, 0, 2)), jnp.transpose(values, (1, 0, 2)), jnp.transpose(positions, (1, 0, 2))))
    attended = low_back(low(jnp.transpose(per_head, (1, 0, 2))))
    out_logit = low_back(jnp.dot(segment_normalized, output_gate_matrix, precision=highest)).reshape(SEQ, HEADS, EXPERTS)
    out_gate = jax.nn.sigmoid(out_logit) * out_pick
    mixed = low(out_gate[..., None] * attended[:, :, None, :]).reshape(SEQ, HEADS * EXPERTS * DH)
    branch_output = low_back(jnp.dot(mixed, output_experts, precision=highest))
    residual = seg_rows + branch_output
    normed_two = low(layer_norm(residual, second_gain, second_shift))
    pre_act = low_back(jnp.dot(normed_two, up_projection_weight, precision=highest) + expand_bias)
    hidden = low(jax.nn.gelu(pre_act, approximate=True))
    return residual + (jnp.dot(hidden, down_projection_weight, precision=highest) + contract_bias)

def reference(block_input, memory_rows, memory_length, value_routes, output_routes, first_gain, first_shift, query_weight, key_weight, position_weight, value_experts, value_router, content_bias, position_bias, output_experts, output_gate_matrix, second_gain, second_shift, up_projection_weight, expand_bias, down_projection_weight, contract_bias, output_cotangent):
    params = tuple((weight.astype(jnp.float32) for weight in (first_gain, first_shift, query_weight, key_weight, position_weight, value_experts, value_router, content_bias, position_bias, output_experts, output_gate_matrix, second_gain, second_shift, up_projection_weight, expand_bias, down_projection_weight, contract_bias)))
    table_low = low(position_table(2 * SEQ, D))
    value_pick = route_mask(value_routes.reshape(SEGS, 2 * SEQ, HEADS, 2), EXPERTS)
    out_pick = route_mask(output_routes, EXPERTS)

    def one_segment(totals, segment):
        seg_rows, mem_rows, mem_count, value_sel, out_sel, cotangent = segment

        def forward(param_list, rows_now):
            return segment_forward(param_list, rows_now, mem_rows, mem_count, value_sel, out_sel, table_low)
        result, pullback = jax.vjp(forward, params, seg_rows)
        param_grads, row_grad = pullback(cotangent)
        return (jax.tree.map(jnp.add, totals, param_grads), (result, row_grad))
    zero_totals = jax.tree.map(jnp.zeros_like, params)
    totals, (outputs, input_grads) = lax.scan(one_segment, zero_totals, (block_input.astype(jnp.float32), memory_rows.astype(jnp.float32), memory_length, value_pick, out_pick, output_cotangent.astype(jnp.float32)))
    return (outputs.astype(jnp.bfloat16), input_grads.astype(jnp.bfloat16), totals[0], totals[1], totals[2], totals[3], totals[4], totals[5], totals[6], totals[7], totals[8], totals[9], totals[10], totals[11], totals[12], totals[13], totals[14], totals[15], totals[16])
```

```python
import functools

import jax
import jax.numpy as jnp
from jax import lax
from jax.experimental import pallas as pl
from jax.experimental.pallas import tpu as pltpu
from jax.sharding import PartitionSpec as P

D = 1024
HEADS = 4
DH = 112
EXPERTS = 5
SEQ = 1024
norm_eps = 1e-05

NEG=-1e30
def nn(a,b): return lax.dot_general(a,b,(((1,),(0,)),((),())),preferred_element_type=jnp.float32)
def nt(a,b): return lax.dot_general(a,b,(((1,),(1,)),((),())),preferred_element_type=jnp.float32)

def fwd_kernel(len_ref,cq_ref,pq_ref,k_ref,v_ref,pos_ref,p_ref,att_ref,kt_s,v_s,*,tiles,block,rc):
    seg=pl.program_id(0)
    start=tiles*block-len_ref[seg]
    dh=cq_ref.shape[2]
    for half in range(2):
        for t in range(tiles):
            c0=(half*tiles+t)*block
            kt_s[:,c0:c0+block]=k_ref[t,0,half]
            v_s[c0:c0+block,:]=v_ref[t,0,half].T
    mem=tiles*block
    for t in range(tiles):
        w=mem+(t+1)*block
        base=(tiles-1-t)*block
        col=lax.broadcasted_iota(jnp.int32,(1,w),1)
        bias=jnp.where(col>=start,0.0,NEG)
        cqt=cq_ref[t,0].T
        pqt=pq_ref[t,0].T
        for r0 in range(0,block,rc):
            raw=nn(pqt[r0:r0+rc],pos_ref[:,base:])
            rel=pltpu.roll(raw,w-(block-1)+r0,1,stride=1,stride_axis=0)
            s=nn(cqt[r0:r0+rc],kt_s[:,:w])+rel
            row=lax.broadcasted_iota(jnp.int32,(rc,w),0)+(mem+t*block+r0)
            colb=lax.broadcasted_iota(jnp.int32,(rc,w),1)
            s=jnp.where(colb<=row,s+bias,NEG)
            m=jnp.max(s,axis=1,keepdims=True)
            e=jnp.exp(s-m)
            l=jnp.sum(e,axis=1,keepdims=True)
            p=(e*(1.0/l)).astype(jnp.bfloat16)
            p_ref[0,t*block+r0:t*block+r0+rc,:w]=p
        o=nn(p_ref[0,t*block:(t+1)*block,:w],v_s[:w,:])
        att_ref[t,0]=o.astype(jnp.bfloat16).T

def fwd(lengths,cq,pq,k,v,post,rc=64,interpret=False):
    tiles,segs,dh,block=cq.shape
    keys=2*tiles*block
    return pl.pallas_call(
        functools.partial(fwd_kernel,tiles=tiles,block=block,rc=rc),
        grid_spec=pltpu.PrefetchScalarGridSpec(
            num_scalar_prefetch=1,grid=(segs,),
            in_specs=[
                pl.BlockSpec((tiles,1,dh,block),lambda s,_:(0,s,0,0)),
                pl.BlockSpec((tiles,1,dh,block),lambda s,_:(0,s,0,0)),
                pl.BlockSpec((tiles,1,2,dh,block),lambda s,_:(0,s,0,0,0)),
                pl.BlockSpec((tiles,1,2,dh,block),lambda s,_:(0,s,0,0,0)),
                pl.BlockSpec((dh,keys),lambda s,_:(0,0)),
            ],
            out_specs=[
                pl.BlockSpec((1,tiles*block,keys),lambda s,_:(s,0,0)),
                pl.BlockSpec((tiles,1,dh,block),lambda s,_:(0,s,0,0)),
            ],
            scratch_shapes=[pltpu.VMEM((dh,keys),jnp.bfloat16),pltpu.VMEM((keys,dh),jnp.bfloat16)],
        ),
        out_shape=[jax.ShapeDtypeStruct((segs,tiles*block,keys),jnp.bfloat16),jax.ShapeDtypeStruct((tiles,segs,dh,block),jnp.bfloat16)],
        compiler_params=pltpu.CompilerParams(vmem_limit_bytes=56<<20),
        interpret=interpret,
        name="attend",
    )(lengths,cq,pq,k,v,post)

def bwd_kernel(p_ref,g_ref,cq_ref,pq_ref,k_ref,v_ref,pos_ref,dq_ref,dk_ref,dv_ref,dpos_ref,cb_ref,pb_ref,k_s,vt_s,posr_s,dkt,dvt,ds_s,dr_s,*,tiles,block,rc,scale):
    seg=pl.program_id(0)
    for half in range(2):
        for t in range(tiles):
            c0=(half*tiles+t)*block
            k_s[c0:c0+block,:]=k_ref[t,0,half].T
            vt_s[:,c0:c0+block]=v_ref[t,0,half]
    @pl.when(seg==0)
    def _():
        posr_s[...]=pos_ref[...].T
    dkt[...]=jnp.zeros_like(dkt)
    dvt[...]=jnp.zeros_like(dvt)
    dpos_ref[...]=jnp.zeros_like(dpos_ref)
    mem=tiles*block
    flip=(lax.broadcasted_iota(jnp.int32,(block,block),0)+lax.broadcasted_iota(jnp.int32,(block,block),1)==block-1)
    flip_low=flip.astype(jnp.bfloat16)
    flip_wide=flip.astype(jnp.float32)
    cb=jnp.zeros((1,cq_ref.shape[2]),jnp.float32)
    pb=jnp.zeros((1,cq_ref.shape[2]),jnp.float32)
    for t in range(tiles):
        w=mem+(t+1)*block
        base=(tiles-1-t)*block
        gt=g_ref[t,0]
        g=gt.T
        for r0 in range(0,block,rc):
            p=p_ref[0,t*block+r0:t*block+r0+rc,:w].astype(jnp.float32)
            gp=nn(g[r0:r0+rc],vt_s[:,:w])
            prod=p*gp
            delta=jnp.sum(prod,axis=1,keepdims=True)
            ds_s[r0:r0+rc,:w]=(prod-p*delta).astype(jnp.bfloat16)
        ds=ds_s[:,:w]
        for r0 in range(0,block,rc):
            fl=nn(flip_low[r0:r0+rc],ds)
            dr_s[r0:r0+rc,:w]=pltpu.roll(fl,r0,1,stride=1,stride_axis=0).astype(jnp.bfloat16)
        dr=dr_s[:,:w]
        dvt[:,:w]+=nn(gt,p_ref[0,t*block:(t+1)*block,:w])
        dkt[:,:w]+=nn(cq_ref[t,0],ds)
        pqf=nn(pq_ref[t,0],flip_low).astype(jnp.bfloat16)
        dpos_ref[0,:,base:]+=nn(pqf,dr)
        dc=nn(ds,k_s[:w,:])
        dp=nn(dr,posr_s[base:,:])
        cb=cb+jnp.sum(dc,axis=0,keepdims=True)
        pb=pb+jnp.sum(dp,axis=0,keepdims=True)
        dpn=lax.dot_general(flip_wide,dp,(((1,),(0,)),((),())),precision=lax.Precision.HIGHEST,preferred_element_type=jnp.float32)
        dq_ref[t,0]=((dc+dpn)*scale).astype(jnp.bfloat16).T
    cb_ref[0]=cb*scale
    pb_ref[0]=pb*scale
    for half in range(2):
        for t in range(tiles):
            c0=(half*tiles+t)*block
            dk_ref[t,0,half]=dkt[:,c0:c0+block].astype(jnp.bfloat16)
            dv_ref[t,0,half]=dvt[:,c0:c0+block].astype(jnp.bfloat16)

def bwd(p,g,cq,pq,k,v,post,scale,rc=64,interpret=False):
    tiles,segs,dh,block=cq.shape
    keys=2*tiles*block
    qs=pl.BlockSpec((tiles,1,dh,block),lambda s:(0,s,0,0))
    ks=pl.BlockSpec((tiles,1,2,dh,block),lambda s:(0,s,0,0,0))
    bs=pl.BlockSpec((1,1,dh),lambda s:(s,0,0))
    low=jnp.bfloat16; f32=jnp.float32
    return pl.pallas_call(
        functools.partial(bwd_kernel,tiles=tiles,block=block,rc=rc,scale=scale),
        grid=(segs,),
        in_specs=[pl.BlockSpec((1,tiles*block,keys),lambda s:(s,0,0)),qs,qs,qs,ks,ks,pl.BlockSpec((dh,keys),lambda s:(0,0))],
        out_specs=[qs,ks,ks,pl.BlockSpec((1,dh,keys),lambda s:(s,0,0)),bs,bs],
        out_shape=[jax.ShapeDtypeStruct(cq.shape,low),jax.ShapeDtypeStruct(k.shape,low),jax.ShapeDtypeStruct(k.shape,low),jax.ShapeDtypeStruct((segs,dh,keys),f32),jax.ShapeDtypeStruct((segs,1,dh),f32),jax.ShapeDtypeStruct((segs,1,dh),f32)],
        scratch_shapes=[pltpu.VMEM((keys,dh),low),pltpu.VMEM((dh,keys),low),pltpu.VMEM((keys,dh),low),pltpu.VMEM((dh,keys),f32),pltpu.VMEM((dh,keys),f32),pltpu.VMEM((block,keys),low),pltpu.VMEM((block,keys),low)],
        compiler_params=pltpu.CompilerParams(vmem_limit_bytes=60<<20),
        interpret=interpret,
        name="attend_back",
    )(p,g,cq,pq,k,v,post)


def to_low(value):
    return value.astype(jnp.bfloat16)


def to_wide(value):
    return value.astype(jnp.float32)


def smooth_act(value):
    return jax.nn.gelu(value, approximate=True)


def mm(spec, left, right):
    return jnp.einsum(spec, left, right, preferred_element_type=jnp.float32)


def layer_norm_parts(row_data, gain_vec, shift_vec):
    center = row_data - jnp.mean(row_data, axis=-1, keepdims=True)
    inv_std = lax.rsqrt(jnp.mean(center * center, axis=-1, keepdims=True) + norm_eps)
    unit_rows = center * inv_std
    return (unit_rows * gain_vec + shift_vec, unit_rows, inv_std)


def layer_norm_back(grad_rows, unit_rows, inv_std, gain_vec):
    grad_unit = grad_rows * gain_vec
    mean_grad = jnp.mean(grad_unit, axis=-1, keepdims=True)
    mean_proj = jnp.mean(grad_unit * unit_rows, axis=-1, keepdims=True)
    return inv_std * (grad_unit - mean_grad - unit_rows * mean_proj)


def position_table(row_count, width_count):
    fine = 64
    inverse_freq = 10000.0 ** (-jnp.arange(0, width_count, 2).astype(jnp.float32) / width_count)
    high = (row_count // fine - 1 - jnp.arange(row_count // fine)) * fine
    low_part = fine - 1 - jnp.arange(fine)
    high_angle = high.astype(jnp.float32)[:, None, None] * inverse_freq
    low_angle = low_part.astype(jnp.float32)[None, :, None] * inverse_freq
    high_sin, high_cos = jnp.sin(high_angle), jnp.cos(high_angle)
    low_sin, low_cos = jnp.sin(low_angle), jnp.cos(low_angle)
    sines = high_sin * low_cos + high_cos * low_sin
    cosines = high_cos * low_cos - high_sin * low_sin
    return to_low(jnp.concatenate([sines, cosines], axis=2)).reshape(row_count, width_count)


def route_mask(routes, expert_count):
    return jnp.sum((routes[..., None] == jnp.arange(expert_count)).astype(jnp.float32), axis=-2)


def bit_of(axis, bit):
    return (lax.axis_index(axis) // bit) % 2


def swap(value, axis, bit):
    pairs = [(i, i ^ bit) for i in range(lax.axis_size(axis))]
    return lax.ppermute(value, axis, pairs)


def pick(value, index, axis):
    return lax.dynamic_index_in_dim(value, index, axis, keepdims=False)


def axis_bits(axis):
    size = lax.axis_size(axis)
    return [1 << k for k in range(size.bit_length() - 1)]


def halve(part, axis, bit, dim):
    mine = bit_of(axis, bit)
    other = swap(pick(part, 1 - mine, dim), axis, bit)
    return to_low(to_wide(pick(part, mine, dim)) + to_wide(other))


def halve_seg(part):
    for bit in axis_bits("seg"):
        part = part.reshape((part.shape[0] // 2, 2) + part.shape[1:])
        part = halve(part, "seg", bit, 1)
    return part[0]


def widen(part, axis, bit, dim):
    mine = bit_of(axis, bit)
    other = swap(part, axis, bit)
    first = jnp.where(mine == 0, part, other)
    second = jnp.where(mine == 0, other, part)
    return jnp.concatenate([first, second], axis=dim)


def scatter_columns(left, right, seg_size, pos_first):
    full = right.shape[1]
    bits = axis_bits("pos")
    n = left.shape[1]
    core = bits[0]
    core_mine = bit_of("pos", core)
    halves = right.reshape(right.shape[0], 2, full // 2)
    kept = pick(halves, core_mine, 1)
    sent = pick(halves, 1 - core_mine, 1)
    got = swap(to_low(mm("rn,rm->nm", left, sent)), "pos", core)
    if pos_first:
        width = full // 2
        rest = bits[1:]
        for bit in rest:
            mine = bit_of("pos", bit)
            kept_pair = kept.reshape(kept.shape[0], 2, width // 2)
            got_pair = got.reshape(n, 2, width // 2)
            go = to_low(mm("rn,rm->nm", left, pick(kept_pair, 1 - mine, 1)) + to_wide(pick(got_pair, 1 - mine, 1)))
            come = swap(go, "pos", bit)
            kept = pick(kept_pair, mine, 1)
            got = to_low(to_wide(pick(got_pair, mine, 1)) + to_wide(come))
            width //= 2
        part = to_low(mm("rn,rm->nm", left, kept) + to_wide(got))
        part = halve_seg(part.reshape(seg_size, n // seg_size, width))
        for bit in reversed(rest):
            part = widen(part, "pos", bit, 1)
    else:
        width = full // 2
        bit = axis_bits("seg")[0]
        mine = bit_of("seg", bit)
        view = left.reshape(left.shape[0], seg_size // 2, 2, n // seg_size)
        got_view = got.reshape(seg_size // 2, 2, n // seg_size, width)
        go = to_low(mm("ran,rm->anm", pick(view, 1 - mine, 2), kept) + to_wide(pick(got_view, 1 - mine, 1)))
        come = swap(go, "seg", bit)
        part = mm("ran,rm->anm", pick(view, mine, 2), kept) + to_wide(pick(got_view, mine, 1)) + to_wide(come)
        part = to_low(part)
        for bit in axis_bits("seg")[1:]:
            part = part.reshape((part.shape[0] // 2, 2) + part.shape[1:])
            part = halve(part, "seg", bit, 1)
        part = part[0]
        for bit in bits[1:]:
            part = to_low(to_wide(part) + to_wide(swap(part, "pos", bit)))
    return to_wide(widen(part, "pos", core, 1))


def scatter_rows(whole, seg_size):
    n, width = whole.shape
    share = n // seg_size
    part = whole
    bits = axis_bits("pos")
    part = part.reshape(seg_size, share, width)
    for bit in bits:
        part = part.reshape(seg_size, 2, part.shape[1] // 2, width)
        part = halve(part, "pos", bit, 1)
    part = halve_seg(part)
    for bit in reversed(bits):
        part = widen(part, "pos", bit, 0)
    return to_wide(part)


def scatter_vectors(vectors, seg_size):
    flat = jnp.concatenate([v.reshape(seg_size, -1) for v in vectors], axis=1)
    part = flat
    for bit in axis_bits("seg"):
        part = part.reshape((part.shape[0] // 2, 2) + part.shape[1:])
        mine = bit_of("seg", bit)
        part = pick(part, mine, 1) + swap(pick(part, 1 - mine, 1), "seg", bit)
    for bit in axis_bits("pos"):
        part = part + swap(part, "pos", bit)
    out = []
    start = 0
    for v in vectors:
        size = v.size // seg_size
        out.append(part[0, start : start + size].reshape((v.shape[0] // seg_size,) + v.shape[1:]))
        start += size
    return out


def local(
    block_input,
    memory_rows,
    memory_length,
    value_routes,
    output_routes,
    first_gain,
    first_shift,
    query_weight,
    key_weight,
    position_weight,
    value_experts,
    value_router,
    content_bias,
    position_bias,
    output_experts,
    output_gate_matrix,
    second_gain,
    second_shift,
    up_projection_weight,
    expand_bias,
    down_projection_weight,
    contract_bias,
    output_cotangent,
):
    seg_count = block_input.shape[0]
    local_rows = block_input.shape[1]
    seg_size = lax.axis_size("seg")
    pos_index = lax.axis_index("pos")
    key_count = 2 * SEQ
    all_rows = seg_count * local_rows
    score_scale = DH ** (-0.5)
    gain_one = to_wide(first_gain)
    shift_one = to_wide(first_shift)
    gain_two = to_wide(second_gain)
    shift_two = to_wide(second_shift)
    rows_in = to_wide(jnp.stack([memory_rows, block_input], axis=1))
    normed, unit_one, inv_one = layer_norm_parts(rows_in, gain_one, shift_one)
    normed_low = to_low(normed)
    segment_normalized = normed_low[:, 1]
    query_triple = query_weight.reshape(D, HEADS, DH)
    key_triple = key_weight.reshape(D, HEADS, DH)
    query_rows = mm("sld,dhc->hscl", segment_normalized, query_triple)
    bias_content = to_wide(content_bias).reshape(HEADS, 1, DH, 1)
    bias_position = to_wide(position_bias).reshape(HEADS, 1, DH, 1)
    content_seq = to_low((query_rows + bias_content) * score_scale)
    position_seq = to_low((query_rows + bias_position) * score_scale)
    key_rows = to_low(mm("srld,dhc->hsrcl", normed_low, key_triple))

    def trade(value):
        return lax.all_to_all(value, "pos", split_axis=0, concat_axis=0, tiled=True)

    content_query = trade(content_seq)
    position_query = trade(position_seq)
    keys = trade(key_rows)
    value_all = mm("srld,dk->srkl", normed_low, value_experts)
    value_all = value_all.reshape(seg_count, 2, HEADS, EXPERTS, DH, local_rows)
    value_logit = mm("srld,dk->srkl", normed_low, value_router)
    value_sig = jax.nn.sigmoid(value_logit.reshape(seg_count, 2, HEADS, EXPERTS, local_rows))
    value_pick = jnp.transpose(route_mask(value_routes, EXPERTS), (0, 1, 3, 4, 2))
    value_gate = value_sig * value_pick
    values_seq = jnp.sum(value_gate[:, :, :, :, None, :] * value_all, axis=3)
    values = trade(to_low(jnp.transpose(values_seq, (2, 0, 1, 3, 4))))

    table_low = position_table(key_count, D)
    weight_local = pick(position_weight.reshape(D, HEADS, DH), pos_index, 1)
    positions = to_low(mm("nd,dc->cn", table_low, weight_local))

    probs, attended_heads = fwd(
        memory_length, content_query, position_query, keys, values, positions
    )
    attended = jnp.transpose(trade(attended_heads), (1, 0, 2, 3))

    out_logit = mm("put,tj->pju", segment_normalized, output_gate_matrix)
    out_sig = jax.nn.sigmoid(out_logit.reshape(seg_count, HEADS, EXPERTS, local_rows))
    out_pick = jnp.transpose(route_mask(output_routes, EXPERTS), (0, 2, 3, 1))
    out_gate = out_sig * out_pick
    attended_wide = to_wide(attended)
    mixed = to_low(out_gate[:, :, :, None, :] * attended_wide[:, :, None, :, :])
    mixed = mixed.reshape(seg_count, HEADS * EXPERTS * DH, local_rows)
    branch_output = mm("wkm,ko->wmo", mixed, output_experts)
    residual = to_wide(block_input) + branch_output
    normed_two, unit_two, inv_two = layer_norm_parts(residual, gain_two, shift_two)
    second_low = to_low(normed_two)
    pre_act = mm("wgq,qz->wgz", second_low, up_projection_weight) + to_wide(expand_bias)
    activated, act_back = jax.vjp(smooth_act, pre_act)
    hidden = to_low(activated)
    ffn_rows = mm("qhn,ne->qhe", hidden, down_projection_weight)
    block_output = to_low(residual + ffn_rows + to_wide(contract_bias))

    grad_out = to_wide(output_cotangent)
    contract_bias_grad = jnp.sum(grad_out, axis=(0, 1))
    hidden_rows = hidden.reshape(all_rows, -1)
    cotangent_rows = output_cotangent.reshape(all_rows, D)
    contract_weight_grad = scatter_columns(hidden_rows, cotangent_rows, seg_size, True)

    grad_hidden = mm("pic,ec->pie", output_cotangent, down_projection_weight)
    grad_pre = to_low(act_back(grad_hidden)[0])
    expand_bias_grad = jnp.sum(to_wide(grad_pre), axis=(0, 1))
    expand_weight_grad = scatter_columns(
        second_low.reshape(all_rows, D), grad_pre.reshape(all_rows, -1), seg_size, False
    )
    grad_normed_two = mm("uke,me->ukm", grad_pre, up_projection_weight)
    second_gain_grad = jnp.sum(grad_normed_two * unit_two, axis=(0, 1))
    second_shift_grad = jnp.sum(grad_normed_two, axis=(0, 1))
    grad_residual = grad_out + layer_norm_back(grad_normed_two, unit_two, inv_two, gain_two)
    grad_branch = to_low(grad_residual)
    mixed_rows = jnp.transpose(mixed, (0, 2, 1)).reshape(all_rows, HEADS * EXPERTS * DH)
    output_experts_grad = scatter_columns(
        mixed_rows, grad_branch.reshape(all_rows, D), seg_size, False
    )
    grad_mixed = mm("byv,kv->bky", grad_branch, output_experts)
    grad_mixed = grad_mixed.reshape(seg_count, HEADS, EXPERTS, DH, local_rows)
    grad_out_gate = jnp.sum(grad_mixed * attended_wide[:, :, None, :, :], axis=3)
    grad_attended = to_low(jnp.sum(grad_mixed * out_gate[:, :, :, None, :], axis=2))
    grad_heads = trade(jnp.transpose(grad_attended, (1, 0, 2, 3)))
    grad_out_logit = to_low(grad_out_gate * out_pick * out_sig * (1.0 - out_sig))
    grad_out_logit = grad_out_logit.reshape(seg_count, HEADS * EXPERTS, local_rows)
    output_router_grad = mm("sld,sjl->dj", segment_normalized, grad_out_logit)
    grad_seg_normed = mm("sjl,dj->sld", grad_out_logit, output_gate_matrix)

    grad_query, grad_keys, grad_values, grad_rel, content_part, position_part = bwd(
        probs, grad_heads, content_query, position_query, keys, values, positions, score_scale
    )

    head_hot = (jnp.arange(HEADS) == pos_index).astype(jnp.float32)[:, None]
    content_bias_grad = (head_hot * jnp.sum(content_part, axis=0)).reshape(HEADS * DH)
    position_bias_grad = (head_hot * jnp.sum(position_part, axis=0)).reshape(HEADS * DH)
    weight_part = mm("nd,snc->dc", table_low, jnp.transpose(to_low(grad_rel), (0, 2, 1)))
    position_weight_grad = (head_hot * weight_part[:, None, :]).reshape(D, HEADS * DH)

    grad_query = trade(grad_query)
    grad_keys = trade(grad_keys)
    grad_values = trade(grad_values)
    query_weight_grad = mm("sld,hscl->dhc", segment_normalized, grad_query).reshape(D, HEADS * DH)
    grad_seg_normed = grad_seg_normed + mm("hscl,dhc->sld", grad_query, query_triple)
    key_weight_grad = mm("srld,hsrcl->dhc", normed_low, grad_keys).reshape(D, HEADS * DH)
    grad_normed = mm("hsrcl,dhc->srld", grad_keys, key_triple)
    grad_values_wide = to_wide(jnp.transpose(grad_values, (1, 2, 0, 3, 4)))[:, :, :, None]
    grad_experts = to_low(value_gate[:, :, :, :, None, :] * grad_values_wide)
    grad_experts = grad_experts.reshape(seg_count, 2, HEADS * EXPERTS * DH, local_rows)
    value_experts_grad = mm("srld,srkl->dk", normed_low, grad_experts)
    grad_normed = grad_normed + mm("srkl,dk->srld", grad_experts, value_experts)
    grad_value_gate = jnp.sum(value_all * grad_values_wide, axis=4)
    grad_value_logit = to_low(grad_value_gate * value_pick * value_sig * (1.0 - value_sig))
    grad_value_logit = grad_value_logit.reshape(seg_count, 2, HEADS * EXPERTS, local_rows)
    value_router_grad = mm("srld,srjl->dj", normed_low, grad_value_logit)
    grad_normed = grad_normed + mm("srjl,dj->srld", grad_value_logit, value_router)
    grad_normed = grad_normed.at[:, 1].add(grad_seg_normed)
    first_gain_grad = jnp.sum(grad_normed * unit_one, axis=(0, 1, 2))
    first_shift_grad = jnp.sum(grad_normed, axis=(0, 1, 2))
    grad_rows = layer_norm_back(grad_normed, unit_one, inv_one, gain_one)
    input_grad = to_low(grad_residual + grad_rows[:, 1])

    late = [value_experts_grad, query_weight_grad, key_weight_grad, position_weight_grad]
    late += [value_router_grad, output_router_grad]
    late_sum = scatter_rows(to_low(jnp.concatenate(late, axis=1)), seg_size)
    late_out = []
    start = 0
    for item in late:
        late_out.append(late_sum[:, start : start + item.shape[1]])
        start += item.shape[1]
    vectors = scatter_vectors(
        [
            first_gain_grad,
            first_shift_grad,
            content_bias_grad,
            position_bias_grad,
            second_gain_grad,
            second_shift_grad,
            expand_bias_grad,
            contract_bias_grad,
        ],
        seg_size,
    )
    return (
        block_output,
        input_grad,
        vectors[0],
        vectors[1],
        late_out[1],
        late_out[2],
        late_out[3],
        late_out[0],
        late_out[4],
        vectors[2],
        vectors[3],
        output_experts_grad,
        late_out[5],
        vectors[4],
        vectors[5],
        expand_weight_grad,
        vectors[6],
        contract_weight_grad,
        vectors[7],
    )


def solution(mesh):
    rows = P("seg", "pos", None)
    whole = P()
    placed = (
        rows,
        rows,
        P("seg"),
        P("seg", None, "pos", None, None),
        P("seg", "pos", None, None),
    )
    placed += (whole,) * 17 + (rows,)
    shares = [P("seg")] * 17
    for index in (2, 3, 4, 5, 6, 9, 10, 13, 15):
        shares[index] = P("seg", None)
    return jax.shard_map(
        local,
        mesh=mesh,
        in_specs=placed,
        out_specs=(rows, rows) + tuple(shares),
        check_vma=False,
    )
```

```python
import functools

import jax
import jax.numpy as jnp
from jax import lax
from jax.experimental import pallas as pl
from jax.experimental.pallas import tpu as pltpu
from jax.sharding import PartitionSpec as P

D = 1024
HEADS = 4
DH = 112
EXPERTS = 5
SEQ = 1024
norm_eps = 1e-05

NEG = -1e30
LANES = 128


def nn(left, right):
    return lax.dot_general(left, right, (((1,), (0,)), ((), ())), preferred_element_type=jnp.float32)


def nt(left, right):
    return lax.dot_general(left, right, (((1,), (1,)), ((), ())), preferred_element_type=jnp.float32)


def to_low(value):
    return value.astype(jnp.bfloat16)


def to_wide(value):
    return value.astype(jnp.float32)


def norm_parts(rows):
    center = rows - jnp.mean(rows, axis=1, keepdims=True)
    inv_std = lax.rsqrt(jnp.mean(center * center, axis=1, keepdims=True) + norm_eps)
    return center * inv_std, inv_std


def once(shape, index_map):
    return pl.BlockSpec(shape, index_map, pipeline_mode=pl.Buffered(1))


def params(megabytes):
    return pltpu.CompilerParams(vmem_limit_bytes=megabytes << 20)


def project_kernel(
    mem_ref, blk_ref, gain_ref, shift_ref, wq_ref, wk_ref, gates_ref, cbias_ref, pbias_ref, pickv_ref, picko_ref,
    qk_ref, norm_ref, gatev_ref, gateo_ref, wqt, wkt, gatest, *, scale,
):
    half = pl.program_id(1)

    @pl.when((pl.program_id(0) == 0) & (half == 0))
    def _():
        wqt[...] = wq_ref[...].T
        wkt[...] = wk_ref[...].T
        gatest[...] = gates_ref[...].T

    rows = to_wide(jnp.where(half == 0, mem_ref[0], blk_ref[0]))
    unit, _ = norm_parts(rows)
    normed = to_low(unit * to_wide(gain_ref[...]) + to_wide(shift_ref[...]))
    norm_ref[0, 0] = normed
    turned = normed.T
    keys = to_low(nn(wkt[...], turned))
    dh = qk_ref.shape[3]
    logits = nn(gatest[...], turned)
    gatev_ref[0, 0] = jax.nn.sigmoid(logits[: pickv_ref.shape[2]]) * pickv_ref[0, 0]

    @pl.when(half == 0)
    def _():
        for h in range(qk_ref.shape[0]):
            qk_ref[h, 0, 2] = keys[h * dh : (h + 1) * dh]

    @pl.when(half == 1)
    def _():
        query = nn(wqt[...], turned)
        content = to_low((query + cbias_ref[...]) * scale)
        position = to_low((query + pbias_ref[...]) * scale)
        for h in range(qk_ref.shape[0]):
            qk_ref[h, 0, 0] = content[h * dh : (h + 1) * dh]
            qk_ref[h, 0, 1] = position[h * dh : (h + 1) * dh]
            qk_ref[h, 0, 3] = keys[h * dh : (h + 1) * dh]
        gateo_ref[0] = jax.nn.sigmoid(logits[logits.shape[0] // 2 :][: picko_ref.shape[1]]) * picko_ref[0]


def project(mem, blk, gain, shift, wq, wk, gates, cbias, pbias, pickv, picko, scale):
    segs, rows, width = blk.shape
    inner = wq.shape[1]
    slots = pickv.shape[2]
    low, f32 = jnp.bfloat16, jnp.float32
    dh = inner // HEADS
    flat = lambda s, r: (0, 0)
    row_spec = pl.BlockSpec((1, rows, width), lambda s, r: (s, 0, 0))
    return pl.pallas_call(
        functools.partial(project_kernel, scale=scale),
        grid=(segs, 2),
        in_specs=[
            row_spec,
            row_spec,
            pl.BlockSpec((1, width), flat),
            pl.BlockSpec((1, width), flat),
            once((width, inner), flat),
            once((width, inner), flat),
            once(gates.shape, flat),
            pl.BlockSpec((inner, 1), flat),
            pl.BlockSpec((inner, 1), flat),
            pl.BlockSpec((1, 1, slots, rows), lambda s, r: (s, r, 0, 0)),
            pl.BlockSpec((1, slots, rows), lambda s, r: (s, 0, 0)),
        ],
        out_specs=[
            pl.BlockSpec((HEADS, 1, 4, dh, rows), lambda s, r: (0, s, 0, 0, 0)),
            pl.BlockSpec((1, 1, rows, width), lambda s, r: (s, r, 0, 0)),
            pl.BlockSpec((1, 1, slots, rows), lambda s, r: (s, r, 0, 0)),
            pl.BlockSpec((1, slots, rows), lambda s, r: (s, 0, 0)),
        ],
        out_shape=[
            jax.ShapeDtypeStruct((HEADS, segs, 4, dh, rows), low),
            jax.ShapeDtypeStruct((segs, 2, rows, width), low),
            jax.ShapeDtypeStruct((segs, 2, slots, rows), f32),
            jax.ShapeDtypeStruct((segs, slots, rows), f32),
        ],
        scratch_shapes=[
            pltpu.VMEM((inner, width), low),
            pltpu.VMEM((inner, width), low),
            pltpu.VMEM((gates.shape[1], width), low),
        ],
        compiler_params=params(48),
        cost_estimate=pl.CostEstimate(flops=3 * 10**9, bytes_accessed=8 * 10**6, transcendentals=0),
        name="project",
    )(mem, blk, gain, shift, wq, wk, gates, cbias, pbias, pickv, picko)


def experts_kernel(norm_ref, ve_ref, gate_ref, v_ref, all_ref, vet):
    @pl.when((pl.program_id(0) == 0) & (pl.program_id(1) == 0))
    def _():
        vet[...] = ve_ref[...].T

    turned = norm_ref[0, 0].T
    heads, dh = v_ref.shape[0], v_ref.shape[3]
    for h in range(heads):
        group = nn(vet[h * EXPERTS * dh : (h + 1) * EXPERTS * dh], turned)
        all_ref[0, 0, h * EXPERTS * dh : (h + 1) * EXPERTS * dh] = to_low(group)
        total = jnp.zeros((dh, turned.shape[1]), jnp.float32)
        for e in range(EXPERTS):
            slot = h * EXPERTS + e
            total = total + gate_ref[0, 0, slot : slot + 1] * group[e * dh : (e + 1) * dh]
        v_ref[h, 0, 0] = to_low(total)


def experts(normed, ve, gate):
    segs, _, rows, width = normed.shape
    inner = ve.shape[1]
    slots = gate.shape[2]
    dh = inner // (HEADS * EXPERTS)
    low = jnp.bfloat16
    return pl.pallas_call(
        experts_kernel,
        grid=(segs, 2),
        in_specs=[
            pl.BlockSpec((1, 1, rows, width), lambda s, r: (s, r, 0, 0)),
            once((width, inner), lambda s, r: (0, 0)),
            pl.BlockSpec((1, 1, slots, rows), lambda s, r: (s, r, 0, 0)),
        ],
        out_specs=[
            pl.BlockSpec((HEADS, 1, 1, dh, rows), lambda s, r: (0, s, r, 0, 0)),
            pl.BlockSpec((1, 1, inner, rows), lambda s, r: (s, r, 0, 0)),
        ],
        out_shape=[
            jax.ShapeDtypeStruct((HEADS, segs, 2, dh, rows), low),
            jax.ShapeDtypeStruct((segs, 2, inner, rows), low),
        ],
        scratch_shapes=[pltpu.VMEM((inner, width), low)],
        compiler_params=params(48),
        cost_estimate=pl.CostEstimate(flops=5 * 10**9, bytes_accessed=12 * 10**6, transcendentals=0),
        name="experts",
    )(normed, ve, gate)


def score_kernel(len_ref, qk_ref, pos_ref, p_ref, kt_s, *, tiles, block, chunk):
    seg = pl.program_id(0)
    start = tiles * block - len_ref[seg]
    for half in range(2):
        for t in range(tiles):
            c0 = (half * tiles + t) * block
            kt_s[:, c0 : c0 + block] = qk_ref[t, 0, 2 + half]
    mem = tiles * block
    for t in range(tiles):
        w = mem + (t + 1) * block
        base = (tiles - 1 - t) * block
        col = lax.broadcasted_iota(jnp.int32, (1, w), 1)
        bias = jnp.where(col >= start, 0.0, NEG)
        content = qk_ref[t, 0, 0].T
        position = qk_ref[t, 0, 1].T
        for r0 in range(0, block, chunk):
            raw = nn(position[r0 : r0 + chunk], pos_ref[:, base:])
            rel = pltpu.roll(raw, w - (block - 1) + r0, 1, stride=1, stride_axis=0)
            s = nn(content[r0 : r0 + chunk], kt_s[:, :w]) + rel
            row = lax.broadcasted_iota(jnp.int32, (chunk, w), 0) + (mem + t * block + r0)
            col_wide = lax.broadcasted_iota(jnp.int32, (chunk, w), 1)
            s = jnp.where(col_wide <= row, s + bias, NEG)
            e = jnp.exp(s - jnp.max(s, axis=1, keepdims=True))
            p = e * (1.0 / jnp.sum(e, axis=1, keepdims=True))
            p_ref[0, t * block + r0 : t * block + r0 + chunk, :w] = to_low(p)


def score(lengths, qk, post):
    tiles, segs, _, dh, block = qk.shape
    keys = 2 * tiles * block
    return pl.pallas_call(
        functools.partial(score_kernel, tiles=tiles, block=block, chunk=64),
        grid_spec=pltpu.PrefetchScalarGridSpec(
            num_scalar_prefetch=1,
            grid=(segs,),
            in_specs=[
                pl.BlockSpec((tiles, 1, 4, dh, block), lambda s, _: (0, s, 0, 0, 0)),
                pl.BlockSpec((dh, keys), lambda s, _: (0, 0)),
            ],
            out_specs=pl.BlockSpec((1, tiles * block, keys), lambda s, _: (s, 0, 0)),
            scratch_shapes=[pltpu.VMEM((dh, keys), jnp.bfloat16)],
        ),
        out_shape=jax.ShapeDtypeStruct((segs, tiles * block, keys), jnp.bfloat16),
        compiler_params=params(48),
        cost_estimate=pl.CostEstimate(flops=12 * 10**9, bytes_accessed=10 * 10**6, transcendentals=4 * 10**6),
        name="score",
    )(lengths, qk, post)


def attend_kernel(p_ref, v_ref, att_ref, v_s, *, tiles, block):
    for half in range(2):
        for t in range(tiles):
            c0 = (half * tiles + t) * block
            v_s[c0 : c0 + block, :] = v_ref[t, 0, half].T
    for t in range(tiles):
        w = tiles * block + (t + 1) * block
        out = nn(p_ref[0, t * block : (t + 1) * block, :w], v_s[:w, :])
        att_ref[t, 0] = to_low(out).T


def attend(p, v):
    tiles, segs, _, dh, block = v.shape
    keys = 2 * tiles * block
    return pl.pallas_call(
        functools.partial(attend_kernel, tiles=tiles, block=block),
        grid=(segs,),
        in_specs=[
            pl.BlockSpec((1, tiles * block, keys), lambda s: (s, 0, 0)),
            pl.BlockSpec((tiles, 1, 2, dh, block), lambda s: (0, s, 0, 0, 0)),
        ],
        out_specs=pl.BlockSpec((tiles, 1, dh, block), lambda s: (0, s, 0, 0)),
        out_shape=jax.ShapeDtypeStruct((tiles, segs, dh, block), jnp.bfloat16),
        scratch_shapes=[pltpu.VMEM((keys, dh), jnp.bfloat16)],
        compiler_params=params(48),
        cost_estimate=pl.CostEstimate(flops=5 * 10**9, bytes_accessed=9 * 10**6, transcendentals=0),
        name="attend",
    )(p, v)


def attend_back_kernel(
    p_ref, g_ref, qk_ref, v_ref, pos_ref, dqk_ref, dv_ref, dpos_ref, sums_ref,
    k_s, vt_s, posr_s, dkt, dvt, dpt, ds_s, dr_s, *, tiles, block, chunk, scale,
):
    seg = pl.program_id(0)
    for half in range(2):
        for t in range(tiles):
            c0 = (half * tiles + t) * block
            k_s[c0 : c0 + block, :] = qk_ref[t, 0, 2 + half].T
            vt_s[:, c0 : c0 + block] = v_ref[t, 0, half]

    @pl.when(seg == 0)
    def _():
        posr_s[...] = pos_ref[...].T

    dkt[...] = jnp.zeros_like(dkt)
    dvt[...] = jnp.zeros_like(dvt)
    dpt[...] = jnp.zeros_like(dpt)
    mem = tiles * block
    dh = v_ref.shape[3]
    flip = (
        lax.broadcasted_iota(jnp.int32, (block, block), 0) + lax.broadcasted_iota(jnp.int32, (block, block), 1)
        == block - 1
    )
    flip_wide = jnp.where(flip, 1.0, 0.0)
    flip_low = to_low(flip_wide)
    content_sum = jnp.zeros((1, dh), jnp.float32)
    position_sum = jnp.zeros((1, dh), jnp.float32)
    for t in range(tiles):
        w = mem + (t + 1) * block
        base = (tiles - 1 - t) * block
        gt = g_ref[t, 0]
        g = gt.T
        for r0 in range(0, block, chunk):
            p = to_wide(p_ref[0, t * block + r0 : t * block + r0 + chunk, :w])
            prod = p * nn(g[r0 : r0 + chunk], vt_s[:, :w])
            delta = jnp.sum(prod, axis=1, keepdims=True)
            ds_s[r0 : r0 + chunk, :w] = to_low(prod - p * delta)
        ds = ds_s[:, :w]
        for r0 in range(0, block, chunk):
            turned = nn(flip_low[r0 : r0 + chunk], ds)
            dr_s[r0 : r0 + chunk, :w] = to_low(pltpu.roll(turned, r0, 1, stride=1, stride_axis=0))
        dr = dr_s[:, :w]
        dvt[:, :w] += nn(gt, p_ref[0, t * block : (t + 1) * block, :w])
        dkt[:, :w] += nn(qk_ref[t, 0, 0], ds)
        position = to_low(nn(qk_ref[t, 0, 1], flip_low))
        dpt[:, base:] += nn(position, dr)
        dc = nn(ds, k_s[:w, :])
        dp = nn(dr, posr_s[base:, :])
        content_sum = content_sum + jnp.sum(dc, axis=0, keepdims=True)
        position_sum = position_sum + jnp.sum(dp, axis=0, keepdims=True)
        dp = lax.dot_general(
            flip_wide,
            dp,
            (((1,), (0,)), ((), ())),
            precision=lax.Precision.HIGHEST,
            preferred_element_type=jnp.float32,
        )
        dqk_ref[t, 0, 0] = to_low((dc + dp) * scale).T
    sums_ref[0, 0:1] = content_sum * scale
    sums_ref[0, 1:2] = position_sum * scale
    dpos_ref[0] = to_low(dpt[...])
    for half in range(2):
        for t in range(tiles):
            c0 = (half * tiles + t) * block
            dqk_ref[t, 0, 1 + half] = to_low(dkt[:, c0 : c0 + block])
            dv_ref[t, 0, half] = to_low(dvt[:, c0 : c0 + block])


def attend_back(p, g, qk, v, post, scale):
    tiles, segs, dh, block = g.shape
    keys = 2 * tiles * block
    low, f32 = jnp.bfloat16, jnp.float32

    def spec(parts):
        return pl.BlockSpec((tiles, 1, parts, dh, block), lambda s: (0, s, 0, 0, 0))

    return pl.pallas_call(
        functools.partial(attend_back_kernel, tiles=tiles, block=block, chunk=64, scale=scale),
        grid=(segs,),
        in_specs=[
            pl.BlockSpec((1, tiles * block, keys), lambda s: (s, 0, 0)),
            pl.BlockSpec((tiles, 1, dh, block), lambda s: (0, s, 0, 0)),
            spec(4),
            spec(2),
            pl.BlockSpec((dh, keys), lambda s: (0, 0)),
        ],
        out_specs=[
            spec(3),
            spec(2),
            pl.BlockSpec((1, dh, keys), lambda s: (s, 0, 0)),
            pl.BlockSpec((1, 2, dh), lambda s: (s, 0, 0)),
        ],
        out_shape=[
            jax.ShapeDtypeStruct((tiles, segs, 3, dh, block), low),
            jax.ShapeDtypeStruct((tiles, segs, 2, dh, block), low),
            jax.ShapeDtypeStruct((segs, dh, keys), low),
            jax.ShapeDtypeStruct((segs, 2, dh), f32),
        ],
        scratch_shapes=[
            pltpu.VMEM((keys, dh), low),
            pltpu.VMEM((dh, keys), low),
            pltpu.VMEM((keys, dh), low),
            pltpu.VMEM((dh, keys), f32),
            pltpu.VMEM((dh, keys), f32),
            pltpu.VMEM((dh, keys), f32),
            pltpu.VMEM((block, keys), low),
            pltpu.VMEM((block, keys), low),
        ],
        compiler_params=params(56),
        cost_estimate=pl.CostEstimate(flops=25 * 10**9, bytes_accessed=14 * 10**6, transcendentals=0),
        name="attend_back",
    )(p, g, qk, v, post)


def middle_kernel(
    core_ref, att_ref, gate_ref, x_ref, g_ref, oe_ref, gain_ref, shift_ref, bd_ref, wu_ref, bu_ref, wd_ref,
    y_ref, gres_ref, gatt_ref, glog_ref, wds_ref, wdk_ref, wus_ref, wuk_ref, oes_ref, oek_ref, bu_out, vec_ref,
    mixed, res, n2, n2t, ffn, gn, *, chunk,
):
    step = pl.program_id(0)
    steps = pl.num_programs(0)
    heads, segs, dh, rows = att_ref.shape
    total, width = x_ref.shape
    half = width // 2
    mine = pl.multiple_of(core_ref[0] * half, half)
    other = pl.multiple_of((1 - core_ref[0]) * half, half)
    count = total // chunk

    @pl.when(step == 0)
    def _():
        for h in range(heads):
            for s in range(segs):
                att = to_wide(att_ref[h, s])
                for e in range(EXPERTS):
                    slot = h * EXPERTS + e
                    mixed[slot * dh : (slot + 1) * dh, s * rows : (s + 1) * rows] = to_low(
                        gate_ref[s, slot : slot + 1] * att
                    )
        res[...] = to_wide(x_ref[...]) + nn(mixed[...].T, oe_ref[...])

        @pl.loop(0, count)
        def _(i):
            at = pl.ds(pl.multiple_of(i * chunk, chunk), chunk)
            unit, _ = norm_parts(res[at, :])
            n2[at, :] = to_low(unit * to_wide(gain_ref[...]) + to_wide(shift_ref[...]))

        n2t[...] = n2[...].T
        ffn[...] = jnp.zeros_like(ffn)
        gn[...] = jnp.zeros_like(gn)

    wu = wu_ref[...]
    wd = wd_ref[...]
    v = nn(n2[...], wu) + to_wide(bu_ref[...])
    root = 0.7978845608028654
    square = v * v
    tanh = jnp.tanh(root * (v + 0.044715 * (square * v)))
    plus = 0.5 * (1.0 + tanh)
    hidden = to_low(v * plus)
    slope = plus + 0.5 * v * (1.0 - tanh * tanh) * (root * (1.0 + 0.134145 * square))
    gp = nt(g_ref[...], wd) * slope
    gp_low = to_low(gp)
    bu_out[...] = jnp.sum(to_wide(gp_low), axis=0, keepdims=True)
    ffn[...] += nn(hidden, wd)
    gn[...] += nt(gp_low, wu)
    wu_grad = to_low(nn(n2t[...], gp_low))

    @pl.when(step < steps // 2)
    def _():
        wus_ref[...] = wu_grad

    @pl.when(step >= steps // 2)
    def _():
        wuk_ref[...] = wu_grad

    turned = hidden.T
    wds_ref[...] = to_low(nn(turned, g_ref[:, pl.ds(other, half)]))
    wdk_ref[...] = to_low(nn(turned, g_ref[:, pl.ds(mine, half)]))

    @pl.when(step == steps - 1)
    def _():
        zero = jnp.zeros((1, width), jnp.float32)

        def rows_back(i, sums):
            at = pl.ds(pl.multiple_of(i * chunk, chunk), chunk)
            r = res[at, :]
            y_ref[at, :] = to_low(r + ffn[at, :] + to_wide(bd_ref[...]))
            unit, inv_std = norm_parts(r)
            grad = gn[at, :]
            g = to_wide(g_ref[at, :])
            q = grad * to_wide(gain_ref[...])
            back = q - jnp.mean(q, axis=1, keepdims=True) - unit * jnp.mean(q * unit, axis=1, keepdims=True)
            out = g + inv_std * back
            gres_ref[at, :] = out
            n2[at, :] = to_low(out)
            return (
                sums[0] + jnp.sum(grad * unit, axis=0, keepdims=True),
                sums[1] + jnp.sum(grad, axis=0, keepdims=True),
                sums[2] + jnp.sum(g, axis=0, keepdims=True),
            )

        sums = lax.fori_loop(0, count, rows_back, (zero, zero, zero))
        for k in range(3):
            vec_ref[k : k + 1] = sums[k]
        n2t[...] = n2[...].T
        for h in range(heads):
            group = nn(oe_ref[h * EXPERTS * dh : (h + 1) * EXPERTS * dh], n2t[...])
            for s in range(segs):
                att = to_wide(att_ref[h, s])
                grad = jnp.zeros((dh, rows), jnp.float32)
                for e in range(EXPERTS):
                    slot = h * EXPERTS + e
                    part = group[e * dh : (e + 1) * dh, s * rows : (s + 1) * rows]
                    gate = gate_ref[s, slot : slot + 1]
                    grad = grad + gate * part
                    logit = jnp.sum(part * att, axis=0, keepdims=True) * (gate * (1.0 - gate))
                    glog_ref[s, slot : slot + 1] = logit
                gatt_ref[h, s] = to_low(grad)
        oes_ref[...] = to_low(nn(mixed[...], n2[:, pl.ds(other, half)]))
        oek_ref[...] = to_low(nn(mixed[...], n2[:, pl.ds(mine, half)]))


def middle(core, att, gate, x, g, oe, gain, shift, bd, wu, bu, wd, fc=256):
    heads, segs, dh, rows = att.shape
    total, width = x.shape
    ff = wu.shape[1]
    steps = ff // fc
    mid = steps // 2
    half = width // 2
    slots = gate.shape[1]
    inner = oe.shape[0]
    low, f32 = jnp.bfloat16, jnp.float32

    def fix(*shape):
        return pl.BlockSpec(shape, lambda i, c: (0,) * len(shape))

    def keep(*shape):
        return once(shape, lambda i, c: (0,) * len(shape))

    def unit(i, c):
        return (i + mid * (1 - c[0])) % steps

    return pl.pallas_call(
        functools.partial(middle_kernel, chunk=64),
        grid_spec=pltpu.PrefetchScalarGridSpec(
            num_scalar_prefetch=1,
            grid=(steps,),
            in_specs=[
                keep(heads, segs, dh, rows),
                keep(segs, slots, rows),
                keep(total, width),
                keep(total, width),
                keep(inner, width),
                fix(1, width),
                fix(1, width),
                fix(1, width),
                pl.BlockSpec((width, fc), lambda i, c: (0, unit(i, c))),
                pl.BlockSpec((1, fc), lambda i, c: (0, unit(i, c))),
                pl.BlockSpec((fc, width), lambda i, c: (unit(i, c), 0)),
            ],
            out_specs=[
                fix(total, width),
                fix(total, width),
                fix(heads, segs, dh, rows),
                fix(segs, slots, rows),
                pl.BlockSpec((fc, half), lambda i, c: (unit(i, c), 0)),
                pl.BlockSpec((fc, half), lambda i, c: (unit(i, c), 0)),
                pl.BlockSpec((width, fc), lambda i, c: (0, jnp.minimum(i, mid - 1))),
                pl.BlockSpec((width, fc), lambda i, c: (0, jnp.maximum(i - mid, 0))),
                fix(inner, half),
                fix(inner, half),
                pl.BlockSpec((1, fc), lambda i, c: (0, unit(i, c))),
                fix(3, width),
            ],
            scratch_shapes=[
                pltpu.VMEM((inner, total), low),
                pltpu.VMEM((total, width), f32),
                pltpu.VMEM((total, width), low),
                pltpu.VMEM((width, total), low),
                pltpu.VMEM((total, width), f32),
                pltpu.VMEM((total, width), f32),
            ],
        ),
        out_shape=[
            jax.ShapeDtypeStruct((total, width), low),
            jax.ShapeDtypeStruct((total, width), f32),
            jax.ShapeDtypeStruct(att.shape, low),
            jax.ShapeDtypeStruct(gate.shape, f32),
            jax.ShapeDtypeStruct((ff, half), low),
            jax.ShapeDtypeStruct((ff, half), low),
            jax.ShapeDtypeStruct((width, ff // 2), low),
            jax.ShapeDtypeStruct((width, ff // 2), low),
            jax.ShapeDtypeStruct((inner, half), low),
            jax.ShapeDtypeStruct((inner, half), low),
            jax.ShapeDtypeStruct((1, ff), f32),
            jax.ShapeDtypeStruct((3, width), f32),
        ],
        compiler_params=params(60),
        cost_estimate=pl.CostEstimate(flops=34 * 10**9, bytes_accessed=60 * 10**6, transcendentals=2 * 10**6),
        name="middle",
    )(core, att, gate, x, g, oe, gain, shift, bd, wu, bu, wd)


def late_rows(dh):
    first = HEADS * EXPERTS * dh
    second = first + HEADS * dh
    third = second + HEADS * dh
    return first, second, third, third + 32, third + 64


def back_kernel(
    mem_ref, blk_ref, gain_ref, shift_ref, dqk_ref, dv_ref, glog_ref, gate_ref, all_ref, ve_ref, wk_ref, wq_ref,
    rv_ref, ro_ref, gres_ref, xg_ref, late_ref, vec_ref, acc, gt,
):
    half = pl.program_id(1)
    first_step = (pl.program_id(0) == 0) & (half == 0)
    heads, dh = dv_ref.shape[0], dv_ref.shape[3]
    slots = gate_ref.shape[2]
    at_key, at_query, at_value, at_out, end = late_rows(dh)

    @pl.when(first_step)
    def _():
        gt[at_value:end] = jnp.zeros((end - at_value, gt.shape[1]), jnp.bfloat16)
        vec_ref[...] = jnp.zeros_like(vec_ref)

    for h in range(heads):
        gv = to_wide(dv_ref[h, 0, 0])
        for e in range(EXPERTS):
            slot = h * EXPERTS + e
            gate = gate_ref[0, 0, slot : slot + 1]
            gt[slot * dh : (slot + 1) * dh] = to_low(gate * gv)
            logit = jnp.sum(to_wide(all_ref[0, 0, slot * dh : (slot + 1) * dh]) * gv, axis=0, keepdims=True)
            gt[at_value + slot : at_value + slot + 1] = to_low(logit * (gate * (1.0 - gate)))

    @pl.when(half == 0)
    def _():
        for h in range(heads):
            gt[at_key + h * dh : at_key + (h + 1) * dh] = dqk_ref[h, 0, 1]
        gt[at_query:at_value] = jnp.zeros((at_value - at_query, gt.shape[1]), jnp.bfloat16)
        gt[at_out : at_out + slots] = jnp.zeros((slots, gt.shape[1]), jnp.bfloat16)

    @pl.when(half == 1)
    def _():
        for h in range(heads):
            gt[at_key + h * dh : at_key + (h + 1) * dh] = dqk_ref[h, 0, 2]
            gt[at_query + h * dh : at_query + (h + 1) * dh] = dqk_ref[h, 0, 0]
        gt[at_out : at_out + slots] = to_low(glog_ref[0])

    rows = to_wide(jnp.where(half == 0, mem_ref[0], blk_ref[0]))
    unit, inv_std = norm_parts(rows)
    gain = to_wide(gain_ref[...])
    normed = to_low(unit * gain + to_wide(shift_ref[...]))
    update = nn(gt[...], normed)

    @pl.when(first_step)
    def _():
        acc[...] = update

    @pl.when(jnp.logical_not(first_step))
    def _():
        acc[...] += update

    grad = nn(ve_ref[...], gt[:at_key]) + nn(wk_ref[...], gt[at_key:at_query])
    grad = grad + nn(wq_ref[...], gt[at_query:at_value])
    grad = grad + nn(rv_ref[...], gt[at_value : at_value + slots]) + nn(ro_ref[...], gt[at_out : at_out + slots])
    grad = grad.T
    vec_ref[0:1] += jnp.sum(grad * unit, axis=0, keepdims=True)
    vec_ref[1:2] += jnp.sum(grad, axis=0, keepdims=True)

    @pl.when(half == 1)
    def _():
        q = grad * gain
        back = q - jnp.mean(q, axis=1, keepdims=True) - unit * jnp.mean(q * unit, axis=1, keepdims=True)
        xg_ref[0] = to_low(gres_ref[0] + inv_std * back)

    @pl.when((pl.program_id(0) == pl.num_programs(0) - 1) & (half == 1))
    def _():
        for k in range(late_ref.shape[0]):
            late_ref[k] = to_low(acc[:, k * LANES : (k + 1) * LANES])


def back(mem, blk, gain, shift, dqk, dv, glog, gate, every, ve, wk, wq, rv, ro, gres):
    segs, rows, width = blk.shape
    heads, _, _, dh, _ = dv.shape
    slots = gate.shape[2]
    end = late_rows(dh)[-1]
    low, f32 = jnp.bfloat16, jnp.float32
    row_spec = pl.BlockSpec((1, rows, width), lambda s, r: (s, 0, 0))
    flat = lambda s, r: (0, 0)
    vector = pl.BlockSpec((1, width), flat)
    return pl.pallas_call(
        back_kernel,
        grid=(segs, 2),
        in_specs=[
            row_spec,
            row_spec,
            vector,
            vector,
            pl.BlockSpec((heads, 1, 3, dh, rows), lambda s, r: (0, s, 0, 0, 0)),
            pl.BlockSpec((heads, 1, 1, dh, rows), lambda s, r: (0, s, r, 0, 0)),
            pl.BlockSpec((1, slots, rows), lambda s, r: (s, 0, 0)),
            pl.BlockSpec((1, 1, slots, rows), lambda s, r: (s, r, 0, 0)),
            pl.BlockSpec((1, 1, every.shape[2], rows), lambda s, r: (s, r, 0, 0)),
            once(ve.shape, flat),
            once(wk.shape, flat),
            once(wq.shape, flat),
            once(rv.shape, flat),
            once(ro.shape, flat),
            row_spec,
        ],
        out_specs=[
            row_spec,
            pl.BlockSpec((width // LANES, end, LANES), lambda s, r: (0, 0, 0)),
            pl.BlockSpec((2, width), flat),
        ],
        out_shape=[
            jax.ShapeDtypeStruct(blk.shape, low),
            jax.ShapeDtypeStruct((width // LANES, end, LANES), low),
            jax.ShapeDtypeStruct((2, width), f32),
        ],
        scratch_shapes=[pltpu.VMEM((end, width), f32), pltpu.VMEM((end, rows), low)],
        compiler_params=params(60),
        cost_estimate=pl.CostEstimate(flops=14 * 10**9, bytes_accessed=25 * 10**6, transcendentals=0),
        name="back",
    )(mem, blk, gain, shift, dqk, dv, glog, gate, every, ve, wk, wq, rv, ro, gres)


def mm(spec, left, right):
    return jnp.einsum(spec, left, right, preferred_element_type=jnp.float32)


def position_table(row_count, width_count):
    fine = 64
    inverse_freq = 10000.0 ** (-jnp.arange(0, width_count, 2).astype(jnp.float32) / width_count)
    high = (row_count // fine - 1 - jnp.arange(row_count // fine)) * fine
    low_part = fine - 1 - jnp.arange(fine)
    high_angle = high.astype(jnp.float32)[:, None, None] * inverse_freq
    low_angle = low_part.astype(jnp.float32)[None, :, None] * inverse_freq
    high_sin, high_cos = jnp.sin(high_angle), jnp.cos(high_angle)
    low_sin, low_cos = jnp.sin(low_angle), jnp.cos(low_angle)
    sines = high_sin * low_cos + high_cos * low_sin
    cosines = high_cos * low_cos - high_sin * low_sin
    return to_low(jnp.concatenate([sines, cosines], axis=2)).reshape(row_count, width_count)


def route_mask(routes, expert_count):
    return jnp.sum((routes[..., None] == jnp.arange(expert_count)).astype(jnp.float32), axis=-2)


def bit_of(axis, bit):
    return (lax.axis_index(axis) // bit) % 2


def swap(value, axis, bit):
    pairs = [(i, i ^ bit) for i in range(lax.axis_size(axis))]
    return lax.ppermute(value, axis, pairs)


def pick(value, index, axis):
    return lax.dynamic_index_in_dim(value, index, axis, keepdims=False)


def cut(value, index, axis):
    size = value.shape[axis] // 2
    return lax.dynamic_slice_in_dim(value, index * size, size, axis)


def axis_bits(axis):
    size = lax.axis_size(axis)
    return [1 << k for k in range(size.bit_length() - 1)]


def add(left, right):
    return to_low(to_wide(left) + to_wide(right))


def halve_seg(part, bits):
    for bit in bits:
        part = part.reshape((part.shape[0] // 2, 2) + part.shape[1:])
        mine = bit_of("seg", bit)
        other = swap(pick(part, 1 - mine, 1), "seg", bit)
        part = add(pick(part, mine, 1), other)
    return part[0]


def widen(part, axis, bit, dim):
    mine = bit_of(axis, bit)
    other = swap(part, axis, bit)
    first = jnp.where(mine == 0, part, other)
    second = jnp.where(mine == 0, other, part)
    return jnp.concatenate([first, second], axis=dim)


def pos_stage(kept, got):
    bit = axis_bits("pos")[1]
    mine = bit_of("pos", bit)
    come = swap(add(cut(kept, 1 - mine, 1), cut(got, 1 - mine, 1)), "pos", bit)
    return cut(kept, mine, 1), cut(got, mine, 1), come


def seg_stage(kept, got, seg_size):
    bit = axis_bits("seg")[0]
    mine = bit_of("seg", bit)
    shape = (seg_size // 2, 2, kept.shape[0] // seg_size, kept.shape[1])
    kept, got = kept.reshape(shape), got.reshape(shape)
    come = swap(add(pick(kept, 1 - mine, 1), pick(got, 1 - mine, 1)), "seg", bit)
    return pick(kept, mine, 1), pick(got, mine, 1), come


def sum_three(parts):
    return to_low(to_wide(parts[0]) + to_wide(parts[1]) + to_wide(parts[2]))


def finish_pos_first(parts, seg_size):
    part = sum_three(parts)
    bits = axis_bits("pos")
    part = halve_seg(part.reshape((seg_size, part.shape[0] // seg_size) + part.shape[1:]), axis_bits("seg"))
    part = widen(part, "pos", bits[1], 1)
    return to_wide(widen(part, "pos", bits[0], 1))


def finish_seg_first(parts):
    part = halve_seg(sum_three(parts), axis_bits("seg")[1:])
    bits = axis_bits("pos")
    part = add(part, swap(part, "pos", bits[1]))
    return to_wide(widen(part, "pos", bits[0], 1))


def scatter_late(late, position, seg_size):
    bits = axis_bits("pos")
    part = late
    for bit in bits:
        mine = bit_of("pos", bit)
        other = swap(cut(part, 1 - mine, 1), "pos", bit)
        part = add(cut(part, mine, 1), other)
    kept = part.shape[1]
    part = jnp.concatenate([part, position], axis=1)
    blocks, rows, lanes = part.shape
    inside = seg_size // blocks
    part = part.reshape(blocks, rows, inside, lanes // inside)
    part = jnp.transpose(part, (0, 2, 1, 3)).reshape(seg_size, rows, lanes // inside)
    part = halve_seg(part, axis_bits("seg"))[None]
    part = widen(part, "pos", bits[1], 0)[None]
    part = widen(part, "pos", bits[0], 0)
    main = part[:, :, :kept].reshape(late.shape[1], -1)
    heads = jnp.transpose(part[:, :, kept:], (1, 0, 2, 3)).reshape(HEADS * position.shape[1], -1)
    return jnp.transpose(to_wide(main)), jnp.transpose(to_wide(heads))


def scatter_vectors(vectors, seg_size):
    flat = jnp.concatenate([v.reshape(seg_size, -1) for v in vectors], axis=1)
    part = flat
    for bit in axis_bits("seg"):
        part = part.reshape((part.shape[0] // 2, 2) + part.shape[1:])
        mine = bit_of("seg", bit)
        part = pick(part, mine, 1) + swap(pick(part, 1 - mine, 1), "seg", bit)
    for bit in axis_bits("pos"):
        part = part + swap(part, "pos", bit)
    out = []
    start = 0
    for v in vectors:
        size = v.size // seg_size
        out.append(part[0, start : start + size])
        start += size
    return out


def local(
    block_input,
    memory_rows,
    memory_length,
    value_routes,
    output_routes,
    first_gain,
    first_shift,
    query_weight,
    key_weight,
    position_weight,
    value_experts,
    value_router,
    content_bias,
    position_bias,
    output_experts,
    output_gate_matrix,
    second_gain,
    second_shift,
    up_projection_weight,
    expand_bias,
    down_projection_weight,
    contract_bias,
    output_cotangent,
):
    seg_count, local_rows, width = block_input.shape
    seg_size = lax.axis_size("seg")
    pos_index = lax.axis_index("pos")
    key_count = 2 * SEQ
    all_rows = seg_count * local_rows
    slots = HEADS * EXPERTS
    score_scale = DH ** (-0.5)
    line = lambda v: v.reshape(1, -1)

    value_pick = jnp.transpose(route_mask(value_routes, EXPERTS), (0, 1, 3, 4, 2))
    value_pick = value_pick.reshape(seg_count, 2, slots, local_rows)
    out_pick = jnp.transpose(route_mask(output_routes, EXPERTS), (0, 2, 3, 1))
    out_pick = out_pick.reshape(seg_count, slots, local_rows)
    pad = ((0, 0), (0, 32 - slots))
    gates = jnp.concatenate([jnp.pad(value_router, pad), jnp.pad(output_gate_matrix, pad)], axis=1)

    def trade(value):
        return lax.all_to_all(value, "pos", split_axis=0, concat_axis=0, tiled=True)

    qk, normed, value_gate, out_gate = project(
        memory_rows,
        block_input,
        line(first_gain),
        line(first_shift),
        query_weight,
        key_weight,
        gates,
        to_wide(content_bias).reshape(-1, 1),
        to_wide(position_bias).reshape(-1, 1),
        value_pick,
        out_pick,
        score_scale,
    )
    qk = trade(qk)
    values, value_all = experts(normed, value_experts, value_gate)
    values = trade(values)

    table_low = position_table(key_count, D)
    weight_local = pick(position_weight.reshape(D, HEADS, DH), pos_index, 1)
    positions = to_low(mm("nd,dc->cn", table_low, weight_local))

    probs = score(memory_length, qk, positions)
    attended = trade(attend(probs, values))

    core = bit_of("pos", 1).astype(jnp.int32).reshape(1)
    (
        block_output,
        grad_residual,
        grad_attended,
        grad_out_logit,
        down_sent,
        down_kept,
        up_sent,
        up_kept,
        mix_sent,
        mix_kept,
        expand_bias_grad,
        middle_sums,
    ) = middle(
        core,
        attended,
        out_gate,
        block_input.reshape(all_rows, width),
        output_cotangent.reshape(all_rows, width),
        output_experts,
        line(second_gain),
        line(second_shift),
        line(contract_bias),
        up_projection_weight,
        line(expand_bias),
        down_projection_weight,
    )
    grad_heads = trade(grad_attended)
    down_got = swap(down_sent, "pos", 1)
    up_got = swap(up_sent, "pos", 1)
    mix_got = swap(mix_sent, "pos", 1)

    grad_qk, grad_values, grad_rel, part_sums = attend_back(
        probs, grad_heads, qk, values, positions, score_scale
    )
    grad_qk, grad_values, down_got, up_got, mix_got = lax.optimization_barrier(
        (grad_qk, grad_values, down_got, up_got, mix_got)
    )
    down_parts = pos_stage(down_kept, down_got)
    up_parts = seg_stage(up_kept, up_got, seg_size)
    mix_parts = seg_stage(mix_kept, mix_got, seg_size)
    grad_values = trade(grad_values)
    grad_qk = trade(grad_qk)

    position_grad = to_low(mm("scn,nd->cd", grad_rel, table_low))
    position_grad = jnp.transpose(position_grad.reshape(DH, D // LANES, LANES), (1, 0, 2))
    head_hot = (jnp.arange(HEADS) == pos_index).astype(jnp.float32)[:, None]
    bias_sums = jnp.sum(part_sums, axis=0)
    content_bias_grad = (head_hot * bias_sums[0]).reshape(HEADS * DH)
    position_bias_grad = (head_hot * bias_sums[1]).reshape(HEADS * DH)

    input_grad, late, back_sums = back(
        memory_rows,
        block_input,
        line(first_gain),
        line(first_shift),
        grad_qk,
        grad_values,
        grad_out_logit,
        value_gate,
        value_all,
        value_experts,
        key_weight,
        query_weight,
        value_router,
        output_gate_matrix,
        grad_residual.reshape(seg_count, local_rows, width),
    )
    late, down_parts, up_parts, mix_parts = lax.optimization_barrier((late, down_parts, up_parts, mix_parts))
    late_sum, position_weight_grad = scatter_late(late, position_grad, seg_size)
    at_key, at_query, at_value, at_out, _ = late_rows(DH)
    contract_weight_grad = finish_pos_first(down_parts, seg_size)
    expand_weight_grad = finish_seg_first(up_parts)
    output_experts_grad = finish_seg_first(mix_parts)
    vectors = scatter_vectors(
        [
            back_sums[0],
            back_sums[1],
            content_bias_grad,
            position_bias_grad,
            middle_sums[0],
            middle_sums[1],
            expand_bias_grad[0],
            middle_sums[2],
        ],
        seg_size,
    )
    return (
        block_output.reshape(block_input.shape),
        input_grad,
        vectors[0],
        vectors[1],
        late_sum[:, at_query:at_value],
        late_sum[:, at_key:at_query],
        position_weight_grad,
        late_sum[:, :at_key],
        late_sum[:, at_value : at_value + slots],
        vectors[2],
        vectors[3],
        output_experts_grad,
        late_sum[:, at_out : at_out + slots],
        vectors[4],
        vectors[5],
        expand_weight_grad,
        vectors[6],
        contract_weight_grad,
        vectors[7],
    )


def solution(mesh):
    rows = P("seg", "pos", None)
    whole = P()
    placed = (
        rows,
        rows,
        P("seg"),
        P("seg", None, "pos", None, None),
        P("seg", "pos", None, None),
    )
    placed += (whole,) * 17 + (rows,)
    shares = [P("seg")] * 17
    for index in (2, 3, 4, 5, 6, 9, 10, 13, 15):
        shares[index] = P("seg", None)
    return jax.shard_map(
        local,
        mesh=mesh,
        in_specs=placed,
        out_specs=(rows, rows) + tuple(shares),
        check_vma=False,
    )
```

```python
import functools

import jax
import jax.numpy as jnp
from jax import lax
from jax.experimental import pallas as pl
from jax.experimental.pallas import tpu as pltpu
from jax.sharding import PartitionSpec as P

D = 1024
HEADS = 4
DH = 112
EXPERTS = 5
SEQ = 1024
norm_eps = 1e-05

NEG = -1e30
LANES = 128


def nn(left, right):
    return lax.dot_general(left, right, (((1,), (0,)), ((), ())), preferred_element_type=jnp.float32)


def nt(left, right):
    return lax.dot_general(left, right, (((1,), (1,)), ((), ())), preferred_element_type=jnp.float32)


def to_low(value):
    return value.astype(jnp.bfloat16)


def to_wide(value):
    return value.astype(jnp.float32)


def norm_parts(rows):
    center = rows - jnp.mean(rows, axis=1, keepdims=True)
    inv_std = lax.rsqrt(jnp.mean(center * center, axis=1, keepdims=True) + norm_eps)
    return center * inv_std, inv_std


def once(shape, index_map):
    return pl.BlockSpec(shape, index_map, pipeline_mode=pl.Buffered(1))


def params(megabytes):
    return pltpu.CompilerParams(vmem_limit_bytes=megabytes << 20)


def project_kernel(
    mem_ref, blk_ref, gain_ref, shift_ref, wq_ref, wk_ref, gates_ref, cbias_ref, pbias_ref, pickv_ref, picko_ref,
    qk_ref, norm_ref, gatev_ref, gateo_ref, *, scale,
):
    half = pl.program_id(1)
    rows = to_wide(jnp.where(half == 0, mem_ref[0], blk_ref[0]))
    unit, _ = norm_parts(rows)
    normed = to_low(unit * to_wide(gain_ref[...]) + to_wide(shift_ref[...]))
    norm_ref[0, 0] = normed
    turned = normed.T
    keys = to_low(nn(wk_ref[...], turned))
    dh = qk_ref.shape[3]
    logits = nn(gates_ref[...], turned)
    gatev_ref[0, 0] = jax.nn.sigmoid(logits[: pickv_ref.shape[2]]) * pickv_ref[0, 0]

    @pl.when(half == 0)
    def _():
        for h in range(qk_ref.shape[0]):
            qk_ref[h, 0, 2] = keys[h * dh : (h + 1) * dh]

    @pl.when(half == 1)
    def _():
        query = nn(wq_ref[...], turned)
        content = to_low((query + cbias_ref[...]) * scale)
        position = to_low((query + pbias_ref[...]) * scale)
        for h in range(qk_ref.shape[0]):
            qk_ref[h, 0, 0] = content[h * dh : (h + 1) * dh]
            qk_ref[h, 0, 1] = position[h * dh : (h + 1) * dh]
            qk_ref[h, 0, 3] = keys[h * dh : (h + 1) * dh]
        gateo_ref[0] = jax.nn.sigmoid(logits[logits.shape[0] // 2 :][: picko_ref.shape[1]]) * picko_ref[0]


def project(mem, blk, gain, shift, wqt, wkt, gates, cbias, pbias, pickv, picko, scale):
    segs, rows, width = blk.shape
    inner = wqt.shape[0]
    slots = pickv.shape[2]
    low, f32 = jnp.bfloat16, jnp.float32
    dh = inner // HEADS
    flat = lambda s, r: (0, 0)
    row_spec = pl.BlockSpec((1, rows, width), lambda s, r: (s, 0, 0))
    return pl.pallas_call(
        functools.partial(project_kernel, scale=scale),
        grid=(segs, 2),
        in_specs=[
            row_spec,
            row_spec,
            pl.BlockSpec((1, width), flat),
            pl.BlockSpec((1, width), flat),
            once(wqt.shape, flat),
            once(wkt.shape, flat),
            once(gates.shape, flat),
            pl.BlockSpec((inner, 1), flat),
            pl.BlockSpec((inner, 1), flat),
            pl.BlockSpec((1, 1, slots, rows), lambda s, r: (s, r, 0, 0)),
            pl.BlockSpec((1, slots, rows), lambda s, r: (s, 0, 0)),
        ],
        out_specs=[
            pl.BlockSpec((HEADS, 1, 4, dh, rows), lambda s, r: (0, s, 0, 0, 0)),
            pl.BlockSpec((1, 1, rows, width), lambda s, r: (s, r, 0, 0)),
            pl.BlockSpec((1, 1, slots, rows), lambda s, r: (s, r, 0, 0)),
            pl.BlockSpec((1, slots, rows), lambda s, r: (s, 0, 0)),
        ],
        out_shape=[
            jax.ShapeDtypeStruct((HEADS, segs, 4, dh, rows), low),
            jax.ShapeDtypeStruct((segs, 2, rows, width), low),
            jax.ShapeDtypeStruct((segs, 2, slots, rows), f32),
            jax.ShapeDtypeStruct((segs, slots, rows), f32),
        ],
        compiler_params=params(48),
        cost_estimate=pl.CostEstimate(flops=3 * 10**9, bytes_accessed=8 * 10**6, transcendentals=0),
        name="project",
    )(mem, blk, gain, shift, wqt, wkt, gates, cbias, pbias, pickv, picko)


def experts_kernel(norm_ref, ve_ref, gate_ref, v_ref, all_ref):
    turned = norm_ref[0, 0].T
    heads, dh = v_ref.shape[0], v_ref.shape[3]
    group = nn(ve_ref[...], turned)
    all_ref[0, 0] = to_low(group)
    for h in range(heads):
        total = jnp.zeros((dh, turned.shape[1]), jnp.float32)
        for e in range(EXPERTS):
            slot = h * EXPERTS + e
            total = total + gate_ref[0, 0, slot : slot + 1] * group[slot * dh : (slot + 1) * dh]
        v_ref[h, 0, 0] = to_low(total)


def experts(normed, vet, gate):
    segs, _, rows, width = normed.shape
    inner = vet.shape[0]
    slots = gate.shape[2]
    dh = inner // (HEADS * EXPERTS)
    low = jnp.bfloat16
    return pl.pallas_call(
        experts_kernel,
        grid=(segs, 2),
        in_specs=[
            pl.BlockSpec((1, 1, rows, width), lambda s, r: (s, r, 0, 0)),
            once(vet.shape, lambda s, r: (0, 0)),
            pl.BlockSpec((1, 1, slots, rows), lambda s, r: (s, r, 0, 0)),
        ],
        out_specs=[
            pl.BlockSpec((HEADS, 1, 1, dh, rows), lambda s, r: (0, s, r, 0, 0)),
            pl.BlockSpec((1, 1, inner, rows), lambda s, r: (s, r, 0, 0)),
        ],
        out_shape=[
            jax.ShapeDtypeStruct((HEADS, segs, 2, dh, rows), low),
            jax.ShapeDtypeStruct((segs, 2, inner, rows), low),
        ],
        compiler_params=params(48),
        cost_estimate=pl.CostEstimate(flops=5 * 10**9, bytes_accessed=12 * 10**6, transcendentals=0),
        name="experts",
    )(normed, vet, gate)


def score_kernel(len_ref, qk_ref, pos_ref, p_ref, kt_s, *, tiles, block, chunk):
    seg = pl.program_id(0)
    start = tiles * block - len_ref[seg]
    for half in range(2):
        for t in range(tiles):
            c0 = (half * tiles + t) * block
            kt_s[:, c0 : c0 + block] = qk_ref[t, 0, 2 + half]
    mem = tiles * block
    for t in range(tiles):
        w = mem + (t + 1) * block
        base = (tiles - 1 - t) * block
        col = lax.broadcasted_iota(jnp.int32, (1, w), 1)
        bias = jnp.where(col >= start, 0.0, NEG)
        content = qk_ref[t, 0, 0].T
        position = qk_ref[t, 0, 1].T
        for r0 in range(0, block, chunk):
            raw = nn(position[r0 : r0 + chunk], pos_ref[:, base:])
            rel = pltpu.roll(raw, w - (block - 1) + r0, 1, stride=1, stride_axis=0)
            s = nn(content[r0 : r0 + chunk], kt_s[:, :w]) + rel
            row = lax.broadcasted_iota(jnp.int32, (chunk, w), 0) + (mem + t * block + r0)
            col_wide = lax.broadcasted_iota(jnp.int32, (chunk, w), 1)
            s = jnp.where(col_wide <= row, s + bias, NEG)
            e = jnp.exp(s - jnp.max(s, axis=1, keepdims=True))
            p = e * (1.0 / jnp.sum(e, axis=1, keepdims=True))
            p_ref[0, t * block + r0 : t * block + r0 + chunk, :w] = to_low(p)


def score(lengths, qk, post):
    tiles, segs, _, dh, block = qk.shape
    keys = 2 * tiles * block
    return pl.pallas_call(
        functools.partial(score_kernel, tiles=tiles, block=block, chunk=64),
        grid_spec=pltpu.PrefetchScalarGridSpec(
            num_scalar_prefetch=1,
            grid=(segs,),
            in_specs=[
                pl.BlockSpec((tiles, 1, 4, dh, block), lambda s, _: (0, s, 0, 0, 0)),
                pl.BlockSpec((dh, keys), lambda s, _: (0, 0)),
            ],
            out_specs=pl.BlockSpec((1, tiles * block, keys), lambda s, _: (s, 0, 0)),
            scratch_shapes=[pltpu.VMEM((dh, keys), jnp.bfloat16)],
        ),
        out_shape=jax.ShapeDtypeStruct((segs, tiles * block, keys), jnp.bfloat16),
        compiler_params=params(48),
        cost_estimate=pl.CostEstimate(flops=12 * 10**9, bytes_accessed=10 * 10**6, transcendentals=4 * 10**6),
        name="score",
    )(lengths, qk, post)


def attend_kernel(p_ref, v_ref, att_ref, v_s, *, tiles, block):
    for half in range(2):
        for t in range(tiles):
            c0 = (half * tiles + t) * block
            v_s[c0 : c0 + block, :] = v_ref[t, 0, half].T
    for t in range(tiles):
        w = tiles * block + (t + 1) * block
        out = nn(p_ref[0, t * block : (t + 1) * block, :w], v_s[:w, :])
        att_ref[t, 0] = to_low(out).T


def attend(p, v):
    tiles, segs, _, dh, block = v.shape
    keys = 2 * tiles * block
    return pl.pallas_call(
        functools.partial(attend_kernel, tiles=tiles, block=block),
        grid=(segs,),
        in_specs=[
            pl.BlockSpec((1, tiles * block, keys), lambda s: (s, 0, 0)),
            pl.BlockSpec((tiles, 1, 2, dh, block), lambda s: (0, s, 0, 0, 0)),
        ],
        out_specs=pl.BlockSpec((tiles, 1, dh, block), lambda s: (0, s, 0, 0)),
        out_shape=jax.ShapeDtypeStruct((tiles, segs, dh, block), jnp.bfloat16),
        scratch_shapes=[pltpu.VMEM((keys, dh), jnp.bfloat16)],
        compiler_params=params(48),
        cost_estimate=pl.CostEstimate(flops=5 * 10**9, bytes_accessed=9 * 10**6, transcendentals=0),
        name="attend",
    )(p, v)


def attend_back_kernel(
    p_ref, g_ref, qk_ref, v_ref, pos_ref, dqk_ref, dv_ref, dpos_ref, sums_ref,
    k_s, vt_s, posr_s, dkt, dvt, dpt, ds_s, dr_s, *, tiles, block, chunk, scale,
):
    seg = pl.program_id(0)
    for half in range(2):
        for t in range(tiles):
            c0 = (half * tiles + t) * block
            k_s[c0 : c0 + block, :] = qk_ref[t, 0, 2 + half].T
            vt_s[:, c0 : c0 + block] = v_ref[t, 0, half]

    @pl.when(seg == 0)
    def _():
        posr_s[...] = pos_ref[...].T

    dkt[...] = jnp.zeros_like(dkt)
    dvt[...] = jnp.zeros_like(dvt)
    dpt[...] = jnp.zeros_like(dpt)
    mem = tiles * block
    dh = v_ref.shape[3]
    flip = (
        lax.broadcasted_iota(jnp.int32, (block, block), 0) + lax.broadcasted_iota(jnp.int32, (block, block), 1)
        == block - 1
    )
    flip_wide = jnp.where(flip, 1.0, 0.0)
    flip_low = to_low(flip_wide)
    content_sum = jnp.zeros((1, dh), jnp.float32)
    position_sum = jnp.zeros((1, dh), jnp.float32)
    for t in range(tiles):
        w = mem + (t + 1) * block
        base = (tiles - 1 - t) * block
        gt = g_ref[t, 0]
        g = gt.T
        for r0 in range(0, block, chunk):
            p = to_wide(p_ref[0, t * block + r0 : t * block + r0 + chunk, :w])
            prod = p * nn(g[r0 : r0 + chunk], vt_s[:, :w])
            delta = jnp.sum(prod, axis=1, keepdims=True)
            ds_s[r0 : r0 + chunk, :w] = to_low(prod - p * delta)
        ds = ds_s[:, :w]
        for r0 in range(0, block, chunk):
            turned = nn(flip_low[r0 : r0 + chunk], ds)
            dr_s[r0 : r0 + chunk, :w] = to_low(pltpu.roll(turned, r0, 1, stride=1, stride_axis=0))
        dr = dr_s[:, :w]
        dvt[:, :w] += nn(gt, p_ref[0, t * block : (t + 1) * block, :w])
        dkt[:, :w] += nn(qk_ref[t, 0, 0], ds)
        position = to_low(nn(qk_ref[t, 0, 1], flip_low))
        dpt[:, base:] += nn(position, dr)
        dc = nn(ds, k_s[:w, :])
        dp = nn(dr, posr_s[base:, :])
        content_sum = content_sum + jnp.sum(dc, axis=0, keepdims=True)
        position_sum = position_sum + jnp.sum(dp, axis=0, keepdims=True)
        dp = lax.dot_general(
            flip_wide,
            dp,
            (((1,), (0,)), ((), ())),
            precision=lax.Precision.HIGHEST,
            preferred_element_type=jnp.float32,
        )
        dqk_ref[t, 0, 0] = to_low((dc + dp) * scale).T
    sums_ref[0, 0:1] = content_sum * scale
    sums_ref[0, 1:2] = position_sum * scale
    dpos_ref[0] = to_low(dpt[...])
    for half in range(2):
        for t in range(tiles):
            c0 = (half * tiles + t) * block
            dqk_ref[t, 0, 1 + half] = to_low(dkt[:, c0 : c0 + block])
            dv_ref[t, 0, half] = to_low(dvt[:, c0 : c0 + block])


def attend_back(p, g, qk, v, post, scale):
    tiles, segs, dh, block = g.shape
    keys = 2 * tiles * block
    low, f32 = jnp.bfloat16, jnp.float32

    def spec(parts):
        return pl.BlockSpec((tiles, 1, parts, dh, block), lambda s: (0, s, 0, 0, 0))

    return pl.pallas_call(
        functools.partial(attend_back_kernel, tiles=tiles, block=block, chunk=64, scale=scale),
        grid=(segs,),
        in_specs=[
            pl.BlockSpec((1, tiles * block, keys), lambda s: (s, 0, 0)),
            pl.BlockSpec((tiles, 1, dh, block), lambda s: (0, s, 0, 0)),
            spec(4),
            spec(2),
            pl.BlockSpec((dh, keys), lambda s: (0, 0)),
        ],
        out_specs=[
            spec(3),
            spec(2),
            pl.BlockSpec((1, dh, keys), lambda s: (s, 0, 0)),
            pl.BlockSpec((1, 2, dh), lambda s: (s, 0, 0)),
        ],
        out_shape=[
            jax.ShapeDtypeStruct((tiles, segs, 3, dh, block), low),
            jax.ShapeDtypeStruct((tiles, segs, 2, dh, block), low),
            jax.ShapeDtypeStruct((segs, dh, keys), low),
            jax.ShapeDtypeStruct((segs, 2, dh), f32),
        ],
        scratch_shapes=[
            pltpu.VMEM((keys, dh), low),
            pltpu.VMEM((dh, keys), low),
            pltpu.VMEM((keys, dh), low),
            pltpu.VMEM((dh, keys), f32),
            pltpu.VMEM((dh, keys), f32),
            pltpu.VMEM((dh, keys), f32),
            pltpu.VMEM((block, keys), low),
            pltpu.VMEM((block, keys), low),
        ],
        compiler_params=params(56),
        cost_estimate=pl.CostEstimate(flops=25 * 10**9, bytes_accessed=14 * 10**6, transcendentals=0),
        name="attend_back",
    )(p, g, qk, v, post)


def mix_rows(mixed, att_ref, gate_ref):
    heads, segs, dh, rows = att_ref.shape
    for h in range(heads):
        for s in range(segs):
            att = to_wide(att_ref[h, s])
            for e in range(EXPERTS):
                slot = h * EXPERTS + e
                mixed[slot * dh : (slot + 1) * dh, s * rows : (s + 1) * rows] = to_low(
                    gate_ref[s, slot : slot + 1] * att
                )


def middle_kernel(
    core_ref, att_ref, gate_ref, x_ref, g_ref, oe_ref, gain_ref, shift_ref, bd_ref, wu_ref, bu_ref, wd_ref,
    y_ref, res, gn, wds_ref, wdk_ref, wus_ref, wuk_ref, bu_out, mixed, n2, n2t, ffn, *, chunk,
):
    step = pl.program_id(0)
    steps = pl.num_programs(0)
    total, width = x_ref.shape
    half = width // 2
    mine = pl.multiple_of(core_ref[0] * half, half)
    other = pl.multiple_of((1 - core_ref[0]) * half, half)
    count = total // chunk

    @pl.when(step == 0)
    def _():
        mix_rows(mixed, att_ref, gate_ref)
        res[...] = to_wide(x_ref[...]) + nn(mixed[...].T, oe_ref[...])

        @pl.loop(0, count)
        def _(i):
            at = pl.ds(pl.multiple_of(i * chunk, chunk), chunk)
            unit, _ = norm_parts(res[at, :])
            n2[at, :] = to_low(unit * to_wide(gain_ref[...]) + to_wide(shift_ref[...]))

        n2t[...] = n2[...].T
        ffn[...] = jnp.zeros_like(ffn)
        gn[...] = jnp.zeros_like(gn)

    wu = wu_ref[...]
    wd = wd_ref[...]
    v = nn(n2[...], wu) + to_wide(bu_ref[...])
    root = 0.7978845608028654
    square = v * v
    tanh = jnp.tanh(root * (v + 0.044715 * (square * v)))
    plus = 0.5 * (1.0 + tanh)
    hidden = to_low(v * plus)
    slope = plus + 0.5 * v * (1.0 - tanh * tanh) * (root * (1.0 + 0.134145 * square))
    gp = nt(g_ref[...], wd) * slope
    gp_low = to_low(gp)
    bu_out[...] = jnp.sum(to_wide(gp_low), axis=0, keepdims=True)
    ffn[...] += nn(hidden, wd)
    gn[...] += nt(gp_low, wu)
    wu_grad = to_low(nn(n2t[...], gp_low))

    @pl.when(step < steps // 2)
    def _():
        wus_ref[...] = wu_grad

    @pl.when(step >= steps // 2)
    def _():
        wuk_ref[...] = wu_grad

    turned = hidden.T
    wds_ref[...] = to_low(nn(turned, g_ref[:, pl.ds(other, half)]))
    wdk_ref[...] = to_low(nn(turned, g_ref[:, pl.ds(mine, half)]))

    @pl.when(step == steps - 1)
    def _():
        @pl.loop(0, count)
        def _(i):
            at = pl.ds(pl.multiple_of(i * chunk, chunk), chunk)
            y_ref[at, :] = to_low(res[at, :] + ffn[at, :] + to_wide(bd_ref[...]))


def middle(core, att, gate, x, g, oe, gain, shift, bd, wu, bu, wd, fc=512):
    heads, segs, dh, rows = att.shape
    total, width = x.shape
    ff = wu.shape[1]
    steps = ff // fc
    mid = steps // 2
    half = width // 2
    slots = gate.shape[1]
    inner = oe.shape[0]
    low, f32 = jnp.bfloat16, jnp.float32

    def fix(*shape):
        return pl.BlockSpec(shape, lambda i, c: (0,) * len(shape))

    def keep(*shape):
        return once(shape, lambda i, c: (0,) * len(shape))

    def unit(i, c):
        return (i + mid * (1 - c[0])) % steps

    return pl.pallas_call(
        functools.partial(middle_kernel, chunk=64),
        grid_spec=pltpu.PrefetchScalarGridSpec(
            num_scalar_prefetch=1,
            grid=(steps,),
            in_specs=[
                keep(heads, segs, dh, rows),
                keep(segs, slots, rows),
                keep(total, width),
                keep(total, width),
                keep(inner, width),
                fix(1, width),
                fix(1, width),
                fix(1, width),
                pl.BlockSpec((width, fc), lambda i, c: (0, unit(i, c))),
                pl.BlockSpec((1, fc), lambda i, c: (0, unit(i, c))),
                pl.BlockSpec((fc, width), lambda i, c: (unit(i, c), 0)),
            ],
            out_specs=[
                fix(total, width),
                fix(total, width),
                fix(total, width),
                pl.BlockSpec((fc, half), lambda i, c: (unit(i, c), 0)),
                pl.BlockSpec((fc, half), lambda i, c: (unit(i, c), 0)),
                pl.BlockSpec((width, fc), lambda i, c: (0, jnp.minimum(i, mid - 1))),
                pl.BlockSpec((width, fc), lambda i, c: (0, jnp.maximum(i - mid, 0))),
                pl.BlockSpec((1, fc), lambda i, c: (0, unit(i, c))),
            ],
            scratch_shapes=[
                pltpu.VMEM((inner, total), low),
                pltpu.VMEM((total, width), low),
                pltpu.VMEM((width, total), low),
                pltpu.VMEM((total, width), f32),
            ],
        ),
        out_shape=[
            jax.ShapeDtypeStruct((total, width), low),
            jax.ShapeDtypeStruct((total, width), f32),
            jax.ShapeDtypeStruct((total, width), f32),
            jax.ShapeDtypeStruct((ff, half), low),
            jax.ShapeDtypeStruct((ff, half), low),
            jax.ShapeDtypeStruct((width, ff // 2), low),
            jax.ShapeDtypeStruct((width, ff // 2), low),
            jax.ShapeDtypeStruct((1, ff), f32),
        ],
        compiler_params=params(60),
        cost_estimate=pl.CostEstimate(flops=28 * 10**9, bytes_accessed=40 * 10**6, transcendentals=2 * 10**6),
        name="middle",
    )(core, att, gate, x, g, oe, gain, shift, bd, wu, bu, wd)


def middle_back_kernel(
    core_ref, res, gn, att_ref, gate_ref, g_ref, oe_ref, gain_ref,
    gres_ref, gatt_ref, glog_ref, oes_ref, oek_ref, vec_ref, mixed, low_grad, turned, *, chunk,
):
    heads, segs, dh, rows = att_ref.shape
    total, width = g_ref.shape
    half = width // 2
    mine = pl.multiple_of(core_ref[0] * half, half)
    other = pl.multiple_of((1 - core_ref[0]) * half, half)
    mix_rows(mixed, att_ref, gate_ref)
    zero = jnp.zeros((1, width), jnp.float32)

    def rows_back(i, sums):
        at = pl.ds(pl.multiple_of(i * chunk, chunk), chunk)
        unit, inv_std = norm_parts(res[at, :])
        grad = gn[at, :]
        g = to_wide(g_ref[at, :])
        q = grad * to_wide(gain_ref[...])
        back = q - jnp.mean(q, axis=1, keepdims=True) - unit * jnp.mean(q * unit, axis=1, keepdims=True)
        out = g + inv_std * back
        gres_ref[at, :] = out
        low_grad[at, :] = to_low(out)
        return (
            sums[0] + jnp.sum(grad * unit, axis=0, keepdims=True),
            sums[1] + jnp.sum(grad, axis=0, keepdims=True),
            sums[2] + jnp.sum(g, axis=0, keepdims=True),
        )

    sums = lax.fori_loop(0, total // chunk, rows_back, (zero, zero, zero))
    for k in range(3):
        vec_ref[k : k + 1] = sums[k]
    turned[...] = low_grad[...].T
    for h in range(heads):
        group = nn(oe_ref[h * EXPERTS * dh : (h + 1) * EXPERTS * dh], turned[...])
        for s in range(segs):
            att = to_wide(att_ref[h, s])
            grad = jnp.zeros((dh, rows), jnp.float32)
            for e in range(EXPERTS):
                slot = h * EXPERTS + e
                part = group[e * dh : (e + 1) * dh, s * rows : (s + 1) * rows]
                gate = gate_ref[s, slot : slot + 1]
                grad = grad + gate * part
                logit = jnp.sum(part * att, axis=0, keepdims=True) * (gate * (1.0 - gate))
                glog_ref[s, slot : slot + 1] = logit
            gatt_ref[h, s] = to_low(grad)
    oes_ref[...] = to_low(nn(mixed[...], low_grad[:, pl.ds(other, half)]))
    oek_ref[...] = to_low(nn(mixed[...], low_grad[:, pl.ds(mine, half)]))


def middle_back(core, res, gn, att, gate, g, oe, gain):
    inner, width = oe.shape
    total = g.shape[0]
    low, f32 = jnp.bfloat16, jnp.float32
    vmem = pl.BlockSpec(memory_space=pltpu.VMEM)
    return pl.pallas_call(
        functools.partial(middle_back_kernel, chunk=64),
        in_specs=[pl.BlockSpec(memory_space=pltpu.SMEM)] + [vmem] * 7,
        out_specs=[vmem] * 6,
        out_shape=[
            jax.ShapeDtypeStruct((total, width), f32),
            jax.ShapeDtypeStruct(att.shape, low),
            jax.ShapeDtypeStruct(gate.shape, f32),
            jax.ShapeDtypeStruct((inner, width // 2), low),
            jax.ShapeDtypeStruct((inner, width // 2), low),
            jax.ShapeDtypeStruct((3, width), f32),
        ],
        scratch_shapes=[
            pltpu.VMEM((inner, total), low),
            pltpu.VMEM((total, width), low),
            pltpu.VMEM((width, total), low),
        ],
        compiler_params=params(60),
        cost_estimate=pl.CostEstimate(flops=5 * 10**9, bytes_accessed=20 * 10**6, transcendentals=0),
        name="middle_back",
    )(core, res, gn, att, gate, g, oe, gain)


def late_rows(dh):
    first = HEADS * EXPERTS * dh
    second = first + HEADS * dh
    third = second + HEADS * dh
    return first, second, third, third + 32, third + 64


def back_kernel(
    mem_ref, blk_ref, gain_ref, shift_ref, dqk_ref, dv_ref, glog_ref, gate_ref, all_ref, ve_ref, wk_ref, wq_ref,
    rv_ref, ro_ref, gres_ref, extra_ref, xg_ref, late_ref, vec, gt, every_gt, every_norm,
):
    half = pl.program_id(1)
    first_step = (pl.program_id(0) == 0) & (half == 0)
    heads, dh = dv_ref.shape[0], dv_ref.shape[3]
    slots = gate_ref.shape[2]
    at_key, at_query, at_value, at_out, end = late_rows(dh)

    @pl.when(first_step)
    def _():
        gt[at_value:end] = jnp.zeros((end - at_value, gt.shape[1]), jnp.bfloat16)
        vec[...] = jnp.zeros_like(vec)

    for h in range(heads):
        gv = to_wide(dv_ref[h, 0, 0])
        for e in range(EXPERTS):
            slot = h * EXPERTS + e
            gate = gate_ref[0, 0, slot : slot + 1]
            gt[slot * dh : (slot + 1) * dh] = to_low(gate * gv)
            logit = jnp.sum(to_wide(all_ref[0, 0, slot * dh : (slot + 1) * dh]) * gv, axis=0, keepdims=True)
            gt[at_value + slot : at_value + slot + 1] = to_low(logit * (gate * (1.0 - gate)))

    @pl.when(half == 0)
    def _():
        for h in range(heads):
            gt[at_key + h * dh : at_key + (h + 1) * dh] = dqk_ref[h, 0, 1]
        gt[at_query:at_value] = jnp.zeros((at_value - at_query, gt.shape[1]), jnp.bfloat16)
        gt[at_out : at_out + slots] = jnp.zeros((slots, gt.shape[1]), jnp.bfloat16)

    @pl.when(half == 1)
    def _():
        for h in range(heads):
            gt[at_key + h * dh : at_key + (h + 1) * dh] = dqk_ref[h, 0, 2]
            gt[at_query + h * dh : at_query + (h + 1) * dh] = dqk_ref[h, 0, 0]
        gt[at_out : at_out + slots] = to_low(glog_ref[0])

    rows = to_wide(jnp.where(half == 0, mem_ref[0], blk_ref[0]))
    unit, inv_std = norm_parts(rows)
    gain = to_wide(gain_ref[...])
    normed = to_low(unit * gain + to_wide(shift_ref[...]))
    count = gt.shape[1]
    at = pl.multiple_of((pl.program_id(0) * 2 + half) * count, count)
    every_gt[:, pl.ds(at, count)] = gt[...]
    every_norm[pl.ds(at, count), :] = normed
    grad = nn(gt[:at_key].T, ve_ref[...]) + nn(gt[at_key:at_query].T, wk_ref[...])
    grad = grad + nn(gt[at_query:at_value].T, wq_ref[...])
    grad = grad + nn(gt[at_value : at_value + slots].T, rv_ref[...])
    grad = grad + nn(gt[at_out : at_out + slots].T, ro_ref[...])
    vec[0:1] += jnp.sum(grad * unit, axis=0, keepdims=True)
    vec[1:2] += jnp.sum(grad, axis=0, keepdims=True)

    @pl.when(half == 1)
    def _():
        q = grad * gain
        back = q - jnp.mean(q, axis=1, keepdims=True) - unit * jnp.mean(q * unit, axis=1, keepdims=True)
        xg_ref[0] = to_low(gres_ref[0] + inv_std * back)

    @pl.when((pl.program_id(0) == pl.num_programs(0) - 1) & (half == 1))
    def _():
        for k in range(0, late_ref.shape[0], 2):
            pair = to_low(nn(every_gt[...], every_norm[:, k * LANES : (k + 2) * LANES]))
            late_ref[k] = pair[:, :LANES]
            late_ref[k + 1] = pair[:, LANES:]
        for k in range(late_ref.shape[0]):
            both = vec[0:2, k * LANES : (k + 1) * LANES]
            late_ref[k, at_value + slots : at_value + slots + 2] = to_low(both)
            late_ref[k, at_out + slots : at_out + slots + 8] = to_low(extra_ref[k])


def back(mem, blk, gain, shift, dqk, dv, glog, gate, every, vet, wkt, wqt, rvt, rot, gres, extra):
    segs, rows, width = blk.shape
    heads, _, _, dh, _ = dv.shape
    slots = gate.shape[2]
    end = late_rows(dh)[-1]
    low, f32 = jnp.bfloat16, jnp.float32
    row_spec = pl.BlockSpec((1, rows, width), lambda s, r: (s, 0, 0))
    flat = lambda s, r: (0, 0)
    vector = pl.BlockSpec((1, width), flat)
    return pl.pallas_call(
        back_kernel,
        grid=(segs, 2),
        in_specs=[
            row_spec,
            row_spec,
            vector,
            vector,
            pl.BlockSpec((heads, 1, 3, dh, rows), lambda s, r: (0, s, 0, 0, 0)),
            pl.BlockSpec((heads, 1, 1, dh, rows), lambda s, r: (0, s, r, 0, 0)),
            pl.BlockSpec((1, slots, rows), lambda s, r: (s, 0, 0)),
            pl.BlockSpec((1, 1, slots, rows), lambda s, r: (s, r, 0, 0)),
            pl.BlockSpec((1, 1, every.shape[2], rows), lambda s, r: (s, r, 0, 0)),
            once(vet.shape, flat),
            once(wkt.shape, flat),
            once(wqt.shape, flat),
            once(rvt.shape, flat),
            once(rot.shape, flat),
            row_spec,
            once(extra.shape, lambda s, r: (0, 0, 0)),
        ],
        out_specs=[
            row_spec,
            pl.BlockSpec((width // LANES, end, LANES), lambda s, r: (0, 0, 0)),
        ],
        out_shape=[
            jax.ShapeDtypeStruct(blk.shape, low),
            jax.ShapeDtypeStruct((width // LANES, end, LANES), low),
        ],
        scratch_shapes=[
            pltpu.VMEM((8, width), f32),
            pltpu.VMEM((end, rows), low),
            pltpu.VMEM((end, 2 * segs * rows), low),
            pltpu.VMEM((2 * segs * rows, width), low),
        ],
        compiler_params=params(60),
        cost_estimate=pl.CostEstimate(flops=14 * 10**9, bytes_accessed=25 * 10**6, transcendentals=0),
        name="back",
    )(mem, blk, gain, shift, dqk, dv, glog, gate, every, vet, wkt, wqt, rvt, rot, gres, extra)


def fold_kernel(bits_ref, *refs, counts):
    at = 0
    outs = sum(counts) * 2
    for k, count in enumerate(counts):
        for part in range(2):
            total = to_wide(refs[at][...])
            for extra in range(1, count):
                total = total + to_wide(refs[at + extra][...])
            refs[outs + 2 * k + part][...] = to_low(total).reshape(refs[outs + 2 * k + part].shape)
            at += count


def fold(items, bits):
    in_specs, arrays, out_specs, out_shape, counts = [], [], [], [], []
    steps = 4
    for k, (addends, dim) in enumerate(items):
        shape = addends[0].shape
        rows, cols = shape[-2:]
        lead = shape[:-2]
        if dim == "columns":
            left, width = lead, cols // 2
        else:
            left, width = lead[:dim] + lead[dim + 1 :], cols
        total = 1
        for size in left:
            total *= size
        group = min(total, steps)
        cut_rows = steps // group
        block_rows = rows // cut_rows
        span = total // group

        def where(i, c, side, k=k, dim=dim, left=left, lead=lead, span=span, cut_rows=cut_rows):
            half = c[k] if side else 1 - c[k]
            index = (i // cut_rows) * span
            coords = []
            for size in reversed(left):
                coords.append(index % size)
                index = index // size
            coords = coords[::-1]
            if dim == "columns":
                return tuple(coords) + (i % cut_rows, half)
            return tuple(coords[:dim]) + (half,) + tuple(coords[dim:]) + (i % cut_rows, 0)

        tail_axes, covered = [], 1
        for size in reversed(left):
            if covered < span:
                covered *= size
                tail_axes.append(size)
            else:
                tail_axes.append(1)
        tail_axes = tail_axes[::-1]
        assert covered == span
        if dim == "columns":
            block = tuple(tail_axes) + (block_rows, width)
        else:
            block = tuple(tail_axes[:dim]) + (1,) + tuple(tail_axes[dim:]) + (block_rows, cols)

        def spec_map(side, where=where, block=block):
            def index(i, c):
                coords = where(i, c, side)
                return tuple(x // b if n < len(block) - 2 else x for n, (x, b) in enumerate(zip(coords, block)))

            return index

        for side in range(2):
            for a in addends:
                arrays.append(a)
                in_specs.append(pl.BlockSpec(block, spec_map(side)))
        out_block = tuple(tail_axes) + (block_rows, width)

        def out_map(i, c, left=left, span=span, cut_rows=cut_rows, tail_axes=tail_axes):
            index = (i // cut_rows) * span
            coords = []
            for size in reversed(left):
                coords.append(index % size)
                index = index // size
            coords = coords[::-1]
            return tuple(x // b for x, b in zip(coords, tail_axes)) + (i % cut_rows, 0)

        for side in range(2):
            out_specs.append(pl.BlockSpec(out_block, out_map))
            out_shape.append(jax.ShapeDtypeStruct(tuple(left) + (rows, width), jnp.bfloat16))
        counts.append(len(addends))
    outs = pl.pallas_call(
        functools.partial(fold_kernel, counts=tuple(counts)),
        grid_spec=pltpu.PrefetchScalarGridSpec(
            num_scalar_prefetch=1, grid=(steps,), in_specs=in_specs, out_specs=out_specs
        ),
        out_shape=out_shape,
        compiler_params=params(48),
        cost_estimate=pl.CostEstimate(flops=10**7, bytes_accessed=30 * 10**6, transcendentals=0),
        name="fold",
    )(bits, *arrays)
    return [(outs[2 * k], outs[2 * k + 1]) for k in range(len(items))]


def finish_kernel(
    late, pos, c0, c1, e0, e1, o0, o1, outc, oute, outo, outl,
    l1, l2, l1c, l2c, l1x, l1m, l1y, l1z, l1w, l2y, l2z, l2x, l2w,
    cs, ck, cx, cw, es, ek, ex, ew, os, ok, oy, ow, sent, came, near,
):
    def place(axis, bit):
        me = lax.axis_index(axis)
        mine = (me // bit) % 2
        return mine, 1 - mine, {axis: me + bit * (1 - 2 * mine)}

    mc, oc, to_core = place("pos", 1)
    mx, ox, to_x = place("pos", 2)
    my, oy_, to_y = place("seg", 1)
    mz, oz, to_z = place("seg", 2)
    mw, ow_, to_w = place("seg", 4)
    barrier = pltpu.get_barrier_semaphore()
    for who in (to_core, to_x, to_y, to_z, to_w):
        pl.semaphore_signal(barrier, inc=1, device_id=who, device_id_type=pl.DeviceIdType.MESH)
    pl.semaphore_wait(barrier, 5)

    copies = []

    def send(src, dst, who):
        number = len(copies)
        copy = pltpu.make_async_remote_copy(
            src_ref=src,
            dst_ref=dst,
            send_sem=sent.at[number],
            recv_sem=came.at[number],
            device_id=who,
            device_id_type=pl.DeviceIdType.MESH,
        )
        copy.start()
        copies.append(copy)
        return copy

    def plus(left, right):
        return to_low(to_wide(left) + to_wide(right))

    half = l1.shape[3]
    quarter = half // 2
    main = 2 * half
    mine_row = pl.multiple_of(mc * main, 16)
    other_row = pl.multiple_of(oc * main, 16)
    keep_one = pltpu.make_async_copy(late.at[:, :, :, pl.ds(mine_row, half)], l1, near.at[0])
    keep_two = pltpu.make_async_copy(late.at[:, :, :, pl.ds(mine_row + half, half)], l2, near.at[1])
    l1_core = send(late.at[:, :, :, pl.ds(other_row, half)], l1c, to_core)
    l2_core = send(late.at[:, :, :, pl.ds(other_row + half, half)], l2c, to_core)
    keep_one.start()
    keep_two.start()

    cols = ck.shape[2]
    for w in range(2):
        at = pl.ds(pl.multiple_of(ox * cols, LANES), cols)
        cs[w] = plus(c0[w, :, at], c1[w, :, at])
    c_x = send(cs, cx, to_x)
    for w in range(2):
        os[w] = plus(o0[w, oy_], o1[w, oy_])
    o_y = send(os, oy, to_y)
    wide = ek.shape[2]
    for w in range(2):
        at = pl.ds(pl.multiple_of(ox * wide, LANES), wide)
        es[w] = plus(e0[w, :, at], e1[w, :, at])
    e_x = send(es, ex, to_x)
    for w in range(2):
        at = pl.ds(pl.multiple_of(mx * cols, LANES), cols)
        ck[w] = plus(c0[w, :, at], c1[w, :, at])
        at = pl.ds(pl.multiple_of(mx * wide, LANES), wide)
        ek[w] = plus(e0[w, :, at], e1[w, :, at])
        ok[w] = plus(o0[w, my], o1[w, my])

    mine_x = pl.ds(pl.multiple_of(mx * quarter, 16), quarter)
    other_x = pl.ds(pl.multiple_of(ox * quarter, 16), quarter)
    keep_one.wait()
    l1_core.wait_recv()

    @pl.loop(0, 8)
    def _(i):
        at = (i // 4, (i // 2) % 2, i % 2, other_x)
        l1[at] = plus(l1[at], l1c[at])

    l1_x = send(l1.at[:, :, :, other_x], l1x, to_x)

    keep_two.wait()
    l2_core.wait_recv()

    @pl.loop(0, 4)
    def _(i):
        at = (i // 2, i % 2, oy_)
        l2[at] = plus(l2[at], l2c[at])

    l2_y = send(l2.at[:, :, oy_], l2y, to_y)

    @pl.loop(0, 8)
    def _(i):
        a, b, c = i // 4, (i // 2) % 2, i % 2
        at = (a, b, c, mine_x)
        l1m[a, b, c, :quarter] = plus(l1[at], l1c[at])
        l1m[a, b, c, quarter:] = pos[a, b, c]

    @pl.loop(0, 4)
    def _(i):
        at = (i // 2, i % 2, my)
        l2[at] = plus(l2[at], l2c[at])

    o_y.wait_recv()
    ok[ow_] = plus(ok[ow_], oy[ow_])
    o_w = send(ok.at[ow_], ow, to_w)
    ok[mw] = plus(ok[mw], oy[mw])
    c_x.wait_recv()
    ck[ow_] = plus(ck[ow_], cx[ow_])
    c_w = send(ck.at[ow_], cw, to_w)
    ck[mw] = plus(ck[mw], cx[mw])
    e_x.wait_recv()
    ek[ow_] = plus(ek[ow_], ex[ow_])
    e_w = send(ek.at[ow_], ew, to_w)
    ek[mw] = plus(ek[mw], ex[mw])

    l2_y.wait_recv()

    @pl.loop(0, 2)
    def _(a):
        l2[a, oz, my] = plus(l2[a, oz, my], l2y[a, oz])

    l2_z = send(l2.at[:, oz, my], l2z, to_z)

    @pl.loop(0, 2)
    def _(a):
        l2[a, mz, my] = plus(l2[a, mz, my], l2y[a, mz])

    l1_x.wait_recv()

    @pl.loop(0, 4)
    def _(i):
        a, b = i // 2, i % 2
        l1m[a, b, oy_, :quarter] = plus(l1m[a, b, oy_, :quarter], l1x[a, b, oy_])

    l1_y = send(l1m.at[:, :, oy_], l1y, to_y)

    @pl.loop(0, 4)
    def _(i):
        a, b = i // 2, i % 2
        l1m[a, b, my, :quarter] = plus(l1m[a, b, my, :quarter], l1x[a, b, my])

    o_w.wait_recv()
    outo[mc, mx] = plus(ok[mw], ow[...])
    o_gx = send(outo.at[mc, mx], outo.at[mc, mx], to_x)
    c_w.wait_recv()
    outc[mc, mx] = plus(ck[mw], cw[...])
    c_gx = send(outc.at[mc, mx], outc.at[mc, mx], to_x)
    e_w.wait_recv()
    oute[mc, mx] = plus(ek[mw], ew[...])
    e_gx = send(oute.at[mc, mx], oute.at[mc, mx], to_x)

    l2_z.wait_recv()

    @pl.loop(0, 2)
    def _(a):
        l2[a, mz, my, other_x] = plus(l2[a, mz, my, other_x], l2z[a, other_x])

    l2_x = send(l2.at[:, mz, my, other_x], l2x, to_x)

    @pl.loop(0, 2)
    def _(a):
        l2[a, mz, my, mine_x] = plus(l2[a, mz, my, mine_x], l2z[a, mine_x])

    l1_y.wait_recv()

    @pl.loop(0, 2)
    def _(a):
        l1m[a, oz, my] = plus(l1m[a, oz, my], l1y[a, oz])

    l1_z = send(l1m.at[:, oz, my], l1z, to_z)

    @pl.loop(0, 2)
    def _(a):
        l1m[a, mz, my] = plus(l1m[a, mz, my], l1y[a, mz])

    l2_x.wait_recv()
    l2[ow_, mz, my, mine_x] = plus(l2[ow_, mz, my, mine_x], l2x[ow_])
    l2_w = send(l2.at[ow_, mz, my, mine_x], l2w, to_w)
    l2[mw, mz, my, mine_x] = plus(l2[mw, mz, my, mine_x], l2x[mw])

    l1_z.wait_recv()
    l1m[ow_, mz, my] = plus(l1m[ow_, mz, my], l1z[ow_])
    l1_w = send(l1m.at[ow_, mz, my], l1w, to_w)
    l1m[mw, mz, my] = plus(l1m[mw, mz, my], l1z[mw])

    o_gx.wait_recv()
    o_gc = send(outo.at[mc], outo.at[mc], to_core)
    c_gx.wait_recv()
    c_gc = send(outc.at[mc], outc.at[mc], to_core)
    e_gx.wait_recv()
    e_gc = send(oute.at[mc], oute.at[mc], to_core)

    first = l1m.shape[3]
    l2_w.wait_recv()
    outl[mc, mx, first:] = plus(l2[mw, mz, my, mine_x], l2w[...])
    l1_w.wait_recv()
    outl[mc, mx, :first] = plus(l1m[mw, mz, my], l1w[...])
    l_gx = send(outl.at[mc, mx], outl.at[mc, mx], to_x)
    l_gx.wait_recv()
    l_gc = send(outl.at[mc], outl.at[mc], to_core)
    for copy in (o_gc, c_gc, e_gc, l_gc):
        copy.wait_recv()
    for copy in copies:
        copy.wait_send()


def finish(late, pos, c, e, o):
    low = jnp.bfloat16
    half = late.shape[1] // 4
    quarter = half // 2
    both = quarter + pos.shape[1]
    cube = (2, 2, 2)
    c_rows, c_cols = c[0].shape[1], c[0].shape[2] // 2
    e_rows, e_cols = e[0].shape[1], e[0].shape[2] // 2
    o_rows, o_cols = o[0].shape[2:]
    vmem = pl.BlockSpec(memory_space=pltpu.VMEM)
    shapes = [
        cube + (half, LANES),
        cube + (half, LANES),
        cube + (half, LANES),
        cube + (half, LANES),
        cube + (quarter, LANES),
        cube + (both, LANES),
        (2, 2, both, LANES),
        (2, both, LANES),
        (both, LANES),
        (2, 2, half, LANES),
        (2, half, LANES),
        (2, quarter, LANES),
        (quarter, LANES),
        (2, c_rows, c_cols),
        (2, c_rows, c_cols),
        (2, c_rows, c_cols),
        (c_rows, c_cols),
        (2, e_rows, e_cols),
        (2, e_rows, e_cols),
        (2, e_rows, e_cols),
        (e_rows, e_cols),
        (2, o_rows, o_cols),
        (2, o_rows, o_cols),
        (2, o_rows, o_cols),
        (o_rows, o_cols),
    ]
    scratch = [pltpu.VMEM(shape, low) for shape in shapes]
    scratch += [pltpu.SemaphoreType.DMA((24,)), pltpu.SemaphoreType.DMA((24,)), pltpu.SemaphoreType.DMA((2,))]
    out = [(c_rows, c_cols), (e_rows, e_cols), (o_rows, o_cols), (both + quarter, LANES)]
    return pl.pallas_call(
        finish_kernel,
        in_specs=[pl.BlockSpec(memory_space=pl.ANY)] + [vmem] * 7,
        out_specs=[vmem] * 4,
        out_shape=[jax.ShapeDtypeStruct((2, 2) + shape, low) for shape in out],
        scratch_shapes=scratch,
        compiler_params=pltpu.CompilerParams(
            vmem_limit_bytes=56 << 20, collective_id=0, has_side_effects=True
        ),
        cost_estimate=pl.CostEstimate(flops=10**7, bytes_accessed=20 * 10**6, transcendentals=0),
        name="finish",
    )(late.reshape(cube + late.shape[1:]), pos.reshape(cube + pos.shape[1:]), *c, *e, *o)


def mm(spec, left, right):
    return jnp.einsum(spec, left, right, preferred_element_type=jnp.float32)


def position_table(row_count, width_count):
    fine = 64
    inverse_freq = 10000.0 ** (-jnp.arange(0, width_count, 2).astype(jnp.float32) / width_count)
    high = (row_count // fine - 1 - jnp.arange(row_count // fine)) * fine
    low_part = fine - 1 - jnp.arange(fine)
    high_angle = high.astype(jnp.float32)[:, None, None] * inverse_freq
    low_angle = low_part.astype(jnp.float32)[None, :, None] * inverse_freq
    high_sin, high_cos = jnp.sin(high_angle), jnp.cos(high_angle)
    low_sin, low_cos = jnp.sin(low_angle), jnp.cos(low_angle)
    sines = high_sin * low_cos + high_cos * low_sin
    cosines = high_cos * low_cos - high_sin * low_sin
    return to_low(jnp.concatenate([sines, cosines], axis=2)).reshape(row_count, width_count)


def route_mask(routes, expert_count):
    return jnp.sum((routes[..., None] == jnp.arange(expert_count)).astype(jnp.float32), axis=-2)


def bit_of(axis, bit):
    return (lax.axis_index(axis) // bit) % 2


def swap(value, axis, bit):
    pairs = [(i, i ^ bit) for i in range(lax.axis_size(axis))]
    return lax.ppermute(value, axis, pairs)


def pick(value, index, axis):
    return lax.dynamic_index_in_dim(value, index, axis, keepdims=False)


def cut(value, index, axis):
    size = value.shape[axis] // 2
    return lax.dynamic_slice_in_dim(value, index * size, size, axis)


def axis_bits(axis):
    size = lax.axis_size(axis)
    return [1 << k for k in range(size.bit_length() - 1)]


def bits_tree(value, seg_size):
    count = len(axis_bits("seg"))
    return value.reshape((2,) * count + (value.shape[0] // seg_size, value.shape[1]))


class Share:
    def __init__(self, addends, bits):
        self.addends = addends
        self.bits = bits

    def total(self):
        out = to_wide(self.addends[0])
        for item in self.addends[1:]:
            out = out + to_wide(item)
        return to_low(out)

    def seg(self, number):
        if number >= len(axis_bits("seg")):
            return self
        bit = axis_bits("seg")[number]
        dim = len(self.bits) - 1 - self.bits.index(bit)
        mine = bit_of("seg", bit)
        sent = Share([pick(a, 1 - mine, dim) for a in self.addends], self.bits).total()
        come = swap(sent, "seg", bit)
        left = [b for b in self.bits if b != bit]
        return Share([pick(a, mine, dim) for a in self.addends] + [come], left)

    def rest(self):
        out = self
        for bit in self.bits:
            out = out.seg(axis_bits("seg").index(bit))
        return out

    def pos(self, number, dim):
        bit = axis_bits("pos")[number]
        mine = bit_of("pos", bit)
        at = len(self.bits) + dim
        sent = Share([cut(a, 1 - mine, at) for a in self.addends], self.bits).total()
        come = swap(sent, "pos", bit)
        return Share([cut(a, mine, at) for a in self.addends] + [come], self.bits)

    def pos_all(self, number):
        part = self.total()
        return Share([part, swap(part, "pos", axis_bits("pos")[number])], self.bits)


def together(stages):
    items, bits, swaps, lefts = [], [], [], []
    for item, axis, number in stages:
        bit = axis_bits(axis)[number]
        bits.append(bit_of(axis, bit))
        swaps.append((axis, bit))
        if axis == "seg":
            items.append((item.addends, len(item.bits) - 1 - item.bits.index(bit)))
            lefts.append([b for b in item.bits if b != bit])
        else:
            items.append((item.addends, "columns"))
            lefts.append(item.bits)
    pairs = fold(items, jnp.stack(bits).astype(jnp.int32))
    out = []
    for (sent, kept), (axis, bit), left in zip(pairs, swaps, lefts):
        out.append(Share([kept, swap(sent, axis, bit)], left))
    return out


def share(values, seg_size):
    return Share([bits_tree(v, seg_size) for v in values], axis_bits("seg"))


def widen(part, number, dim):
    bit = axis_bits("pos")[number]
    mine = bit_of("pos", bit)
    other = swap(part, "pos", bit)
    first = jnp.where(mine == 0, part, other)
    second = jnp.where(mine == 0, other, part)
    return jnp.concatenate([first, second], axis=dim)


def seg_blocks(value, seg_size):
    blocks, rows, lanes = value.shape
    inside = seg_size // blocks
    value = value.reshape(blocks, rows, inside, lanes // inside)
    value = jnp.transpose(value, (0, 2, 1, 3))
    count = len(axis_bits("seg"))
    return value.reshape((2,) * count + (rows, lanes // inside))


def vector_rows(vectors, seg_size):
    lanes = D // seg_size
    rows = jnp.concatenate([v.reshape(seg_size, -1, lanes) for v in vectors], axis=1)
    blocks = D // LANES
    rows = rows.reshape(blocks, seg_size // blocks, rows.shape[1], lanes)
    return jnp.transpose(rows, (0, 2, 1, 3)).reshape(blocks, -1, LANES)


def local(
    block_input,
    memory_rows,
    memory_length,
    value_routes,
    output_routes,
    first_gain,
    first_shift,
    query_weight,
    key_weight,
    position_weight,
    value_experts,
    value_router,
    content_bias,
    position_bias,
    output_experts,
    output_gate_matrix,
    second_gain,
    second_shift,
    up_projection_weight,
    expand_bias,
    down_projection_weight,
    contract_bias,
    output_cotangent,
):
    seg_count, local_rows, width = block_input.shape
    seg_size = lax.axis_size("seg")
    pos_index = lax.axis_index("pos")
    key_count = 2 * SEQ
    all_rows = seg_count * local_rows
    slots = HEADS * EXPERTS
    score_scale = DH ** (-0.5)
    line = lambda v: v.reshape(1, -1)

    value_pick = jnp.transpose(route_mask(value_routes, EXPERTS), (0, 1, 3, 4, 2))
    value_pick = value_pick.reshape(seg_count, 2, slots, local_rows)
    out_pick = jnp.transpose(route_mask(output_routes, EXPERTS), (0, 2, 3, 1))
    out_pick = out_pick.reshape(seg_count, slots, local_rows)
    pad = ((0, 0), (0, 32 - slots))
    gates = jnp.concatenate([jnp.pad(value_router, pad).T, jnp.pad(output_gate_matrix, pad).T], axis=0)

    def trade(value):
        return lax.all_to_all(value, "pos", split_axis=0, concat_axis=0, tiled=True)

    qk, normed, value_gate, out_gate = project(
        memory_rows,
        block_input,
        line(first_gain),
        line(first_shift),
        query_weight.T,
        key_weight.T,
        gates,
        to_wide(content_bias).reshape(-1, 1),
        to_wide(position_bias).reshape(-1, 1),
        value_pick,
        out_pick,
        score_scale,
    )
    qk = trade(qk)
    values, value_all = experts(normed, value_experts.T, value_gate)
    values = trade(values)

    table_low = position_table(key_count, D)
    weight_local = pick(position_weight.reshape(D, HEADS, DH), pos_index, 1)
    positions = to_low(mm("nd,dc->cn", table_low, weight_local))

    probs = score(memory_length, qk, positions)
    attended = trade(attend(probs, values))

    core = bit_of("pos", 1).astype(jnp.int32).reshape(1)
    cotangent = output_cotangent.reshape(all_rows, width)
    (
        block_output,
        residual,
        grad_normed_two,
        down_sent,
        down_kept,
        up_sent,
        up_kept,
        expand_bias_grad,
    ) = middle(
        core,
        attended,
        out_gate,
        block_input.reshape(all_rows, width),
        cotangent,
        output_experts,
        line(second_gain),
        line(second_shift),
        line(contract_bias),
        up_projection_weight,
        line(expand_bias),
        down_projection_weight,
    )
    down_got = swap(down_sent, "pos", 1)
    up_got = swap(up_sent, "pos", 1)
    grad_residual, grad_attended, grad_out_logit, mix_sent, mix_kept, middle_sums = middle_back(
        core, residual, grad_normed_two, attended, out_gate, cotangent, output_experts, line(second_gain)
    )
    grad_heads = trade(grad_attended)
    mix_got = swap(mix_sent, "pos", 1)
    grad_heads, down_got, up_got, mix_got = lax.optimization_barrier((grad_heads, down_got, up_got, mix_got))
    down = share([down_kept, down_got], seg_size)
    up = share([up_kept, up_got], seg_size)
    mix = share([mix_kept, mix_got], seg_size)
    cube = seg_size * LANES == D and lax.axis_size("pos") == 4
    if cube:
        down, up, mix = together([(down, "seg", 1), (up, "seg", 0), (mix, "pos", 1)])
    else:
        down, up, mix = down.seg(1), up.seg(0), mix.pos(1, 1)

    grad_qk, grad_values, grad_rel, part_sums = attend_back(
        probs, grad_heads, qk, values, positions, score_scale
    )
    grad_values = trade(grad_values)
    grad_qk, grad_values, grad_rel, part_sums, down.addends, up.addends, mix.addends = lax.optimization_barrier(
        (grad_qk, grad_values, grad_rel, part_sums, down.addends, up.addends, mix.addends)
    )
    grad_qk = trade(grad_qk)
    if cube:
        down, up, mix = together([(down, "seg", 0), (up, "seg", 1), (mix, "seg", 1)])
    else:
        down, up, mix = down.seg(0), up.seg(1), mix.seg(0)

    position_grad = to_low(mm("scn,nd->cd", grad_rel, table_low))
    position_grad = jnp.transpose(position_grad.reshape(DH, D // LANES, LANES), (1, 0, 2))
    head_hot = (jnp.arange(HEADS) == pos_index).astype(jnp.float32)[:, None]
    bias_sums = jnp.sum(part_sums, axis=0)
    biases = [(head_hot * bias_sums[k]).reshape(seg_size, -1) for k in range(2)]
    bias_row = jnp.concatenate(biases, axis=1)
    bias_row = jnp.pad(bias_row, ((0, 0), (0, D // seg_size - bias_row.shape[1])))
    extra = vector_rows(
        [middle_sums[0], middle_sums[1], middle_sums[2], expand_bias_grad[0], bias_row], seg_size
    )

    input_grad, late = back(
        memory_rows,
        block_input,
        line(first_gain),
        line(first_shift),
        grad_qk,
        grad_values,
        grad_out_logit,
        value_gate,
        value_all,
        value_experts.T,
        key_weight.T,
        query_weight.T,
        value_router.T,
        output_gate_matrix.T,
        grad_residual.reshape(seg_count, local_rows, width),
        extra,
    )
    late, position_grad, down.addends, up.addends, mix.addends = lax.optimization_barrier(
        (late, position_grad, down.addends, up.addends, mix.addends)
    )
    if cube:
        quarters = finish(late, position_grad, down.addends, up.addends, mix.addends)
        grids = [jnp.transpose(to_wide(q), (2, 0, 1, 3)) for q in quarters[:3]]
        contract_weight_grad, expand_weight_grad, output_experts_grad = [
            g.reshape(g.shape[0], -1) for g in grids
        ]
        tail = to_wide(quarters[3])
        lanes = LANES
        share_rows = late.shape[1] // 4
        piece_rows = share_rows // 2
    else:
        late = Share([late], []).pos(0, 1).total()
        share_rows = late.shape[1] // 2
        one = Share([late[:, :share_rows]], []).pos(1, 1).total()
        piece_rows = one.shape[1]
        one = jnp.concatenate([one, position_grad], axis=1)
        one = Share([seg_blocks(one, seg_size)], axis_bits("seg")).rest().total()
        two = Share([seg_blocks(late[:, share_rows:], seg_size)], axis_bits("seg"))
        two = two.rest().pos(1, 0).total()
        tail = jnp.concatenate([one, two], axis=0)
        tail = to_wide(widen(widen(tail[None], 1, 0)[None], 0, 0))
        lanes = tail.shape[3]
        up = up.pos(1, 1).rest().total()
        expand_weight_grad = to_wide(widen(widen(up, 1, 1), 0, 1))
        down = down.pos(1, 1).rest().total()
        contract_weight_grad = to_wide(widen(widen(down, 1, 1), 0, 1))
        mix = mix.rest().total()
        output_experts_grad = to_wide(widen(widen(mix, 1, 1), 0, 1))
    parts = [tail[:, :, :piece_rows], tail[:, :, tail.shape[2] - piece_rows :]]
    main = jnp.concatenate([p.reshape(2, share_rows, lanes) for p in parts], axis=1).reshape(-1, lanes)
    heads = jnp.transpose(tail[:, :, piece_rows : tail.shape[2] - piece_rows], (1, 0, 2, 3))
    position_weight_grad = heads.reshape(HEADS * DH, lanes).T

    at_key, at_query, at_value, at_out, _ = late_rows(DH)
    first = at_value + slots
    second = at_out + slots
    piece = DH * HEADS // seg_size
    return (
        block_output.reshape(block_input.shape),
        input_grad,
        main[first],
        main[first + 1],
        main[at_query:at_value].T,
        main[at_key:at_query].T,
        position_weight_grad,
        main[:at_key].T,
        main[at_value:first].T,
        main[second + 7, :piece],
        main[second + 7, piece : 2 * piece],
        output_experts_grad,
        main[at_out:second].T,
        main[second],
        main[second + 1],
        expand_weight_grad,
        main[second + 3 : second + 7].reshape(-1),
        contract_weight_grad,
        main[second + 2],
    )


def solution(mesh):
    rows = P("seg", "pos", None)
    whole = P()
    placed = (
        rows,
        rows,
        P("seg"),
        P("seg", None, "pos", None, None),
        P("seg", "pos", None, None),
    )
    placed += (whole,) * 17 + (rows,)
    shares = [P("seg")] * 17
    for index in (2, 3, 4, 5, 6, 9, 10, 13, 15):
        shares[index] = P("seg", None)
    return jax.shard_map(
        local,
        mesh=mesh,
        in_specs=placed,
        out_specs=(rows, rows) + tuple(shares),
        check_vma=False,
    )
```

```python
import functools

import jax
import jax.numpy as jnp
from jax import lax
from jax.experimental import pallas as pl
from jax.experimental.pallas import tpu as pltpu
from jax.sharding import PartitionSpec as P

D = 1024
HEADS = 4
DH = 112
EXPERTS = 5
SEQ = 1024
norm_eps = 1e-05

NEG = -1e30
LANES = 128


def nn(left, right):
    return lax.dot_general(left, right, (((1,), (0,)), ((), ())), preferred_element_type=jnp.float32)


def nt(left, right):
    return lax.dot_general(left, right, (((1,), (1,)), ((), ())), preferred_element_type=jnp.float32)


def to_low(value):
    return value.astype(jnp.bfloat16)


def to_wide(value):
    return value.astype(jnp.float32)


def norm_parts(rows):
    center = rows - jnp.mean(rows, axis=1, keepdims=True)
    inv_std = lax.rsqrt(jnp.mean(center * center, axis=1, keepdims=True) + norm_eps)
    return center * inv_std, inv_std


def vector(value):
    return once(value.shape, lambda *_: (0,))


def once(shape, index_map):
    return pl.BlockSpec(shape, index_map, pipeline_mode=pl.Buffered(1))


def row(ref):
    return to_wide(ref[...]).reshape(1, -1)


def params(megabytes):
    return pltpu.CompilerParams(vmem_limit_bytes=megabytes << 20)


def project_kernel(
    mem_ref, blk_ref, gain_ref, shift_ref, cbias_ref, pbias_ref, wq_ref, wk_ref, gates_ref, pickv_ref, picko_ref,
    qk_ref, norm_ref, gatev_ref, gateo_ref, *, scale,
):
    half = pl.program_id(1)
    rows = to_wide(jnp.where(half == 0, mem_ref[0], blk_ref[0]))
    unit, _ = norm_parts(rows)
    normed = to_low(unit * row(gain_ref) + row(shift_ref))
    norm_ref[0, 0] = normed
    turned = normed.T
    keys = to_low(nn(wk_ref[...], turned))
    dh = qk_ref.shape[3]
    logits = nn(gates_ref[...], turned)
    gatev_ref[0, 0] = jax.nn.sigmoid(logits[: pickv_ref.shape[2]]) * pickv_ref[0, 0]

    @pl.when(half == 0)
    def _():
        for h in range(qk_ref.shape[0]):
            qk_ref[h, 0, 2] = keys[h * dh : (h + 1) * dh]

    @pl.when(half == 1)
    def _():
        query = nn(wq_ref[...], turned)
        inner = query.shape[0]
        biases = [jnp.broadcast_to(row(ref), (LANES, inner)).T[:, :1] for ref in (cbias_ref, pbias_ref)]
        content = to_low((query + biases[0]) * scale)
        position = to_low((query + biases[1]) * scale)
        for h in range(qk_ref.shape[0]):
            qk_ref[h, 0, 0] = content[h * dh : (h + 1) * dh]
            qk_ref[h, 0, 1] = position[h * dh : (h + 1) * dh]
            qk_ref[h, 0, 3] = keys[h * dh : (h + 1) * dh]
        gateo_ref[0] = jax.nn.sigmoid(logits[logits.shape[0] // 2 :][: picko_ref.shape[1]]) * picko_ref[0]


def project(mem, blk, gain, shift, cbias, pbias, wqt, wkt, gates, pickv, picko, scale):
    segs, rows, width = blk.shape
    inner = wqt.shape[0]
    slots = pickv.shape[2]
    low, f32 = jnp.bfloat16, jnp.float32
    dh = inner // HEADS
    flat = lambda s, r: (0, 0)
    row_spec = pl.BlockSpec((1, rows, width), lambda s, r: (s, 0, 0))
    return pl.pallas_call(
        functools.partial(project_kernel, scale=scale),
        grid=(segs, 2),
        in_specs=[
            row_spec,
            row_spec,
            vector(gain),
            vector(shift),
            vector(cbias),
            vector(pbias),
            once(wqt.shape, flat),
            once(wkt.shape, flat),
            once(gates.shape, flat),
            pl.BlockSpec((1, 1, slots, rows), lambda s, r: (s, r, 0, 0)),
            pl.BlockSpec((1, slots, rows), lambda s, r: (s, 0, 0)),
        ],
        out_specs=[
            pl.BlockSpec((HEADS, 1, 4, dh, rows), lambda s, r: (0, s, 0, 0, 0)),
            pl.BlockSpec((1, 1, rows, width), lambda s, r: (s, r, 0, 0)),
            pl.BlockSpec((1, 1, slots, rows), lambda s, r: (s, r, 0, 0)),
            pl.BlockSpec((1, slots, rows), lambda s, r: (s, 0, 0)),
        ],
        out_shape=[
            jax.ShapeDtypeStruct((HEADS, segs, 4, dh, rows), low),
            jax.ShapeDtypeStruct((segs, 2, rows, width), low),
            jax.ShapeDtypeStruct((segs, 2, slots, rows), f32),
            jax.ShapeDtypeStruct((segs, slots, rows), f32),
        ],
        compiler_params=params(60),
        cost_estimate=pl.CostEstimate(flops=3 * 10**9, bytes_accessed=8 * 10**6, transcendentals=0),
        name="project",
    )(mem, blk, gain, shift, cbias, pbias, wqt, wkt, gates, pickv, picko)


def experts_kernel(norm_ref, ve_ref, gate_ref, v_ref, all_ref):
    turned = norm_ref[0, 0].T
    heads, dh = v_ref.shape[0], v_ref.shape[3]
    group = nn(ve_ref[...], turned)
    all_ref[0, 0] = to_low(group)
    for h in range(heads):
        total = jnp.zeros((dh, turned.shape[1]), jnp.float32)
        for e in range(EXPERTS):
            slot = h * EXPERTS + e
            total = total + gate_ref[0, 0, slot : slot + 1] * group[slot * dh : (slot + 1) * dh]
        v_ref[h, 0, 0] = to_low(total)


def experts(normed, vet, gate):
    segs, _, rows, width = normed.shape
    inner = vet.shape[0]
    slots = gate.shape[2]
    dh = inner // (HEADS * EXPERTS)
    low = jnp.bfloat16
    return pl.pallas_call(
        experts_kernel,
        grid=(segs, 2),
        in_specs=[
            pl.BlockSpec((1, 1, rows, width), lambda s, r: (s, r, 0, 0)),
            once(vet.shape, lambda s, r: (0, 0)),
            pl.BlockSpec((1, 1, slots, rows), lambda s, r: (s, r, 0, 0)),
        ],
        out_specs=[
            pl.BlockSpec((HEADS, 1, 1, dh, rows), lambda s, r: (0, s, r, 0, 0)),
            pl.BlockSpec((1, 1, inner, rows), lambda s, r: (s, r, 0, 0)),
        ],
        out_shape=[
            jax.ShapeDtypeStruct((HEADS, segs, 2, dh, rows), low),
            jax.ShapeDtypeStruct((segs, 2, inner, rows), low),
        ],
        compiler_params=params(48),
        cost_estimate=pl.CostEstimate(flops=5 * 10**9, bytes_accessed=12 * 10**6, transcendentals=0),
        name="experts",
    )(normed, vet, gate)


def score_kernel(len_ref, qk_ref, pos_ref, p_ref, kt_s, *, tiles, block, chunk):
    seg = pl.program_id(0)
    start = tiles * block - len_ref[seg]
    for half in range(2):
        for t in range(tiles):
            c0 = (half * tiles + t) * block
            kt_s[:, c0 : c0 + block] = qk_ref[t, 0, 2 + half]
    mem = tiles * block
    for t in range(tiles):
        w = mem + (t + 1) * block
        base = (tiles - 1 - t) * block
        col = lax.broadcasted_iota(jnp.int32, (1, w), 1)
        bias = jnp.where(col >= start, 0.0, NEG)
        content = qk_ref[t, 0, 0].T
        position = qk_ref[t, 0, 1].T
        for r0 in range(0, block, chunk):
            raw = nn(position[r0 : r0 + chunk], pos_ref[:, base:])
            rel = pltpu.roll(raw, w - (block - 1) + r0, 1, stride=1, stride_axis=0)
            s = nn(content[r0 : r0 + chunk], kt_s[:, :w]) + rel
            row = lax.broadcasted_iota(jnp.int32, (chunk, w), 0) + (mem + t * block + r0)
            col_wide = lax.broadcasted_iota(jnp.int32, (chunk, w), 1)
            s = jnp.where(col_wide <= row, s + bias, NEG)
            e = jnp.exp(s - jnp.max(s, axis=1, keepdims=True))
            p = e * (1.0 / jnp.sum(e, axis=1, keepdims=True))
            p_ref[0, t * block + r0 : t * block + r0 + chunk, :w] = to_low(p)


def score(lengths, qk, post):
    tiles, segs, _, dh, block = qk.shape
    keys = 2 * tiles * block
    return pl.pallas_call(
        functools.partial(score_kernel, tiles=tiles, block=block, chunk=64),
        grid_spec=pltpu.PrefetchScalarGridSpec(
            num_scalar_prefetch=1,
            grid=(segs,),
            in_specs=[
                pl.BlockSpec((tiles, 1, 4, dh, block), lambda s, _: (0, s, 0, 0, 0)),
                pl.BlockSpec((dh, keys), lambda s, _: (0, 0)),
            ],
            out_specs=pl.BlockSpec((1, tiles * block, keys), lambda s, _: (s, 0, 0)),
            scratch_shapes=[pltpu.VMEM((dh, keys), jnp.bfloat16)],
        ),
        out_shape=jax.ShapeDtypeStruct((segs, tiles * block, keys), jnp.bfloat16),
        compiler_params=params(48),
        cost_estimate=pl.CostEstimate(flops=12 * 10**9, bytes_accessed=10 * 10**6, transcendentals=4 * 10**6),
        name="score",
    )(lengths, qk, post)


def attend_kernel(p_ref, v_ref, att_ref, v_s, *, tiles, block):
    for half in range(2):
        for t in range(tiles):
            c0 = (half * tiles + t) * block
            v_s[c0 : c0 + block, :] = v_ref[t, 0, half].T
    for t in range(tiles):
        w = tiles * block + (t + 1) * block
        out = nn(p_ref[0, t * block : (t + 1) * block, :w], v_s[:w, :])
        att_ref[t, 0] = to_low(out).T


def attend(p, v):
    tiles, segs, _, dh, block = v.shape
    keys = 2 * tiles * block
    return pl.pallas_call(
        functools.partial(attend_kernel, tiles=tiles, block=block),
        grid=(segs,),
        in_specs=[
            pl.BlockSpec((1, tiles * block, keys), lambda s: (s, 0, 0)),
            pl.BlockSpec((tiles, 1, 2, dh, block), lambda s: (0, s, 0, 0, 0)),
        ],
        out_specs=pl.BlockSpec((tiles, 1, dh, block), lambda s: (0, s, 0, 0)),
        out_shape=jax.ShapeDtypeStruct((tiles, segs, dh, block), jnp.bfloat16),
        scratch_shapes=[pltpu.VMEM((keys, dh), jnp.bfloat16)],
        compiler_params=params(48),
        cost_estimate=pl.CostEstimate(flops=5 * 10**9, bytes_accessed=9 * 10**6, transcendentals=0),
        name="attend",
    )(p, v)


def attend_back_kernel(
    p_ref, g_ref, qk_ref, v_ref, pos_ref, d_ref, dpos_ref, sums_ref,
    k_s, vt_s, posr_s, dkt, dvt, dpt, ds_s, dr_s, *, tiles, block, chunk, scale,
):
    seg = pl.program_id(0)
    for half in range(2):
        for t in range(tiles):
            c0 = (half * tiles + t) * block
            k_s[c0 : c0 + block, :] = qk_ref[t, 0, 2 + half].T
            vt_s[:, c0 : c0 + block] = v_ref[t, 0, half]

    @pl.when(seg == 0)
    def _():
        posr_s[...] = pos_ref[...].T

    dkt[...] = jnp.zeros_like(dkt)
    dvt[...] = jnp.zeros_like(dvt)
    dpt[...] = jnp.zeros_like(dpt)
    mem = tiles * block
    dh = v_ref.shape[3]
    flip = (
        lax.broadcasted_iota(jnp.int32, (block, block), 0) + lax.broadcasted_iota(jnp.int32, (block, block), 1)
        == block - 1
    )
    flip_wide = jnp.where(flip, 1.0, 0.0)
    flip_low = to_low(flip_wide)
    content_sum = jnp.zeros((1, dh), jnp.float32)
    position_sum = jnp.zeros((1, dh), jnp.float32)
    for t in range(tiles):
        w = mem + (t + 1) * block
        base = (tiles - 1 - t) * block
        gt = g_ref[t, 0]
        g = gt.T
        for r0 in range(0, block, chunk):
            p = to_wide(p_ref[0, t * block + r0 : t * block + r0 + chunk, :w])
            prod = p * nn(g[r0 : r0 + chunk], vt_s[:, :w])
            delta = jnp.sum(prod, axis=1, keepdims=True)
            ds_s[r0 : r0 + chunk, :w] = to_low(prod - p * delta)
        ds = ds_s[:, :w]
        for r0 in range(0, block, chunk):
            turned = nn(flip_low[r0 : r0 + chunk], ds)
            dr_s[r0 : r0 + chunk, :w] = to_low(pltpu.roll(turned, r0, 1, stride=1, stride_axis=0))
        dr = dr_s[:, :w]
        dvt[:, :w] += nn(gt, p_ref[0, t * block : (t + 1) * block, :w])
        dkt[:, :w] += nn(qk_ref[t, 0, 0], ds)
        position = to_low(nn(qk_ref[t, 0, 1], flip_low))
        dpt[:, base:] += nn(position, dr)
        dc = nn(ds, k_s[:w, :])
        dp = nn(dr, posr_s[base:, :])
        content_sum = content_sum + jnp.sum(dc, axis=0, keepdims=True)
        position_sum = position_sum + jnp.sum(dp, axis=0, keepdims=True)
        dp = lax.dot_general(
            flip_wide,
            dp,
            (((1,), (0,)), ((), ())),
            precision=lax.Precision.HIGHEST,
            preferred_element_type=jnp.float32,
        )
        d_ref[t, 0, 0] = to_low((dc + dp) * scale).T
    sums_ref[0, 0:1] = content_sum * scale
    sums_ref[0, 1:2] = position_sum * scale
    dpos_ref[0] = to_low(dpt[...])
    for half in range(2):
        for t in range(tiles):
            c0 = (half * tiles + t) * block
            d_ref[t, 0, 1 + half] = to_low(dkt[:, c0 : c0 + block])
            d_ref[t, 0, 3 + half] = to_low(dvt[:, c0 : c0 + block])


def attend_back(p, g, qk, v, post, scale):
    tiles, segs, dh, block = g.shape
    keys = 2 * tiles * block
    low, f32 = jnp.bfloat16, jnp.float32

    def spec(parts):
        return pl.BlockSpec((tiles, 1, parts, dh, block), lambda s: (0, s, 0, 0, 0))

    return pl.pallas_call(
        functools.partial(attend_back_kernel, tiles=tiles, block=block, chunk=64, scale=scale),
        grid=(segs,),
        in_specs=[
            pl.BlockSpec((1, tiles * block, keys), lambda s: (s, 0, 0)),
            pl.BlockSpec((tiles, 1, dh, block), lambda s: (0, s, 0, 0)),
            spec(4),
            spec(2),
            pl.BlockSpec((dh, keys), lambda s: (0, 0)),
        ],
        out_specs=[
            spec(5),
            pl.BlockSpec((1, dh, keys), lambda s: (s, 0, 0)),
            pl.BlockSpec((1, 2, dh), lambda s: (s, 0, 0)),
        ],
        out_shape=[
            jax.ShapeDtypeStruct((tiles, segs, 5, dh, block), low),
            jax.ShapeDtypeStruct((segs, dh, keys), low),
            jax.ShapeDtypeStruct((segs, 2, dh), f32),
        ],
        scratch_shapes=[
            pltpu.VMEM((keys, dh), low),
            pltpu.VMEM((dh, keys), low),
            pltpu.VMEM((keys, dh), low),
            pltpu.VMEM((dh, keys), f32),
            pltpu.VMEM((dh, keys), f32),
            pltpu.VMEM((dh, keys), f32),
            pltpu.VMEM((block, keys), low),
            pltpu.VMEM((block, keys), low),
        ],
        compiler_params=params(56),
        cost_estimate=pl.CostEstimate(flops=25 * 10**9, bytes_accessed=14 * 10**6, transcendentals=0),
        name="attend_back",
    )(p, g, qk, v, post)


def mix_rows(mixed, att_ref, gate_ref):
    heads, segs, dh, rows = att_ref.shape
    for h in range(heads):
        for s in range(segs):
            att = to_wide(att_ref[h, s])
            for e in range(EXPERTS):
                slot = h * EXPERTS + e
                mixed[slot * dh : (slot + 1) * dh, s * rows : (s + 1) * rows] = to_low(
                    gate_ref[s, slot : slot + 1] * att
                )


def middle_kernel(
    core_ref, att_ref, gate_ref, x_ref, g_ref, oe_ref, gain_ref, shift_ref, bd_ref, wu_ref, bu_ref, wd_ref,
    y_ref, res, gn, wds_ref, wdk_ref, wus_ref, wuk_ref, bu_out, mixed, n2, n2t, ffn, *, chunk,
):
    step = pl.program_id(0)
    steps = pl.num_programs(0)
    total, width = x_ref.shape
    half = width // 2
    mine = pl.multiple_of(core_ref[0] * half, half)
    other = pl.multiple_of((1 - core_ref[0]) * half, half)
    count = total // chunk

    @pl.when(step == 0)
    def _():
        mix_rows(mixed, att_ref, gate_ref)
        res[...] = to_wide(x_ref[...]) + nn(mixed[...].T, oe_ref[...])

        @pl.loop(0, count)
        def _(i):
            at = pl.ds(pl.multiple_of(i * chunk, chunk), chunk)
            unit, _ = norm_parts(res[at, :])
            n2[at, :] = to_low(unit * row(gain_ref) + row(shift_ref))

        n2t[...] = n2[...].T
        ffn[...] = jnp.zeros_like(ffn)
        gn[...] = jnp.zeros_like(gn)

    wu = wu_ref[...]
    wd = wd_ref[...]
    v = nn(n2[...], wu) + to_wide(bu_ref[...])
    root = 0.7978845608028654
    square = v * v
    tanh = jnp.tanh(root * (v + 0.044715 * (square * v)))
    plus = 0.5 * (1.0 + tanh)
    hidden = to_low(v * plus)
    slope = plus + 0.5 * v * (1.0 - tanh * tanh) * (root * (1.0 + 0.134145 * square))
    gp = nt(g_ref[...], wd) * slope
    gp_low = to_low(gp)
    bu_out[...] = jnp.sum(to_wide(gp_low), axis=0, keepdims=True)
    ffn[...] += nn(hidden, wd)
    gn[...] += nt(gp_low, wu)
    wu_grad = to_low(nn(n2t[...], gp_low))

    @pl.when(step < steps // 2)
    def _():
        wus_ref[...] = wu_grad

    @pl.when(step >= steps // 2)
    def _():
        wuk_ref[...] = wu_grad

    turned = hidden.T
    wds_ref[...] = to_low(nn(turned, g_ref[:, pl.ds(other, half)]))
    wdk_ref[...] = to_low(nn(turned, g_ref[:, pl.ds(mine, half)]))

    @pl.when(step == steps - 1)
    def _():
        @pl.loop(0, count)
        def _(i):
            at = pl.ds(pl.multiple_of(i * chunk, chunk), chunk)
            y_ref[at, :] = to_low(res[at, :] + ffn[at, :] + row(bd_ref))


def middle(core, att, gate, x, g, oe, gain, shift, bd, wu, bu, wd, fc=512):
    heads, segs, dh, rows = att.shape
    total, width = x.shape
    ff = wu.shape[1]
    steps = ff // fc
    mid = steps // 2
    half = width // 2
    slots = gate.shape[1]
    inner = oe.shape[0]
    low, f32 = jnp.bfloat16, jnp.float32

    def fix(*shape):
        return pl.BlockSpec(shape, lambda i, c: (0,) * len(shape))

    def keep(*shape):
        return once(shape, lambda i, c: (0,) * len(shape))

    def unit(i, c):
        return (i + mid * (1 - c[0])) % steps

    return pl.pallas_call(
        functools.partial(middle_kernel, chunk=64),
        grid_spec=pltpu.PrefetchScalarGridSpec(
            num_scalar_prefetch=1,
            grid=(steps,),
            in_specs=[
                keep(heads, segs, dh, rows),
                keep(segs, slots, rows),
                keep(total, width),
                keep(total, width),
                keep(inner, width),
                vector(gain),
                vector(shift),
                vector(bd),
                pl.BlockSpec((width, fc), lambda i, c: (0, unit(i, c))),
                pl.BlockSpec((1, fc), lambda i, c: (0, unit(i, c))),
                pl.BlockSpec((fc, width), lambda i, c: (unit(i, c), 0)),
            ],
            out_specs=[
                fix(total, width),
                fix(total, width),
                fix(total, width),
                pl.BlockSpec((fc, half), lambda i, c: (unit(i, c), 0)),
                pl.BlockSpec((fc, half), lambda i, c: (unit(i, c), 0)),
                pl.BlockSpec((width, fc), lambda i, c: (0, jnp.minimum(i, mid - 1))),
                pl.BlockSpec((width, fc), lambda i, c: (0, jnp.maximum(i - mid, 0))),
                pl.BlockSpec((1, fc), lambda i, c: (0, unit(i, c))),
            ],
            scratch_shapes=[
                pltpu.VMEM((inner, total), low),
                pltpu.VMEM((total, width), low),
                pltpu.VMEM((width, total), low),
                pltpu.VMEM((total, width), f32),
            ],
        ),
        out_shape=[
            jax.ShapeDtypeStruct((total, width), low),
            jax.ShapeDtypeStruct((total, width), f32),
            jax.ShapeDtypeStruct((total, width), f32),
            jax.ShapeDtypeStruct((ff, half), low),
            jax.ShapeDtypeStruct((ff, half), low),
            jax.ShapeDtypeStruct((width, ff // 2), low),
            jax.ShapeDtypeStruct((width, ff // 2), low),
            jax.ShapeDtypeStruct((1, ff), f32),
        ],
        compiler_params=params(60),
        cost_estimate=pl.CostEstimate(flops=28 * 10**9, bytes_accessed=40 * 10**6, transcendentals=2 * 10**6),
        name="middle",
    )(core, att, gate, x, g, oe, gain, shift, bd, wu, bu, wd)


def middle_back_kernel(
    core_ref, res, gn, att_ref, gate_ref, g_ref, oe_ref, gain_ref,
    gres_ref, gatt_ref, glog_ref, oes_ref, oek_ref, vec_ref, mixed, low_grad, turned, *, chunk,
):
    heads, segs, dh, rows = att_ref.shape
    total, width = g_ref.shape
    half = width // 2
    mine = pl.multiple_of(core_ref[0] * half, half)
    other = pl.multiple_of((1 - core_ref[0]) * half, half)
    mix_rows(mixed, att_ref, gate_ref)
    zero = jnp.zeros((1, width), jnp.float32)

    def rows_back(i, sums):
        at = pl.ds(pl.multiple_of(i * chunk, chunk), chunk)
        unit, inv_std = norm_parts(res[at, :])
        grad = gn[at, :]
        g = to_wide(g_ref[at, :])
        q = grad * row(gain_ref)
        back = q - jnp.mean(q, axis=1, keepdims=True) - unit * jnp.mean(q * unit, axis=1, keepdims=True)
        out = g + inv_std * back
        gres_ref[at, :] = out
        low_grad[at, :] = to_low(out)
        return (
            sums[0] + jnp.sum(grad * unit, axis=0, keepdims=True),
            sums[1] + jnp.sum(grad, axis=0, keepdims=True),
            sums[2] + jnp.sum(g, axis=0, keepdims=True),
        )

    sums = lax.fori_loop(0, total // chunk, rows_back, (zero, zero, zero))
    for k in range(3):
        vec_ref[k : k + 1] = sums[k]
    turned[...] = low_grad[...].T
    for h in range(heads):
        group = nn(oe_ref[h * EXPERTS * dh : (h + 1) * EXPERTS * dh], turned[...])
        for s in range(segs):
            att = to_wide(att_ref[h, s])
            grad = jnp.zeros((dh, rows), jnp.float32)
            for e in range(EXPERTS):
                slot = h * EXPERTS + e
                part = group[e * dh : (e + 1) * dh, s * rows : (s + 1) * rows]
                gate = gate_ref[s, slot : slot + 1]
                grad = grad + gate * part
                logit = jnp.sum(part * att, axis=0, keepdims=True) * (gate * (1.0 - gate))
                glog_ref[s, slot : slot + 1] = logit
            gatt_ref[h, s] = to_low(grad)
    oes_ref[...] = to_low(nn(mixed[...], low_grad[:, pl.ds(other, half)]))
    oek_ref[...] = to_low(nn(mixed[...], low_grad[:, pl.ds(mine, half)]))


def middle_back(core, res, gn, att, gate, g, oe, gain):
    inner, width = oe.shape
    total = g.shape[0]
    low, f32 = jnp.bfloat16, jnp.float32
    vmem = pl.BlockSpec(memory_space=pltpu.VMEM)
    return pl.pallas_call(
        functools.partial(middle_back_kernel, chunk=64),
        in_specs=[pl.BlockSpec(memory_space=pltpu.SMEM)] + [vmem] * 7,
        out_specs=[vmem] * 6,
        out_shape=[
            jax.ShapeDtypeStruct((total, width), f32),
            jax.ShapeDtypeStruct(att.shape, low),
            jax.ShapeDtypeStruct(gate.shape, f32),
            jax.ShapeDtypeStruct((inner, width // 2), low),
            jax.ShapeDtypeStruct((inner, width // 2), low),
            jax.ShapeDtypeStruct((3, width), f32),
        ],
        scratch_shapes=[
            pltpu.VMEM((inner, total), low),
            pltpu.VMEM((total, width), low),
            pltpu.VMEM((width, total), low),
        ],
        compiler_params=params(60),
        cost_estimate=pl.CostEstimate(flops=5 * 10**9, bytes_accessed=20 * 10**6, transcendentals=0),
        name="middle_back",
    )(core, res, gn, att, gate, g, oe, gain)


def late_rows(dh):
    first = HEADS * EXPERTS * dh
    second = first + HEADS * dh
    third = second + HEADS * dh
    return first, second, third, third + 32, third + 64


def back_kernel(
    mem_ref, blk_ref, gain_ref, shift_ref, d_ref, glog_ref, gate_ref, all_ref, ve_ref, wk_ref, wq_ref,
    rv_ref, ro_ref, gres_ref, extra_ref, xg_ref, late_ref, vec, gt, every_gt, every_norm,
):
    half = pl.program_id(1)
    first_step = (pl.program_id(0) == 0) & (half == 0)
    heads, dh = d_ref.shape[0], d_ref.shape[3]
    slots = gate_ref.shape[2]
    at_key, at_query, at_value, at_out, end = late_rows(dh)

    @pl.when(first_step)
    def _():
        gt[at_value:end] = jnp.zeros((end - at_value, gt.shape[1]), jnp.bfloat16)
        vec[...] = jnp.zeros_like(vec)

    for h in range(heads):
        gv = to_wide(jnp.where(half == 0, d_ref[h, 0, 3], d_ref[h, 0, 4]))
        for e in range(EXPERTS):
            slot = h * EXPERTS + e
            gate = gate_ref[0, 0, slot : slot + 1]
            gt[slot * dh : (slot + 1) * dh] = to_low(gate * gv)
            logit = jnp.sum(to_wide(all_ref[0, 0, slot * dh : (slot + 1) * dh]) * gv, axis=0, keepdims=True)
            gt[at_value + slot : at_value + slot + 1] = to_low(logit * (gate * (1.0 - gate)))

    @pl.when(half == 0)
    def _():
        for h in range(heads):
            gt[at_key + h * dh : at_key + (h + 1) * dh] = d_ref[h, 0, 1]
        gt[at_query:at_value] = jnp.zeros((at_value - at_query, gt.shape[1]), jnp.bfloat16)
        gt[at_out : at_out + slots] = jnp.zeros((slots, gt.shape[1]), jnp.bfloat16)

    @pl.when(half == 1)
    def _():
        for h in range(heads):
            gt[at_key + h * dh : at_key + (h + 1) * dh] = d_ref[h, 0, 2]
            gt[at_query + h * dh : at_query + (h + 1) * dh] = d_ref[h, 0, 0]
        gt[at_out : at_out + slots] = to_low(glog_ref[0])

    rows = to_wide(jnp.where(half == 0, mem_ref[0], blk_ref[0]))
    unit, inv_std = norm_parts(rows)
    gain = row(gain_ref)
    normed = to_low(unit * gain + row(shift_ref))
    count = gt.shape[1]
    at = pl.multiple_of((pl.program_id(0) * 2 + half) * count, count)
    every_gt[:, pl.ds(at, count)] = gt[...]
    every_norm[pl.ds(at, count), :] = normed
    grad = nn(gt[:at_key].T, ve_ref[...]) + nn(gt[at_key:at_query].T, wk_ref[...])
    grad = grad + nn(gt[at_query:at_value].T, wq_ref[...])
    grad = grad + nn(gt[at_value : at_value + slots].T, rv_ref[...])
    grad = grad + nn(gt[at_out : at_out + slots].T, ro_ref[...])
    vec[0:1] += jnp.sum(grad * unit, axis=0, keepdims=True)
    vec[1:2] += jnp.sum(grad, axis=0, keepdims=True)

    @pl.when(half == 1)
    def _():
        q = grad * gain
        back = q - jnp.mean(q, axis=1, keepdims=True) - unit * jnp.mean(q * unit, axis=1, keepdims=True)
        xg_ref[0] = to_low(gres_ref[0] + inv_std * back)

    @pl.when((pl.program_id(0) == pl.num_programs(0) - 1) & (half == 1))
    def _():
        for k in range(0, late_ref.shape[0], 2):
            pair = to_low(nn(every_gt[...], every_norm[:, k * LANES : (k + 2) * LANES]))
            late_ref[k] = pair[:, :LANES]
            late_ref[k + 1] = pair[:, LANES:]
        for k in range(late_ref.shape[0]):
            both = vec[0:2, k * LANES : (k + 1) * LANES]
            late_ref[k, at_value + slots : at_value + slots + 2] = to_low(both)
            late_ref[k, at_out + slots : at_out + slots + 8] = to_low(extra_ref[k])


def back(mem, blk, gain, shift, grads, glog, gate, every, vet, wkt, wqt, rvt, rot, gres, extra):
    segs, rows, width = blk.shape
    heads, _, _, dh, _ = grads.shape
    slots = gate.shape[2]
    end = late_rows(dh)[-1]
    low, f32 = jnp.bfloat16, jnp.float32
    row_spec = pl.BlockSpec((1, rows, width), lambda s, r: (s, 0, 0))
    flat = lambda s, r: (0, 0)
    return pl.pallas_call(
        back_kernel,
        grid=(segs, 2),
        in_specs=[
            row_spec,
            row_spec,
            vector(gain),
            vector(shift),
            pl.BlockSpec((heads, 1, 5, dh, rows), lambda s, r: (0, s, 0, 0, 0)),
            pl.BlockSpec((1, slots, rows), lambda s, r: (s, 0, 0)),
            pl.BlockSpec((1, 1, slots, rows), lambda s, r: (s, r, 0, 0)),
            pl.BlockSpec((1, 1, every.shape[2], rows), lambda s, r: (s, r, 0, 0)),
            once(vet.shape, flat),
            once(wkt.shape, flat),
            once(wqt.shape, flat),
            once(rvt.shape, flat),
            once(rot.shape, flat),
            row_spec,
            once(extra.shape, lambda s, r: (0, 0, 0)),
        ],
        out_specs=[
            row_spec,
            pl.BlockSpec((width // LANES, end, LANES), lambda s, r: (0, 0, 0)),
        ],
        out_shape=[
            jax.ShapeDtypeStruct(blk.shape, low),
            jax.ShapeDtypeStruct((width // LANES, end, LANES), low),
        ],
        scratch_shapes=[
            pltpu.VMEM((8, width), f32),
            pltpu.VMEM((end, rows), low),
            pltpu.VMEM((end, 2 * segs * rows), low),
            pltpu.VMEM((2 * segs * rows, width), low),
        ],
        compiler_params=params(60),
        cost_estimate=pl.CostEstimate(flops=14 * 10**9, bytes_accessed=25 * 10**6, transcendentals=0),
        name="back",
    )(mem, blk, gain, shift, grads, glog, gate, every, vet, wkt, wqt, rvt, rot, gres, extra)


def fold_kernel(bits_ref, *refs, counts):
    at = 0
    outs = sum(counts) * 2
    for k, count in enumerate(counts):
        for part in range(2):
            total = to_wide(refs[at][...])
            for extra in range(1, count):
                total = total + to_wide(refs[at + extra][...])
            refs[outs + 2 * k + part][...] = to_low(total).reshape(refs[outs + 2 * k + part].shape)
            at += count


def fold(items, bits):
    in_specs, arrays, out_specs, out_shape, counts = [], [], [], [], []
    steps = 4
    for k, (addends, dim) in enumerate(items):
        shape = addends[0].shape
        rows, cols = shape[-2:]
        lead = shape[:-2]
        if dim == "columns":
            left, width = lead, cols // 2
        else:
            left, width = lead[:dim] + lead[dim + 1 :], cols
        total = 1
        for size in left:
            total *= size
        group = min(total, steps)
        cut_rows = steps // group
        block_rows = rows // cut_rows
        span = total // group

        def where(i, c, side, k=k, dim=dim, left=left, lead=lead, span=span, cut_rows=cut_rows):
            half = c[k] if side else 1 - c[k]
            index = (i // cut_rows) * span
            coords = []
            for size in reversed(left):
                coords.append(index % size)
                index = index // size
            coords = coords[::-1]
            if dim == "columns":
                return tuple(coords) + (i % cut_rows, half)
            return tuple(coords[:dim]) + (half,) + tuple(coords[dim:]) + (i % cut_rows, 0)

        tail_axes, covered = [], 1
        for size in reversed(left):
            if covered < span:
                covered *= size
                tail_axes.append(size)
            else:
                tail_axes.append(1)
        tail_axes = tail_axes[::-1]
        assert covered == span
        if dim == "columns":
            block = tuple(tail_axes) + (block_rows, width)
        else:
            block = tuple(tail_axes[:dim]) + (1,) + tuple(tail_axes[dim:]) + (block_rows, cols)

        def spec_map(side, where=where, block=block):
            def index(i, c):
                coords = where(i, c, side)
                return tuple(x // b if n < len(block) - 2 else x for n, (x, b) in enumerate(zip(coords, block)))

            return index

        for side in range(2):
            for a in addends:
                arrays.append(a)
                in_specs.append(pl.BlockSpec(block, spec_map(side)))
        out_block = tuple(tail_axes) + (block_rows, width)

        def out_map(i, c, left=left, span=span, cut_rows=cut_rows, tail_axes=tail_axes):
            index = (i // cut_rows) * span
            coords = []
            for size in reversed(left):
                coords.append(index % size)
                index = index // size
            coords = coords[::-1]
            return tuple(x // b for x, b in zip(coords, tail_axes)) + (i % cut_rows, 0)

        for side in range(2):
            out_specs.append(pl.BlockSpec(out_block, out_map))
            out_shape.append(jax.ShapeDtypeStruct(tuple(left) + (rows, width), jnp.bfloat16))
        counts.append(len(addends))
    outs = pl.pallas_call(
        functools.partial(fold_kernel, counts=tuple(counts)),
        grid_spec=pltpu.PrefetchScalarGridSpec(
            num_scalar_prefetch=1, grid=(steps,), in_specs=in_specs, out_specs=out_specs
        ),
        out_shape=out_shape,
        compiler_params=params(48),
        cost_estimate=pl.CostEstimate(flops=10**7, bytes_accessed=30 * 10**6, transcendentals=0),
        name="fold",
    )(bits, *arrays)
    return [(outs[2 * k], outs[2 * k + 1]) for k in range(len(items))]


class Chain:
    def __init__(self, axes, stages, shape, halve):
        self.axes, self.stages, self.shape, self.halve = axes, stages, shape, halve

    def landing(self, extra=0):
        free, size, out = list(self.axes), list(self.shape), []
        for stage in self.stages:
            if stage in free:
                free.remove(stage)
            elif stage == "x":
                size[self.halve] //= 2
            elif stage != "c":
                break
            out.append((2,) * len(free) + tuple(size))
            if stage == "x":
                size[0] += extra
        return out


def plus(left, right):
    return to_low(to_wide(left) + to_wide(right))


LATE = ("L1", "L2", "L3")


def late_cut(share):
    third = share // 96 * 32
    return (third, (share - third) // 2, (share - third) // 2)


ORDER = (
    "L10 L20 L30 C0",
    "O0 L11 E0 L31",
    "L21 E1 L12 C1",
    "O1 L22 L32 L13",
    "E2 E3 L23 O2",
    "C2 L14 L33 C3",
    "L24 O3 L34 L15",
    "O4 L25 L16 L35",
    "L26 L36",
)
STARTS = ("C", "O", "E")


def chains(c, e, o, share_rows):
    ends = ["GX", "GC"]
    return {
        "C": Chain(["w"], ["x", "w"] + ends, c, 1),
        "E": Chain(["w"], ["w", "x"] + ends, e, 1),
        "O": Chain(["w", "z", "y"], ["y", "z", "w"] + ends, o, 1),
    } | {
        name: Chain(["w", "z", "y"], ["c"] + list(stages) + ends, (rows, LANES), 0)
        for name, stages, rows in zip(LATE, ("xyzw", "yxzw", "zyxw"), late_cut(share_rows))
    }


def finish_kernel(late, pos, c0, c1, e0, e1, o0, o1, outc, oute, outo, outl, *scratch, table):
    def place(axis, bit):
        me = lax.axis_index(axis)
        mine = (me // bit) % 2
        return mine, {axis: me + bit * (1 - 2 * mine)}

    mine, who = {}, {}
    for name, axis, bit in (("c", "pos", 1), ("x", "pos", 2), ("y", "seg", 1), ("z", "seg", 2), ("w", "seg", 4)):
        mine[name], who[name] = place(axis, bit)
    barrier = pltpu.get_barrier_semaphore()
    for target in who.values():
        pl.semaphore_signal(barrier, inc=1, device_id=target, device_id_type=pl.DeviceIdType.MESH)
    pl.semaphore_wait(barrier, len(who))

    scratch = list(scratch)
    sent, came, near = scratch[-3:]
    work = dict(zip(("C", "E", "O") + LATE + ("L1m",), scratch[:7]))
    landed, at = {}, 7
    for name, chain in table.items():
        stages = len(chain.landing())
        landed[name] = scratch[at : at + stages]
        at += stages
    both = {"C": (c0, c1), "E": (e0, e1), "O": (o0, o1)}
    lead_rows = pos.shape[3]
    late_half = table["L1"].shape[0] // 2
    outs = {"C": (outc, None), "E": (oute, None), "O": (outo, None)}
    first = 0
    for name in LATE:
        size = table[name].shape[0] // 2 + (lead_rows if name == "L1" else 0)
        outs[name] = (outl, (first, size))
        first += size
    started = {}
    copies = []

    def send(key, src, dst, target):
        copy = pltpu.make_async_remote_copy(
            src_ref=src,
            dst_ref=dst,
            send_sem=sent.at[len(copies)],
            recv_sem=came.at[len(copies)],
            device_id=who[target],
            device_id_type=pl.DeviceIdType.MESH,
        )
        copy.start()
        copies.append(copy)
        started[key] = copy

    free = {name: list(chain.axes) for name, chain in table.items()}
    span = {name: (None, chain.shape[chain.halve]) for name, chain in table.items()}

    def pieces(name, start, size):
        halve = table[name].halve
        if start is None:
            return (slice(None), slice(None))
        one = pl.ds(pl.multiple_of(start, 16 if halve == 0 else LANES), size)
        return (one, slice(None)) if halve == 0 else (slice(None), one)

    def part(name, axis, value):
        start, size = span[name]
        fixed = {a: mine[a] for a in table[name].axes if a not in free[name]}
        left = list(free[name])
        relative = None
        if axis == "x":
            size = size // 2
            relative = value * size
            start = relative if start is None else start + relative
        elif axis is not None:
            fixed[axis] = value
            left.remove(axis)
        return left, fixed, start, size, relative

    def total(name, stage, axis, value, store=None):
        left, fixed, start, size, relative = part(name, axis, value)
        chain = table[name]
        switch = name == "L1" and stage is not None and chain.stages[stage] == "x"
        buffer = work[name]

        def one(values):
            index = tuple(values[a] if a in values else fixed[a] for a in chain.axes)
            full = index + pieces(name, start, size)
            if stage is None:
                left_ref, right_ref = both[name]
                got = plus(left_ref[full], right_ref[full])
            else:
                lead = tuple(values[a] if a in values else fixed[a] for a in free[name])
                got = plus(buffer[full], landed[name][stage][lead + pieces(name, relative, size)])
            if store is not None:
                store(got)
            elif switch:
                work["L1m"][index + (slice(0, size), slice(None))] = got
                work["L1m"][index + (slice(size, None), slice(None))] = pos[index]
            else:
                buffer[full] = got

        count = 1 << len(left)
        if count == 1:
            one({})
        elif count == 2:
            for k in range(2):
                one({left[0]: k})
        else:

            @pl.loop(0, count)
            def _(i):
                one({a: (i // (1 << (len(left) - 1 - k))) % 2 for k, a in enumerate(left)})

    def advance(name, stage):
        chain = table[name]
        following = chain.stages[0 if stage is None else stage + 1]
        switch = name == "L1" and stage is not None and chain.stages[stage] == "x"
        number = 0 if stage is None else stage + 1
        out, rows = outs[name]
        place_out = (slice(None), slice(None)) if rows is None else (slice(rows[0], rows[0] + rows[1]), slice(None))
        if following == "GX":

            def store(got):
                out[(mine["c"], mine["x"]) + place_out] = got

            total(name, stage, None, None, store)
            at = out.at[(mine["c"], mine["x"]) + place_out]
            send((name, number), at, at, "x")
            return
        if following == "GC":
            at = out.at[(mine["c"], slice(None)) + place_out]
            send((name, number), at, at, "c")
            return
        other = 1 - mine[following]
        total(name, stage, following, other)
        if switch:
            left, fixed, _, _, _ = part(name, following, other)
            source = work["L1m"]
            index = tuple(slice(None) if a in left else fixed[a] for a in chain.axes) + (slice(None), slice(None))
        else:
            left, fixed, start, size, _ = part(name, following, other)
            source = work[name]
            index = tuple(slice(None) if a in left else fixed[a] for a in chain.axes) + pieces(name, start, size)
        send((name, number), source.at[index], landed[name][number], following)
        total(name, stage, following, mine[following])
        if switch:
            work["L1"] = work["L1m"]
            span["L1"] = (None, late_half + lead_rows)
        if following == "x":
            start, size = span[name]
            half = size // 2
            span[name] = (mine["x"] * half if start is None else start + mine["x"] * half, half)
        else:
            free[name].remove(following)

    share = sum(table[name].shape[0] for name in LATE)
    keep = {}
    first = 0
    for number, name in enumerate(LATE):
        size = table[name].shape[0]
        own = pl.multiple_of(mine["c"] * share + first, 16)
        theirs = pl.multiple_of((1 - mine["c"]) * share + first, 16)
        send((name, 0), late.at[:, :, :, pl.ds(theirs, size)], landed[name][0], "c")
        keep[name] = pltpu.make_async_copy(late.at[:, :, :, pl.ds(own, size)], work[name], near.at[number])
        keep[name].start()
        first += size
    for name in STARTS:
        advance(name, None)
    for event in " ".join(ORDER).split():
        name, stage = event[:-1], int(event[-1])
        started[(name, stage)].wait_recv()
        if stage == 0 and name in keep:
            keep[name].wait()
        if stage + 1 < len(table[name].stages):
            advance(name, stage)
    for copy in copies:
        copy.wait_send()


def finish(late, pos, c, e, o):
    low = jnp.bfloat16
    cube = (2, 2, 2)
    share = late.shape[1] // 2
    table = chains(c[0].shape[1:], e[0].shape[1:], o[0].shape[3:], share)
    lead_rows = pos.shape[1]
    vmem = pl.BlockSpec(memory_space=pltpu.VMEM)
    shapes = [c[0].shape, e[0].shape, o[0].shape]
    shapes += [cube + table[name].shape for name in LATE]
    shapes += [cube + (table["L1"].shape[0] // 2 + lead_rows, LANES)]
    for name, chain in table.items():
        shapes += chain.landing(lead_rows if name == "L1" else 0)
    scratch = [pltpu.VMEM(shape, low) for shape in shapes]
    count = sum(len(chain.stages) for chain in table.values())
    scratch += [pltpu.SemaphoreType.DMA((count,)), pltpu.SemaphoreType.DMA((count,)), pltpu.SemaphoreType.DMA((3,))]
    out = [
        (c[0].shape[1], c[0].shape[2] // 2),
        (e[0].shape[1], e[0].shape[2] // 2),
        o[0].shape[3:],
        (share // 2 + lead_rows, LANES),
    ]
    return pl.pallas_call(
        functools.partial(finish_kernel, table=table),
        in_specs=[pl.BlockSpec(memory_space=pl.ANY)] + [vmem] * 7,
        out_specs=[vmem] * 4,
        out_shape=[jax.ShapeDtypeStruct((2, 2) + shape, low) for shape in out],
        scratch_shapes=scratch,
        compiler_params=pltpu.CompilerParams(vmem_limit_bytes=56 << 20, collective_id=0, has_side_effects=True),
        cost_estimate=pl.CostEstimate(flops=10**7, bytes_accessed=20 * 10**6, transcendentals=0),
        name="finish",
    )(late.reshape(cube + late.shape[1:]), pos.reshape(cube + pos.shape[1:]), *c, *e, *o)


def emit_kernel(c_hbm, e_hbm, o_hbm, l_hbm, *refs, plan, slots):
    outs, (c_ref, e_ref, o_ref, l_ref, vals, sems) = refs[:-6], refs[-6:]
    pairs = ((l_hbm, l_ref), (c_hbm, c_ref), (e_hbm, e_ref), (o_hbm, o_ref))
    copies = [pltpu.make_async_copy(a, b, sems.at[k]) for k, (a, b) in enumerate(pairs)]
    for copy in copies:
        copy.start()
    copies[0].wait()
    experts, keys, queries, positions, values, gates = outs[3:9]
    targets = (experts, keys, queries, vals, positions)
    for core, x, start, number, to, rows in plan:
        targets[number][to : to + rows] = to_wide(l_ref[core, x, start : start + rows])
    half = vals.shape[0] // 2
    values[...] = vals[:slots]
    gates[...] = vals[half : half + slots]
    first_gain, first_shift, second_gain, second_shift, contract, expand, content, position = outs[9:]
    lines = ((first_gain, slots), (first_shift, slots + 1))
    lines += tuple((ref, half + slots + k) for k, ref in enumerate((second_gain, second_shift, contract)))
    for ref, number in lines:
        ref[...] = vals[number]
    for k in range(4):
        expand[k * LANES : (k + 1) * LANES] = vals[half + slots + 3 + k]
    size = content.shape[0]
    content[...] = vals[half + slots + 7, :size]
    position[...] = vals[half + slots + 7, size : 2 * size]
    for k, ref in enumerate((c_ref, e_ref, o_ref)):
        width = ref.shape[3]
        copies[k + 1].wait()
        for core in range(2):
            for x in range(2):
                at = (core * 2 + x) * width
                outs[k][:, at : at + width] = to_wide(ref[core, x])


def emit(quarters, dh):
    c, e, o, tail = quarters
    f32 = jnp.float32
    slots = HEADS * EXPERTS
    at_key, at_query, at_value, _, end = late_rows(dh)
    halves = [rows // 2 for rows in late_cut(end // 2)]
    sizes = [at_key, at_query - at_key, at_value - at_query, end - at_value]
    starts = [0, at_key, at_query, at_value]
    plan = []
    for core in range(2):
        for x in range(2):
            for part, piece in enumerate(halves):
                source = sum(halves[:part]) + (dh if part else 0)
                low_end = core * (end // 2) + 2 * sum(halves[:part]) + x * piece
                for k, (first, size) in enumerate(zip(starts, sizes)):
                    a, b = max(first, low_end), min(first + size, low_end + piece)
                    if a < b:
                        plan.append((core, x, source + a - low_end, k, a - first, b - a))
            plan.append((core, x, halves[0], 4, (2 * x + core) * dh, dh))
    vmem = pl.BlockSpec(memory_space=pltpu.VMEM)
    shapes = [(q.shape[2], 4 * q.shape[3]) for q in (c, e, o)] + [(n, LANES) for n in sizes[:3] + [HEADS * dh]]
    shapes += [(slots, LANES)] * 2 + [(LANES,)] * 5 + [(4 * LANES,)] + [(HEADS * dh * LANES // D,)] * 2
    return pl.pallas_call(
        functools.partial(emit_kernel, plan=tuple(plan), slots=slots),
        in_specs=[pl.BlockSpec(memory_space=pl.ANY)] * 4,
        out_specs=[vmem] * len(shapes),
        out_shape=[jax.ShapeDtypeStruct(shape, f32) for shape in shapes],
        scratch_shapes=[pltpu.VMEM(q.shape, q.dtype) for q in quarters]
        + [pltpu.VMEM((end - at_value, LANES), f32), pltpu.SemaphoreType.DMA((4,))],
        compiler_params=params(60),
        name="emit",
    )(c, e, o, tail)


def mm(spec, left, right):
    return jnp.einsum(spec, left, right, preferred_element_type=jnp.float32)


def position_table(row_count, width_count):
    fine = 64
    inverse_freq = 10000.0 ** (-jnp.arange(0, width_count, 2).astype(jnp.float32) / width_count)
    high = (row_count // fine - 1 - jnp.arange(row_count // fine)) * fine
    low_part = fine - 1 - jnp.arange(fine)
    high_angle = high.astype(jnp.float32)[:, None, None] * inverse_freq
    low_angle = low_part.astype(jnp.float32)[None, :, None] * inverse_freq
    high_sin, high_cos = jnp.sin(high_angle), jnp.cos(high_angle)
    low_sin, low_cos = jnp.sin(low_angle), jnp.cos(low_angle)
    sines = high_sin * low_cos + high_cos * low_sin
    cosines = high_cos * low_cos - high_sin * low_sin
    return to_low(jnp.concatenate([sines, cosines], axis=2)).reshape(row_count, width_count)


def route_mask(routes, expert_count):
    return jnp.sum((routes[..., None] == jnp.arange(expert_count)).astype(jnp.float32), axis=-2)


def bit_of(axis, bit):
    return (lax.axis_index(axis) // bit) % 2


def swap(value, axis, bit):
    pairs = [(i, i ^ bit) for i in range(lax.axis_size(axis))]
    return lax.ppermute(value, axis, pairs)


def pick(value, index, axis):
    return lax.dynamic_index_in_dim(value, index, axis, keepdims=False)


def cut(value, index, axis):
    size = value.shape[axis] // 2
    return lax.dynamic_slice_in_dim(value, index * size, size, axis)


def axis_bits(axis):
    size = lax.axis_size(axis)
    return [1 << k for k in range(size.bit_length() - 1)]


def bits_tree(value, seg_size):
    count = len(axis_bits("seg"))
    return value.reshape((2,) * count + (value.shape[0] // seg_size, value.shape[1]))


class Share:
    def __init__(self, addends, bits):
        self.addends = addends
        self.bits = bits

    def total(self):
        out = to_wide(self.addends[0])
        for item in self.addends[1:]:
            out = out + to_wide(item)
        return to_low(out)

    def seg(self, number):
        if number >= len(axis_bits("seg")):
            return self
        bit = axis_bits("seg")[number]
        dim = len(self.bits) - 1 - self.bits.index(bit)
        mine = bit_of("seg", bit)
        sent = Share([pick(a, 1 - mine, dim) for a in self.addends], self.bits).total()
        come = swap(sent, "seg", bit)
        left = [b for b in self.bits if b != bit]
        return Share([pick(a, mine, dim) for a in self.addends] + [come], left)

    def rest(self):
        out = self
        for bit in self.bits:
            out = out.seg(axis_bits("seg").index(bit))
        return out

    def pos(self, number, dim):
        bit = axis_bits("pos")[number]
        mine = bit_of("pos", bit)
        at = len(self.bits) + dim
        sent = Share([cut(a, 1 - mine, at) for a in self.addends], self.bits).total()
        come = swap(sent, "pos", bit)
        return Share([cut(a, mine, at) for a in self.addends] + [come], self.bits)

    def pos_all(self, number):
        part = self.total()
        return Share([part, swap(part, "pos", axis_bits("pos")[number])], self.bits)


def together(stages):
    items, bits, swaps, lefts = [], [], [], []
    for item, axis, number in stages:
        bit = axis_bits(axis)[number]
        bits.append(bit_of(axis, bit))
        swaps.append((axis, bit))
        if axis == "seg":
            items.append((item.addends, len(item.bits) - 1 - item.bits.index(bit)))
            lefts.append([b for b in item.bits if b != bit])
        else:
            items.append((item.addends, "columns"))
            lefts.append(item.bits)
    pairs = fold(items, jnp.stack(bits).astype(jnp.int32))
    out = []
    for (sent, kept), (axis, bit), left in zip(pairs, swaps, lefts):
        out.append(Share([kept, swap(sent, axis, bit)], left))
    return out


def share(values, seg_size):
    return Share([bits_tree(v, seg_size) for v in values], axis_bits("seg"))


def widen(part, number, dim):
    bit = axis_bits("pos")[number]
    mine = bit_of("pos", bit)
    other = swap(part, "pos", bit)
    first = jnp.where(mine == 0, part, other)
    second = jnp.where(mine == 0, other, part)
    return jnp.concatenate([first, second], axis=dim)


def seg_blocks(value, seg_size):
    blocks, rows, lanes = value.shape
    inside = seg_size // blocks
    value = value.reshape(blocks, rows, inside, lanes // inside)
    value = jnp.transpose(value, (0, 2, 1, 3))
    count = len(axis_bits("seg"))
    return value.reshape((2,) * count + (rows, lanes // inside))


def vector_rows(vectors, seg_size):
    lanes = D // seg_size
    rows = jnp.concatenate([v.reshape(seg_size, -1, lanes) for v in vectors], axis=1)
    blocks = D // LANES
    rows = rows.reshape(blocks, seg_size // blocks, rows.shape[1], lanes)
    return jnp.transpose(rows, (0, 2, 1, 3)).reshape(blocks, -1, LANES)


def local(
    block_input,
    memory_rows,
    memory_length,
    value_routes,
    output_routes,
    first_gain,
    first_shift,
    query_weight,
    key_weight,
    position_weight,
    value_experts,
    value_router,
    content_bias,
    position_bias,
    output_experts,
    output_gate_matrix,
    second_gain,
    second_shift,
    up_projection_weight,
    expand_bias,
    down_projection_weight,
    contract_bias,
    output_cotangent,
):
    seg_count, local_rows, width = block_input.shape
    seg_size = lax.axis_size("seg")
    pos_index = lax.axis_index("pos")
    key_count = 2 * SEQ
    all_rows = seg_count * local_rows
    slots = HEADS * EXPERTS
    score_scale = DH ** (-0.5)
    line = lambda v: v.reshape(1, -1)

    value_pick = jnp.transpose(route_mask(value_routes, EXPERTS), (0, 1, 3, 4, 2))
    value_pick = value_pick.reshape(seg_count, 2, slots, local_rows)
    out_pick = jnp.transpose(route_mask(output_routes, EXPERTS), (0, 2, 3, 1))
    out_pick = out_pick.reshape(seg_count, slots, local_rows)
    pad = ((0, 0), (0, 32 - slots))
    gates = jnp.concatenate([jnp.pad(value_router, pad).T, jnp.pad(output_gate_matrix, pad).T], axis=0)

    def trade(value):
        return lax.all_to_all(value, "pos", split_axis=0, concat_axis=0, tiled=True)

    qk, normed, value_gate, out_gate = project(
        memory_rows,
        block_input,
        first_gain,
        first_shift,
        content_bias,
        position_bias,
        query_weight.T,
        key_weight.T,
        gates,
        value_pick,
        out_pick,
        score_scale,
    )
    qk = trade(qk)
    values, value_all = experts(normed, value_experts.T, value_gate)
    values = trade(values)

    table_low = position_table(key_count, D)
    weight_local = pick(position_weight.reshape(D, HEADS, DH), pos_index, 1)
    positions = to_low(mm("nd,dc->cn", table_low, weight_local))

    probs = score(memory_length, qk, positions)
    attended = trade(attend(probs, values))

    core = bit_of("pos", 1).astype(jnp.int32).reshape(1)
    cotangent = output_cotangent.reshape(all_rows, width)
    (
        block_output,
        residual,
        grad_normed_two,
        down_sent,
        down_kept,
        up_sent,
        up_kept,
        expand_bias_grad,
    ) = middle(
        core,
        attended,
        out_gate,
        block_input.reshape(all_rows, width),
        cotangent,
        output_experts,
        second_gain,
        second_shift,
        contract_bias,
        up_projection_weight,
        line(expand_bias),
        down_projection_weight,
    )
    down_got = swap(down_sent, "pos", 1)
    up_got = swap(up_sent, "pos", 1)
    grad_residual, grad_attended, grad_out_logit, mix_sent, mix_kept, middle_sums = middle_back(
        core, residual, grad_normed_two, attended, out_gate, cotangent, output_experts, second_gain
    )
    grad_heads = trade(grad_attended)
    mix_got = swap(mix_sent, "pos", 1)
    down = share([down_kept, down_got], seg_size)
    up = share([up_kept, up_got], seg_size)
    mix = share([mix_kept, mix_got], seg_size)
    cube = seg_size * LANES == D and lax.axis_size("pos") == 4
    if cube:
        down, up = together([(down, "seg", 1), (up, "seg", 0)])
    else:
        down, up = down.seg(1), up.seg(0)

    grads, grad_rel, part_sums = attend_back(
        probs, grad_heads, qk, values, positions, score_scale
    )
    grads = trade(grads)
    part_sums, down.addends, up.addends, mix.addends = lax.optimization_barrier(
        (part_sums, down.addends, up.addends, mix.addends)
    )
    if cube:
        down, up, mix = together([(down, "seg", 0), (up, "seg", 1), (mix, "pos", 1)])
    else:
        down, up, mix = down.seg(0), up.seg(1), mix.pos(1, 1)

    position_grad = to_low(mm("scn,nd->cd", grad_rel, table_low))
    position_grad = jnp.transpose(position_grad.reshape(DH, D // LANES, LANES), (1, 0, 2))
    head_hot = (jnp.arange(HEADS) == pos_index).astype(jnp.float32)[:, None]
    bias_sums = jnp.sum(part_sums, axis=0)
    biases = [(head_hot * bias_sums[k]).reshape(seg_size, -1) for k in range(2)]
    bias_row = jnp.concatenate(biases, axis=1)
    bias_row = jnp.pad(bias_row, ((0, 0), (0, D // seg_size - bias_row.shape[1])))
    extra = vector_rows(
        [middle_sums[0], middle_sums[1], middle_sums[2], expand_bias_grad[0], bias_row], seg_size
    )

    input_grad, late = back(
        memory_rows,
        block_input,
        first_gain,
        first_shift,
        grads,
        grad_out_logit,
        value_gate,
        value_all,
        value_experts.T,
        key_weight.T,
        query_weight.T,
        value_router.T,
        output_gate_matrix.T,
        grad_residual.reshape(seg_count, local_rows, width),
        extra,
    )
    late, position_grad, down.addends, up.addends, mix.addends = lax.optimization_barrier(
        (late, position_grad, down.addends, up.addends, mix.addends)
    )
    if cube:
        quarters = finish(late, position_grad, down.addends, up.addends, mix.addends)
        contract_weight_grad, expand_weight_grad, output_experts_grad, *rows_out = emit(quarters, DH)
        experts_grad, keys_grad, queries_grad, positions_grad, value_grad, out_grad = rows_out[:6]
        vectors = rows_out[6:]
    else:
        late = Share([late], []).pos(0, 1).total()
        share_rows = late.shape[1] // 2
        one = Share([late[:, :share_rows]], []).pos(1, 1).total()
        piece_rows = one.shape[1]
        one = jnp.concatenate([one, position_grad], axis=1)
        one = Share([seg_blocks(one, seg_size)], axis_bits("seg")).rest().total()
        two = Share([seg_blocks(late[:, share_rows:], seg_size)], axis_bits("seg"))
        two = two.rest().pos(1, 0).total()
        tail = jnp.concatenate([one, two], axis=0)
        tail = to_wide(widen(widen(tail[None], 1, 0)[None], 0, 0))
        lanes = tail.shape[3]
        up = up.pos(1, 1).rest().total()
        expand_weight_grad = to_wide(widen(widen(up, 1, 1), 0, 1))
        down = down.pos(1, 1).rest().total()
        contract_weight_grad = to_wide(widen(widen(down, 1, 1), 0, 1))
        mix = mix.rest().total()
        output_experts_grad = to_wide(widen(widen(mix, 1, 1), 0, 1))
        parts = [tail[:, :, :piece_rows], tail[:, :, tail.shape[2] - piece_rows :]]
        main = jnp.concatenate([p.reshape(2, share_rows, lanes) for p in parts], axis=1).reshape(-1, lanes)
        heads = jnp.transpose(tail[:, :, piece_rows : tail.shape[2] - piece_rows], (1, 0, 2, 3))
        edges = (0,) + late_rows(DH)
        rows_out = [main[a:b] for a, b in zip(edges, edges[1:])] + [heads.reshape(HEADS * DH, lanes)]
        experts_grad, keys_grad, queries_grad, value_rows, out_rows, positions_grad = rows_out
        value_grad, out_grad = value_rows[:slots], out_rows[:slots]
        extra = out_rows[slots : slots + 8]
        piece = DH * HEADS // seg_size
        vectors = [value_rows[slots], value_rows[slots + 1], extra[0], extra[1], extra[2]]
        vectors += [extra[3:7].reshape(-1), extra[7, :piece], extra[7, piece : 2 * piece]]
    return (
        block_output.reshape(block_input.shape),
        input_grad,
        vectors[0],
        vectors[1],
        queries_grad.T,
        keys_grad.T,
        positions_grad.T,
        experts_grad.T,
        value_grad.T,
        vectors[6],
        vectors[7],
        output_experts_grad,
        out_grad.T,
        vectors[2],
        vectors[3],
        expand_weight_grad,
        vectors[5],
        contract_weight_grad,
        vectors[4],
    )


def solution(mesh):
    rows = P("seg", "pos", None)
    whole = P()
    placed = (
        rows,
        rows,
        P("seg"),
        P("seg", None, "pos", None, None),
        P("seg", "pos", None, None),
    )
    placed += (whole,) * 17 + (rows,)
    shares = [P("seg")] * 17
    for index in (2, 3, 4, 5, 6, 9, 10, 13, 15):
        shares[index] = P("seg", None)
    return jax.shard_map(
        local,
        mesh=mesh,
        in_specs=placed,
        out_specs=(rows, rows) + tuple(shares),
        check_vma=False,
    )
```

```python
import functools

import jax
import jax.numpy as jnp
from jax import lax
from jax.experimental import pallas as pl
from jax.experimental.pallas import tpu as pltpu
from jax.sharding import PartitionSpec as P

D = 1024
HEADS = 4
DH = 112
EXPERTS = 5
SEQ = 1024
norm_eps = 1e-05

NEG = -1e30
LANES = 128


def nn(left, right):
    return lax.dot_general(left, right, (((1,), (0,)), ((), ())), preferred_element_type=jnp.float32)


def nt(left, right):
    return lax.dot_general(left, right, (((1,), (1,)), ((), ())), preferred_element_type=jnp.float32)


def to_low(value):
    return value.astype(jnp.bfloat16)


def to_wide(value):
    return value.astype(jnp.float32)


def norm_parts(rows):
    center = rows - jnp.mean(rows, axis=1, keepdims=True)
    inv_std = lax.rsqrt(jnp.mean(center * center, axis=1, keepdims=True) + norm_eps)
    return center * inv_std, inv_std


def vector(value):
    return once(value.shape, lambda *_: (0,))


def once(shape, index_map):
    return pl.BlockSpec(shape, index_map, pipeline_mode=pl.Buffered(1))


def row(ref):
    return to_wide(ref[...]).reshape(1, -1)


def params(megabytes):
    return pltpu.CompilerParams(vmem_limit_bytes=megabytes << 20)


def project_kernel(
    mem_ref, blk_ref, gain_ref, shift_ref, wq_ref, wk_ref, gates_ref, pickv_ref, picko_ref,
    qk_ref, norm_ref, gatev_ref, gateo_ref,
):
    half = pl.program_id(1)
    rows = to_wide(jnp.where(half == 0, mem_ref[0], blk_ref[0]))
    unit, _ = norm_parts(rows)
    normed = to_low(unit * row(gain_ref) + row(shift_ref))
    norm_ref[0, 0] = normed
    turned = normed.T
    keys = to_low(nn(wk_ref[...], turned))
    dh = qk_ref.shape[3]
    logits = nn(gates_ref[...], turned)
    gatev_ref[0, 0] = jax.nn.sigmoid(logits[: pickv_ref.shape[2]]) * pickv_ref[0, 0]

    @pl.when(half == 0)
    def _():
        for h in range(qk_ref.shape[0]):
            qk_ref[h, 0, 1] = keys[h * dh : (h + 1) * dh]

    @pl.when(half == 1)
    def _():
        query = to_low(nn(wq_ref[...], turned))
        for h in range(qk_ref.shape[0]):
            qk_ref[h, 0, 0] = query[h * dh : (h + 1) * dh]
            qk_ref[h, 0, 2] = keys[h * dh : (h + 1) * dh]
        gateo_ref[0] = jax.nn.sigmoid(logits[logits.shape[0] // 2 :][: picko_ref.shape[1]]) * picko_ref[0]


def project(mem, blk, gain, shift, wqt, wkt, gates, pickv, picko):
    segs, rows, width = blk.shape
    inner = wqt.shape[0]
    slots = pickv.shape[2]
    low, f32 = jnp.bfloat16, jnp.float32
    dh = inner // HEADS
    flat = lambda s, r: (0, 0)
    row_spec = pl.BlockSpec((1, rows, width), lambda s, r: (s, 0, 0))
    return pl.pallas_call(
        project_kernel,
        grid=(segs, 2),
        in_specs=[
            row_spec,
            row_spec,
            vector(gain),
            vector(shift),
            once(wqt.shape, flat),
            once(wkt.shape, flat),
            once(gates.shape, flat),
            pl.BlockSpec((1, 1, slots, rows), lambda s, r: (s, r, 0, 0)),
            pl.BlockSpec((1, slots, rows), lambda s, r: (s, 0, 0)),
        ],
        out_specs=[
            pl.BlockSpec((HEADS, 1, 3, dh, rows), lambda s, r: (0, s, 0, 0, 0)),
            pl.BlockSpec((1, 1, rows, width), lambda s, r: (s, r, 0, 0)),
            pl.BlockSpec((1, 1, slots, rows), lambda s, r: (s, r, 0, 0)),
            pl.BlockSpec((1, slots, rows), lambda s, r: (s, 0, 0)),
        ],
        out_shape=[
            jax.ShapeDtypeStruct((HEADS, segs, 3, dh, rows), low),
            jax.ShapeDtypeStruct((segs, 2, rows, width), low),
            jax.ShapeDtypeStruct((segs, 2, slots, rows), f32),
            jax.ShapeDtypeStruct((segs, slots, rows), f32),
        ],
        compiler_params=params(60),
        cost_estimate=pl.CostEstimate(flops=3 * 10**9, bytes_accessed=8 * 10**6, transcendentals=0),
        name="project",
    )(mem, blk, gain, shift, wqt, wkt, gates, pickv, picko)


def experts_kernel(norm_ref, ve_ref, gate_ref, v_ref, all_ref):
    turned = norm_ref[0, 0].T
    heads, dh = v_ref.shape[0], v_ref.shape[3]
    group = nn(ve_ref[...], turned)
    all_ref[0, 0] = to_low(group)
    for h in range(heads):
        total = jnp.zeros((dh, turned.shape[1]), jnp.float32)
        for e in range(EXPERTS):
            slot = h * EXPERTS + e
            total = total + gate_ref[0, 0, slot : slot + 1] * group[slot * dh : (slot + 1) * dh]
        v_ref[h, 0, 0] = to_low(total)


def experts(normed, vet, gate):
    segs, _, rows, width = normed.shape
    inner = vet.shape[0]
    slots = gate.shape[2]
    dh = inner // (HEADS * EXPERTS)
    low = jnp.bfloat16
    return pl.pallas_call(
        experts_kernel,
        grid=(segs, 2),
        in_specs=[
            pl.BlockSpec((1, 1, rows, width), lambda s, r: (s, r, 0, 0)),
            once(vet.shape, lambda s, r: (0, 0)),
            pl.BlockSpec((1, 1, slots, rows), lambda s, r: (s, r, 0, 0)),
        ],
        out_specs=[
            pl.BlockSpec((HEADS, 1, 1, dh, rows), lambda s, r: (0, s, r, 0, 0)),
            pl.BlockSpec((1, 1, inner, rows), lambda s, r: (s, r, 0, 0)),
        ],
        out_shape=[
            jax.ShapeDtypeStruct((HEADS, segs, 2, dh, rows), low),
            jax.ShapeDtypeStruct((segs, 2, inner, rows), low),
        ],
        compiler_params=params(48),
        cost_estimate=pl.CostEstimate(flops=5 * 10**9, bytes_accessed=12 * 10**6, transcendentals=0),
        name="experts",
    )(normed, vet, gate)


def column(ref):
    value = row(ref)
    return jnp.broadcast_to(value, (LANES, value.shape[1])).T[:, :1]


def biased(query, bias, scale):
    return to_low((to_wide(query) + bias) * scale)


def score_kernel(len_ref, qk_ref, pos_ref, cb_ref, pb_ref, p_ref, kt_s, *, tiles, block, chunk, scale):
    seg = pl.program_id(0)
    start = tiles * block - len_ref[seg]
    for half in range(2):
        for t in range(tiles):
            c0 = (half * tiles + t) * block
            kt_s[:, c0 : c0 + block] = qk_ref[t, 0, 1 + half]
    mem = tiles * block
    cb, pb = column(cb_ref), column(pb_ref)
    for t in range(tiles):
        w = mem + (t + 1) * block
        base = (tiles - 1 - t) * block
        col = lax.broadcasted_iota(jnp.int32, (1, w), 1)
        bias = jnp.where(col >= start, 0.0, NEG)
        content = biased(qk_ref[t, 0, 0], cb, scale).T
        position = biased(qk_ref[t, 0, 0], pb, scale).T
        for r0 in range(0, block, chunk):
            raw = nn(position[r0 : r0 + chunk], pos_ref[:, base:])
            rel = pltpu.roll(raw, w - (block - 1) + r0, 1, stride=1, stride_axis=0)
            s = nn(content[r0 : r0 + chunk], kt_s[:, :w]) + rel
            row = lax.broadcasted_iota(jnp.int32, (chunk, w), 0) + (mem + t * block + r0)
            col_wide = lax.broadcasted_iota(jnp.int32, (chunk, w), 1)
            s = jnp.where(col_wide <= row, s + bias, NEG)
            e = jnp.exp(s - jnp.max(s, axis=1, keepdims=True))
            p = e * (1.0 / jnp.sum(e, axis=1, keepdims=True))
            p_ref[0, t * block + r0 : t * block + r0 + chunk, :w] = to_low(p)


def score(lengths, qk, post, cbias, pbias, scale):
    tiles, segs, _, dh, block = qk.shape
    keys = 2 * tiles * block
    return pl.pallas_call(
        functools.partial(score_kernel, tiles=tiles, block=block, chunk=64, scale=scale),
        grid_spec=pltpu.PrefetchScalarGridSpec(
            num_scalar_prefetch=1,
            grid=(segs,),
            in_specs=[
                pl.BlockSpec((tiles, 1, 3, dh, block), lambda s, _: (0, s, 0, 0, 0)),
                pl.BlockSpec((dh, keys), lambda s, _: (0, 0)),
                vector(cbias),
                vector(pbias),
            ],
            out_specs=pl.BlockSpec((1, tiles * block, keys), lambda s, _: (s, 0, 0)),
            scratch_shapes=[pltpu.VMEM((dh, keys), jnp.bfloat16)],
        ),
        out_shape=jax.ShapeDtypeStruct((segs, tiles * block, keys), jnp.bfloat16),
        compiler_params=params(48),
        cost_estimate=pl.CostEstimate(flops=12 * 10**9, bytes_accessed=10 * 10**6, transcendentals=4 * 10**6),
        name="score",
    )(lengths, qk, post, cbias, pbias)


def attend_kernel(p_ref, v_ref, out_ref, v_s, buf, sent, came, near, *, tiles, block):
    seg = pl.program_id(0)
    segs = buf.shape[1]
    me = lax.axis_index("pos")
    peers = [(me + d) % tiles for d in range(1, tiles)]

    @pl.when(seg == 0)
    def _():
        barrier = pltpu.get_barrier_semaphore()
        for peer in peers:
            pl.semaphore_signal(barrier, inc=1, device_id={"pos": peer}, device_id_type=pl.DeviceIdType.MESH)

    for half in range(2):
        for t in range(tiles):
            c0 = (half * tiles + t) * block
            v_s[c0 : c0 + block, :] = v_ref[t, 0, half].T
    for t in range(tiles):
        w = tiles * block + (t + 1) * block
        out = nn(p_ref[0, t * block : (t + 1) * block, :w], v_s[:w, :])
        buf[t, seg] = to_low(out).T

    @pl.when(seg == 0)
    def _():
        pl.semaphore_wait(pltpu.get_barrier_semaphore(), tiles - 1)

    def moves(s):
        away = [
            pltpu.make_async_remote_copy(
                src_ref=buf.at[peer, s],
                dst_ref=out_ref.at[me, s],
                send_sem=sent.at[d, s],
                recv_sem=came.at[d, s],
                device_id={"pos": peer},
                device_id_type=pl.DeviceIdType.MESH,
            )
            for d, peer in enumerate(peers)
        ]
        return away, pltpu.make_async_copy(buf.at[me, s], out_ref.at[me, s], near.at[s])

    away, here = moves(seg)
    for copy in away:
        copy.start()
    here.start()

    @pl.when(seg == segs - 1)
    def _():
        for s in range(segs):
            away, here = moves(s)
            for copy in away:
                copy.wait()
            here.wait()


def attend(p, v):
    tiles, segs, _, dh, block = v.shape
    keys = 2 * tiles * block
    return pl.pallas_call(
        functools.partial(attend_kernel, tiles=tiles, block=block),
        grid=(segs,),
        in_specs=[
            pl.BlockSpec((1, tiles * block, keys), lambda s: (s, 0, 0)),
            pl.BlockSpec((tiles, 1, 2, dh, block), lambda s: (0, s, 0, 0, 0)),
        ],
        out_specs=pl.BlockSpec(memory_space=pl.ANY),
        out_shape=jax.ShapeDtypeStruct((tiles, segs, dh, block), jnp.bfloat16),
        scratch_shapes=[
            pltpu.VMEM((keys, dh), jnp.bfloat16),
            pltpu.VMEM((tiles, segs, dh, block), jnp.bfloat16),
            pltpu.SemaphoreType.DMA((tiles - 1, segs)),
            pltpu.SemaphoreType.DMA((tiles - 1, segs)),
            pltpu.SemaphoreType.DMA((segs,)),
        ],
        compiler_params=pltpu.CompilerParams(vmem_limit_bytes=48 << 20, collective_id=1, has_side_effects=True),
        cost_estimate=pl.CostEstimate(flops=5 * 10**9, bytes_accessed=9 * 10**6, transcendentals=0),
        name="attend",
    )(p, v)


def attend_back_kernel(
    p_ref, g_ref, qk_ref, v_ref, pos_ref, cb_ref, pb_ref, d_ref, dpos_ref, sums_ref,
    k_s, vt_s, posr_s, dkt, dvt, dpt, ds_s, dr_s, *, tiles, block, chunk, scale,
):
    seg = pl.program_id(0)
    for half in range(2):
        for t in range(tiles):
            c0 = (half * tiles + t) * block
            k_s[c0 : c0 + block, :] = qk_ref[t, 0, 1 + half].T
            vt_s[:, c0 : c0 + block] = v_ref[t, 0, half]

    @pl.when(seg == 0)
    def _():
        posr_s[...] = pos_ref[...].T

    dkt[...] = jnp.zeros_like(dkt)
    dvt[...] = jnp.zeros_like(dvt)
    dpt[...] = jnp.zeros_like(dpt)
    mem = tiles * block
    dh = v_ref.shape[3]
    flip = (
        lax.broadcasted_iota(jnp.int32, (block, block), 0) + lax.broadcasted_iota(jnp.int32, (block, block), 1)
        == block - 1
    )
    flip_wide = jnp.where(flip, 1.0, 0.0)
    flip_low = to_low(flip_wide)
    cb, pb = column(cb_ref), column(pb_ref)
    content_sum = jnp.zeros((1, dh), jnp.float32)
    position_sum = jnp.zeros((1, dh), jnp.float32)
    for t in range(tiles):
        w = mem + (t + 1) * block
        base = (tiles - 1 - t) * block
        gt = g_ref[t, 0]
        g = gt.T
        for r0 in range(0, block, chunk):
            p = to_wide(p_ref[0, t * block + r0 : t * block + r0 + chunk, :w])
            prod = p * nn(g[r0 : r0 + chunk], vt_s[:, :w])
            delta = jnp.sum(prod, axis=1, keepdims=True)
            ds_s[r0 : r0 + chunk, :w] = to_low(prod - p * delta)
        ds = ds_s[:, :w]
        for r0 in range(0, block, chunk):
            turned = nn(flip_low[r0 : r0 + chunk], ds)
            dr_s[r0 : r0 + chunk, :w] = to_low(pltpu.roll(turned, r0, 1, stride=1, stride_axis=0))
        dr = dr_s[:, :w]
        dvt[:, :w] += nn(gt, p_ref[0, t * block : (t + 1) * block, :w])
        dkt[:, :w] += nn(biased(qk_ref[t, 0, 0], cb, scale), ds)
        position = to_low(nn(biased(qk_ref[t, 0, 0], pb, scale), flip_low))
        dpt[:, base:] += nn(position, dr)
        dc = nn(ds, k_s[:w, :])
        dp = nn(dr, posr_s[base:, :])
        content_sum = content_sum + jnp.sum(dc, axis=0, keepdims=True)
        position_sum = position_sum + jnp.sum(dp, axis=0, keepdims=True)
        dp = lax.dot_general(
            flip_wide,
            dp,
            (((1,), (0,)), ((), ())),
            precision=lax.Precision.HIGHEST,
            preferred_element_type=jnp.float32,
        )
        d_ref[t, 0, 0] = to_low((dc + dp) * scale).T
    sums_ref[0, 0:1] = content_sum * scale
    sums_ref[0, 1:2] = position_sum * scale
    dpos_ref[0] = to_low(dpt[...])
    for half in range(2):
        for t in range(tiles):
            c0 = (half * tiles + t) * block
            d_ref[t, 0, 1 + half] = to_low(dkt[:, c0 : c0 + block])
            d_ref[t, 0, 3 + half] = to_low(dvt[:, c0 : c0 + block])


def attend_back(p, g, qk, v, post, cbias, pbias, scale):
    tiles, segs, dh, block = g.shape
    keys = 2 * tiles * block
    low, f32 = jnp.bfloat16, jnp.float32

    def spec(parts):
        return pl.BlockSpec((tiles, 1, parts, dh, block), lambda s: (0, s, 0, 0, 0))

    return pl.pallas_call(
        functools.partial(attend_back_kernel, tiles=tiles, block=block, chunk=64, scale=scale),
        grid=(segs,),
        in_specs=[
            pl.BlockSpec((1, tiles * block, keys), lambda s: (s, 0, 0)),
            pl.BlockSpec((tiles, 1, dh, block), lambda s: (0, s, 0, 0)),
            spec(3),
            spec(2),
            pl.BlockSpec((dh, keys), lambda s: (0, 0)),
            vector(cbias),
            vector(pbias),
        ],
        out_specs=[
            spec(5),
            pl.BlockSpec((1, dh, keys), lambda s: (s, 0, 0)),
            pl.BlockSpec((1, 2, dh), lambda s: (s, 0, 0)),
        ],
        out_shape=[
            jax.ShapeDtypeStruct((tiles, segs, 5, dh, block), low),
            jax.ShapeDtypeStruct((segs, dh, keys), low),
            jax.ShapeDtypeStruct((segs, 2, dh), f32),
        ],
        scratch_shapes=[
            pltpu.VMEM((keys, dh), low),
            pltpu.VMEM((dh, keys), low),
            pltpu.VMEM((keys, dh), low),
            pltpu.VMEM((dh, keys), f32),
            pltpu.VMEM((dh, keys), f32),
            pltpu.VMEM((dh, keys), f32),
            pltpu.VMEM((block, keys), low),
            pltpu.VMEM((block, keys), low),
        ],
        compiler_params=params(56),
        cost_estimate=pl.CostEstimate(flops=25 * 10**9, bytes_accessed=14 * 10**6, transcendentals=0),
        name="attend_back",
    )(p, g, qk, v, post, cbias, pbias)


def mix_rows(mixed, att_ref, gate_ref):
    heads, segs, dh, rows = att_ref.shape
    for h in range(heads):
        for s in range(segs):
            att = to_wide(att_ref[h, s])
            for e in range(EXPERTS):
                slot = h * EXPERTS + e
                mixed[slot * dh : (slot + 1) * dh, s * rows : (s + 1) * rows] = to_low(
                    gate_ref[s, slot : slot + 1] * att
                )


def middle_kernel(
    core_ref, att_ref, gate_ref, x_ref, g_ref, oe_ref, gain_ref, shift_ref, bd_ref, wu_ref, bu_ref, wd_ref,
    y_ref, res, gn, wds_ref, wdk_ref, wus_ref, wuk_ref, bu_out, mixed, n2, n2t, ffn, *, chunk,
):
    step = pl.program_id(0)
    steps = pl.num_programs(0)
    total, width = x_ref.shape
    half = width // 2
    mine = pl.multiple_of(core_ref[0] * half, half)
    other = pl.multiple_of((1 - core_ref[0]) * half, half)
    count = total // chunk

    @pl.when(step == 0)
    def _():
        mix_rows(mixed, att_ref, gate_ref)
        res[...] = to_wide(x_ref[...]) + nn(mixed[...].T, oe_ref[...])

        @pl.loop(0, count)
        def _(i):
            at = pl.ds(pl.multiple_of(i * chunk, chunk), chunk)
            unit, _ = norm_parts(res[at, :])
            n2[at, :] = to_low(unit * row(gain_ref) + row(shift_ref))

        n2t[...] = n2[...].T
        ffn[...] = jnp.zeros_like(ffn)
        gn[...] = jnp.zeros_like(gn)

    wu = wu_ref[...]
    wd = wd_ref[...]
    v = nn(n2[...], wu) + to_wide(bu_ref[...])
    root = 0.7978845608028654
    square = v * v
    tanh = jnp.tanh(root * (v + 0.044715 * (square * v)))
    plus = 0.5 * (1.0 + tanh)
    hidden = to_low(v * plus)
    slope = plus + 0.5 * v * (1.0 - tanh * tanh) * (root * (1.0 + 0.134145 * square))
    gp = nt(g_ref[...], wd) * slope
    gp_low = to_low(gp)
    bu_out[...] = jnp.sum(to_wide(gp_low), axis=0, keepdims=True)
    ffn[...] += nn(hidden, wd)
    gn[...] += nt(gp_low, wu)
    wu_grad = to_low(nn(n2t[...], gp_low))

    @pl.when(step < steps // 2)
    def _():
        wus_ref[...] = wu_grad

    @pl.when(step >= steps // 2)
    def _():
        wuk_ref[...] = wu_grad

    turned = hidden.T
    wds_ref[...] = to_low(nn(turned, g_ref[:, pl.ds(other, half)]))
    wdk_ref[...] = to_low(nn(turned, g_ref[:, pl.ds(mine, half)]))

    @pl.when(step == steps - 1)
    def _():
        @pl.loop(0, count)
        def _(i):
            at = pl.ds(pl.multiple_of(i * chunk, chunk), chunk)
            y_ref[at, :] = to_low(res[at, :] + ffn[at, :] + row(bd_ref))


def middle(core, att, gate, x, g, oe, gain, shift, bd, wu, bu, wd, fc=512):
    heads, segs, dh, rows = att.shape
    total, width = x.shape
    ff = wu.shape[1]
    steps = ff // fc
    mid = steps // 2
    half = width // 2
    slots = gate.shape[1]
    inner = oe.shape[0]
    low, f32 = jnp.bfloat16, jnp.float32

    def fix(*shape):
        return pl.BlockSpec(shape, lambda i, c: (0,) * len(shape))

    def keep(*shape):
        return once(shape, lambda i, c: (0,) * len(shape))

    def unit(i, c):
        return (i + mid * (1 - c[0])) % steps

    return pl.pallas_call(
        functools.partial(middle_kernel, chunk=64),
        grid_spec=pltpu.PrefetchScalarGridSpec(
            num_scalar_prefetch=1,
            grid=(steps,),
            in_specs=[
                keep(heads, segs, dh, rows),
                keep(segs, slots, rows),
                keep(total, width),
                keep(total, width),
                keep(inner, width),
                vector(gain),
                vector(shift),
                vector(bd),
                pl.BlockSpec((width, fc), lambda i, c: (0, unit(i, c))),
                pl.BlockSpec((1, fc), lambda i, c: (0, unit(i, c))),
                pl.BlockSpec((fc, width), lambda i, c: (unit(i, c), 0)),
            ],
            out_specs=[
                fix(total, width),
                fix(total, width),
                fix(total, width),
                pl.BlockSpec((fc, half), lambda i, c: (unit(i, c), 0)),
                pl.BlockSpec((fc, half), lambda i, c: (unit(i, c), 0)),
                pl.BlockSpec((width, fc), lambda i, c: (0, jnp.minimum(i, mid - 1))),
                pl.BlockSpec((width, fc), lambda i, c: (0, jnp.maximum(i - mid, 0))),
                pl.BlockSpec((1, fc), lambda i, c: (0, unit(i, c))),
            ],
            scratch_shapes=[
                pltpu.VMEM((inner, total), low),
                pltpu.VMEM((total, width), low),
                pltpu.VMEM((width, total), low),
                pltpu.VMEM((total, width), f32),
            ],
        ),
        out_shape=[
            jax.ShapeDtypeStruct((total, width), low),
            jax.ShapeDtypeStruct((total, width), f32),
            jax.ShapeDtypeStruct((total, width), f32),
            jax.ShapeDtypeStruct((ff, half), low),
            jax.ShapeDtypeStruct((ff, half), low),
            jax.ShapeDtypeStruct((width, ff // 2), low),
            jax.ShapeDtypeStruct((width, ff // 2), low),
            jax.ShapeDtypeStruct((1, ff), f32),
        ],
        compiler_params=params(60),
        cost_estimate=pl.CostEstimate(flops=28 * 10**9, bytes_accessed=40 * 10**6, transcendentals=2 * 10**6),
        name="middle",
    )(core, att, gate, x, g, oe, gain, shift, bd, wu, bu, wd)


def middle_back_kernel(
    core_ref, res, gn, att_ref, gate_ref, g_ref, oe_ref, gain_ref,
    gres_ref, gatt_ref, glog_ref, oes_ref, oek_ref, vec_ref, mixed, low_grad, turned, *, chunk,
):
    heads, segs, dh, rows = att_ref.shape
    total, width = g_ref.shape
    half = width // 2
    mine = pl.multiple_of(core_ref[0] * half, half)
    other = pl.multiple_of((1 - core_ref[0]) * half, half)
    mix_rows(mixed, att_ref, gate_ref)
    zero = jnp.zeros((1, width), jnp.float32)

    def rows_back(i, sums):
        at = pl.ds(pl.multiple_of(i * chunk, chunk), chunk)
        unit, inv_std = norm_parts(res[at, :])
        grad = gn[at, :]
        g = to_wide(g_ref[at, :])
        q = grad * row(gain_ref)
        back = q - jnp.mean(q, axis=1, keepdims=True) - unit * jnp.mean(q * unit, axis=1, keepdims=True)
        out = g + inv_std * back
        gres_ref[at, :] = out
        low_grad[at, :] = to_low(out)
        return (
            sums[0] + jnp.sum(grad * unit, axis=0, keepdims=True),
            sums[1] + jnp.sum(grad, axis=0, keepdims=True),
            sums[2] + jnp.sum(g, axis=0, keepdims=True),
        )

    sums = lax.fori_loop(0, total // chunk, rows_back, (zero, zero, zero))
    for k in range(3):
        vec_ref[k : k + 1] = sums[k]
    turned[...] = low_grad[...].T
    for h in range(heads):
        group = nn(oe_ref[h * EXPERTS * dh : (h + 1) * EXPERTS * dh], turned[...])
        for s in range(segs):
            att = to_wide(att_ref[h, s])
            grad = jnp.zeros((dh, rows), jnp.float32)
            for e in range(EXPERTS):
                slot = h * EXPERTS + e
                part = group[e * dh : (e + 1) * dh, s * rows : (s + 1) * rows]
                gate = gate_ref[s, slot : slot + 1]
                grad = grad + gate * part
                logit = jnp.sum(part * att, axis=0, keepdims=True) * (gate * (1.0 - gate))
                glog_ref[s, slot : slot + 1] = logit
            gatt_ref[h, s] = to_low(grad)
    oes_ref[...] = to_low(nn(mixed[...], low_grad[:, pl.ds(other, half)]))
    oek_ref[...] = to_low(nn(mixed[...], low_grad[:, pl.ds(mine, half)]))


def middle_back(core, res, gn, att, gate, g, oe, gain):
    inner, width = oe.shape
    total = g.shape[0]
    low, f32 = jnp.bfloat16, jnp.float32
    vmem = pl.BlockSpec(memory_space=pltpu.VMEM)
    return pl.pallas_call(
        functools.partial(middle_back_kernel, chunk=64),
        in_specs=[pl.BlockSpec(memory_space=pltpu.SMEM)] + [vmem] * 7,
        out_specs=[vmem] * 6,
        out_shape=[
            jax.ShapeDtypeStruct((total, width), f32),
            jax.ShapeDtypeStruct(att.shape, low),
            jax.ShapeDtypeStruct(gate.shape, f32),
            jax.ShapeDtypeStruct((inner, width // 2), low),
            jax.ShapeDtypeStruct((inner, width // 2), low),
            jax.ShapeDtypeStruct((3, width), f32),
        ],
        scratch_shapes=[
            pltpu.VMEM((inner, total), low),
            pltpu.VMEM((total, width), low),
            pltpu.VMEM((width, total), low),
        ],
        compiler_params=params(60),
        cost_estimate=pl.CostEstimate(flops=5 * 10**9, bytes_accessed=20 * 10**6, transcendentals=0),
        name="middle_back",
    )(core, res, gn, att, gate, g, oe, gain)


def late_rows(dh):
    first = HEADS * EXPERTS * dh
    second = first + HEADS * dh
    third = second + HEADS * dh
    return first, second, third, third + 32, third + 64


def back_kernel(
    mem_ref, blk_ref, gain_ref, shift_ref, d_ref, glog_ref, gate_ref, all_ref, ve_ref, wk_ref, wq_ref,
    rv_ref, ro_ref, gres_ref, extra_ref, xg_ref, late_ref, vec, gt, every_gt, every_norm,
):
    half = pl.program_id(1)
    first_step = (pl.program_id(0) == 0) & (half == 0)
    heads, dh = d_ref.shape[0], d_ref.shape[3]
    slots = gate_ref.shape[2]
    at_key, at_query, at_value, at_out, end = late_rows(dh)

    @pl.when(first_step)
    def _():
        gt[at_value:end] = jnp.zeros((end - at_value, gt.shape[1]), jnp.bfloat16)
        vec[...] = jnp.zeros_like(vec)

    for h in range(heads):
        gv = to_wide(jnp.where(half == 0, d_ref[h, 0, 3], d_ref[h, 0, 4]))
        for e in range(EXPERTS):
            slot = h * EXPERTS + e
            gate = gate_ref[0, 0, slot : slot + 1]
            gt[slot * dh : (slot + 1) * dh] = to_low(gate * gv)
            logit = jnp.sum(to_wide(all_ref[0, 0, slot * dh : (slot + 1) * dh]) * gv, axis=0, keepdims=True)
            gt[at_value + slot : at_value + slot + 1] = to_low(logit * (gate * (1.0 - gate)))

    @pl.when(half == 0)
    def _():
        for h in range(heads):
            gt[at_key + h * dh : at_key + (h + 1) * dh] = d_ref[h, 0, 1]
        gt[at_query:at_value] = jnp.zeros((at_value - at_query, gt.shape[1]), jnp.bfloat16)
        gt[at_out : at_out + slots] = jnp.zeros((slots, gt.shape[1]), jnp.bfloat16)

    @pl.when(half == 1)
    def _():
        for h in range(heads):
            gt[at_key + h * dh : at_key + (h + 1) * dh] = d_ref[h, 0, 2]
            gt[at_query + h * dh : at_query + (h + 1) * dh] = d_ref[h, 0, 0]
        gt[at_out : at_out + slots] = to_low(glog_ref[0])

    rows = to_wide(jnp.where(half == 0, mem_ref[0], blk_ref[0]))
    unit, inv_std = norm_parts(rows)
    gain = row(gain_ref)
    normed = to_low(unit * gain + row(shift_ref))
    count = gt.shape[1]
    at = pl.multiple_of((pl.program_id(0) * 2 + half) * count, count)
    every_gt[:, pl.ds(at, count)] = gt[...]
    every_norm[pl.ds(at, count), :] = normed
    grad = nn(gt[:at_key].T, ve_ref[...]) + nn(gt[at_key:at_query].T, wk_ref[...])
    grad = grad + nn(gt[at_query:at_value].T, wq_ref[...])
    grad = grad + nn(gt[at_value : at_value + slots].T, rv_ref[...])
    grad = grad + nn(gt[at_out : at_out + slots].T, ro_ref[...])
    vec[0:1] += jnp.sum(grad * unit, axis=0, keepdims=True)
    vec[1:2] += jnp.sum(grad, axis=0, keepdims=True)

    @pl.when(half == 1)
    def _():
        q = grad * gain
        back = q - jnp.mean(q, axis=1, keepdims=True) - unit * jnp.mean(q * unit, axis=1, keepdims=True)
        xg_ref[0] = to_low(gres_ref[0] + inv_std * back)

    @pl.when((pl.program_id(0) == pl.num_programs(0) - 1) & (half == 1))
    def _():
        for k in range(0, late_ref.shape[0], 2):
            pair = to_low(nn(every_gt[...], every_norm[:, k * LANES : (k + 2) * LANES]))
            late_ref[k] = pair[:, :LANES]
            late_ref[k + 1] = pair[:, LANES:]
        for k in range(late_ref.shape[0]):
            both = vec[0:2, k * LANES : (k + 1) * LANES]
            late_ref[k, at_value + slots : at_value + slots + 2] = to_low(both)
            late_ref[k, at_out + slots : at_out + slots + 8] = to_low(extra_ref[k])


def back(mem, blk, gain, shift, grads, glog, gate, every, vet, wkt, wqt, rvt, rot, gres, extra):
    segs, rows, width = blk.shape
    heads, _, _, dh, _ = grads.shape
    slots = gate.shape[2]
    end = late_rows(dh)[-1]
    low, f32 = jnp.bfloat16, jnp.float32
    row_spec = pl.BlockSpec((1, rows, width), lambda s, r: (s, 0, 0))
    flat = lambda s, r: (0, 0)
    return pl.pallas_call(
        back_kernel,
        grid=(segs, 2),
        in_specs=[
            row_spec,
            row_spec,
            vector(gain),
            vector(shift),
            pl.BlockSpec((heads, 1, 5, dh, rows), lambda s, r: (0, s, 0, 0, 0)),
            pl.BlockSpec((1, slots, rows), lambda s, r: (s, 0, 0)),
            pl.BlockSpec((1, 1, slots, rows), lambda s, r: (s, r, 0, 0)),
            pl.BlockSpec((1, 1, every.shape[2], rows), lambda s, r: (s, r, 0, 0)),
            once(vet.shape, flat),
            once(wkt.shape, flat),
            once(wqt.shape, flat),
            once(rvt.shape, flat),
            once(rot.shape, flat),
            row_spec,
            once(extra.shape, lambda s, r: (0, 0, 0)),
        ],
        out_specs=[
            row_spec,
            pl.BlockSpec((width // LANES, end, LANES), lambda s, r: (0, 0, 0)),
        ],
        out_shape=[
            jax.ShapeDtypeStruct(blk.shape, low),
            jax.ShapeDtypeStruct((width // LANES, end, LANES), low),
        ],
        scratch_shapes=[
            pltpu.VMEM((8, width), f32),
            pltpu.VMEM((end, rows), low),
            pltpu.VMEM((end, 2 * segs * rows), low),
            pltpu.VMEM((2 * segs * rows, width), low),
        ],
        compiler_params=params(60),
        cost_estimate=pl.CostEstimate(flops=14 * 10**9, bytes_accessed=25 * 10**6, transcendentals=0),
        name="back",
    )(mem, blk, gain, shift, grads, glog, gate, every, vet, wkt, wqt, rvt, rot, gres, extra)


def fold_kernel(bits_ref, *refs, counts):
    at = 0
    outs = sum(counts) * 2
    for k, count in enumerate(counts):
        for part in range(2):
            total = to_wide(refs[at][...])
            for extra in range(1, count):
                total = total + to_wide(refs[at + extra][...])
            refs[outs + 2 * k + part][...] = to_low(total).reshape(refs[outs + 2 * k + part].shape)
            at += count


def fold(items, bits):
    in_specs, arrays, out_specs, out_shape, counts = [], [], [], [], []
    steps = 4
    for k, (addends, dim) in enumerate(items):
        shape = addends[0].shape
        rows, cols = shape[-2:]
        lead = shape[:-2]
        if dim == "columns":
            left, width = lead, cols // 2
        else:
            left, width = lead[:dim] + lead[dim + 1 :], cols
        total = 1
        for size in left:
            total *= size
        group = min(total, steps)
        cut_rows = steps // group
        block_rows = rows // cut_rows
        span = total // group

        def where(i, c, side, k=k, dim=dim, left=left, lead=lead, span=span, cut_rows=cut_rows):
            half = c[k] if side else 1 - c[k]
            index = (i // cut_rows) * span
            coords = []
            for size in reversed(left):
                coords.append(index % size)
                index = index // size
            coords = coords[::-1]
            if dim == "columns":
                return tuple(coords) + (i % cut_rows, half)
            return tuple(coords[:dim]) + (half,) + tuple(coords[dim:]) + (i % cut_rows, 0)

        tail_axes, covered = [], 1
        for size in reversed(left):
            if covered < span:
                covered *= size
                tail_axes.append(size)
            else:
                tail_axes.append(1)
        tail_axes = tail_axes[::-1]
        assert covered == span
        if dim == "columns":
            block = tuple(tail_axes) + (block_rows, width)
        else:
            block = tuple(tail_axes[:dim]) + (1,) + tuple(tail_axes[dim:]) + (block_rows, cols)

        def spec_map(side, where=where, block=block):
            def index(i, c):
                coords = where(i, c, side)
                return tuple(x // b if n < len(block) - 2 else x for n, (x, b) in enumerate(zip(coords, block)))

            return index

        for side in range(2):
            for a in addends:
                arrays.append(a)
                in_specs.append(pl.BlockSpec(block, spec_map(side)))
        out_block = tuple(tail_axes) + (block_rows, width)

        def out_map(i, c, left=left, span=span, cut_rows=cut_rows, tail_axes=tail_axes):
            index = (i // cut_rows) * span
            coords = []
            for size in reversed(left):
                coords.append(index % size)
                index = index // size
            coords = coords[::-1]
            return tuple(x // b for x, b in zip(coords, tail_axes)) + (i % cut_rows, 0)

        for side in range(2):
            out_specs.append(pl.BlockSpec(out_block, out_map))
            out_shape.append(jax.ShapeDtypeStruct(tuple(left) + (rows, width), jnp.bfloat16))
        counts.append(len(addends))
    outs = pl.pallas_call(
        functools.partial(fold_kernel, counts=tuple(counts)),
        grid_spec=pltpu.PrefetchScalarGridSpec(
            num_scalar_prefetch=1, grid=(steps,), in_specs=in_specs, out_specs=out_specs
        ),
        out_shape=out_shape,
        compiler_params=params(48),
        cost_estimate=pl.CostEstimate(flops=10**7, bytes_accessed=30 * 10**6, transcendentals=0),
        name="fold",
    )(bits, *arrays)
    return [(outs[2 * k], outs[2 * k + 1]) for k in range(len(items))]


class Chain:
    def __init__(self, axes, stages, shape, halve):
        self.axes, self.stages, self.shape, self.halve = axes, stages, shape, halve

    def landing(self, extra=0):
        free, size, out = list(self.axes), list(self.shape), []
        for stage in self.stages:
            if stage in free:
                free.remove(stage)
            elif stage == "x":
                size[self.halve] //= 2
            elif stage != "c":
                break
            out.append((2,) * len(free) + tuple(size))
            if stage == "x":
                size[0] += extra
        return out


def plus(left, right):
    return to_low(to_wide(left) + to_wide(right))


LATE = ("L1", "L2", "L3")


def late_cut(share):
    third = share // 96 * 32
    return (third, (share - third) // 2, (share - third) // 2)


ORDER = (
    "L10 L20 L30 C0",
    "O0 L11 E0 L31",
    "L21 E1 L12 C1",
    "O1 L22 L32 L13",
    "E2 E3 L23 O2",
    "C2 L14 L33 C3",
    "L24 O3 L34 L15",
    "O4 L25 L16 L35",
    "L26 L36",
)
STARTS = ("C", "O", "E")


def chains(c, e, o, share_rows):
    ends = ["GX", "GC"]
    return {
        "C": Chain(["w"], ["x", "w"] + ends, c, 1),
        "E": Chain(["w"], ["w", "x"] + ends, e, 1),
        "O": Chain(["w", "z", "y"], ["y", "z", "w"] + ends, o, 1),
    } | {
        name: Chain(["w", "z", "y"], ["c"] + list(stages) + ends, (rows, LANES), 0)
        for name, stages, rows in zip(LATE, ("xyzw", "yxzw", "zyxw"), late_cut(share_rows))
    }


def finish_kernel(late, pos, c0, c1, e0, e1, o0, o1, outc, oute, outo, outl, *scratch, table):
    def place(axis, bit):
        me = lax.axis_index(axis)
        mine = (me // bit) % 2
        return mine, {axis: me + bit * (1 - 2 * mine)}

    mine, who = {}, {}
    for name, axis, bit in (("c", "pos", 1), ("x", "pos", 2), ("y", "seg", 1), ("z", "seg", 2), ("w", "seg", 4)):
        mine[name], who[name] = place(axis, bit)
    barrier = pltpu.get_barrier_semaphore()
    for target in who.values():
        pl.semaphore_signal(barrier, inc=1, device_id=target, device_id_type=pl.DeviceIdType.MESH)
    pl.semaphore_wait(barrier, len(who))

    scratch = list(scratch)
    sent, came, near = scratch[-3:]
    work = dict(zip(("C", "E", "O") + LATE + ("L1m",), scratch[:7]))
    landed, at = {}, 7
    for name, chain in table.items():
        stages = len(chain.landing())
        landed[name] = scratch[at : at + stages]
        at += stages
    both = {"C": (c0, c1), "E": (e0, e1), "O": (o0, o1)}
    lead_rows = pos.shape[3]
    late_half = table["L1"].shape[0] // 2
    outs = {"C": (outc, None), "E": (oute, None), "O": (outo, None)}
    first = 0
    for name in LATE:
        size = table[name].shape[0] // 2 + (lead_rows if name == "L1" else 0)
        outs[name] = (outl, (first, size))
        first += size
    started = {}
    copies = []

    def send(key, src, dst, target):
        copy = pltpu.make_async_remote_copy(
            src_ref=src,
            dst_ref=dst,
            send_sem=sent.at[len(copies)],
            recv_sem=came.at[len(copies)],
            device_id=who[target],
            device_id_type=pl.DeviceIdType.MESH,
        )
        copy.start()
        copies.append(copy)
        started[key] = copy

    free = {name: list(chain.axes) for name, chain in table.items()}
    span = {name: (None, chain.shape[chain.halve]) for name, chain in table.items()}

    def pieces(name, start, size):
        halve = table[name].halve
        if start is None:
            return (slice(None), slice(None))
        one = pl.ds(pl.multiple_of(start, 16 if halve == 0 else LANES), size)
        return (one, slice(None)) if halve == 0 else (slice(None), one)

    def part(name, axis, value):
        start, size = span[name]
        fixed = {a: mine[a] for a in table[name].axes if a not in free[name]}
        left = list(free[name])
        relative = None
        if axis == "x":
            size = size // 2
            relative = value * size
            start = relative if start is None else start + relative
        elif axis is not None:
            fixed[axis] = value
            left.remove(axis)
        return left, fixed, start, size, relative

    def total(name, stage, axis, value, store=None):
        left, fixed, start, size, relative = part(name, axis, value)
        chain = table[name]
        switch = name == "L1" and stage is not None and chain.stages[stage] == "x"
        buffer = work[name]

        def one(values):
            index = tuple(values[a] if a in values else fixed[a] for a in chain.axes)
            full = index + pieces(name, start, size)
            if stage is None:
                left_ref, right_ref = both[name]
                got = plus(left_ref[full], right_ref[full])
            else:
                lead = tuple(values[a] if a in values else fixed[a] for a in free[name])
                got = plus(buffer[full], landed[name][stage][lead + pieces(name, relative, size)])
            if store is not None:
                store(got)
            elif switch:
                work["L1m"][index + (slice(0, size), slice(None))] = got
                work["L1m"][index + (slice(size, None), slice(None))] = pos[index]
            else:
                buffer[full] = got

        count = 1 << len(left)
        if count == 1:
            one({})
        elif count == 2:
            for k in range(2):
                one({left[0]: k})
        else:

            @pl.loop(0, count)
            def _(i):
                one({a: (i // (1 << (len(left) - 1 - k))) % 2 for k, a in enumerate(left)})

    def advance(name, stage):
        chain = table[name]
        following = chain.stages[0 if stage is None else stage + 1]
        switch = name == "L1" and stage is not None and chain.stages[stage] == "x"
        number = 0 if stage is None else stage + 1
        out, rows = outs[name]
        place_out = (slice(None), slice(None)) if rows is None else (slice(rows[0], rows[0] + rows[1]), slice(None))
        if following == "GX":

            def store(got):
                out[(mine["c"], mine["x"]) + place_out] = got

            total(name, stage, None, None, store)
            at = out.at[(mine["c"], mine["x"]) + place_out]
            send((name, number), at, at, "x")
            return
        if following == "GC":
            at = out.at[(mine["c"], slice(None)) + place_out]
            send((name, number), at, at, "c")
            return
        other = 1 - mine[following]
        total(name, stage, following, other)
        if switch:
            left, fixed, _, _, _ = part(name, following, other)
            source = work["L1m"]
            index = tuple(slice(None) if a in left else fixed[a] for a in chain.axes) + (slice(None), slice(None))
        else:
            left, fixed, start, size, _ = part(name, following, other)
            source = work[name]
            index = tuple(slice(None) if a in left else fixed[a] for a in chain.axes) + pieces(name, start, size)
        send((name, number), source.at[index], landed[name][number], following)
        total(name, stage, following, mine[following])
        if switch:
            work["L1"] = work["L1m"]
            span["L1"] = (None, late_half + lead_rows)
        if following == "x":
            start, size = span[name]
            half = size // 2
            span[name] = (mine["x"] * half if start is None else start + mine["x"] * half, half)
        else:
            free[name].remove(following)

    share = sum(table[name].shape[0] for name in LATE)
    keep = {}
    first = 0
    for number, name in enumerate(LATE):
        size = table[name].shape[0]
        own = pl.multiple_of(mine["c"] * share + first, 16)
        theirs = pl.multiple_of((1 - mine["c"]) * share + first, 16)
        send((name, 0), late.at[:, :, :, pl.ds(theirs, size)], landed[name][0], "c")
        keep[name] = pltpu.make_async_copy(late.at[:, :, :, pl.ds(own, size)], work[name], near.at[number])
        keep[name].start()
        first += size
    for name in STARTS:
        advance(name, None)
    for event in " ".join(ORDER).split():
        name, stage = event[:-1], int(event[-1])
        started[(name, stage)].wait_recv()
        if stage == 0 and name in keep:
            keep[name].wait()
        if stage + 1 < len(table[name].stages):
            advance(name, stage)
    for copy in copies:
        copy.wait_send()


def finish(late, pos, c, e, o):
    low = jnp.bfloat16
    cube = (2, 2, 2)
    share = late.shape[1] // 2
    table = chains(c[0].shape[1:], e[0].shape[1:], o[0].shape[3:], share)
    lead_rows = pos.shape[1]
    vmem = pl.BlockSpec(memory_space=pltpu.VMEM)
    shapes = [c[0].shape, e[0].shape, o[0].shape]
    shapes += [cube + table[name].shape for name in LATE]
    shapes += [cube + (table["L1"].shape[0] // 2 + lead_rows, LANES)]
    for name, chain in table.items():
        shapes += chain.landing(lead_rows if name == "L1" else 0)
    scratch = [pltpu.VMEM(shape, low) for shape in shapes]
    count = sum(len(chain.stages) for chain in table.values())
    scratch += [pltpu.SemaphoreType.DMA((count,)), pltpu.SemaphoreType.DMA((count,)), pltpu.SemaphoreType.DMA((3,))]
    out = [
        (c[0].shape[1], c[0].shape[2] // 2),
        (e[0].shape[1], e[0].shape[2] // 2),
        o[0].shape[3:],
        (share // 2 + lead_rows, LANES),
    ]
    return pl.pallas_call(
        functools.partial(finish_kernel, table=table),
        in_specs=[pl.BlockSpec(memory_space=pl.ANY)] + [vmem] * 7,
        out_specs=[vmem] * 4,
        out_shape=[jax.ShapeDtypeStruct((2, 2) + shape, low) for shape in out],
        scratch_shapes=scratch,
        compiler_params=pltpu.CompilerParams(vmem_limit_bytes=56 << 20, collective_id=0, has_side_effects=True),
        cost_estimate=pl.CostEstimate(flops=10**7, bytes_accessed=20 * 10**6, transcendentals=0),
        name="finish",
    )(late.reshape(cube + late.shape[1:]), pos.reshape(cube + pos.shape[1:]), *c, *e, *o)


def emit_kernel(c_hbm, e_hbm, o_hbm, l_hbm, *refs, plan, slots):
    outs, (c_ref, e_ref, o_ref, l_ref, vals, sems) = refs[:-6], refs[-6:]
    pairs = ((l_hbm, l_ref), (c_hbm, c_ref), (e_hbm, e_ref), (o_hbm, o_ref))
    copies = [pltpu.make_async_copy(a, b, sems.at[k]) for k, (a, b) in enumerate(pairs)]
    for copy in copies:
        copy.start()
    copies[0].wait()
    experts, keys, queries, positions, values, gates = outs[3:9]
    targets = (experts, keys, queries, vals, positions)
    for core, x, start, number, to, rows in plan:
        targets[number][to : to + rows] = to_wide(l_ref[core, x, start : start + rows])
    half = vals.shape[0] // 2
    values[...] = vals[:slots]
    gates[...] = vals[half : half + slots]
    first_gain, first_shift, second_gain, second_shift, contract, expand, content, position = outs[9:]
    lines = ((first_gain, slots), (first_shift, slots + 1))
    lines += tuple((ref, half + slots + k) for k, ref in enumerate((second_gain, second_shift, contract)))
    for ref, number in lines:
        ref[...] = vals[number]
    for k in range(4):
        expand[k * LANES : (k + 1) * LANES] = vals[half + slots + 3 + k]
    size = content.shape[0]
    content[...] = vals[half + slots + 7, :size]
    position[...] = vals[half + slots + 7, size : 2 * size]
    for k, ref in enumerate((c_ref, e_ref, o_ref)):
        width = ref.shape[3]
        copies[k + 1].wait()
        for core in range(2):
            for x in range(2):
                at = (core * 2 + x) * width
                outs[k][:, at : at + width] = to_wide(ref[core, x])


def emit(quarters, dh):
    c, e, o, tail = quarters
    f32 = jnp.float32
    slots = HEADS * EXPERTS
    at_key, at_query, at_value, _, end = late_rows(dh)
    halves = [rows // 2 for rows in late_cut(end // 2)]
    sizes = [at_key, at_query - at_key, at_value - at_query, end - at_value]
    starts = [0, at_key, at_query, at_value]
    plan = []
    for core in range(2):
        for x in range(2):
            for part, piece in enumerate(halves):
                source = sum(halves[:part]) + (dh if part else 0)
                low_end = core * (end // 2) + 2 * sum(halves[:part]) + x * piece
                for k, (first, size) in enumerate(zip(starts, sizes)):
                    a, b = max(first, low_end), min(first + size, low_end + piece)
                    if a < b:
                        plan.append((core, x, source + a - low_end, k, a - first, b - a))
            plan.append((core, x, halves[0], 4, (2 * x + core) * dh, dh))
    vmem = pl.BlockSpec(memory_space=pltpu.VMEM)
    shapes = [(q.shape[2], 4 * q.shape[3]) for q in (c, e, o)] + [(n, LANES) for n in sizes[:3] + [HEADS * dh]]
    shapes += [(slots, LANES)] * 2 + [(LANES,)] * 5 + [(4 * LANES,)] + [(HEADS * dh * LANES // D,)] * 2
    return pl.pallas_call(
        functools.partial(emit_kernel, plan=tuple(plan), slots=slots),
        in_specs=[pl.BlockSpec(memory_space=pl.ANY)] * 4,
        out_specs=[vmem] * len(shapes),
        out_shape=[jax.ShapeDtypeStruct(shape, f32) for shape in shapes],
        scratch_shapes=[pltpu.VMEM(q.shape, q.dtype) for q in quarters]
        + [pltpu.VMEM((end - at_value, LANES), f32), pltpu.SemaphoreType.DMA((4,))],
        compiler_params=params(60),
        name="emit",
    )(c, e, o, tail)


def mm(spec, left, right):
    return jnp.einsum(spec, left, right, preferred_element_type=jnp.float32)


def position_table(row_count, width_count):
    fine = 64
    inverse_freq = 10000.0 ** (-jnp.arange(0, width_count, 2).astype(jnp.float32) / width_count)
    high = (row_count // fine - 1 - jnp.arange(row_count // fine)) * fine
    low_part = fine - 1 - jnp.arange(fine)
    high_angle = high.astype(jnp.float32)[:, None, None] * inverse_freq
    low_angle = low_part.astype(jnp.float32)[None, :, None] * inverse_freq
    high_sin, high_cos = jnp.sin(high_angle), jnp.cos(high_angle)
    low_sin, low_cos = jnp.sin(low_angle), jnp.cos(low_angle)
    sines = high_sin * low_cos + high_cos * low_sin
    cosines = high_cos * low_cos - high_sin * low_sin
    return to_low(jnp.concatenate([sines, cosines], axis=2)).reshape(row_count, width_count)


def route_mask(routes, expert_count):
    return jnp.sum((routes[..., None] == jnp.arange(expert_count)).astype(jnp.float32), axis=-2)


def bit_of(axis, bit):
    return (lax.axis_index(axis) // bit) % 2


def swap(value, axis, bit):
    pairs = [(i, i ^ bit) for i in range(lax.axis_size(axis))]
    return lax.ppermute(value, axis, pairs)


def pick(value, index, axis):
    return lax.dynamic_index_in_dim(value, index, axis, keepdims=False)


def cut(value, index, axis):
    size = value.shape[axis] // 2
    return lax.dynamic_slice_in_dim(value, index * size, size, axis)


def axis_bits(axis):
    size = lax.axis_size(axis)
    return [1 << k for k in range(size.bit_length() - 1)]


def bits_tree(value, seg_size):
    count = len(axis_bits("seg"))
    return value.reshape((2,) * count + (value.shape[0] // seg_size, value.shape[1]))


class Share:
    def __init__(self, addends, bits):
        self.addends = addends
        self.bits = bits

    def total(self):
        out = to_wide(self.addends[0])
        for item in self.addends[1:]:
            out = out + to_wide(item)
        return to_low(out)

    def seg(self, number):
        if number >= len(axis_bits("seg")):
            return self
        bit = axis_bits("seg")[number]
        dim = len(self.bits) - 1 - self.bits.index(bit)
        mine = bit_of("seg", bit)
        sent = Share([pick(a, 1 - mine, dim) for a in self.addends], self.bits).total()
        come = swap(sent, "seg", bit)
        left = [b for b in self.bits if b != bit]
        return Share([pick(a, mine, dim) for a in self.addends] + [come], left)

    def rest(self):
        out = self
        for bit in self.bits:
            out = out.seg(axis_bits("seg").index(bit))
        return out

    def pos(self, number, dim):
        bit = axis_bits("pos")[number]
        mine = bit_of("pos", bit)
        at = len(self.bits) + dim
        sent = Share([cut(a, 1 - mine, at) for a in self.addends], self.bits).total()
        come = swap(sent, "pos", bit)
        return Share([cut(a, mine, at) for a in self.addends] + [come], self.bits)

    def pos_all(self, number):
        part = self.total()
        return Share([part, swap(part, "pos", axis_bits("pos")[number])], self.bits)


def together(stages):
    items, bits, swaps, lefts = [], [], [], []
    for item, axis, number in stages:
        bit = axis_bits(axis)[number]
        bits.append(bit_of(axis, bit))
        swaps.append((axis, bit))
        if axis == "seg":
            items.append((item.addends, len(item.bits) - 1 - item.bits.index(bit)))
            lefts.append([b for b in item.bits if b != bit])
        else:
            items.append((item.addends, "columns"))
            lefts.append(item.bits)
    pairs = fold(items, jnp.stack(bits).astype(jnp.int32))
    out = []
    for (sent, kept), (axis, bit), left in zip(pairs, swaps, lefts):
        out.append(Share([kept, swap(sent, axis, bit)], left))
    return out


def share(values, seg_size):
    return Share([bits_tree(v, seg_size) for v in values], axis_bits("seg"))


def widen(part, number, dim):
    bit = axis_bits("pos")[number]
    mine = bit_of("pos", bit)
    other = swap(part, "pos", bit)
    first = jnp.where(mine == 0, part, other)
    second = jnp.where(mine == 0, other, part)
    return jnp.concatenate([first, second], axis=dim)


def seg_blocks(value, seg_size):
    blocks, rows, lanes = value.shape
    inside = seg_size // blocks
    value = value.reshape(blocks, rows, inside, lanes // inside)
    value = jnp.transpose(value, (0, 2, 1, 3))
    count = len(axis_bits("seg"))
    return value.reshape((2,) * count + (rows, lanes // inside))


def vector_rows(vectors, seg_size):
    lanes = D // seg_size
    rows = jnp.concatenate([v.reshape(seg_size, -1, lanes) for v in vectors], axis=1)
    blocks = D // LANES
    rows = rows.reshape(blocks, seg_size // blocks, rows.shape[1], lanes)
    return jnp.transpose(rows, (0, 2, 1, 3)).reshape(blocks, -1, LANES)


def local(
    block_input,
    memory_rows,
    memory_length,
    value_routes,
    output_routes,
    first_gain,
    first_shift,
    query_weight,
    key_weight,
    position_weight,
    value_experts,
    value_router,
    content_bias,
    position_bias,
    output_experts,
    output_gate_matrix,
    second_gain,
    second_shift,
    up_projection_weight,
    expand_bias,
    down_projection_weight,
    contract_bias,
    output_cotangent,
):
    seg_count, local_rows, width = block_input.shape
    seg_size = lax.axis_size("seg")
    pos_index = lax.axis_index("pos")
    key_count = 2 * SEQ
    all_rows = seg_count * local_rows
    slots = HEADS * EXPERTS
    score_scale = DH ** (-0.5)
    line = lambda v: v.reshape(1, -1)

    value_pick = jnp.transpose(route_mask(value_routes, EXPERTS), (0, 1, 3, 4, 2))
    value_pick = value_pick.reshape(seg_count, 2, slots, local_rows)
    out_pick = jnp.transpose(route_mask(output_routes, EXPERTS), (0, 2, 3, 1))
    out_pick = out_pick.reshape(seg_count, slots, local_rows)
    pad = ((0, 0), (0, 32 - slots))
    gates = jnp.concatenate([jnp.pad(value_router, pad).T, jnp.pad(output_gate_matrix, pad).T], axis=0)

    def trade(value):
        return lax.all_to_all(value, "pos", split_axis=0, concat_axis=0, tiled=True)

    qk, normed, value_gate, out_gate = project(
        memory_rows,
        block_input,
        first_gain,
        first_shift,
        query_weight.T,
        key_weight.T,
        gates,
        value_pick,
        out_pick,
    )
    qk = trade(qk)
    values, value_all = experts(normed, value_experts.T, value_gate)
    values = trade(values)

    table_low = position_table(key_count, D)
    weight_local = pick(position_weight.reshape(D, HEADS, DH), pos_index, 1)
    positions = to_low(mm("nd,dc->cn", table_low, weight_local))

    head_content = pick(content_bias.reshape(HEADS, DH), pos_index, 0)
    head_position = pick(position_bias.reshape(HEADS, DH), pos_index, 0)
    probs = score(memory_length, qk, positions, head_content, head_position, score_scale)
    attended = attend(probs, values)

    core = bit_of("pos", 1).astype(jnp.int32).reshape(1)
    cotangent = output_cotangent.reshape(all_rows, width)
    (
        block_output,
        residual,
        grad_normed_two,
        down_sent,
        down_kept,
        up_sent,
        up_kept,
        expand_bias_grad,
    ) = middle(
        core,
        attended,
        out_gate,
        block_input.reshape(all_rows, width),
        cotangent,
        output_experts,
        second_gain,
        second_shift,
        contract_bias,
        up_projection_weight,
        line(expand_bias),
        down_projection_weight,
    )
    down_got = swap(down_sent, "pos", 1)
    up_got = swap(up_sent, "pos", 1)
    grad_residual, grad_attended, grad_out_logit, mix_sent, mix_kept, middle_sums = middle_back(
        core, residual, grad_normed_two, attended, out_gate, cotangent, output_experts, second_gain
    )
    grad_heads = trade(grad_attended)
    mix_got = swap(mix_sent, "pos", 1)
    down = share([down_kept, down_got], seg_size)
    up = share([up_kept, up_got], seg_size)
    mix = share([mix_kept, mix_got], seg_size)
    cube = seg_size * LANES == D and lax.axis_size("pos") == 4
    if cube:
        down, up = together([(down, "seg", 1), (up, "seg", 0)])
    else:
        down, up = down.seg(1), up.seg(0)

    grads, grad_rel, part_sums = attend_back(
        probs, grad_heads, qk, values, positions, head_content, head_position, score_scale
    )
    grads = trade(grads)
    part_sums, down.addends, up.addends, mix.addends = lax.optimization_barrier(
        (part_sums, down.addends, up.addends, mix.addends)
    )
    if cube:
        down, up, mix = together([(down, "seg", 0), (up, "seg", 1), (mix, "pos", 1)])
    else:
        down, up, mix = down.seg(0), up.seg(1), mix.pos(1, 1)

    position_grad = to_low(mm("scn,nd->cd", grad_rel, table_low))
    position_grad = jnp.transpose(position_grad.reshape(DH, D // LANES, LANES), (1, 0, 2))
    head_hot = (jnp.arange(HEADS) == pos_index).astype(jnp.float32)[:, None]
    bias_sums = jnp.sum(part_sums, axis=0)
    biases = [(head_hot * bias_sums[k]).reshape(seg_size, -1) for k in range(2)]
    bias_row = jnp.concatenate(biases, axis=1)
    bias_row = jnp.pad(bias_row, ((0, 0), (0, D // seg_size - bias_row.shape[1])))
    extra = vector_rows(
        [middle_sums[0], middle_sums[1], middle_sums[2], expand_bias_grad[0], bias_row], seg_size
    )

    input_grad, late = back(
        memory_rows,
        block_input,
        first_gain,
        first_shift,
        grads,
        grad_out_logit,
        value_gate,
        value_all,
        value_experts.T,
        key_weight.T,
        query_weight.T,
        value_router.T,
        output_gate_matrix.T,
        grad_residual.reshape(seg_count, local_rows, width),
        extra,
    )
    late, position_grad, down.addends, up.addends, mix.addends = lax.optimization_barrier(
        (late, position_grad, down.addends, up.addends, mix.addends)
    )
    if cube:
        quarters = finish(late, position_grad, down.addends, up.addends, mix.addends)
        contract_weight_grad, expand_weight_grad, output_experts_grad, *rows_out = emit(quarters, DH)
        experts_grad, keys_grad, queries_grad, positions_grad, value_grad, out_grad = rows_out[:6]
        vectors = rows_out[6:]
    else:
        late = Share([late], []).pos(0, 1).total()
        share_rows = late.shape[1] // 2
        one = Share([late[:, :share_rows]], []).pos(1, 1).total()
        piece_rows = one.shape[1]
        one = jnp.concatenate([one, position_grad], axis=1)
        one = Share([seg_blocks(one, seg_size)], axis_bits("seg")).rest().total()
        two = Share([seg_blocks(late[:, share_rows:], seg_size)], axis_bits("seg"))
        two = two.rest().pos(1, 0).total()
        tail = jnp.concatenate([one, two], axis=0)
        tail = to_wide(widen(widen(tail[None], 1, 0)[None], 0, 0))
        lanes = tail.shape[3]
        up = up.pos(1, 1).rest().total()
        expand_weight_grad = to_wide(widen(widen(up, 1, 1), 0, 1))
        down = down.pos(1, 1).rest().total()
        contract_weight_grad = to_wide(widen(widen(down, 1, 1), 0, 1))
        mix = mix.rest().total()
        output_experts_grad = to_wide(widen(widen(mix, 1, 1), 0, 1))
        parts = [tail[:, :, :piece_rows], tail[:, :, tail.shape[2] - piece_rows :]]
        main = jnp.concatenate([p.reshape(2, share_rows, lanes) for p in parts], axis=1).reshape(-1, lanes)
        heads = jnp.transpose(tail[:, :, piece_rows : tail.shape[2] - piece_rows], (1, 0, 2, 3))
        edges = (0,) + late_rows(DH)
        rows_out = [main[a:b] for a, b in zip(edges, edges[1:])] + [heads.reshape(HEADS * DH, lanes)]
        experts_grad, keys_grad, queries_grad, value_rows, out_rows, positions_grad = rows_out
        value_grad, out_grad = value_rows[:slots], out_rows[:slots]
        extra = out_rows[slots : slots + 8]
        piece = DH * HEADS // seg_size
        vectors = [value_rows[slots], value_rows[slots + 1], extra[0], extra[1], extra[2]]
        vectors += [extra[3:7].reshape(-1), extra[7, :piece], extra[7, piece : 2 * piece]]
    return (
        block_output.reshape(block_input.shape),
        input_grad,
        vectors[0],
        vectors[1],
        queries_grad.T,
        keys_grad.T,
        positions_grad.T,
        experts_grad.T,
        value_grad.T,
        vectors[6],
        vectors[7],
        output_experts_grad,
        out_grad.T,
        vectors[2],
        vectors[3],
        expand_weight_grad,
        vectors[5],
        contract_weight_grad,
        vectors[4],
    )


def solution(mesh):
    rows = P("seg", "pos", None)
    whole = P()
    placed = (
        rows,
        rows,
        P("seg"),
        P("seg", None, "pos", None, None),
        P("seg", "pos", None, None),
    )
    placed += (whole,) * 17 + (rows,)
    shares = [P("seg")] * 17
    for index in (2, 3, 4, 5, 6, 9, 10, 13, 15):
        shares[index] = P("seg", None)
    return jax.shard_map(
        local,
        mesh=mesh,
        in_specs=placed,
        out_specs=(rows, rows) + tuple(shares),
        check_vma=False,
    )
```

```python
import functools

import jax
import jax.numpy as jnp
from jax import lax
from jax.experimental import pallas as pl
from jax.experimental.pallas import tpu as pltpu
from jax.sharding import PartitionSpec as P

D = 1024
HEADS = 4
DH = 112
EXPERTS = 5
SEQ = 1024
norm_eps = 1e-05

NEG = -1e30
LANES = 128


def nn(left, right):
    return lax.dot_general(left, right, (((1,), (0,)), ((), ())), preferred_element_type=jnp.float32)


def nt(left, right):
    return lax.dot_general(left, right, (((1,), (1,)), ((), ())), preferred_element_type=jnp.float32)


def to_low(value):
    return value.astype(jnp.bfloat16)


def to_wide(value):
    return value.astype(jnp.float32)


def norm_parts(rows):
    center = rows - jnp.mean(rows, axis=1, keepdims=True)
    inv_std = lax.rsqrt(jnp.mean(center * center, axis=1, keepdims=True) + norm_eps)
    return center * inv_std, inv_std


def vector(value):
    return once(value.shape, lambda *_: (0,))


def once(shape, index_map):
    return pl.BlockSpec(shape, index_map, pipeline_mode=pl.Buffered(1))


def row(ref):
    return to_wide(ref[...]).reshape(1, -1)


def params(megabytes):
    return pltpu.CompilerParams(vmem_limit_bytes=megabytes << 20)


def project_kernel(
    mem_ref, blk_ref, gain_ref, shift_ref, wq_ref, wk_ref, gates_ref, pickv_ref, picko_ref,
    qk_ref, norm_ref, gatev_ref, gateo_ref,
):
    half = pl.program_id(1)
    rows = to_wide(jnp.where(half == 0, mem_ref[0], blk_ref[0]))
    unit, _ = norm_parts(rows)
    normed = to_low(unit * row(gain_ref) + row(shift_ref))
    norm_ref[0, 0] = normed
    turned = normed.T
    keys = to_low(nn(wk_ref[...], turned))
    dh = qk_ref.shape[3]
    logits = nn(gates_ref[...], turned)
    gatev_ref[0, 0] = jax.nn.sigmoid(logits[: pickv_ref.shape[2]]) * pickv_ref[0, 0]

    @pl.when(half == 0)
    def _():
        for h in range(qk_ref.shape[0]):
            qk_ref[h, 0, 1] = keys[h * dh : (h + 1) * dh]

    @pl.when(half == 1)
    def _():
        query = to_low(nn(wq_ref[...], turned))
        for h in range(qk_ref.shape[0]):
            qk_ref[h, 0, 0] = query[h * dh : (h + 1) * dh]
            qk_ref[h, 0, 2] = keys[h * dh : (h + 1) * dh]
        gateo_ref[0] = jax.nn.sigmoid(logits[logits.shape[0] // 2 :][: picko_ref.shape[1]]) * picko_ref[0]


def project(mem, blk, gain, shift, wqt, wkt, gates, pickv, picko):
    segs, rows, width = blk.shape
    inner = wqt.shape[0]
    slots = pickv.shape[2]
    low, f32 = jnp.bfloat16, jnp.float32
    dh = inner // HEADS
    flat = lambda s, r: (0, 0)
    row_spec = pl.BlockSpec((1, rows, width), lambda s, r: (s, 0, 0))
    return pl.pallas_call(
        project_kernel,
        grid=(segs, 2),
        in_specs=[
            row_spec,
            row_spec,
            vector(gain),
            vector(shift),
            once(wqt.shape, flat),
            once(wkt.shape, flat),
            once(gates.shape, flat),
            pl.BlockSpec((1, 1, slots, rows), lambda s, r: (s, r, 0, 0)),
            pl.BlockSpec((1, slots, rows), lambda s, r: (s, 0, 0)),
        ],
        out_specs=[
            pl.BlockSpec((HEADS, 1, 3, dh, rows), lambda s, r: (0, s, 0, 0, 0)),
            pl.BlockSpec((1, 1, rows, width), lambda s, r: (s, r, 0, 0)),
            pl.BlockSpec((1, 1, slots, rows), lambda s, r: (s, r, 0, 0)),
            pl.BlockSpec((1, slots, rows), lambda s, r: (s, 0, 0)),
        ],
        out_shape=[
            jax.ShapeDtypeStruct((HEADS, segs, 3, dh, rows), low),
            jax.ShapeDtypeStruct((segs, 2, rows, width), low),
            jax.ShapeDtypeStruct((segs, 2, slots, rows), f32),
            jax.ShapeDtypeStruct((segs, slots, rows), f32),
        ],
        compiler_params=params(60),
        cost_estimate=pl.CostEstimate(flops=3 * 10**9, bytes_accessed=8 * 10**6, transcendentals=0),
        name="project",
    )(mem, blk, gain, shift, wqt, wkt, gates, pickv, picko)


def experts_kernel(norm_ref, ve_ref, gate_ref, v_ref, all_ref):
    turned = norm_ref[0, 0].T
    heads, dh = v_ref.shape[0], v_ref.shape[3]
    group = nn(ve_ref[...], turned)
    all_ref[0, 0] = to_low(group)
    for h in range(heads):
        total = jnp.zeros((dh, turned.shape[1]), jnp.float32)
        for e in range(EXPERTS):
            slot = h * EXPERTS + e
            total = total + gate_ref[0, 0, slot : slot + 1] * group[slot * dh : (slot + 1) * dh]
        v_ref[h, 0, 0] = to_low(total)


def experts(normed, vet, gate):
    segs, _, rows, width = normed.shape
    inner = vet.shape[0]
    slots = gate.shape[2]
    dh = inner // (HEADS * EXPERTS)
    low = jnp.bfloat16
    return pl.pallas_call(
        experts_kernel,
        grid=(segs, 2),
        in_specs=[
            pl.BlockSpec((1, 1, rows, width), lambda s, r: (s, r, 0, 0)),
            once(vet.shape, lambda s, r: (0, 0)),
            pl.BlockSpec((1, 1, slots, rows), lambda s, r: (s, r, 0, 0)),
        ],
        out_specs=[
            pl.BlockSpec((HEADS, 1, 1, dh, rows), lambda s, r: (0, s, r, 0, 0)),
            pl.BlockSpec((1, 1, inner, rows), lambda s, r: (s, r, 0, 0)),
        ],
        out_shape=[
            jax.ShapeDtypeStruct((HEADS, segs, 2, dh, rows), low),
            jax.ShapeDtypeStruct((segs, 2, inner, rows), low),
        ],
        compiler_params=params(48),
        cost_estimate=pl.CostEstimate(flops=5 * 10**9, bytes_accessed=12 * 10**6, transcendentals=0),
        name="experts",
    )(normed, vet, gate)


def column(ref):
    value = row(ref)
    return jnp.broadcast_to(value, (LANES, value.shape[1])).T[:, :1]


def biased(query, bias, scale):
    return to_low((to_wide(query) + bias) * scale)


def score_kernel(len_ref, qk_ref, pos_ref, cb_ref, pb_ref, p_ref, kt_s, *, tiles, block, chunk, scale):
    seg = pl.program_id(0)
    start = tiles * block - len_ref[seg]
    for half in range(2):
        for t in range(tiles):
            c0 = (half * tiles + t) * block
            kt_s[:, c0 : c0 + block] = qk_ref[t, 0, 1 + half]
    mem = tiles * block
    cb, pb = column(cb_ref), column(pb_ref)
    for t in range(tiles):
        w = mem + (t + 1) * block
        base = (tiles - 1 - t) * block
        col = lax.broadcasted_iota(jnp.int32, (1, w), 1)
        bias = jnp.where(col >= start, 0.0, NEG)
        content = biased(qk_ref[t, 0, 0], cb, scale).T
        position = biased(qk_ref[t, 0, 0], pb, scale).T
        for r0 in range(0, block, chunk):
            raw = nn(position[r0 : r0 + chunk], pos_ref[:, base:])
            rel = pltpu.roll(raw, w - (block - 1) + r0, 1, stride=1, stride_axis=0)
            s = nn(content[r0 : r0 + chunk], kt_s[:, :w]) + rel
            row = lax.broadcasted_iota(jnp.int32, (chunk, w), 0) + (mem + t * block + r0)
            col_wide = lax.broadcasted_iota(jnp.int32, (chunk, w), 1)
            s = jnp.where(col_wide <= row, s + bias, NEG)
            e = jnp.exp(s - jnp.max(s, axis=1, keepdims=True))
            p = e * (1.0 / jnp.sum(e, axis=1, keepdims=True))
            p_ref[0, t * block + r0 : t * block + r0 + chunk, :w] = to_low(p)


def score(lengths, qk, post, cbias, pbias, scale):
    tiles, segs, _, dh, block = qk.shape
    keys = 2 * tiles * block
    return pl.pallas_call(
        functools.partial(score_kernel, tiles=tiles, block=block, chunk=64, scale=scale),
        grid_spec=pltpu.PrefetchScalarGridSpec(
            num_scalar_prefetch=1,
            grid=(segs,),
            in_specs=[
                pl.BlockSpec((tiles, 1, 3, dh, block), lambda s, _: (0, s, 0, 0, 0)),
                pl.BlockSpec((dh, keys), lambda s, _: (0, 0)),
                vector(cbias),
                vector(pbias),
            ],
            out_specs=pl.BlockSpec((1, tiles * block, keys), lambda s, _: (s, 0, 0)),
            scratch_shapes=[pltpu.VMEM((dh, keys), jnp.bfloat16)],
        ),
        out_shape=jax.ShapeDtypeStruct((segs, tiles * block, keys), jnp.bfloat16),
        compiler_params=params(48),
        cost_estimate=pl.CostEstimate(flops=12 * 10**9, bytes_accessed=10 * 10**6, transcendentals=4 * 10**6),
        name="score",
    )(lengths, qk, post, cbias, pbias)


def attend_kernel(p_ref, v_ref, out_ref, v_s, buf, sent, came, near, *, tiles, block):
    seg = pl.program_id(0)
    segs = buf.shape[1]
    me = lax.axis_index("pos")
    peers = [(me + d) % tiles for d in range(1, tiles)]

    @pl.when(seg == 0)
    def _():
        barrier = pltpu.get_barrier_semaphore()
        for peer in peers:
            pl.semaphore_signal(barrier, inc=1, device_id={"pos": peer}, device_id_type=pl.DeviceIdType.MESH)

    for half in range(2):
        for t in range(tiles):
            c0 = (half * tiles + t) * block
            v_s[c0 : c0 + block, :] = v_ref[t, 0, half].T
    for t in range(tiles):
        w = tiles * block + (t + 1) * block
        out = nn(p_ref[0, t * block : (t + 1) * block, :w], v_s[:w, :])
        buf[t, seg] = to_low(out).T

    @pl.when(seg == 0)
    def _():
        pl.semaphore_wait(pltpu.get_barrier_semaphore(), tiles - 1)

    def moves(s):
        away = [
            pltpu.make_async_remote_copy(
                src_ref=buf.at[peer, s],
                dst_ref=out_ref.at[me, s],
                send_sem=sent.at[d, s],
                recv_sem=came.at[d, s],
                device_id={"pos": peer},
                device_id_type=pl.DeviceIdType.MESH,
            )
            for d, peer in enumerate(peers)
        ]
        return away, pltpu.make_async_copy(buf.at[me, s], out_ref.at[me, s], near.at[s])

    away, here = moves(seg)
    for copy in away:
        copy.start()
    here.start()

    @pl.when(seg == segs - 1)
    def _():
        for s in range(segs):
            away, here = moves(s)
            for copy in away:
                copy.wait()
            here.wait()


def attend(p, v):
    tiles, segs, _, dh, block = v.shape
    keys = 2 * tiles * block
    return pl.pallas_call(
        functools.partial(attend_kernel, tiles=tiles, block=block),
        grid=(segs,),
        in_specs=[
            pl.BlockSpec((1, tiles * block, keys), lambda s: (s, 0, 0)),
            pl.BlockSpec((tiles, 1, 2, dh, block), lambda s: (0, s, 0, 0, 0)),
        ],
        out_specs=pl.BlockSpec(memory_space=pl.ANY),
        out_shape=jax.ShapeDtypeStruct((tiles, segs, dh, block), jnp.bfloat16),
        scratch_shapes=[
            pltpu.VMEM((keys, dh), jnp.bfloat16),
            pltpu.VMEM((tiles, segs, dh, block), jnp.bfloat16),
            pltpu.SemaphoreType.DMA((tiles - 1, segs)),
            pltpu.SemaphoreType.DMA((tiles - 1, segs)),
            pltpu.SemaphoreType.DMA((segs,)),
        ],
        compiler_params=pltpu.CompilerParams(vmem_limit_bytes=48 << 20, collective_id=1, has_side_effects=True),
        cost_estimate=pl.CostEstimate(flops=5 * 10**9, bytes_accessed=9 * 10**6, transcendentals=0),
        name="attend",
    )(p, v)


def attend_back_kernel(
    p_ref, g_ref, qk_ref, v_ref, pos_ref, cb_ref, pb_ref, d_ref, dpos_ref, sums_ref,
    k_s, vt_s, posr_s, dkt, dvt, dpt, ds_s, dr_s, *, tiles, block, chunk, scale,
):
    seg = pl.program_id(0)
    for half in range(2):
        for t in range(tiles):
            c0 = (half * tiles + t) * block
            k_s[c0 : c0 + block, :] = qk_ref[t, 0, 1 + half].T
            vt_s[:, c0 : c0 + block] = v_ref[t, 0, half]

    @pl.when(seg == 0)
    def _():
        posr_s[...] = pos_ref[...].T

    dkt[...] = jnp.zeros_like(dkt)
    dvt[...] = jnp.zeros_like(dvt)
    dpt[...] = jnp.zeros_like(dpt)
    mem = tiles * block
    dh = v_ref.shape[3]
    flip = (
        lax.broadcasted_iota(jnp.int32, (block, block), 0) + lax.broadcasted_iota(jnp.int32, (block, block), 1)
        == block - 1
    )
    flip_wide = jnp.where(flip, 1.0, 0.0)
    flip_low = to_low(flip_wide)
    cb, pb = column(cb_ref), column(pb_ref)
    content_sum = jnp.zeros((1, dh), jnp.float32)
    position_sum = jnp.zeros((1, dh), jnp.float32)
    for t in range(tiles):
        w = mem + (t + 1) * block
        base = (tiles - 1 - t) * block
        gt = g_ref[t, 0]
        g = gt.T
        for r0 in range(0, block, chunk):
            p = to_wide(p_ref[0, t * block + r0 : t * block + r0 + chunk, :w])
            prod = p * nn(g[r0 : r0 + chunk], vt_s[:, :w])
            delta = jnp.sum(prod, axis=1, keepdims=True)
            ds_s[r0 : r0 + chunk, :w] = to_low(prod - p * delta)
        ds = ds_s[:, :w]
        for r0 in range(0, block, chunk):
            turned = nn(flip_low[r0 : r0 + chunk], ds)
            dr_s[r0 : r0 + chunk, :w] = to_low(pltpu.roll(turned, r0, 1, stride=1, stride_axis=0))
        dr = dr_s[:, :w]
        dvt[:, :w] += nn(gt, p_ref[0, t * block : (t + 1) * block, :w])
        dkt[:, :w] += nn(biased(qk_ref[t, 0, 0], cb, scale), ds)
        position = to_low(nn(biased(qk_ref[t, 0, 0], pb, scale), flip_low))
        dpt[:, base:] += nn(position, dr)
        dc = nn(ds, k_s[:w, :])
        dp = nn(dr, posr_s[base:, :])
        content_sum = content_sum + jnp.sum(dc, axis=0, keepdims=True)
        position_sum = position_sum + jnp.sum(dp, axis=0, keepdims=True)
        dp = lax.dot_general(
            flip_wide,
            dp,
            (((1,), (0,)), ((), ())),
            precision=lax.Precision.HIGHEST,
            preferred_element_type=jnp.float32,
        )
        d_ref[t, 0, 0] = to_low((dc + dp) * scale).T
    sums_ref[0, 0:1] = content_sum * scale
    sums_ref[0, 1:2] = position_sum * scale
    dpos_ref[0] = to_low(dpt[...])
    for half in range(2):
        for t in range(tiles):
            c0 = (half * tiles + t) * block
            d_ref[t, 0, 1 + half] = to_low(dkt[:, c0 : c0 + block])
            d_ref[t, 0, 3 + half] = to_low(dvt[:, c0 : c0 + block])


def attend_back(p, g, qk, v, post, cbias, pbias, scale):
    tiles, segs, dh, block = g.shape
    keys = 2 * tiles * block
    low, f32 = jnp.bfloat16, jnp.float32

    def spec(parts):
        return pl.BlockSpec((tiles, 1, parts, dh, block), lambda s: (0, s, 0, 0, 0))

    return pl.pallas_call(
        functools.partial(attend_back_kernel, tiles=tiles, block=block, chunk=64, scale=scale),
        grid=(segs,),
        in_specs=[
            pl.BlockSpec((1, tiles * block, keys), lambda s: (s, 0, 0)),
            pl.BlockSpec((tiles, 1, dh, block), lambda s: (0, s, 0, 0)),
            spec(3),
            spec(2),
            pl.BlockSpec((dh, keys), lambda s: (0, 0)),
            vector(cbias),
            vector(pbias),
        ],
        out_specs=[
            spec(5),
            pl.BlockSpec((1, dh, keys), lambda s: (s, 0, 0)),
            pl.BlockSpec((1, 2, dh), lambda s: (s, 0, 0)),
        ],
        out_shape=[
            jax.ShapeDtypeStruct((tiles, segs, 5, dh, block), low),
            jax.ShapeDtypeStruct((segs, dh, keys), low),
            jax.ShapeDtypeStruct((segs, 2, dh), f32),
        ],
        scratch_shapes=[
            pltpu.VMEM((keys, dh), low),
            pltpu.VMEM((dh, keys), low),
            pltpu.VMEM((keys, dh), low),
            pltpu.VMEM((dh, keys), f32),
            pltpu.VMEM((dh, keys), f32),
            pltpu.VMEM((dh, keys), f32),
            pltpu.VMEM((block, keys), low),
            pltpu.VMEM((block, keys), low),
        ],
        compiler_params=params(56),
        cost_estimate=pl.CostEstimate(flops=25 * 10**9, bytes_accessed=14 * 10**6, transcendentals=0),
        name="attend_back",
    )(p, g, qk, v, post, cbias, pbias)


def mix_rows(mixed, att_ref, gate_ref):
    heads, segs, dh, rows = att_ref.shape
    for h in range(heads):
        for s in range(segs):
            att = to_wide(att_ref[h, s])
            for e in range(EXPERTS):
                slot = h * EXPERTS + e
                mixed[slot * dh : (slot + 1) * dh, s * rows : (s + 1) * rows] = to_low(
                    gate_ref[s, slot : slot + 1] * att
                )


def middle_kernel(
    core_ref, att_ref, gate_ref, x_ref, g_ref, oe_ref, gain_ref, shift_ref, wu_ref, bu_ref, wd_ref,
    hid_ref, res, gn, wds_ref, wdk_ref, wus_ref, wuk_ref, bu_out, mixed, n2, n2t, *, chunk,
):
    step = pl.program_id(0)
    steps = pl.num_programs(0)
    total, width = x_ref.shape
    half = width // 2
    mine = pl.multiple_of(core_ref[0] * half, half)
    other = pl.multiple_of((1 - core_ref[0]) * half, half)
    count = total // chunk

    @pl.when(step == 0)
    def _():
        mix_rows(mixed, att_ref, gate_ref)
        res[...] = to_wide(x_ref[...]) + nn(mixed[...].T, oe_ref[...])

        @pl.loop(0, count)
        def _(i):
            at = pl.ds(pl.multiple_of(i * chunk, chunk), chunk)
            unit, _ = norm_parts(res[at, :])
            n2[at, :] = to_low(unit * row(gain_ref) + row(shift_ref))

        n2t[...] = n2[...].T
        gn[...] = jnp.zeros_like(gn)

    wu = wu_ref[...]
    wd = wd_ref[...]
    v = nn(n2[...], wu) + to_wide(bu_ref[...])
    root = 0.7978845608028654
    square = v * v
    tanh = jnp.tanh(root * (v + 0.044715 * (square * v)))
    plus = 0.5 * (1.0 + tanh)
    hidden = to_low(v * plus)
    slope = plus + 0.5 * v * (1.0 - tanh * tanh) * (root * (1.0 + 0.134145 * square))
    gp = nt(g_ref[...], wd) * slope
    gp_low = to_low(gp)
    bu_out[...] = jnp.sum(to_wide(gp_low), axis=0, keepdims=True)
    hid_ref[...] = hidden
    gn[...] += nt(gp_low, wu)
    wu_grad = to_low(nn(n2t[...], gp_low))

    @pl.when(step < steps // 2)
    def _():
        wus_ref[...] = wu_grad

    @pl.when(step >= steps // 2)
    def _():
        wuk_ref[...] = wu_grad

    turned = hidden.T
    wds_ref[...] = to_low(nn(turned, g_ref[:, pl.ds(other, half)]))
    wdk_ref[...] = to_low(nn(turned, g_ref[:, pl.ds(mine, half)]))


def middle(core, att, gate, x, g, oe, gain, shift, wu, bu, wd, fc=512):
    heads, segs, dh, rows = att.shape
    total, width = x.shape
    ff = wu.shape[1]
    steps = ff // fc
    mid = steps // 2
    half = width // 2
    slots = gate.shape[1]
    inner = oe.shape[0]
    low, f32 = jnp.bfloat16, jnp.float32

    def fix(*shape):
        return pl.BlockSpec(shape, lambda i, c: (0,) * len(shape))

    def keep(*shape):
        return once(shape, lambda i, c: (0,) * len(shape))

    def unit(i, c):
        return (i + mid * (1 - c[0])) % steps

    return pl.pallas_call(
        functools.partial(middle_kernel, chunk=64),
        grid_spec=pltpu.PrefetchScalarGridSpec(
            num_scalar_prefetch=1,
            grid=(steps,),
            in_specs=[
                keep(heads, segs, dh, rows),
                keep(segs, slots, rows),
                keep(total, width),
                keep(total, width),
                keep(inner, width),
                vector(gain),
                vector(shift),
                pl.BlockSpec((width, fc), lambda i, c: (0, unit(i, c))),
                pl.BlockSpec((1, fc), lambda i, c: (0, unit(i, c))),
                pl.BlockSpec((fc, width), lambda i, c: (unit(i, c), 0)),
            ],
            out_specs=[
                pl.BlockSpec((total, fc), lambda i, c: (0, unit(i, c))),
                fix(total, width),
                fix(total, width),
                pl.BlockSpec((fc, half), lambda i, c: (unit(i, c), 0)),
                pl.BlockSpec((fc, half), lambda i, c: (unit(i, c), 0)),
                pl.BlockSpec((width, fc), lambda i, c: (0, jnp.minimum(i, mid - 1))),
                pl.BlockSpec((width, fc), lambda i, c: (0, jnp.maximum(i - mid, 0))),
                pl.BlockSpec((1, fc), lambda i, c: (0, unit(i, c))),
            ],
            scratch_shapes=[
                pltpu.VMEM((inner, total), low),
                pltpu.VMEM((total, width), low),
                pltpu.VMEM((width, total), low),
            ],
        ),
        out_shape=[
            jax.ShapeDtypeStruct((total, ff), low),
            jax.ShapeDtypeStruct((total, width), f32),
            jax.ShapeDtypeStruct((total, width), f32),
            jax.ShapeDtypeStruct((ff, half), low),
            jax.ShapeDtypeStruct((ff, half), low),
            jax.ShapeDtypeStruct((width, ff // 2), low),
            jax.ShapeDtypeStruct((width, ff // 2), low),
            jax.ShapeDtypeStruct((1, ff), f32),
        ],
        compiler_params=params(60),
        cost_estimate=pl.CostEstimate(flops=28 * 10**9, bytes_accessed=40 * 10**6, transcendentals=2 * 10**6),
        name="middle",
    )(core, att, gate, x, g, oe, gain, shift, wu, bu, wd)


def middle_back_kernel(
    core_ref, res, gn, att_ref, gate_ref, g_ref, oe_ref, gain_ref,
    gres_ref, gatt_ref, glog_ref, oes_ref, oek_ref, vec_ref, mixed, low_grad, turned, *, chunk,
):
    heads, segs, dh, rows = att_ref.shape
    total, width = g_ref.shape
    half = width // 2
    mine = pl.multiple_of(core_ref[0] * half, half)
    other = pl.multiple_of((1 - core_ref[0]) * half, half)
    mix_rows(mixed, att_ref, gate_ref)
    zero = jnp.zeros((1, width), jnp.float32)

    def rows_back(i, sums):
        at = pl.ds(pl.multiple_of(i * chunk, chunk), chunk)
        unit, inv_std = norm_parts(res[at, :])
        grad = gn[at, :]
        g = to_wide(g_ref[at, :])
        q = grad * row(gain_ref)
        back = q - jnp.mean(q, axis=1, keepdims=True) - unit * jnp.mean(q * unit, axis=1, keepdims=True)
        out = g + inv_std * back
        gres_ref[at, :] = out
        low_grad[at, :] = to_low(out)
        return (
            sums[0] + jnp.sum(grad * unit, axis=0, keepdims=True),
            sums[1] + jnp.sum(grad, axis=0, keepdims=True),
            sums[2] + jnp.sum(g, axis=0, keepdims=True),
        )

    sums = lax.fori_loop(0, total // chunk, rows_back, (zero, zero, zero))
    for k in range(3):
        vec_ref[k : k + 1] = sums[k]
    turned[...] = low_grad[...].T
    for h in range(heads):
        group = nn(oe_ref[h * EXPERTS * dh : (h + 1) * EXPERTS * dh], turned[...])
        for s in range(segs):
            att = to_wide(att_ref[h, s])
            grad = jnp.zeros((dh, rows), jnp.float32)
            for e in range(EXPERTS):
                slot = h * EXPERTS + e
                part = group[e * dh : (e + 1) * dh, s * rows : (s + 1) * rows]
                gate = gate_ref[s, slot : slot + 1]
                grad = grad + gate * part
                logit = jnp.sum(part * att, axis=0, keepdims=True) * (gate * (1.0 - gate))
                glog_ref[s, slot : slot + 1] = logit
            gatt_ref[h, s] = to_low(grad)
    oes_ref[...] = to_low(nn(mixed[...], low_grad[:, pl.ds(other, half)]))
    oek_ref[...] = to_low(nn(mixed[...], low_grad[:, pl.ds(mine, half)]))


def middle_back(core, res, gn, att, gate, g, oe, gain):
    inner, width = oe.shape
    total = g.shape[0]
    low, f32 = jnp.bfloat16, jnp.float32
    vmem = pl.BlockSpec(memory_space=pltpu.VMEM)
    return pl.pallas_call(
        functools.partial(middle_back_kernel, chunk=64),
        in_specs=[pl.BlockSpec(memory_space=pltpu.SMEM)] + [vmem] * 7,
        out_specs=[vmem] * 6,
        out_shape=[
            jax.ShapeDtypeStruct((total, width), f32),
            jax.ShapeDtypeStruct(att.shape, low),
            jax.ShapeDtypeStruct(gate.shape, f32),
            jax.ShapeDtypeStruct((inner, width // 2), low),
            jax.ShapeDtypeStruct((inner, width // 2), low),
            jax.ShapeDtypeStruct((3, width), f32),
        ],
        scratch_shapes=[
            pltpu.VMEM((inner, total), low),
            pltpu.VMEM((total, width), low),
            pltpu.VMEM((width, total), low),
        ],
        compiler_params=params(60),
        cost_estimate=pl.CostEstimate(flops=5 * 10**9, bytes_accessed=20 * 10**6, transcendentals=0),
        name="middle_back",
    )(core, res, gn, att, gate, g, oe, gain)


def feed_kernel(hid_ref, wd_ref, res_ref, bd_ref, y_ref, acc):
    step = pl.program_id(0)
    part = nn(hid_ref[...], wd_ref[...])

    @pl.when(step == 0)
    def _():
        acc[...] = res_ref[...] + part

    @pl.when(step > 0)
    def _():
        acc[...] += part

    @pl.when(step == pl.num_programs(0) - 1)
    def _():
        y_ref[...] = to_low(acc[...] + row(bd_ref))


def feed(hidden, wd, res, bd, fc=1024):
    total, ff = hidden.shape
    width = wd.shape[1]
    return pl.pallas_call(
        feed_kernel,
        grid=(ff // fc,),
        in_specs=[
            pl.BlockSpec((total, fc), lambda i: (0, i)),
            pl.BlockSpec((fc, width), lambda i: (i, 0)),
            once((total, width), lambda i: (0, 0)),
            vector(bd),
        ],
        out_specs=pl.BlockSpec((total, width), lambda i: (0, 0)),
        out_shape=jax.ShapeDtypeStruct((total, width), jnp.bfloat16),
        scratch_shapes=[pltpu.VMEM((total, width), jnp.float32)],
        compiler_params=params(60),
        cost_estimate=pl.CostEstimate(flops=1000, bytes_accessed=1000, transcendentals=0),
        name="feed",
    )(hidden, wd, res, bd)


def late_rows(dh):
    first = HEADS * EXPERTS * dh
    second = first + HEADS * dh
    third = second + HEADS * dh
    return first, second, third, third + 32, third + 64


def back_kernel(
    mem_ref, blk_ref, gain_ref, shift_ref, d_ref, glog_ref, gate_ref, all_ref, ve_ref, wk_ref, wq_ref,
    rv_ref, ro_ref, gres_ref, extra_ref, xg_ref, late_ref, vec, gt, every_gt, every_norm,
):
    half = pl.program_id(1)
    first_step = (pl.program_id(0) == 0) & (half == 0)
    heads, dh = d_ref.shape[0], d_ref.shape[3]
    slots = gate_ref.shape[2]
    at_key, at_query, at_value, at_out, end = late_rows(dh)

    @pl.when(first_step)
    def _():
        gt[at_value:end] = jnp.zeros((end - at_value, gt.shape[1]), jnp.bfloat16)
        vec[...] = jnp.zeros_like(vec)

    for h in range(heads):
        gv = to_wide(jnp.where(half == 0, d_ref[h, 0, 3], d_ref[h, 0, 4]))
        for e in range(EXPERTS):
            slot = h * EXPERTS + e
            gate = gate_ref[0, 0, slot : slot + 1]
            gt[slot * dh : (slot + 1) * dh] = to_low(gate * gv)
            logit = jnp.sum(to_wide(all_ref[0, 0, slot * dh : (slot + 1) * dh]) * gv, axis=0, keepdims=True)
            gt[at_value + slot : at_value + slot + 1] = to_low(logit * (gate * (1.0 - gate)))

    @pl.when(half == 0)
    def _():
        for h in range(heads):
            gt[at_key + h * dh : at_key + (h + 1) * dh] = d_ref[h, 0, 1]
        gt[at_query:at_value] = jnp.zeros((at_value - at_query, gt.shape[1]), jnp.bfloat16)
        gt[at_out : at_out + slots] = jnp.zeros((slots, gt.shape[1]), jnp.bfloat16)

    @pl.when(half == 1)
    def _():
        for h in range(heads):
            gt[at_key + h * dh : at_key + (h + 1) * dh] = d_ref[h, 0, 2]
            gt[at_query + h * dh : at_query + (h + 1) * dh] = d_ref[h, 0, 0]
        gt[at_out : at_out + slots] = to_low(glog_ref[0])

    rows = to_wide(jnp.where(half == 0, mem_ref[0], blk_ref[0]))
    unit, inv_std = norm_parts(rows)
    gain = row(gain_ref)
    normed = to_low(unit * gain + row(shift_ref))
    count = gt.shape[1]
    at = pl.multiple_of((pl.program_id(0) * 2 + half) * count, count)
    every_gt[:, pl.ds(at, count)] = gt[...]
    every_norm[pl.ds(at, count), :] = normed
    grad = nn(gt[:at_key].T, ve_ref[...]) + nn(gt[at_key:at_query].T, wk_ref[...])
    grad = grad + nn(gt[at_query:at_value].T, wq_ref[...])
    grad = grad + nn(gt[at_value : at_value + slots].T, rv_ref[...])
    grad = grad + nn(gt[at_out : at_out + slots].T, ro_ref[...])
    vec[0:1] += jnp.sum(grad * unit, axis=0, keepdims=True)
    vec[1:2] += jnp.sum(grad, axis=0, keepdims=True)

    @pl.when(half == 1)
    def _():
        q = grad * gain
        back = q - jnp.mean(q, axis=1, keepdims=True) - unit * jnp.mean(q * unit, axis=1, keepdims=True)
        xg_ref[0] = to_low(gres_ref[0] + inv_std * back)

    @pl.when((pl.program_id(0) == pl.num_programs(0) - 1) & (half == 1))
    def _():
        for k in range(0, late_ref.shape[0], 2):
            pair = to_low(nn(every_gt[...], every_norm[:, k * LANES : (k + 2) * LANES]))
            late_ref[k] = pair[:, :LANES]
            late_ref[k + 1] = pair[:, LANES:]
        for k in range(late_ref.shape[0]):
            both = vec[0:2, k * LANES : (k + 1) * LANES]
            late_ref[k, at_value + slots : at_value + slots + 2] = to_low(both)
            late_ref[k, at_out + slots : at_out + slots + 8] = to_low(extra_ref[k])


def back(mem, blk, gain, shift, grads, glog, gate, every, vet, wkt, wqt, rvt, rot, gres, extra):
    segs, rows, width = blk.shape
    heads, _, _, dh, _ = grads.shape
    slots = gate.shape[2]
    end = late_rows(dh)[-1]
    low, f32 = jnp.bfloat16, jnp.float32
    row_spec = pl.BlockSpec((1, rows, width), lambda s, r: (s, 0, 0))
    flat = lambda s, r: (0, 0)
    return pl.pallas_call(
        back_kernel,
        grid=(segs, 2),
        in_specs=[
            row_spec,
            row_spec,
            vector(gain),
            vector(shift),
            pl.BlockSpec((heads, 1, 5, dh, rows), lambda s, r: (0, s, 0, 0, 0)),
            pl.BlockSpec((1, slots, rows), lambda s, r: (s, 0, 0)),
            pl.BlockSpec((1, 1, slots, rows), lambda s, r: (s, r, 0, 0)),
            pl.BlockSpec((1, 1, every.shape[2], rows), lambda s, r: (s, r, 0, 0)),
            once(vet.shape, flat),
            once(wkt.shape, flat),
            once(wqt.shape, flat),
            once(rvt.shape, flat),
            once(rot.shape, flat),
            row_spec,
            once(extra.shape, lambda s, r: (0, 0, 0)),
        ],
        out_specs=[
            row_spec,
            pl.BlockSpec((width // LANES, end, LANES), lambda s, r: (0, 0, 0)),
        ],
        out_shape=[
            jax.ShapeDtypeStruct(blk.shape, low),
            jax.ShapeDtypeStruct((width // LANES, end, LANES), low),
        ],
        scratch_shapes=[
            pltpu.VMEM((8, width), f32),
            pltpu.VMEM((end, rows), low),
            pltpu.VMEM((end, 2 * segs * rows), low),
            pltpu.VMEM((2 * segs * rows, width), low),
        ],
        compiler_params=params(60),
        cost_estimate=pl.CostEstimate(flops=14 * 10**9, bytes_accessed=25 * 10**6, transcendentals=0),
        name="back",
    )(mem, blk, gain, shift, grads, glog, gate, every, vet, wkt, wqt, rvt, rot, gres, extra)


def lean_kernel(
    mem_ref, blk_ref, gain_ref, shift_ref, d_ref, glog_ref, gate_ref, all_ref, extra_ref, late_ref, gt, every_gt,
    every_norm,
):
    half = pl.program_id(1)
    first_step = (pl.program_id(0) == 0) & (half == 0)
    heads, dh = d_ref.shape[0], d_ref.shape[3]
    slots = gate_ref.shape[2]
    at_key, at_query, at_value, at_out, end = late_rows(dh)
    count = gt.shape[1]
    gt[at_value:end] = jnp.zeros((end - at_value, count), jnp.bfloat16)
    for h in range(heads):
        gv = to_wide(jnp.where(half == 0, d_ref[h, 0, 3], d_ref[h, 0, 4]))
        for e in range(EXPERTS):
            slot = h * EXPERTS + e
            gate = gate_ref[0, 0, slot : slot + 1]
            gt[slot * dh : (slot + 1) * dh] = to_low(gate * gv)
            logit = jnp.sum(to_wide(all_ref[0, 0, slot * dh : (slot + 1) * dh]) * gv, axis=0, keepdims=True)
            gt[at_value + slot : at_value + slot + 1] = to_low(logit * (gate * (1.0 - gate)))

    @pl.when(half == 0)
    def _():
        for h in range(heads):
            gt[at_key + h * dh : at_key + (h + 1) * dh] = d_ref[h, 0, 1]
        gt[at_query:at_value] = jnp.zeros((at_value - at_query, count), jnp.bfloat16)

    @pl.when(half == 1)
    def _():
        for h in range(heads):
            gt[at_key + h * dh : at_key + (h + 1) * dh] = d_ref[h, 0, 2]
            gt[at_query + h * dh : at_query + (h + 1) * dh] = d_ref[h, 0, 0]
        gt[at_out : at_out + slots] = to_low(glog_ref[0])

    unit, _ = norm_parts(to_wide(jnp.where(half == 0, mem_ref[0], blk_ref[0])))
    at = pl.multiple_of((pl.program_id(0) * 2 + half) * count, count)
    every_gt[:, pl.ds(at, count)] = gt[...]
    every_norm[pl.ds(at, count), :] = to_low(unit * row(gain_ref) + row(shift_ref))

    @pl.when((pl.program_id(0) == pl.num_programs(0) - 1) & (half == 1))
    def _():
        for k in range(0, late_ref.shape[0], 2):
            pair = to_low(nn(every_gt[...], every_norm[:, k * LANES : (k + 2) * LANES]))
            late_ref[k] = pair[:, :LANES]
            late_ref[k + 1] = pair[:, LANES:]
        for k in range(late_ref.shape[0]):
            late_ref[k, at_out + slots : at_out + slots + 8] = to_low(extra_ref[k])


def lean(mem, blk, gain, shift, grads, glog, gate, every, extra):
    segs, rows, width = blk.shape
    heads, _, _, dh, _ = grads.shape
    slots = gate.shape[2]
    end = late_rows(dh)[-1]
    low = jnp.bfloat16
    row_spec = pl.BlockSpec((1, rows, width), lambda s, r: (s, 0, 0))
    return pl.pallas_call(
        lean_kernel,
        grid=(segs, 2),
        in_specs=[
            row_spec,
            row_spec,
            vector(gain),
            vector(shift),
            pl.BlockSpec((heads, 1, 5, dh, rows), lambda s, r: (0, s, 0, 0, 0)),
            pl.BlockSpec((1, slots, rows), lambda s, r: (s, 0, 0)),
            pl.BlockSpec((1, 1, slots, rows), lambda s, r: (s, r, 0, 0)),
            pl.BlockSpec((1, 1, every.shape[2], rows), lambda s, r: (s, r, 0, 0)),
            once(extra.shape, lambda s, r: (0, 0, 0)),
        ],
        out_specs=[
            pl.BlockSpec((width // LANES, end, LANES), lambda s, r: (0, 0, 0)),
            pl.BlockSpec((end, rows), lambda s, r: (0, s * 2 + r)),
        ],
        out_shape=[
            jax.ShapeDtypeStruct((width // LANES, end, LANES), low),
            jax.ShapeDtypeStruct((end, 2 * segs * rows), low),
        ],
        scratch_shapes=[
            pltpu.VMEM((end, 2 * segs * rows), low),
            pltpu.VMEM((2 * segs * rows, width), low),
        ],
        compiler_params=params(60),
        cost_estimate=pl.CostEstimate(flops=7 * 10**9, bytes_accessed=25 * 10**6, transcendentals=0),
        name="lean",
    )(mem, blk, gain, shift, grads, glog, gate, every, extra)


def fold_kernel(bits_ref, *refs, counts):
    at = 0
    outs = sum(counts) * 2
    for k, count in enumerate(counts):
        for part in range(2):
            total = to_wide(refs[at][...])
            for extra in range(1, count):
                total = total + to_wide(refs[at + extra][...])
            refs[outs + 2 * k + part][...] = to_low(total).reshape(refs[outs + 2 * k + part].shape)
            at += count


def fold(items, bits):
    in_specs, arrays, out_specs, out_shape, counts = [], [], [], [], []
    steps = 4
    for k, (addends, dim) in enumerate(items):
        shape = addends[0].shape
        rows, cols = shape[-2:]
        lead = shape[:-2]
        if dim == "columns":
            left, width = lead, cols // 2
        else:
            left, width = lead[:dim] + lead[dim + 1 :], cols
        total = 1
        for size in left:
            total *= size
        group = min(total, steps)
        cut_rows = steps // group
        block_rows = rows // cut_rows
        span = total // group

        def where(i, c, side, k=k, dim=dim, left=left, lead=lead, span=span, cut_rows=cut_rows):
            half = c[k] if side else 1 - c[k]
            index = (i // cut_rows) * span
            coords = []
            for size in reversed(left):
                coords.append(index % size)
                index = index // size
            coords = coords[::-1]
            if dim == "columns":
                return tuple(coords) + (i % cut_rows, half)
            return tuple(coords[:dim]) + (half,) + tuple(coords[dim:]) + (i % cut_rows, 0)

        tail_axes, covered = [], 1
        for size in reversed(left):
            if covered < span:
                covered *= size
                tail_axes.append(size)
            else:
                tail_axes.append(1)
        tail_axes = tail_axes[::-1]
        assert covered == span
        if dim == "columns":
            block = tuple(tail_axes) + (block_rows, width)
        else:
            block = tuple(tail_axes[:dim]) + (1,) + tuple(tail_axes[dim:]) + (block_rows, cols)

        def spec_map(side, where=where, block=block):
            def index(i, c):
                coords = where(i, c, side)
                return tuple(x // b if n < len(block) - 2 else x for n, (x, b) in enumerate(zip(coords, block)))

            return index

        for side in range(2):
            for a in addends:
                arrays.append(a)
                in_specs.append(pl.BlockSpec(block, spec_map(side)))
        out_block = tuple(tail_axes) + (block_rows, width)

        def out_map(i, c, left=left, span=span, cut_rows=cut_rows, tail_axes=tail_axes):
            index = (i // cut_rows) * span
            coords = []
            for size in reversed(left):
                coords.append(index % size)
                index = index // size
            coords = coords[::-1]
            return tuple(x // b for x, b in zip(coords, tail_axes)) + (i % cut_rows, 0)

        for side in range(2):
            out_specs.append(pl.BlockSpec(out_block, out_map))
            out_shape.append(jax.ShapeDtypeStruct(tuple(left) + (rows, width), jnp.bfloat16))
        counts.append(len(addends))
    outs = pl.pallas_call(
        functools.partial(fold_kernel, counts=tuple(counts)),
        grid_spec=pltpu.PrefetchScalarGridSpec(
            num_scalar_prefetch=1, grid=(steps,), in_specs=in_specs, out_specs=out_specs
        ),
        out_shape=out_shape,
        compiler_params=params(48),
        cost_estimate=pl.CostEstimate(flops=10**7, bytes_accessed=30 * 10**6, transcendentals=0),
        name="fold",
    )(bits, *arrays)
    return [(outs[2 * k], outs[2 * k + 1]) for k in range(len(items))]


class Chain:
    def __init__(self, axes, stages, shape, halve):
        self.axes, self.stages, self.shape, self.halve = axes, stages, shape, halve

    def landing(self, extra=0):
        free, size, out = list(self.axes), list(self.shape), []
        for stage in self.stages:
            if stage in free:
                free.remove(stage)
            elif stage == "x":
                size[self.halve] //= 2
            elif stage != "c":
                break
            out.append((2,) * len(free) + tuple(size))
            if stage == "x":
                size[0] += extra
        return out


def plus(left, right):
    return to_low(to_wide(left) + to_wide(right))


LATE = ("L1", "L2", "L3")


def late_cut(share):
    third = share // 96 * 32
    return (third, (share - third) // 2, (share - third) // 2)


ORDER = (
    "L10 L20 L30 C0",
    "O0 B0 L11 E0",
    "L31 L21 E1 L12",
    "C1 O1 B1 L22",
    "L32 L13 E2 E3",
    "L23 V0 O2 C2",
    "L14 V1 L33 C3",
    "L24 O3 V2 L34",
    "L15 O4 V3 L25",
    "L16 L35 V4 L26",
    "L36",
)
STARTS = ("C", "O", "E")


def chains(c, e, o, share_rows):
    ends = ["GX", "GC"]
    return {
        "C": Chain(["w"], ["x", "w"] + ends, c, 1),
        "E": Chain(["w"], ["w", "x"] + ends, e, 1),
        "O": Chain(["w", "z", "y"], ["y", "z", "w"] + ends, o, 1),
    } | {
        name: Chain(["w", "z", "y"], ["c"] + list(stages) + ends, (rows, LANES), 0)
        for name, stages, rows in zip(LATE, ("xyzw", "yxzw", "zyxw"), late_cut(share_rows))
    }


def finish_kernel(
    late, gt_hbm, ve_hbm, wk_hbm, wq_hbm, mem_hbm, blk_hbm, gres_hbm, rv_ref, ro_ref, gain_ref, pos, c0, c1, e0, e1,
    o0, o1, outc, oute, outo, outl, outv, xg_ref, *scratch, table,
):
    def place(axis, bit):
        me = lax.axis_index(axis)
        mine = (me // bit) % 2
        return mine, {axis: me + bit * (1 - 2 * mine)}

    mine, who = {}, {}
    for name, axis, bit in (("c", "pos", 1), ("x", "pos", 2), ("y", "seg", 1), ("z", "seg", 2), ("w", "seg", 4)):
        mine[name], who[name] = place(axis, bit)
    barrier = pltpu.get_barrier_semaphore()
    for target in who.values():
        pl.semaphore_signal(barrier, inc=1, device_id=target, device_id_type=pl.DeviceIdType.MESH)
    pl.semaphore_wait(barrier, len(who))

    scratch = list(scratch)
    sent, came, near, loads = scratch[-4:]
    gt, ve, wk, wq, rows_in, gres, sums = scratch[-11:-4]
    vec = scratch[-19:-11]
    work = dict(zip(("C", "E", "O") + LATE + ("L1m",), scratch[:7]))
    landed, at = {}, 7
    for name, chain in table.items():
        stages = len(chain.landing())
        landed[name] = scratch[at : at + stages]
        at += stages
    both = {"C": (c0, c1), "E": (e0, e1), "O": (o0, o1)}
    lead_rows = pos.shape[3]
    late_half = table["L1"].shape[0] // 2
    outs = {"C": (outc, None), "E": (oute, None), "O": (outo, None)}
    first = 0
    for name in LATE:
        size = table[name].shape[0] // 2 + (lead_rows if name == "L1" else 0)
        outs[name] = (outl, (first, size))
        first += size
    started = {}
    copies = []

    def send(key, src, dst, target):
        copy = pltpu.make_async_remote_copy(
            src_ref=src,
            dst_ref=dst,
            send_sem=sent.at[len(copies)],
            recv_sem=came.at[len(copies)],
            device_id=who[target],
            device_id_type=pl.DeviceIdType.MESH,
        )
        copy.start()
        copies.append(copy)
        started[key] = copy

    free = {name: list(chain.axes) for name, chain in table.items()}
    span = {name: (None, chain.shape[chain.halve]) for name, chain in table.items()}

    def pieces(name, start, size):
        halve = table[name].halve
        if start is None:
            return (slice(None), slice(None))
        one = pl.ds(pl.multiple_of(start, 16 if halve == 0 else LANES), size)
        return (one, slice(None)) if halve == 0 else (slice(None), one)

    def part(name, axis, value):
        start, size = span[name]
        fixed = {a: mine[a] for a in table[name].axes if a not in free[name]}
        left = list(free[name])
        relative = None
        if axis == "x":
            size = size // 2
            relative = value * size
            start = relative if start is None else start + relative
        elif axis is not None:
            fixed[axis] = value
            left.remove(axis)
        return left, fixed, start, size, relative

    def total(name, stage, axis, value, store=None):
        left, fixed, start, size, relative = part(name, axis, value)
        chain = table[name]
        switch = name == "L1" and stage is not None and chain.stages[stage] == "x"
        buffer = work[name]

        def one(values):
            index = tuple(values[a] if a in values else fixed[a] for a in chain.axes)
            full = index + pieces(name, start, size)
            if stage is None:
                left_ref, right_ref = both[name]
                got = plus(left_ref[full], right_ref[full])
            else:
                lead = tuple(values[a] if a in values else fixed[a] for a in free[name])
                got = plus(buffer[full], landed[name][stage][lead + pieces(name, relative, size)])
            if store is not None:
                store(got)
            elif switch:
                work["L1m"][index + (slice(0, size), slice(None))] = got
                work["L1m"][index + (slice(size, None), slice(None))] = pos[index]
            else:
                buffer[full] = got

        count = 1 << len(left)
        if count == 1:
            one({})
        elif count == 2:
            for k in range(2):
                one({left[0]: k})
        else:

            @pl.loop(0, count)
            def _(i):
                one({a: (i // (1 << (len(left) - 1 - k))) % 2 for k, a in enumerate(left)})

    def advance(name, stage):
        chain = table[name]
        following = chain.stages[0 if stage is None else stage + 1]
        switch = name == "L1" and stage is not None and chain.stages[stage] == "x"
        number = 0 if stage is None else stage + 1
        out, rows = outs[name]
        place_out = (slice(None), slice(None)) if rows is None else (slice(rows[0], rows[0] + rows[1]), slice(None))
        if following == "GX":

            def store(got):
                out[(mine["c"], mine["x"]) + place_out] = got

            total(name, stage, None, None, store)
            at = out.at[(mine["c"], mine["x"]) + place_out]
            send((name, number), at, at, "x")
            return
        if following == "GC":
            at = out.at[(mine["c"], slice(None)) + place_out]
            send((name, number), at, at, "c")
            return
        other = 1 - mine[following]
        total(name, stage, following, other)
        if switch:
            left, fixed, _, _, _ = part(name, following, other)
            source = work["L1m"]
            index = tuple(slice(None) if a in left else fixed[a] for a in chain.axes) + (slice(None), slice(None))
        else:
            left, fixed, start, size, _ = part(name, following, other)
            source = work[name]
            index = tuple(slice(None) if a in left else fixed[a] for a in chain.axes) + pieces(name, start, size)
        send((name, number), source.at[index], landed[name][number], following)
        total(name, stage, following, mine[following])
        if switch:
            work["L1"] = work["L1m"]
            span["L1"] = (None, late_half + lead_rows)
        if following == "x":
            start, size = span[name]
            half = size // 2
            span[name] = (mine["x"] * half if start is None else start + mine["x"] * half, half)
        else:
            free[name].remove(following)

    share = sum(table[name].shape[0] for name in LATE)
    keep = {}
    first = 0
    for number, name in enumerate(LATE):
        size = table[name].shape[0]
        own = pl.multiple_of(mine["c"] * share + first, 16)
        theirs = pl.multiple_of((1 - mine["c"]) * share + first, 16)
        send((name, 0), late.at[:, :, :, pl.ds(theirs, size)], landed[name][0], "c")
        keep[name] = pltpu.make_async_copy(late.at[:, :, :, pl.ds(own, size)], work[name], near.at[number])
        keep[name].start()
        first += size
    for name in STARTS:
        advance(name, None)

    moves = [(gt_hbm, gt), (ve_hbm, ve), (wk_hbm, wk), (wq_hbm, wq), (gres_hbm, gres)]
    moves += [(mem_hbm, rows_in.at[:, 0]), (blk_hbm, rows_in.at[:, 1])]
    moves = [pltpu.make_async_copy(a, b, loads.at[k]) for k, (a, b) in enumerate(moves)]
    for move in moves:
        move.start()
    rows = rows_in.shape[2]
    slots = rv_ref.shape[0]
    at_key, at_query, at_value, at_out, _ = late_rows(pos.shape[3])

    def inputs(begin):
        @pl.loop(begin, begin + 2)
        def _(b):
            mine_gt = gt[:, pl.ds(pl.multiple_of(b * rows, rows), rows)]
            grad = nn(mine_gt[:at_key].T, ve[...]) + nn(mine_gt[at_key:at_query].T, wk[...])
            grad = grad + nn(mine_gt[at_query:at_value].T, wq[...])
            grad = grad + nn(mine_gt[at_value : at_value + slots].T, rv_ref[...])
            grad = grad + nn(mine_gt[at_out : at_out + slots].T, ro_ref[...])
            unit, inv_std = norm_parts(to_wide(rows_in[b // 2, b % 2]))
            sums[0:1] += jnp.sum(grad * unit, axis=0, keepdims=True)
            sums[1:2] += jnp.sum(grad, axis=0, keepdims=True)

            @pl.when(b % 2 == 1)
            def _():
                q = grad * row(gain_ref)
                back = q - jnp.mean(q, axis=1, keepdims=True) - unit * jnp.mean(q * unit, axis=1, keepdims=True)
                xg_ref[b // 2] = to_low(gres[b // 2] + inv_std * back)

    v0, v1, v2, vc, vx, vy, vz, vw = vec
    my, mz, mw = mine["y"], mine["z"], mine["w"]

    def vectors(stage):
        if stage < 0:
            for k in range(8):
                v0[k // 4, (k // 2) % 2, k % 2] = to_low(sums[:, k * LANES : (k + 1) * LANES])
            send(("V", 0), v0, vc, "c")
        elif stage == 0:
            v1[...] = plus(v0[...], vc[...])
            send(("V", 1), v1, vx, "x")
        elif stage == 1:
            v2[...] = plus(v1[...], vx[...])
            send(("V", 2), v2.at[:, :, 1 - my], vy, "y")
        elif stage == 2:
            for a in range(2):
                for b in range(2):
                    v2[a, b, my] = plus(v2[a, b, my], vy[a, b])
            send(("V", 3), v2.at[:, 1 - mz, my], vz, "z")
        elif stage == 3:
            for a in range(2):
                v2[a, mz, my] = plus(v2[a, mz, my], vz[a])
            send(("V", 4), v2.at[1 - mw, mz, my], vw, "w")
        else:
            outv[...] = to_wide(v2[mw, mz, my]) + to_wide(vw[...])

    for event in " ".join(ORDER).split():
        name, stage = event[:-1], int(event[-1])
        if name == "B":
            if stage == 0:
                for move in moves:
                    move.wait()
                sums[...] = jnp.zeros_like(sums)
            inputs(2 * stage)
            if stage == 1:
                vectors(-1)
            continue
        if name == "V":
            started[(name, stage)].wait_recv()
            vectors(stage)
            continue
        started[(name, stage)].wait_recv()
        if stage == 0 and name in keep:
            keep[name].wait()
        if stage + 1 < len(table[name].stages):
            advance(name, stage)
    for copy in copies:
        copy.wait_send()


def finish(late, gt, weights, rows, gres, gain, pos, c, e, o):
    low, f32 = jnp.bfloat16, jnp.float32
    cube = (2, 2, 2)
    share = late.shape[1] // 2
    table = chains(c[0].shape[1:], e[0].shape[1:], o[0].shape[3:], share)
    lead_rows = pos.shape[1]
    vmem = pl.BlockSpec(memory_space=pltpu.VMEM)
    hbm = pl.BlockSpec(memory_space=pl.ANY)
    shapes = [c[0].shape, e[0].shape, o[0].shape]
    shapes += [cube + table[name].shape for name in LATE]
    shapes += [cube + (table["L1"].shape[0] // 2 + lead_rows, LANES)]
    for name, chain in table.items():
        shapes += chain.landing(lead_rows if name == "L1" else 0)
    small = (16, LANES)
    shapes += [cube + small] * 5 + [(2, 2) + small, (2,) + small, small]
    segs, length, width = rows[0].shape
    shapes += [gt.shape] + [w.shape for w in weights[:3]] + [(segs, 2, length, width)]
    scratch = [pltpu.VMEM(shape, low) for shape in shapes]
    scratch += [pltpu.VMEM(gres.shape, f32), pltpu.VMEM((16, width), f32)]
    count = sum(len(chain.stages) for chain in table.values()) + 5
    scratch += [pltpu.SemaphoreType.DMA((count,)), pltpu.SemaphoreType.DMA((count,)), pltpu.SemaphoreType.DMA((3,))]
    scratch += [pltpu.SemaphoreType.DMA((7,))]
    out = [
        (c[0].shape[1], c[0].shape[2] // 2),
        (e[0].shape[1], e[0].shape[2] // 2),
        o[0].shape[3:],
        (share // 2 + lead_rows, LANES),
    ]
    out = [jax.ShapeDtypeStruct((2, 2) + shape, low) for shape in out]
    out += [jax.ShapeDtypeStruct(small, f32), jax.ShapeDtypeStruct(rows[0].shape, low)]
    return pl.pallas_call(
        functools.partial(finish_kernel, table=table),
        in_specs=[hbm] * 8 + [vmem] * 10,
        out_specs=[vmem] * 6,
        out_shape=out,
        scratch_shapes=scratch,
        compiler_params=pltpu.CompilerParams(vmem_limit_bytes=62 << 20, collective_id=0, has_side_effects=True),
        cost_estimate=pl.CostEstimate(flops=7 * 10**9, bytes_accessed=40 * 10**6, transcendentals=0),
        name="finish",
    )(
        late.reshape(cube + late.shape[1:]),
        gt,
        *weights[:3],
        *rows,
        gres,
        *weights[3:],
        gain,
        pos.reshape(cube + pos.shape[1:]),
        *c,
        *e,
        *o,
    )


def emit_kernel(c_hbm, e_hbm, o_hbm, l_hbm, vec_ref, *refs, plan, slots):
    outs, (c_ref, e_ref, o_ref, l_ref, vals, sems) = refs[:-6], refs[-6:]
    pairs = ((l_hbm, l_ref), (c_hbm, c_ref), (e_hbm, e_ref), (o_hbm, o_ref))
    copies = [pltpu.make_async_copy(a, b, sems.at[k]) for k, (a, b) in enumerate(pairs)]
    for copy in copies:
        copy.start()
    copies[0].wait()
    experts, keys, queries, positions, values, gates = outs[3:9]
    targets = (experts, keys, queries, vals, positions)
    for core, x, start, number, to, rows in plan:
        targets[number][to : to + rows] = to_wide(l_ref[core, x, start : start + rows])
    half = vals.shape[0] // 2
    values[...] = vals[:slots]
    gates[...] = vals[half : half + slots]
    first_gain, first_shift, second_gain, second_shift, contract, expand, content, position = outs[9:]
    first_gain[...] = vec_ref[0]
    first_shift[...] = vec_ref[1]
    lines = tuple((ref, half + slots + k) for k, ref in enumerate((second_gain, second_shift, contract)))
    for ref, number in lines:
        ref[...] = vals[number]
    for k in range(4):
        expand[k * LANES : (k + 1) * LANES] = vals[half + slots + 3 + k]
    size = content.shape[0]
    content[...] = vals[half + slots + 7, :size]
    position[...] = vals[half + slots + 7, size : 2 * size]
    for k, ref in enumerate((c_ref, e_ref, o_ref)):
        width = ref.shape[3]
        copies[k + 1].wait()
        for core in range(2):
            for x in range(2):
                at = (core * 2 + x) * width
                outs[k][:, at : at + width] = to_wide(ref[core, x])


def emit(quarters, vec, dh):
    c, e, o, tail = quarters
    f32 = jnp.float32
    slots = HEADS * EXPERTS
    at_key, at_query, at_value, _, end = late_rows(dh)
    halves = [rows // 2 for rows in late_cut(end // 2)]
    sizes = [at_key, at_query - at_key, at_value - at_query, end - at_value]
    starts = [0, at_key, at_query, at_value]
    plan = []
    for core in range(2):
        for x in range(2):
            for part, piece in enumerate(halves):
                source = sum(halves[:part]) + (dh if part else 0)
                low_end = core * (end // 2) + 2 * sum(halves[:part]) + x * piece
                for k, (first, size) in enumerate(zip(starts, sizes)):
                    a, b = max(first, low_end), min(first + size, low_end + piece)
                    if a < b:
                        plan.append((core, x, source + a - low_end, k, a - first, b - a))
            plan.append((core, x, halves[0], 4, (2 * x + core) * dh, dh))
    vmem = pl.BlockSpec(memory_space=pltpu.VMEM)
    shapes = [(q.shape[2], 4 * q.shape[3]) for q in (c, e, o)] + [(n, LANES) for n in sizes[:3] + [HEADS * dh]]
    shapes += [(slots, LANES)] * 2 + [(LANES,)] * 5 + [(4 * LANES,)] + [(HEADS * dh * LANES // D,)] * 2
    return pl.pallas_call(
        functools.partial(emit_kernel, plan=tuple(plan), slots=slots),
        in_specs=[pl.BlockSpec(memory_space=pl.ANY)] * 4 + [vmem],
        out_specs=[vmem] * len(shapes),
        out_shape=[jax.ShapeDtypeStruct(shape, f32) for shape in shapes],
        scratch_shapes=[pltpu.VMEM(q.shape, q.dtype) for q in quarters]
        + [pltpu.VMEM((end - at_value, LANES), f32), pltpu.SemaphoreType.DMA((4,))],
        compiler_params=params(60),
        name="emit",
    )(c, e, o, tail, vec)


def mm(spec, left, right):
    return jnp.einsum(spec, left, right, preferred_element_type=jnp.float32)


def position_table(row_count, width_count):
    fine = 64
    inverse_freq = 10000.0 ** (-jnp.arange(0, width_count, 2).astype(jnp.float32) / width_count)
    high = (row_count // fine - 1 - jnp.arange(row_count // fine)) * fine
    low_part = fine - 1 - jnp.arange(fine)
    high_angle = high.astype(jnp.float32)[:, None, None] * inverse_freq
    low_angle = low_part.astype(jnp.float32)[None, :, None] * inverse_freq
    high_sin, high_cos = jnp.sin(high_angle), jnp.cos(high_angle)
    low_sin, low_cos = jnp.sin(low_angle), jnp.cos(low_angle)
    sines = high_sin * low_cos + high_cos * low_sin
    cosines = high_cos * low_cos - high_sin * low_sin
    return to_low(jnp.concatenate([sines, cosines], axis=2)).reshape(row_count, width_count)


def route_mask(routes, expert_count):
    return jnp.sum((routes[..., None] == jnp.arange(expert_count)).astype(jnp.float32), axis=-2)


def bit_of(axis, bit):
    return (lax.axis_index(axis) // bit) % 2


def swap(value, axis, bit):
    pairs = [(i, i ^ bit) for i in range(lax.axis_size(axis))]
    return lax.ppermute(value, axis, pairs)


def pick(value, index, axis):
    return lax.dynamic_index_in_dim(value, index, axis, keepdims=False)


def cut(value, index, axis):
    size = value.shape[axis] // 2
    return lax.dynamic_slice_in_dim(value, index * size, size, axis)


def axis_bits(axis):
    size = lax.axis_size(axis)
    return [1 << k for k in range(size.bit_length() - 1)]


def bits_tree(value, seg_size):
    count = len(axis_bits("seg"))
    return value.reshape((2,) * count + (value.shape[0] // seg_size, value.shape[1]))


class Share:
    def __init__(self, addends, bits):
        self.addends = addends
        self.bits = bits

    def total(self):
        out = to_wide(self.addends[0])
        for item in self.addends[1:]:
            out = out + to_wide(item)
        return to_low(out)

    def seg(self, number):
        if number >= len(axis_bits("seg")):
            return self
        bit = axis_bits("seg")[number]
        dim = len(self.bits) - 1 - self.bits.index(bit)
        mine = bit_of("seg", bit)
        sent = Share([pick(a, 1 - mine, dim) for a in self.addends], self.bits).total()
        come = swap(sent, "seg", bit)
        left = [b for b in self.bits if b != bit]
        return Share([pick(a, mine, dim) for a in self.addends] + [come], left)

    def rest(self):
        out = self
        for bit in self.bits:
            out = out.seg(axis_bits("seg").index(bit))
        return out

    def pos(self, number, dim):
        bit = axis_bits("pos")[number]
        mine = bit_of("pos", bit)
        at = len(self.bits) + dim
        sent = Share([cut(a, 1 - mine, at) for a in self.addends], self.bits).total()
        come = swap(sent, "pos", bit)
        return Share([cut(a, mine, at) for a in self.addends] + [come], self.bits)

    def pos_all(self, number):
        part = self.total()
        return Share([part, swap(part, "pos", axis_bits("pos")[number])], self.bits)


def together(stages):
    items, bits, swaps, lefts = [], [], [], []
    for item, axis, number in stages:
        bit = axis_bits(axis)[number]
        bits.append(bit_of(axis, bit))
        swaps.append((axis, bit))
        if axis == "seg":
            items.append((item.addends, len(item.bits) - 1 - item.bits.index(bit)))
            lefts.append([b for b in item.bits if b != bit])
        else:
            items.append((item.addends, "columns"))
            lefts.append(item.bits)
    pairs = fold(items, jnp.stack(bits).astype(jnp.int32))
    out = []
    for (sent, kept), (axis, bit), left in zip(pairs, swaps, lefts):
        out.append(Share([kept, swap(sent, axis, bit)], left))
    return out


def share(values, seg_size):
    return Share([bits_tree(v, seg_size) for v in values], axis_bits("seg"))


def widen(part, number, dim):
    bit = axis_bits("pos")[number]
    mine = bit_of("pos", bit)
    other = swap(part, "pos", bit)
    first = jnp.where(mine == 0, part, other)
    second = jnp.where(mine == 0, other, part)
    return jnp.concatenate([first, second], axis=dim)


def seg_blocks(value, seg_size):
    blocks, rows, lanes = value.shape
    inside = seg_size // blocks
    value = value.reshape(blocks, rows, inside, lanes // inside)
    value = jnp.transpose(value, (0, 2, 1, 3))
    count = len(axis_bits("seg"))
    return value.reshape((2,) * count + (rows, lanes // inside))


def vector_rows(vectors, seg_size):
    lanes = D // seg_size
    rows = jnp.concatenate([v.reshape(seg_size, -1, lanes) for v in vectors], axis=1)
    blocks = D // LANES
    rows = rows.reshape(blocks, seg_size // blocks, rows.shape[1], lanes)
    return jnp.transpose(rows, (0, 2, 1, 3)).reshape(blocks, -1, LANES)


def local(
    block_input,
    memory_rows,
    memory_length,
    value_routes,
    output_routes,
    first_gain,
    first_shift,
    query_weight,
    key_weight,
    position_weight,
    value_experts,
    value_router,
    content_bias,
    position_bias,
    output_experts,
    output_gate_matrix,
    second_gain,
    second_shift,
    up_projection_weight,
    expand_bias,
    down_projection_weight,
    contract_bias,
    output_cotangent,
):
    seg_count, local_rows, width = block_input.shape
    seg_size = lax.axis_size("seg")
    pos_index = lax.axis_index("pos")
    key_count = 2 * SEQ
    all_rows = seg_count * local_rows
    slots = HEADS * EXPERTS
    score_scale = DH ** (-0.5)
    line = lambda v: v.reshape(1, -1)

    value_pick = jnp.transpose(route_mask(value_routes, EXPERTS), (0, 1, 3, 4, 2))
    value_pick = value_pick.reshape(seg_count, 2, slots, local_rows)
    out_pick = jnp.transpose(route_mask(output_routes, EXPERTS), (0, 2, 3, 1))
    out_pick = out_pick.reshape(seg_count, slots, local_rows)
    pad = ((0, 0), (0, 32 - slots))
    gates = jnp.concatenate([jnp.pad(value_router, pad).T, jnp.pad(output_gate_matrix, pad).T], axis=0)

    def trade(value):
        return lax.all_to_all(value, "pos", split_axis=0, concat_axis=0, tiled=True)

    qk, normed, value_gate, out_gate = project(
        memory_rows,
        block_input,
        first_gain,
        first_shift,
        query_weight.T,
        key_weight.T,
        gates,
        value_pick,
        out_pick,
    )
    qk = trade(qk)
    values, value_all = experts(normed, value_experts.T, value_gate)
    values = trade(values)

    table_low = position_table(key_count, D)
    weight_local = pick(position_weight.reshape(D, HEADS, DH), pos_index, 1)
    positions = to_low(mm("nd,dc->cn", table_low, weight_local))

    head_content = pick(content_bias.reshape(HEADS, DH), pos_index, 0)
    head_position = pick(position_bias.reshape(HEADS, DH), pos_index, 0)
    probs = score(memory_length, qk, positions, head_content, head_position, score_scale)
    attended = attend(probs, values)

    core = bit_of("pos", 1).astype(jnp.int32).reshape(1)
    cotangent = output_cotangent.reshape(all_rows, width)
    (
        hidden,
        residual,
        grad_normed_two,
        down_sent,
        down_kept,
        up_sent,
        up_kept,
        expand_bias_grad,
    ) = middle(
        core,
        attended,
        out_gate,
        block_input.reshape(all_rows, width),
        cotangent,
        output_experts,
        second_gain,
        second_shift,
        up_projection_weight,
        line(expand_bias),
        down_projection_weight,
    )
    down_got = swap(down_sent, "pos", 1)
    up_got = swap(up_sent, "pos", 1)
    grad_residual, grad_attended, grad_out_logit, mix_sent, mix_kept, middle_sums = middle_back(
        core, residual, grad_normed_two, attended, out_gate, cotangent, output_experts, second_gain
    )
    grad_heads = trade(grad_attended)
    mix_got = swap(mix_sent, "pos", 1)
    down = share([down_kept, down_got], seg_size)
    up = share([up_kept, up_got], seg_size)
    mix = share([mix_kept, mix_got], seg_size)
    cube = seg_size * LANES == D and lax.axis_size("pos") == 4
    if cube:
        down, up = together([(down, "seg", 1), (up, "seg", 0)])
    else:
        down, up = down.seg(1), up.seg(0)

    grads, grad_rel, part_sums = attend_back(
        probs, grad_heads, qk, values, positions, head_content, head_position, score_scale
    )
    grads = trade(grads)
    part_sums, hidden = lax.optimization_barrier((part_sums, hidden))
    block_output = feed(hidden, down_projection_weight, residual, contract_bias)
    part_sums, block_output, down.addends, up.addends, mix.addends = lax.optimization_barrier(
        (part_sums, block_output, down.addends, up.addends, mix.addends)
    )
    if cube:
        down, up, mix = together([(down, "seg", 0), (up, "seg", 1), (mix, "pos", 1)])
    else:
        down, up, mix = down.seg(0), up.seg(1), mix.pos(1, 1)

    position_grad = to_low(mm("scn,nd->cd", grad_rel, table_low))
    position_grad = jnp.transpose(position_grad.reshape(DH, D // LANES, LANES), (1, 0, 2))
    head_hot = (jnp.arange(HEADS) == pos_index).astype(jnp.float32)[:, None]
    bias_sums = jnp.sum(part_sums, axis=0)
    biases = [(head_hot * bias_sums[k]).reshape(seg_size, -1) for k in range(2)]
    bias_row = jnp.concatenate(biases, axis=1)
    bias_row = jnp.pad(bias_row, ((0, 0), (0, D // seg_size - bias_row.shape[1])))
    extra = vector_rows(
        [middle_sums[0], middle_sums[1], middle_sums[2], expand_bias_grad[0], bias_row], seg_size
    )

    if cube:
        late, all_grads = lean(
            memory_rows,
            block_input,
            first_gain,
            first_shift,
            grads,
            grad_out_logit,
            value_gate,
            value_all,
            extra,
        )
    else:
        input_grad, late = back(
            memory_rows,
            block_input,
            first_gain,
            first_shift,
            grads,
            grad_out_logit,
            value_gate,
            value_all,
            value_experts.T,
            key_weight.T,
            query_weight.T,
            value_router.T,
            output_gate_matrix.T,
            grad_residual.reshape(seg_count, local_rows, width),
            extra,
        )
    late, position_grad, down.addends, up.addends, mix.addends = lax.optimization_barrier(
        (late, position_grad, down.addends, up.addends, mix.addends)
    )
    if cube:
        weights = (value_experts.T, key_weight.T, query_weight.T, value_router.T, output_gate_matrix.T)
        *quarters, vec, input_grad = finish(
            late,
            all_grads,
            weights,
            (memory_rows, block_input),
            grad_residual.reshape(seg_count, local_rows, width),
            first_gain,
            position_grad,
            down.addends,
            up.addends,
            mix.addends,
        )
        contract_weight_grad, expand_weight_grad, output_experts_grad, *rows_out = emit(quarters, vec, DH)
        experts_grad, keys_grad, queries_grad, positions_grad, value_grad, out_grad = rows_out[:6]
        vectors = rows_out[6:]
    else:
        late = Share([late], []).pos(0, 1).total()
        share_rows = late.shape[1] // 2
        one = Share([late[:, :share_rows]], []).pos(1, 1).total()
        piece_rows = one.shape[1]
        one = jnp.concatenate([one, position_grad], axis=1)
        one = Share([seg_blocks(one, seg_size)], axis_bits("seg")).rest().total()
        two = Share([seg_blocks(late[:, share_rows:], seg_size)], axis_bits("seg"))
        two = two.rest().pos(1, 0).total()
        tail = jnp.concatenate([one, two], axis=0)
        tail = to_wide(widen(widen(tail[None], 1, 0)[None], 0, 0))
        lanes = tail.shape[3]
        up = up.pos(1, 1).rest().total()
        expand_weight_grad = to_wide(widen(widen(up, 1, 1), 0, 1))
        down = down.pos(1, 1).rest().total()
        contract_weight_grad = to_wide(widen(widen(down, 1, 1), 0, 1))
        mix = mix.rest().total()
        output_experts_grad = to_wide(widen(widen(mix, 1, 1), 0, 1))
        parts = [tail[:, :, :piece_rows], tail[:, :, tail.shape[2] - piece_rows :]]
        main = jnp.concatenate([p.reshape(2, share_rows, lanes) for p in parts], axis=1).reshape(-1, lanes)
        heads = jnp.transpose(tail[:, :, piece_rows : tail.shape[2] - piece_rows], (1, 0, 2, 3))
        edges = (0,) + late_rows(DH)
        rows_out = [main[a:b] for a, b in zip(edges, edges[1:])] + [heads.reshape(HEADS * DH, lanes)]
        experts_grad, keys_grad, queries_grad, value_rows, out_rows, positions_grad = rows_out
        value_grad, out_grad = value_rows[:slots], out_rows[:slots]
        extra = out_rows[slots : slots + 8]
        piece = DH * HEADS // seg_size
        vectors = [value_rows[slots], value_rows[slots + 1], extra[0], extra[1], extra[2]]
        vectors += [extra[3:7].reshape(-1), extra[7, :piece], extra[7, piece : 2 * piece]]
    return (
        block_output.reshape(block_input.shape),
        input_grad,
        vectors[0],
        vectors[1],
        queries_grad.T,
        keys_grad.T,
        positions_grad.T,
        experts_grad.T,
        value_grad.T,
        vectors[6],
        vectors[7],
        output_experts_grad,
        out_grad.T,
        vectors[2],
        vectors[3],
        expand_weight_grad,
        vectors[5],
        contract_weight_grad,
        vectors[4],
    )


def solution(mesh):
    rows = P("seg", "pos", None)
    whole = P()
    placed = (
        rows,
        rows,
        P("seg"),
        P("seg", None, "pos", None, None),
        P("seg", "pos", None, None),
    )
    placed += (whole,) * 17 + (rows,)
    shares = [P("seg")] * 17
    for index in (2, 3, 4, 5, 6, 9, 10, 13, 15):
        shares[index] = P("seg", None)
    return jax.shard_map(
        local,
        mesh=mesh,
        in_specs=placed,
        out_specs=(rows, rows) + tuple(shares),
        check_vma=False,
    )
```

```python
import functools

import jax
import jax.numpy as jnp
from jax import lax
from jax.experimental import pallas as pl
from jax.experimental.pallas import tpu as pltpu
from jax.sharding import PartitionSpec as P

D = 1024
HEADS = 4
DH = 112
EXPERTS = 5
SEQ = 1024
norm_eps = 1e-05

NEG = -1e30
LANES = 128


def nn(left, right):
    return lax.dot_general(left, right, (((1,), (0,)), ((), ())), preferred_element_type=jnp.float32)


def nt(left, right):
    return lax.dot_general(left, right, (((1,), (1,)), ((), ())), preferred_element_type=jnp.float32)


def to_low(value):
    return value.astype(jnp.bfloat16)


def to_wide(value):
    return value.astype(jnp.float32)


def norm_parts(rows):
    center = rows - jnp.mean(rows, axis=1, keepdims=True)
    inv_std = lax.rsqrt(jnp.mean(center * center, axis=1, keepdims=True) + norm_eps)
    return center * inv_std, inv_std


def vector(value):
    return once(value.shape, lambda *_: (0,))


def once(shape, index_map):
    return pl.BlockSpec(shape, index_map, pipeline_mode=pl.Buffered(1))


def row(ref):
    return to_wide(ref[...]).reshape(1, -1)


def params(megabytes):
    return pltpu.CompilerParams(vmem_limit_bytes=megabytes << 20)


def project_kernel(
    mem_ref, blk_ref, gain_ref, shift_ref, wq_ref, wk_ref, gates_ref, pickv_ref, picko_ref,
    qk_ref, norm_ref, gatev_ref, gateo_ref,
):
    half = pl.program_id(1)
    rows = to_wide(jnp.where(half == 0, mem_ref[0], blk_ref[0]))
    unit, _ = norm_parts(rows)
    normed = to_low(unit * row(gain_ref) + row(shift_ref))
    norm_ref[0, 0] = normed
    turned = normed.T
    keys = to_low(nn(wk_ref[...], turned))
    dh = qk_ref.shape[3]
    logits = nn(gates_ref[...], turned)
    gatev_ref[0, 0] = jax.nn.sigmoid(logits[: pickv_ref.shape[2]]) * pickv_ref[0, 0]

    @pl.when(half == 0)
    def _():
        for h in range(qk_ref.shape[0]):
            qk_ref[h, 0, 1] = keys[h * dh : (h + 1) * dh]

    @pl.when(half == 1)
    def _():
        query = to_low(nn(wq_ref[...], turned))
        for h in range(qk_ref.shape[0]):
            qk_ref[h, 0, 0] = query[h * dh : (h + 1) * dh]
            qk_ref[h, 0, 2] = keys[h * dh : (h + 1) * dh]
        gateo_ref[0] = jax.nn.sigmoid(logits[logits.shape[0] // 2 :][: picko_ref.shape[1]]) * picko_ref[0]


def project(mem, blk, gain, shift, wqt, wkt, gates, pickv, picko):
    segs, rows, width = blk.shape
    inner = wqt.shape[0]
    slots = pickv.shape[2]
    low, f32 = jnp.bfloat16, jnp.float32
    dh = inner // HEADS
    flat = lambda s, r: (0, 0)
    row_spec = pl.BlockSpec((1, rows, width), lambda s, r: (s, 0, 0))
    return pl.pallas_call(
        project_kernel,
        grid=(segs, 2),
        in_specs=[
            row_spec,
            row_spec,
            vector(gain),
            vector(shift),
            once(wqt.shape, flat),
            once(wkt.shape, flat),
            once(gates.shape, flat),
            pl.BlockSpec((1, 1, slots, rows), lambda s, r: (s, r, 0, 0)),
            pl.BlockSpec((1, slots, rows), lambda s, r: (s, 0, 0)),
        ],
        out_specs=[
            pl.BlockSpec((HEADS, 1, 3, dh, rows), lambda s, r: (0, s, 0, 0, 0)),
            pl.BlockSpec((1, 1, rows, width), lambda s, r: (s, r, 0, 0)),
            pl.BlockSpec((1, 1, slots, rows), lambda s, r: (s, r, 0, 0)),
            pl.BlockSpec((1, slots, rows), lambda s, r: (s, 0, 0)),
        ],
        out_shape=[
            jax.ShapeDtypeStruct((HEADS, segs, 3, dh, rows), low),
            jax.ShapeDtypeStruct((segs, 2, rows, width), low),
            jax.ShapeDtypeStruct((segs, 2, slots, rows), f32),
            jax.ShapeDtypeStruct((segs, slots, rows), f32),
        ],
        compiler_params=params(60),
        cost_estimate=pl.CostEstimate(flops=3 * 10**9, bytes_accessed=8 * 10**6, transcendentals=0),
        name="project",
    )(mem, blk, gain, shift, wqt, wkt, gates, pickv, picko)


def experts_kernel(norm_ref, ve_ref, gate_ref, v_ref, all_ref):
    turned = norm_ref[0, 0].T
    heads, dh = v_ref.shape[0], v_ref.shape[3]
    group = nn(ve_ref[...], turned)
    all_ref[0, 0] = to_low(group)
    for h in range(heads):
        total = jnp.zeros((dh, turned.shape[1]), jnp.float32)
        for e in range(EXPERTS):
            slot = h * EXPERTS + e
            total = total + gate_ref[0, 0, slot : slot + 1] * group[slot * dh : (slot + 1) * dh]
        v_ref[h, 0, 0] = to_low(total)


def experts(normed, vet, gate):
    segs, _, rows, width = normed.shape
    inner = vet.shape[0]
    slots = gate.shape[2]
    dh = inner // (HEADS * EXPERTS)
    low = jnp.bfloat16
    return pl.pallas_call(
        experts_kernel,
        grid=(segs, 2),
        in_specs=[
            pl.BlockSpec((1, 1, rows, width), lambda s, r: (s, r, 0, 0)),
            once(vet.shape, lambda s, r: (0, 0)),
            pl.BlockSpec((1, 1, slots, rows), lambda s, r: (s, r, 0, 0)),
        ],
        out_specs=[
            pl.BlockSpec((HEADS, 1, 1, dh, rows), lambda s, r: (0, s, r, 0, 0)),
            pl.BlockSpec((1, 1, inner, rows), lambda s, r: (s, r, 0, 0)),
        ],
        out_shape=[
            jax.ShapeDtypeStruct((HEADS, segs, 2, dh, rows), low),
            jax.ShapeDtypeStruct((segs, 2, inner, rows), low),
        ],
        compiler_params=params(48),
        cost_estimate=pl.CostEstimate(flops=5 * 10**9, bytes_accessed=12 * 10**6, transcendentals=0),
        name="experts",
    )(normed, vet, gate)


def column(ref):
    value = row(ref)
    return jnp.broadcast_to(value, (LANES, value.shape[1])).T[:, :1]


def biased(query, bias, scale):
    return to_low((to_wide(query) + bias) * scale)


def score_kernel(len_ref, qk_ref, pos_ref, cb_ref, pb_ref, p_ref, kt_s, *, tiles, block, chunk, scale):
    seg = pl.program_id(0)
    start = tiles * block - len_ref[seg]
    for half in range(2):
        for t in range(tiles):
            c0 = (half * tiles + t) * block
            kt_s[:, c0 : c0 + block] = qk_ref[t, 0, 1 + half]
    mem = tiles * block
    cb, pb = column(cb_ref), column(pb_ref)
    for t in range(tiles):
        w = mem + (t + 1) * block
        base = (tiles - 1 - t) * block
        col = lax.broadcasted_iota(jnp.int32, (1, w), 1)
        bias = jnp.where(col >= start, 0.0, NEG)
        content = biased(qk_ref[t, 0, 0], cb, scale).T
        position = biased(qk_ref[t, 0, 0], pb, scale).T
        for r0 in range(0, block, chunk):
            raw = nn(position[r0 : r0 + chunk], pos_ref[:, base:])
            rel = pltpu.roll(raw, w - (block - 1) + r0, 1, stride=1, stride_axis=0)
            s = nn(content[r0 : r0 + chunk], kt_s[:, :w]) + rel
            row = lax.broadcasted_iota(jnp.int32, (chunk, w), 0) + (mem + t * block + r0)
            col_wide = lax.broadcasted_iota(jnp.int32, (chunk, w), 1)
            s = jnp.where(col_wide <= row, s + bias, NEG)
            e = jnp.exp(s - jnp.max(s, axis=1, keepdims=True))
            p = e * (1.0 / jnp.sum(e, axis=1, keepdims=True))
            p_ref[0, t * block + r0 : t * block + r0 + chunk, :w] = to_low(p)


def score(lengths, qk, post, cbias, pbias, scale):
    tiles, segs, _, dh, block = qk.shape
    keys = 2 * tiles * block
    return pl.pallas_call(
        functools.partial(score_kernel, tiles=tiles, block=block, chunk=64, scale=scale),
        grid_spec=pltpu.PrefetchScalarGridSpec(
            num_scalar_prefetch=1,
            grid=(segs,),
            in_specs=[
                pl.BlockSpec((tiles, 1, 3, dh, block), lambda s, _: (0, s, 0, 0, 0)),
                pl.BlockSpec((dh, keys), lambda s, _: (0, 0)),
                vector(cbias),
                vector(pbias),
            ],
            out_specs=pl.BlockSpec((1, tiles * block, keys), lambda s, _: (s, 0, 0)),
            scratch_shapes=[pltpu.VMEM((dh, keys), jnp.bfloat16)],
        ),
        out_shape=jax.ShapeDtypeStruct((segs, tiles * block, keys), jnp.bfloat16),
        compiler_params=params(48),
        cost_estimate=pl.CostEstimate(flops=12 * 10**9, bytes_accessed=10 * 10**6, transcendentals=4 * 10**6),
        name="score",
    )(lengths, qk, post, cbias, pbias)


def attend_kernel(p_ref, v_ref, out_ref, v_s, buf, sent, came, near, *, tiles, block):
    seg = pl.program_id(0)
    segs = buf.shape[1]
    me = lax.axis_index("pos")
    peers = [(me + d) % tiles for d in range(1, tiles)]

    @pl.when(seg == 0)
    def _():
        barrier = pltpu.get_barrier_semaphore()
        for peer in peers:
            pl.semaphore_signal(barrier, inc=1, device_id={"pos": peer}, device_id_type=pl.DeviceIdType.MESH)

    for half in range(2):
        for t in range(tiles):
            c0 = (half * tiles + t) * block
            v_s[c0 : c0 + block, :] = v_ref[t, 0, half].T
    for t in range(tiles):
        w = tiles * block + (t + 1) * block
        out = nn(p_ref[0, t * block : (t + 1) * block, :w], v_s[:w, :])
        buf[t, seg] = to_low(out).T

    @pl.when(seg == 0)
    def _():
        pl.semaphore_wait(pltpu.get_barrier_semaphore(), tiles - 1)

    def moves(s):
        away = [
            pltpu.make_async_remote_copy(
                src_ref=buf.at[peer, s],
                dst_ref=out_ref.at[me, s],
                send_sem=sent.at[d, s],
                recv_sem=came.at[d, s],
                device_id={"pos": peer},
                device_id_type=pl.DeviceIdType.MESH,
            )
            for d, peer in enumerate(peers)
        ]
        return away, pltpu.make_async_copy(buf.at[me, s], out_ref.at[me, s], near.at[s])

    away, here = moves(seg)
    for copy in away:
        copy.start()
    here.start()

    @pl.when(seg == segs - 1)
    def _():
        for s in range(segs):
            away, here = moves(s)
            for copy in away:
                copy.wait()
            here.wait()


def attend(p, v):
    tiles, segs, _, dh, block = v.shape
    keys = 2 * tiles * block
    return pl.pallas_call(
        functools.partial(attend_kernel, tiles=tiles, block=block),
        grid=(segs,),
        in_specs=[
            pl.BlockSpec((1, tiles * block, keys), lambda s: (s, 0, 0)),
            pl.BlockSpec((tiles, 1, 2, dh, block), lambda s: (0, s, 0, 0, 0)),
        ],
        out_specs=pl.BlockSpec(memory_space=pl.ANY),
        out_shape=jax.ShapeDtypeStruct((tiles, segs, dh, block), jnp.bfloat16),
        scratch_shapes=[
            pltpu.VMEM((keys, dh), jnp.bfloat16),
            pltpu.VMEM((tiles, segs, dh, block), jnp.bfloat16),
            pltpu.SemaphoreType.DMA((tiles - 1, segs)),
            pltpu.SemaphoreType.DMA((tiles - 1, segs)),
            pltpu.SemaphoreType.DMA((segs,)),
        ],
        compiler_params=pltpu.CompilerParams(vmem_limit_bytes=48 << 20, collective_id=1, has_side_effects=True),
        cost_estimate=pl.CostEstimate(flops=5 * 10**9, bytes_accessed=9 * 10**6, transcendentals=0),
        name="attend",
    )(p, v)


def attend_back_kernel(
    p_ref, g_ref, qk_ref, v_ref, pos_ref, cb_ref, pb_ref, d_ref, dpos_ref, sums_ref,
    k_s, vt_s, posr_s, dkt, dvt, dpt, ds_s, dr_s, *, tiles, block, chunk, scale,
):
    seg = pl.program_id(0)
    for half in range(2):
        for t in range(tiles):
            c0 = (half * tiles + t) * block
            k_s[c0 : c0 + block, :] = qk_ref[t, 0, 1 + half].T
            vt_s[:, c0 : c0 + block] = v_ref[t, 0, half]

    @pl.when(seg == 0)
    def _():
        posr_s[...] = pos_ref[...].T

    dkt[...] = jnp.zeros_like(dkt)
    dvt[...] = jnp.zeros_like(dvt)
    dpt[...] = jnp.zeros_like(dpt)
    mem = tiles * block
    dh = v_ref.shape[3]
    flip = (
        lax.broadcasted_iota(jnp.int32, (block, block), 0) + lax.broadcasted_iota(jnp.int32, (block, block), 1)
        == block - 1
    )
    flip_wide = jnp.where(flip, 1.0, 0.0)
    flip_low = to_low(flip_wide)
    cb, pb = column(cb_ref), column(pb_ref)
    content_sum = jnp.zeros((1, dh), jnp.float32)
    position_sum = jnp.zeros((1, dh), jnp.float32)
    for t in range(tiles):
        w = mem + (t + 1) * block
        base = (tiles - 1 - t) * block
        gt = g_ref[t, 0]
        g = gt.T
        for r0 in range(0, block, chunk):
            p = to_wide(p_ref[0, t * block + r0 : t * block + r0 + chunk, :w])
            prod = p * nn(g[r0 : r0 + chunk], vt_s[:, :w])
            delta = jnp.sum(prod, axis=1, keepdims=True)
            ds_s[r0 : r0 + chunk, :w] = to_low(prod - p * delta)
        ds = ds_s[:, :w]
        for r0 in range(0, block, chunk):
            turned = nn(flip_low[r0 : r0 + chunk], ds)
            dr_s[r0 : r0 + chunk, :w] = to_low(pltpu.roll(turned, r0, 1, stride=1, stride_axis=0))
        dr = dr_s[:, :w]
        dvt[:, :w] += nn(gt, p_ref[0, t * block : (t + 1) * block, :w])
        dkt[:, :w] += nn(biased(qk_ref[t, 0, 0], cb, scale), ds)
        position = to_low(nn(biased(qk_ref[t, 0, 0], pb, scale), flip_low))
        dpt[:, base:] += nn(position, dr)
        dc = nn(ds, k_s[:w, :])
        dp = nn(dr, posr_s[base:, :])
        content_sum = content_sum + jnp.sum(dc, axis=0, keepdims=True)
        position_sum = position_sum + jnp.sum(dp, axis=0, keepdims=True)
        dp = lax.dot_general(
            flip_wide,
            dp,
            (((1,), (0,)), ((), ())),
            precision=lax.Precision.HIGHEST,
            preferred_element_type=jnp.float32,
        )
        d_ref[t, 0, 0] = to_low((dc + dp) * scale).T
    sums_ref[0, 0:1] = content_sum * scale
    sums_ref[0, 1:2] = position_sum * scale
    dpos_ref[0] = to_low(dpt[...])
    for half in range(2):
        for t in range(tiles):
            c0 = (half * tiles + t) * block
            d_ref[t, 0, 1 + half] = to_low(dkt[:, c0 : c0 + block])
            d_ref[t, 0, 3 + half] = to_low(dvt[:, c0 : c0 + block])


def attend_back(p, g, qk, v, post, cbias, pbias, scale):
    tiles, segs, dh, block = g.shape
    keys = 2 * tiles * block
    low, f32 = jnp.bfloat16, jnp.float32

    def spec(parts):
        return pl.BlockSpec((tiles, 1, parts, dh, block), lambda s: (0, s, 0, 0, 0))

    return pl.pallas_call(
        functools.partial(attend_back_kernel, tiles=tiles, block=block, chunk=64, scale=scale),
        grid=(segs,),
        in_specs=[
            pl.BlockSpec((1, tiles * block, keys), lambda s: (s, 0, 0)),
            pl.BlockSpec((tiles, 1, dh, block), lambda s: (0, s, 0, 0)),
            spec(3),
            spec(2),
            pl.BlockSpec((dh, keys), lambda s: (0, 0)),
            vector(cbias),
            vector(pbias),
        ],
        out_specs=[
            spec(5),
            pl.BlockSpec((1, dh, keys), lambda s: (s, 0, 0)),
            pl.BlockSpec((1, 2, dh), lambda s: (s, 0, 0)),
        ],
        out_shape=[
            jax.ShapeDtypeStruct((tiles, segs, 5, dh, block), low),
            jax.ShapeDtypeStruct((segs, dh, keys), low),
            jax.ShapeDtypeStruct((segs, 2, dh), f32),
        ],
        scratch_shapes=[
            pltpu.VMEM((keys, dh), low),
            pltpu.VMEM((dh, keys), low),
            pltpu.VMEM((keys, dh), low),
            pltpu.VMEM((dh, keys), f32),
            pltpu.VMEM((dh, keys), f32),
            pltpu.VMEM((dh, keys), f32),
            pltpu.VMEM((block, keys), low),
            pltpu.VMEM((block, keys), low),
        ],
        compiler_params=params(56),
        cost_estimate=pl.CostEstimate(flops=25 * 10**9, bytes_accessed=14 * 10**6, transcendentals=0),
        name="attend_back",
    )(p, g, qk, v, post, cbias, pbias)


def mix_rows(mixed, att_ref, gate_ref):
    heads, segs, dh, rows = att_ref.shape
    for h in range(heads):
        for s in range(segs):
            att = to_wide(att_ref[h, s])
            for e in range(EXPERTS):
                slot = h * EXPERTS + e
                mixed[slot * dh : (slot + 1) * dh, s * rows : (s + 1) * rows] = to_low(
                    gate_ref[s, slot : slot + 1] * att
                )


def middle_kernel(
    core_ref, att_ref, gate_ref, x_ref, g_ref, oe_ref, gain_ref, shift_ref, wu_ref, bu_ref, wd_ref,
    hid_ref, res, gn, wds_ref, wdk_ref, wus_ref, wuk_ref, bu_out, mixed, n2, n2t, *, chunk,
):
    step = pl.program_id(0)
    steps = pl.num_programs(0)
    total, width = x_ref.shape
    half = width // 2
    mine = pl.multiple_of(core_ref[0] * half, half)
    other = pl.multiple_of((1 - core_ref[0]) * half, half)
    count = total // chunk

    @pl.when(step == 0)
    def _():
        mix_rows(mixed, att_ref, gate_ref)
        res[...] = to_wide(x_ref[...]) + nn(mixed[...].T, oe_ref[...])

        @pl.loop(0, count)
        def _(i):
            at = pl.ds(pl.multiple_of(i * chunk, chunk), chunk)
            unit, _ = norm_parts(res[at, :])
            n2[at, :] = to_low(unit * row(gain_ref) + row(shift_ref))

        n2t[...] = n2[...].T
        gn[...] = jnp.zeros_like(gn)

    wu = wu_ref[...]
    wd = wd_ref[...]
    v = nn(n2[...], wu) + to_wide(bu_ref[...])
    root = 0.7978845608028654
    square = v * v
    tanh = jnp.tanh(root * (v + 0.044715 * (square * v)))
    plus = 0.5 * (1.0 + tanh)
    hidden = to_low(v * plus)
    slope = plus + 0.5 * v * (1.0 - tanh * tanh) * (root * (1.0 + 0.134145 * square))
    gp = nt(g_ref[...], wd) * slope
    gp_low = to_low(gp)
    bu_out[...] = jnp.sum(to_wide(gp_low), axis=0, keepdims=True)
    hid_ref[...] = hidden
    gn[...] += nt(gp_low, wu)
    wu_grad = to_low(nn(n2t[...], gp_low))

    @pl.when(step < steps // 2)
    def _():
        wus_ref[...] = wu_grad

    @pl.when(step >= steps // 2)
    def _():
        wuk_ref[...] = wu_grad

    turned = hidden.T
    wds_ref[...] = to_low(nn(turned, g_ref[:, pl.ds(other, half)]))
    wdk_ref[...] = to_low(nn(turned, g_ref[:, pl.ds(mine, half)]))


def middle(core, att, gate, x, g, oe, gain, shift, wu, bu, wd, fc=512):
    heads, segs, dh, rows = att.shape
    total, width = x.shape
    ff = wu.shape[1]
    steps = ff // fc
    mid = steps // 2
    half = width // 2
    slots = gate.shape[1]
    inner = oe.shape[0]
    low, f32 = jnp.bfloat16, jnp.float32

    def fix(*shape):
        return pl.BlockSpec(shape, lambda i, c: (0,) * len(shape))

    def keep(*shape):
        return once(shape, lambda i, c: (0,) * len(shape))

    def unit(i, c):
        return (i + mid * (1 - c[0])) % steps

    return pl.pallas_call(
        functools.partial(middle_kernel, chunk=64),
        grid_spec=pltpu.PrefetchScalarGridSpec(
            num_scalar_prefetch=1,
            grid=(steps,),
            in_specs=[
                keep(heads, segs, dh, rows),
                keep(segs, slots, rows),
                keep(total, width),
                keep(total, width),
                keep(inner, width),
                vector(gain),
                vector(shift),
                pl.BlockSpec((width, fc), lambda i, c: (0, unit(i, c))),
                pl.BlockSpec((1, fc), lambda i, c: (0, unit(i, c))),
                pl.BlockSpec((fc, width), lambda i, c: (unit(i, c), 0)),
            ],
            out_specs=[
                pl.BlockSpec((total, fc), lambda i, c: (0, unit(i, c))),
                fix(total, width),
                fix(total, width),
                pl.BlockSpec((fc, half), lambda i, c: (unit(i, c), 0)),
                pl.BlockSpec((fc, half), lambda i, c: (unit(i, c), 0)),
                pl.BlockSpec((width, fc), lambda i, c: (0, jnp.minimum(i, mid - 1))),
                pl.BlockSpec((width, fc), lambda i, c: (0, jnp.maximum(i - mid, 0))),
                pl.BlockSpec((1, fc), lambda i, c: (0, unit(i, c))),
            ],
            scratch_shapes=[
                pltpu.VMEM((inner, total), low),
                pltpu.VMEM((total, width), low),
                pltpu.VMEM((width, total), low),
            ],
        ),
        out_shape=[
            jax.ShapeDtypeStruct((total, ff), low),
            jax.ShapeDtypeStruct((total, width), f32),
            jax.ShapeDtypeStruct((total, width), f32),
            jax.ShapeDtypeStruct((ff, half), low),
            jax.ShapeDtypeStruct((ff, half), low),
            jax.ShapeDtypeStruct((width, ff // 2), low),
            jax.ShapeDtypeStruct((width, ff // 2), low),
            jax.ShapeDtypeStruct((1, ff), f32),
        ],
        compiler_params=params(60),
        cost_estimate=pl.CostEstimate(flops=28 * 10**9, bytes_accessed=40 * 10**6, transcendentals=2 * 10**6),
        name="middle",
    )(core, att, gate, x, g, oe, gain, shift, wu, bu, wd)


def middle_back_kernel(
    core_ref, res, gn, att_ref, gate_ref, g_ref, oe_ref, gain_ref,
    gres_ref, gatt_ref, glog_ref, oes_ref, oek_ref, vec_ref, mixed, low_grad, turned, *, chunk,
):
    heads, segs, dh, rows = att_ref.shape
    total, width = g_ref.shape
    half = width // 2
    mine = pl.multiple_of(core_ref[0] * half, half)
    other = pl.multiple_of((1 - core_ref[0]) * half, half)
    mix_rows(mixed, att_ref, gate_ref)
    zero = jnp.zeros((1, width), jnp.float32)

    def rows_back(i, sums):
        at = pl.ds(pl.multiple_of(i * chunk, chunk), chunk)
        unit, inv_std = norm_parts(res[at, :])
        grad = gn[at, :]
        g = to_wide(g_ref[at, :])
        q = grad * row(gain_ref)
        back = q - jnp.mean(q, axis=1, keepdims=True) - unit * jnp.mean(q * unit, axis=1, keepdims=True)
        out = g + inv_std * back
        gres_ref[at, :] = out
        low_grad[at, :] = to_low(out)
        return (
            sums[0] + jnp.sum(grad * unit, axis=0, keepdims=True),
            sums[1] + jnp.sum(grad, axis=0, keepdims=True),
            sums[2] + jnp.sum(g, axis=0, keepdims=True),
        )

    sums = lax.fori_loop(0, total // chunk, rows_back, (zero, zero, zero))
    for k in range(3):
        vec_ref[k : k + 1] = sums[k]
    turned[...] = low_grad[...].T
    for h in range(heads):
        group = nn(oe_ref[h * EXPERTS * dh : (h + 1) * EXPERTS * dh], turned[...])
        for s in range(segs):
            att = to_wide(att_ref[h, s])
            grad = jnp.zeros((dh, rows), jnp.float32)
            for e in range(EXPERTS):
                slot = h * EXPERTS + e
                part = group[e * dh : (e + 1) * dh, s * rows : (s + 1) * rows]
                gate = gate_ref[s, slot : slot + 1]
                grad = grad + gate * part
                logit = jnp.sum(part * att, axis=0, keepdims=True) * (gate * (1.0 - gate))
                glog_ref[s, slot : slot + 1] = logit
            gatt_ref[h, s] = to_low(grad)
    oes_ref[...] = to_low(nn(mixed[...], low_grad[:, pl.ds(other, half)]))
    oek_ref[...] = to_low(nn(mixed[...], low_grad[:, pl.ds(mine, half)]))


def middle_back(core, res, gn, att, gate, g, oe, gain):
    inner, width = oe.shape
    total = g.shape[0]
    low, f32 = jnp.bfloat16, jnp.float32
    vmem = pl.BlockSpec(memory_space=pltpu.VMEM)
    return pl.pallas_call(
        functools.partial(middle_back_kernel, chunk=64),
        in_specs=[pl.BlockSpec(memory_space=pltpu.SMEM)] + [vmem] * 7,
        out_specs=[vmem] * 6,
        out_shape=[
            jax.ShapeDtypeStruct((total, width), f32),
            jax.ShapeDtypeStruct(att.shape, low),
            jax.ShapeDtypeStruct(gate.shape, f32),
            jax.ShapeDtypeStruct((inner, width // 2), low),
            jax.ShapeDtypeStruct((inner, width // 2), low),
            jax.ShapeDtypeStruct((3, width), f32),
        ],
        scratch_shapes=[
            pltpu.VMEM((inner, total), low),
            pltpu.VMEM((total, width), low),
            pltpu.VMEM((width, total), low),
        ],
        compiler_params=params(60),
        cost_estimate=pl.CostEstimate(flops=5 * 10**9, bytes_accessed=20 * 10**6, transcendentals=0),
        name="middle_back",
    )(core, res, gn, att, gate, g, oe, gain)


def feed_kernel(hid_ref, wd_ref, res_ref, bd_ref, y_ref, acc):
    step = pl.program_id(0)
    part = nn(hid_ref[...], wd_ref[...])

    @pl.when(step == 0)
    def _():
        acc[...] = res_ref[...] + part

    @pl.when(step > 0)
    def _():
        acc[...] += part

    @pl.when(step == pl.num_programs(0) - 1)
    def _():
        y_ref[...] = to_low(acc[...] + row(bd_ref))


def feed(hidden, wd, res, bd, fc=1024):
    total, ff = hidden.shape
    width = wd.shape[1]
    return pl.pallas_call(
        feed_kernel,
        grid=(ff // fc,),
        in_specs=[
            pl.BlockSpec((total, fc), lambda i: (0, i)),
            pl.BlockSpec((fc, width), lambda i: (i, 0)),
            once((total, width), lambda i: (0, 0)),
            vector(bd),
        ],
        out_specs=pl.BlockSpec((total, width), lambda i: (0, 0)),
        out_shape=jax.ShapeDtypeStruct((total, width), jnp.bfloat16),
        scratch_shapes=[pltpu.VMEM((total, width), jnp.float32)],
        compiler_params=params(60),
        cost_estimate=pl.CostEstimate(flops=1000, bytes_accessed=1000, transcendentals=0),
        name="feed",
    )(hidden, wd, res, bd)


def late_rows(dh):
    first = HEADS * EXPERTS * dh
    second = first + HEADS * dh
    third = second + HEADS * dh
    return first, second, third, third + 32, third + 64


def back_kernel(
    mem_ref, blk_ref, gain_ref, shift_ref, d_ref, glog_ref, gate_ref, all_ref, ve_ref, wk_ref, wq_ref,
    rv_ref, ro_ref, gres_ref, extra_ref, xg_ref, late_ref, vec, gt, every_gt, every_norm,
):
    half = pl.program_id(1)
    first_step = (pl.program_id(0) == 0) & (half == 0)
    heads, dh = d_ref.shape[0], d_ref.shape[3]
    slots = gate_ref.shape[2]
    at_key, at_query, at_value, at_out, end = late_rows(dh)

    @pl.when(first_step)
    def _():
        gt[at_value:end] = jnp.zeros((end - at_value, gt.shape[1]), jnp.bfloat16)
        vec[...] = jnp.zeros_like(vec)

    for h in range(heads):
        gv = to_wide(jnp.where(half == 0, d_ref[h, 0, 3], d_ref[h, 0, 4]))
        for e in range(EXPERTS):
            slot = h * EXPERTS + e
            gate = gate_ref[0, 0, slot : slot + 1]
            gt[slot * dh : (slot + 1) * dh] = to_low(gate * gv)
            logit = jnp.sum(to_wide(all_ref[0, 0, slot * dh : (slot + 1) * dh]) * gv, axis=0, keepdims=True)
            gt[at_value + slot : at_value + slot + 1] = to_low(logit * (gate * (1.0 - gate)))

    @pl.when(half == 0)
    def _():
        for h in range(heads):
            gt[at_key + h * dh : at_key + (h + 1) * dh] = d_ref[h, 0, 1]
        gt[at_query:at_value] = jnp.zeros((at_value - at_query, gt.shape[1]), jnp.bfloat16)
        gt[at_out : at_out + slots] = jnp.zeros((slots, gt.shape[1]), jnp.bfloat16)

    @pl.when(half == 1)
    def _():
        for h in range(heads):
            gt[at_key + h * dh : at_key + (h + 1) * dh] = d_ref[h, 0, 2]
            gt[at_query + h * dh : at_query + (h + 1) * dh] = d_ref[h, 0, 0]
        gt[at_out : at_out + slots] = to_low(glog_ref[0])

    rows = to_wide(jnp.where(half == 0, mem_ref[0], blk_ref[0]))
    unit, inv_std = norm_parts(rows)
    gain = row(gain_ref)
    normed = to_low(unit * gain + row(shift_ref))
    count = gt.shape[1]
    at = pl.multiple_of((pl.program_id(0) * 2 + half) * count, count)
    every_gt[:, pl.ds(at, count)] = gt[...]
    every_norm[pl.ds(at, count), :] = normed
    grad = nn(gt[:at_key].T, ve_ref[...]) + nn(gt[at_key:at_query].T, wk_ref[...])
    grad = grad + nn(gt[at_query:at_value].T, wq_ref[...])
    grad = grad + nn(gt[at_value : at_value + slots].T, rv_ref[...])
    grad = grad + nn(gt[at_out : at_out + slots].T, ro_ref[...])
    vec[0:1] += jnp.sum(grad * unit, axis=0, keepdims=True)
    vec[1:2] += jnp.sum(grad, axis=0, keepdims=True)

    @pl.when(half == 1)
    def _():
        q = grad * gain
        back = q - jnp.mean(q, axis=1, keepdims=True) - unit * jnp.mean(q * unit, axis=1, keepdims=True)
        xg_ref[0] = to_low(gres_ref[0] + inv_std * back)

    @pl.when((pl.program_id(0) == pl.num_programs(0) - 1) & (half == 1))
    def _():
        for k in range(0, late_ref.shape[0], 2):
            pair = to_low(nn(every_gt[...], every_norm[:, k * LANES : (k + 2) * LANES]))
            late_ref[k] = pair[:, :LANES]
            late_ref[k + 1] = pair[:, LANES:]
        for k in range(late_ref.shape[0]):
            both = vec[0:2, k * LANES : (k + 1) * LANES]
            late_ref[k, at_value + slots : at_value + slots + 2] = to_low(both)
            late_ref[k, at_out + slots : at_out + slots + 8] = to_low(extra_ref[k])


def back(mem, blk, gain, shift, grads, glog, gate, every, vet, wkt, wqt, rvt, rot, gres, extra):
    segs, rows, width = blk.shape
    heads, _, _, dh, _ = grads.shape
    slots = gate.shape[2]
    end = late_rows(dh)[-1]
    low, f32 = jnp.bfloat16, jnp.float32
    row_spec = pl.BlockSpec((1, rows, width), lambda s, r: (s, 0, 0))
    flat = lambda s, r: (0, 0)
    return pl.pallas_call(
        back_kernel,
        grid=(segs, 2),
        in_specs=[
            row_spec,
            row_spec,
            vector(gain),
            vector(shift),
            pl.BlockSpec((heads, 1, 5, dh, rows), lambda s, r: (0, s, 0, 0, 0)),
            pl.BlockSpec((1, slots, rows), lambda s, r: (s, 0, 0)),
            pl.BlockSpec((1, 1, slots, rows), lambda s, r: (s, r, 0, 0)),
            pl.BlockSpec((1, 1, every.shape[2], rows), lambda s, r: (s, r, 0, 0)),
            once(vet.shape, flat),
            once(wkt.shape, flat),
            once(wqt.shape, flat),
            once(rvt.shape, flat),
            once(rot.shape, flat),
            row_spec,
            once(extra.shape, lambda s, r: (0, 0, 0)),
        ],
        out_specs=[
            row_spec,
            pl.BlockSpec((width // LANES, end, LANES), lambda s, r: (0, 0, 0)),
        ],
        out_shape=[
            jax.ShapeDtypeStruct(blk.shape, low),
            jax.ShapeDtypeStruct((width // LANES, end, LANES), low),
        ],
        scratch_shapes=[
            pltpu.VMEM((8, width), f32),
            pltpu.VMEM((end, rows), low),
            pltpu.VMEM((end, 2 * segs * rows), low),
            pltpu.VMEM((2 * segs * rows, width), low),
        ],
        compiler_params=params(60),
        cost_estimate=pl.CostEstimate(flops=14 * 10**9, bytes_accessed=25 * 10**6, transcendentals=0),
        name="back",
    )(mem, blk, gain, shift, grads, glog, gate, every, vet, wkt, wqt, rvt, rot, gres, extra)


def lean_kernel(
    mem_ref, blk_ref, gain_ref, shift_ref, d_ref, glog_ref, gate_ref, all_ref, extra_ref, late_ref, gt, every_gt,
    every_norm,
):
    half = pl.program_id(1)
    first_step = (pl.program_id(0) == 0) & (half == 0)
    heads, dh = d_ref.shape[0], d_ref.shape[3]
    slots = gate_ref.shape[2]
    at_key, at_query, at_value, at_out, end = late_rows(dh)
    count = gt.shape[1]
    gt[at_value:end] = jnp.zeros((end - at_value, count), jnp.bfloat16)
    for h in range(heads):
        gv = to_wide(jnp.where(half == 0, d_ref[h, 0, 3], d_ref[h, 0, 4]))
        for e in range(EXPERTS):
            slot = h * EXPERTS + e
            gate = gate_ref[0, 0, slot : slot + 1]
            gt[slot * dh : (slot + 1) * dh] = to_low(gate * gv)
            logit = jnp.sum(to_wide(all_ref[0, 0, slot * dh : (slot + 1) * dh]) * gv, axis=0, keepdims=True)
            gt[at_value + slot : at_value + slot + 1] = to_low(logit * (gate * (1.0 - gate)))

    @pl.when(half == 0)
    def _():
        for h in range(heads):
            gt[at_key + h * dh : at_key + (h + 1) * dh] = d_ref[h, 0, 1]
        gt[at_query:at_value] = jnp.zeros((at_value - at_query, count), jnp.bfloat16)

    @pl.when(half == 1)
    def _():
        for h in range(heads):
            gt[at_key + h * dh : at_key + (h + 1) * dh] = d_ref[h, 0, 2]
            gt[at_query + h * dh : at_query + (h + 1) * dh] = d_ref[h, 0, 0]
        gt[at_out : at_out + slots] = to_low(glog_ref[0])

    unit, _ = norm_parts(to_wide(jnp.where(half == 0, mem_ref[0], blk_ref[0])))
    at = pl.multiple_of((pl.program_id(0) * 2 + half) * count, count)
    every_gt[:, pl.ds(at, count)] = gt[...]
    every_norm[pl.ds(at, count), :] = to_low(unit * row(gain_ref) + row(shift_ref))

    @pl.when((pl.program_id(0) == pl.num_programs(0) - 1) & (half == 1))
    def _():
        for k in range(0, late_ref.shape[0], 2):
            pair = to_low(nn(every_gt[...], every_norm[:, k * LANES : (k + 2) * LANES]))
            late_ref[k] = pair[:, :LANES]
            late_ref[k + 1] = pair[:, LANES:]
        for k in range(late_ref.shape[0]):
            late_ref[k, at_out + slots : at_out + slots + 8] = to_low(extra_ref[k])


def lean(mem, blk, gain, shift, grads, glog, gate, every, extra):
    segs, rows, width = blk.shape
    heads, _, _, dh, _ = grads.shape
    slots = gate.shape[2]
    end = late_rows(dh)[-1]
    low = jnp.bfloat16
    row_spec = pl.BlockSpec((1, rows, width), lambda s, r: (s, 0, 0))
    return pl.pallas_call(
        lean_kernel,
        grid=(segs, 2),
        in_specs=[
            row_spec,
            row_spec,
            vector(gain),
            vector(shift),
            pl.BlockSpec((heads, 1, 5, dh, rows), lambda s, r: (0, s, 0, 0, 0)),
            pl.BlockSpec((1, slots, rows), lambda s, r: (s, 0, 0)),
            pl.BlockSpec((1, 1, slots, rows), lambda s, r: (s, r, 0, 0)),
            pl.BlockSpec((1, 1, every.shape[2], rows), lambda s, r: (s, r, 0, 0)),
            once(extra.shape, lambda s, r: (0, 0, 0)),
        ],
        out_specs=[
            pl.BlockSpec((width // LANES, end, LANES), lambda s, r: (0, 0, 0)),
            pl.BlockSpec((end, rows), lambda s, r: (0, s * 2 + r)),
        ],
        out_shape=[
            jax.ShapeDtypeStruct((width // LANES, end, LANES), low),
            jax.ShapeDtypeStruct((end, 2 * segs * rows), low),
        ],
        scratch_shapes=[
            pltpu.VMEM((end, 2 * segs * rows), low),
            pltpu.VMEM((2 * segs * rows, width), low),
        ],
        compiler_params=params(60),
        cost_estimate=pl.CostEstimate(flops=7 * 10**9, bytes_accessed=25 * 10**6, transcendentals=0),
        name="lean",
    )(mem, blk, gain, shift, grads, glog, gate, every, extra)


def fold_kernel(bits_ref, *refs, counts):
    at = 0
    outs = sum(counts) * 2
    for k, count in enumerate(counts):
        for part in range(2):
            total = to_wide(refs[at][...])
            for extra in range(1, count):
                total = total + to_wide(refs[at + extra][...])
            refs[outs + 2 * k + part][...] = to_low(total).reshape(refs[outs + 2 * k + part].shape)
            at += count


def fold(items, bits):
    in_specs, arrays, out_specs, out_shape, counts = [], [], [], [], []
    steps = 4
    for k, (addends, dim) in enumerate(items):
        shape = addends[0].shape
        rows, cols = shape[-2:]
        lead = shape[:-2]
        if dim == "columns":
            left, width = lead, cols // 2
        else:
            left, width = lead[:dim] + lead[dim + 1 :], cols
        total = 1
        for size in left:
            total *= size
        group = min(total, steps)
        cut_rows = steps // group
        block_rows = rows // cut_rows
        span = total // group

        def where(i, c, side, k=k, dim=dim, left=left, lead=lead, span=span, cut_rows=cut_rows):
            half = c[k] if side else 1 - c[k]
            index = (i // cut_rows) * span
            coords = []
            for size in reversed(left):
                coords.append(index % size)
                index = index // size
            coords = coords[::-1]
            if dim == "columns":
                return tuple(coords) + (i % cut_rows, half)
            return tuple(coords[:dim]) + (half,) + tuple(coords[dim:]) + (i % cut_rows, 0)

        tail_axes, covered = [], 1
        for size in reversed(left):
            if covered < span:
                covered *= size
                tail_axes.append(size)
            else:
                tail_axes.append(1)
        tail_axes = tail_axes[::-1]
        assert covered == span
        if dim == "columns":
            block = tuple(tail_axes) + (block_rows, width)
        else:
            block = tuple(tail_axes[:dim]) + (1,) + tuple(tail_axes[dim:]) + (block_rows, cols)

        def spec_map(side, where=where, block=block):
            def index(i, c):
                coords = where(i, c, side)
                return tuple(x // b if n < len(block) - 2 else x for n, (x, b) in enumerate(zip(coords, block)))

            return index

        for side in range(2):
            for a in addends:
                arrays.append(a)
                in_specs.append(pl.BlockSpec(block, spec_map(side)))
        out_block = tuple(tail_axes) + (block_rows, width)

        def out_map(i, c, left=left, span=span, cut_rows=cut_rows, tail_axes=tail_axes):
            index = (i // cut_rows) * span
            coords = []
            for size in reversed(left):
                coords.append(index % size)
                index = index // size
            coords = coords[::-1]
            return tuple(x // b for x, b in zip(coords, tail_axes)) + (i % cut_rows, 0)

        for side in range(2):
            out_specs.append(pl.BlockSpec(out_block, out_map))
            out_shape.append(jax.ShapeDtypeStruct(tuple(left) + (rows, width), jnp.bfloat16))
        counts.append(len(addends))
    outs = pl.pallas_call(
        functools.partial(fold_kernel, counts=tuple(counts)),
        grid_spec=pltpu.PrefetchScalarGridSpec(
            num_scalar_prefetch=1, grid=(steps,), in_specs=in_specs, out_specs=out_specs
        ),
        out_shape=out_shape,
        compiler_params=params(48),
        cost_estimate=pl.CostEstimate(flops=10**7, bytes_accessed=30 * 10**6, transcendentals=0),
        name="fold",
    )(bits, *arrays)
    return [(outs[2 * k], outs[2 * k + 1]) for k in range(len(items))]


class Chain:
    def __init__(self, axes, stages, shape, halve):
        self.axes, self.stages, self.shape, self.halve = axes, stages, shape, halve

    def landing(self, extra=0):
        free, size, out = list(self.axes), list(self.shape), []
        for stage in self.stages:
            if stage in free:
                free.remove(stage)
            elif stage == "x":
                size[self.halve] //= 2
            elif stage != "c":
                break
            out.append((2,) * len(free) + tuple(size))
            if stage == "x":
                size[0] += extra
        return out


def plus(left, right):
    return to_low(to_wide(left) + to_wide(right))


LATE = ("L1", "L2", "L3")


def late_cut(share):
    return tuple(share // 50 * part for part in (13, 19, 18))


ORDER = (
    "L10 L20 L30 E0",
    "L21 L11 C0 B0",
    "O0 L22 L31 C1",
    "E1 L12 O1 L32",
    "B1 L13 L23 C2",
    "V0 O2 L33 C3",
    "E2 V1 L24 L14",
    "E3 V2 O3 L34",
    "L25 V3 O4 L15",
    "L26 V4 L35 L16",
    "L36",
)
STARTS = ("E", "C", "O")


def chains(c, e, o, share_rows):
    ends = ["GX", "GC"]
    return {
        "C": Chain(["w"], ["w", "x"] + ends, c, 1),
        "E": Chain(["w"], ["x", "w"] + ends, e, 1),
        "O": Chain(["w", "z", "y"], ["z", "y", "w"] + ends, o, 1),
    } | {
        name: Chain(["w", "z", "y"], ["c"] + list(stages) + ends, (rows, LANES), 0)
        for name, stages, rows in zip(LATE, ("xzyw", "yxwz", "yxzw"), late_cut(share_rows))
    }


def finish_kernel(
    late, gt_hbm, ve_hbm, wk_hbm, wq_hbm, mem_hbm, blk_hbm, gres_hbm, rv_ref, ro_ref, gain_ref, pos, c0, c1, e0, e1,
    o0, o1, outc, oute, outo, outl, outv, xg_ref, *scratch, table,
):
    def place(axis, bit):
        me = lax.axis_index(axis)
        mine = (me // bit) % 2
        return mine, {axis: me + bit * (1 - 2 * mine)}

    mine, who = {}, {}
    for name, axis, bit in (("c", "pos", 1), ("x", "pos", 2), ("y", "seg", 1), ("z", "seg", 2), ("w", "seg", 4)):
        mine[name], who[name] = place(axis, bit)
    barrier = pltpu.get_barrier_semaphore()
    for target in who.values():
        pl.semaphore_signal(barrier, inc=1, device_id=target, device_id_type=pl.DeviceIdType.MESH)
    pl.semaphore_wait(barrier, len(who))

    scratch = list(scratch)
    sent, came, near, loads = scratch[-4:]
    gt, ve, wk, wq, rows_in, gres, sums = scratch[-11:-4]
    vec = scratch[-19:-11]
    work = dict(zip(("C", "E", "O") + LATE + ("L1m",), scratch[:7]))
    landed, at = {}, 7
    for name, chain in table.items():
        stages = len(chain.landing())
        landed[name] = scratch[at : at + stages]
        at += stages
    both = {"C": (c0, c1), "E": (e0, e1), "O": (o0, o1)}
    lead_rows = pos.shape[3]
    late_half = table["L1"].shape[0] // 2
    outs = {"C": (outc, None), "E": (oute, None), "O": (outo, None)}
    first = 0
    for name in LATE:
        size = table[name].shape[0] // 2 + (lead_rows if name == "L1" else 0)
        outs[name] = (outl, (first, size))
        first += size
    started = {}
    copies = []

    def send(key, src, dst, target):
        copy = pltpu.make_async_remote_copy(
            src_ref=src,
            dst_ref=dst,
            send_sem=sent.at[len(copies)],
            recv_sem=came.at[len(copies)],
            device_id=who[target],
            device_id_type=pl.DeviceIdType.MESH,
        )
        copy.start()
        copies.append(copy)
        started[key] = copy

    free = {name: list(chain.axes) for name, chain in table.items()}
    span = {name: (None, chain.shape[chain.halve]) for name, chain in table.items()}

    def pieces(name, start, size):
        halve = table[name].halve
        if start is None:
            return (slice(None), slice(None))
        one = pl.ds(pl.multiple_of(start, 16 if halve == 0 else LANES), size)
        return (one, slice(None)) if halve == 0 else (slice(None), one)

    def part(name, axis, value):
        start, size = span[name]
        fixed = {a: mine[a] for a in table[name].axes if a not in free[name]}
        left = list(free[name])
        relative = None
        if axis == "x":
            size = size // 2
            relative = value * size
            start = relative if start is None else start + relative
        elif axis is not None:
            fixed[axis] = value
            left.remove(axis)
        return left, fixed, start, size, relative

    def total(name, stage, axis, value, store=None):
        left, fixed, start, size, relative = part(name, axis, value)
        chain = table[name]
        switch = name == "L1" and stage is not None and chain.stages[stage] == "x"
        buffer = work[name]

        def one(values):
            index = tuple(values[a] if a in values else fixed[a] for a in chain.axes)
            full = index + pieces(name, start, size)
            if stage is None:
                left_ref, right_ref = both[name]
                got = plus(left_ref[full], right_ref[full])
            else:
                lead = tuple(values[a] if a in values else fixed[a] for a in free[name])
                got = plus(buffer[full], landed[name][stage][lead + pieces(name, relative, size)])
            if store is not None:
                store(got)
            elif switch:
                work["L1m"][index + (slice(0, size), slice(None))] = got
                work["L1m"][index + (slice(size, None), slice(None))] = pos[index]
            else:
                buffer[full] = got

        count = 1 << len(left)
        if count == 1:
            one({})
        elif count == 2:
            for k in range(2):
                one({left[0]: k})
        else:

            @pl.loop(0, count)
            def _(i):
                one({a: (i // (1 << (len(left) - 1 - k))) % 2 for k, a in enumerate(left)})

    def advance(name, stage):
        chain = table[name]
        following = chain.stages[0 if stage is None else stage + 1]
        switch = name == "L1" and stage is not None and chain.stages[stage] == "x"
        number = 0 if stage is None else stage + 1
        out, rows = outs[name]
        place_out = (slice(None), slice(None)) if rows is None else (slice(rows[0], rows[0] + rows[1]), slice(None))
        if following == "GX":

            def store(got):
                out[(mine["c"], mine["x"]) + place_out] = got

            total(name, stage, None, None, store)
            at = out.at[(mine["c"], mine["x"]) + place_out]
            send((name, number), at, at, "x")
            return
        if following == "GC":
            at = out.at[(mine["c"], slice(None)) + place_out]
            send((name, number), at, at, "c")
            return
        other = 1 - mine[following]
        total(name, stage, following, other)
        if switch:
            left, fixed, _, _, _ = part(name, following, other)
            source = work["L1m"]
            index = tuple(slice(None) if a in left else fixed[a] for a in chain.axes) + (slice(None), slice(None))
        else:
            left, fixed, start, size, _ = part(name, following, other)
            source = work[name]
            index = tuple(slice(None) if a in left else fixed[a] for a in chain.axes) + pieces(name, start, size)
        send((name, number), source.at[index], landed[name][number], following)
        total(name, stage, following, mine[following])
        if switch:
            work["L1"] = work["L1m"]
            span["L1"] = (None, late_half + lead_rows)
        if following == "x":
            start, size = span[name]
            half = size // 2
            span[name] = (mine["x"] * half if start is None else start + mine["x"] * half, half)
        else:
            free[name].remove(following)

    share = sum(table[name].shape[0] for name in LATE)
    keep = {}
    first = 0
    for number, name in enumerate(LATE):
        size = table[name].shape[0]
        own = pl.multiple_of(mine["c"] * share + first, 16)
        theirs = pl.multiple_of((1 - mine["c"]) * share + first, 16)
        send((name, 0), late.at[:, :, :, pl.ds(theirs, size)], landed[name][0], "c")
        keep[name] = pltpu.make_async_copy(late.at[:, :, :, pl.ds(own, size)], work[name], near.at[number])
        keep[name].start()
        first += size
    for name in STARTS:
        advance(name, None)

    moves = [(gt_hbm, gt), (ve_hbm, ve), (wk_hbm, wk), (wq_hbm, wq), (gres_hbm, gres)]
    moves += [(mem_hbm, rows_in.at[:, 0]), (blk_hbm, rows_in.at[:, 1])]
    moves = [pltpu.make_async_copy(a, b, loads.at[k]) for k, (a, b) in enumerate(moves)]
    for move in moves:
        move.start()
    rows = rows_in.shape[2]
    slots = rv_ref.shape[0]
    at_key, at_query, at_value, at_out, _ = late_rows(pos.shape[3])

    def inputs(begin):
        @pl.loop(begin, begin + 2)
        def _(b):
            mine_gt = gt[:, pl.ds(pl.multiple_of(b * rows, rows), rows)]
            grad = nn(mine_gt[:at_key].T, ve[...]) + nn(mine_gt[at_key:at_query].T, wk[...])
            grad = grad + nn(mine_gt[at_query:at_value].T, wq[...])
            grad = grad + nn(mine_gt[at_value : at_value + slots].T, rv_ref[...])
            grad = grad + nn(mine_gt[at_out : at_out + slots].T, ro_ref[...])
            unit, inv_std = norm_parts(to_wide(rows_in[b // 2, b % 2]))
            sums[0:1] += jnp.sum(grad * unit, axis=0, keepdims=True)
            sums[1:2] += jnp.sum(grad, axis=0, keepdims=True)

            @pl.when(b % 2 == 1)
            def _():
                q = grad * row(gain_ref)
                back = q - jnp.mean(q, axis=1, keepdims=True) - unit * jnp.mean(q * unit, axis=1, keepdims=True)
                xg_ref[b // 2] = to_low(gres[b // 2] + inv_std * back)

    v0, v1, v2, vc, vx, vy, vz, vw = vec
    my, mz, mw = mine["y"], mine["z"], mine["w"]

    def vectors(stage):
        if stage < 0:
            for k in range(8):
                v0[k // 4, (k // 2) % 2, k % 2] = to_low(sums[:, k * LANES : (k + 1) * LANES])
            send(("V", 0), v0, vc, "c")
        elif stage == 0:
            v1[...] = plus(v0[...], vc[...])
            send(("V", 1), v1, vx, "x")
        elif stage == 1:
            v2[...] = plus(v1[...], vx[...])
            send(("V", 2), v2.at[:, :, 1 - my], vy, "y")
        elif stage == 2:
            for a in range(2):
                for b in range(2):
                    v2[a, b, my] = plus(v2[a, b, my], vy[a, b])
            send(("V", 3), v2.at[:, 1 - mz, my], vz, "z")
        elif stage == 3:
            for a in range(2):
                v2[a, mz, my] = plus(v2[a, mz, my], vz[a])
            send(("V", 4), v2.at[1 - mw, mz, my], vw, "w")
        else:
            outv[...] = to_wide(v2[mw, mz, my]) + to_wide(vw[...])

    for event in " ".join(ORDER).split():
        name, stage = event[:-1], int(event[-1])
        if name == "B":
            if stage == 0:
                for move in moves:
                    move.wait()
                sums[...] = jnp.zeros_like(sums)
            inputs(2 * stage)
            if stage == 1:
                vectors(-1)
            continue
        if name == "V":
            started[(name, stage)].wait_recv()
            vectors(stage)
            continue
        started[(name, stage)].wait_recv()
        if stage == 0 and name in keep:
            keep[name].wait()
        if stage + 1 < len(table[name].stages):
            advance(name, stage)
    for copy in copies:
        copy.wait_send()


def finish(late, gt, weights, rows, gres, gain, pos, c, e, o):
    low, f32 = jnp.bfloat16, jnp.float32
    cube = (2, 2, 2)
    share = late.shape[1] // 2
    table = chains(c[0].shape[1:], e[0].shape[1:], o[0].shape[3:], share)
    lead_rows = pos.shape[1]
    vmem = pl.BlockSpec(memory_space=pltpu.VMEM)
    hbm = pl.BlockSpec(memory_space=pl.ANY)
    shapes = [c[0].shape, e[0].shape, o[0].shape]
    shapes += [cube + table[name].shape for name in LATE]
    shapes += [cube + (table["L1"].shape[0] // 2 + lead_rows, LANES)]
    for name, chain in table.items():
        shapes += chain.landing(lead_rows if name == "L1" else 0)
    small = (16, LANES)
    shapes += [cube + small] * 5 + [(2, 2) + small, (2,) + small, small]
    segs, length, width = rows[0].shape
    shapes += [gt.shape] + [w.shape for w in weights[:3]] + [(segs, 2, length, width)]
    scratch = [pltpu.VMEM(shape, low) for shape in shapes]
    scratch += [pltpu.VMEM(gres.shape, f32), pltpu.VMEM((16, width), f32)]
    count = sum(len(chain.stages) for chain in table.values()) + 5
    scratch += [pltpu.SemaphoreType.DMA((count,)), pltpu.SemaphoreType.DMA((count,)), pltpu.SemaphoreType.DMA((3,))]
    scratch += [pltpu.SemaphoreType.DMA((7,))]
    out = [
        (c[0].shape[1], c[0].shape[2] // 2),
        (e[0].shape[1], e[0].shape[2] // 2),
        o[0].shape[3:],
        (share // 2 + lead_rows, LANES),
    ]
    out = [jax.ShapeDtypeStruct((2, 2) + shape, low) for shape in out]
    out += [jax.ShapeDtypeStruct(small, f32), jax.ShapeDtypeStruct(rows[0].shape, low)]
    return pl.pallas_call(
        functools.partial(finish_kernel, table=table),
        in_specs=[hbm] * 8 + [vmem] * 10,
        out_specs=[vmem] * 6,
        out_shape=out,
        scratch_shapes=scratch,
        compiler_params=pltpu.CompilerParams(vmem_limit_bytes=62 << 20, collective_id=0, has_side_effects=True),
        cost_estimate=pl.CostEstimate(flops=7 * 10**9, bytes_accessed=40 * 10**6, transcendentals=0),
        name="finish",
    )(
        late.reshape(cube + late.shape[1:]),
        gt,
        *weights[:3],
        *rows,
        gres,
        *weights[3:],
        gain,
        pos.reshape(cube + pos.shape[1:]),
        *c,
        *e,
        *o,
    )


def emit_kernel(c_hbm, e_hbm, o_hbm, l_hbm, vec_ref, *refs, plan, slots):
    outs, (c_ref, e_ref, o_ref, l_ref, vals, sems) = refs[:-6], refs[-6:]
    pairs = ((l_hbm, l_ref), (c_hbm, c_ref), (e_hbm, e_ref), (o_hbm, o_ref))
    copies = [pltpu.make_async_copy(a, b, sems.at[k]) for k, (a, b) in enumerate(pairs)]
    for copy in copies:
        copy.start()
    copies[0].wait()
    experts, keys, queries, positions, values, gates = outs[3:9]
    targets = (experts, keys, queries, vals, positions)
    for core, x, start, number, to, rows in plan:
        targets[number][to : to + rows] = to_wide(l_ref[core, x, start : start + rows])
    half = vals.shape[0] // 2
    values[...] = vals[:slots]
    gates[...] = vals[half : half + slots]
    first_gain, first_shift, second_gain, second_shift, contract, expand, content, position = outs[9:]
    first_gain[...] = vec_ref[0]
    first_shift[...] = vec_ref[1]
    lines = tuple((ref, half + slots + k) for k, ref in enumerate((second_gain, second_shift, contract)))
    for ref, number in lines:
        ref[...] = vals[number]
    for k in range(4):
        expand[k * LANES : (k + 1) * LANES] = vals[half + slots + 3 + k]
    size = content.shape[0]
    content[...] = vals[half + slots + 7, :size]
    position[...] = vals[half + slots + 7, size : 2 * size]
    for k, ref in enumerate((c_ref, e_ref, o_ref)):
        width = ref.shape[3]
        copies[k + 1].wait()
        for core in range(2):
            for x in range(2):
                at = (core * 2 + x) * width
                outs[k][:, at : at + width] = to_wide(ref[core, x])


def emit(quarters, vec, dh):
    c, e, o, tail = quarters
    f32 = jnp.float32
    slots = HEADS * EXPERTS
    at_key, at_query, at_value, _, end = late_rows(dh)
    halves = [rows // 2 for rows in late_cut(end // 2)]
    sizes = [at_key, at_query - at_key, at_value - at_query, end - at_value]
    starts = [0, at_key, at_query, at_value]
    plan = []
    for core in range(2):
        for x in range(2):
            for part, piece in enumerate(halves):
                source = sum(halves[:part]) + (dh if part else 0)
                low_end = core * (end // 2) + 2 * sum(halves[:part]) + x * piece
                for k, (first, size) in enumerate(zip(starts, sizes)):
                    a, b = max(first, low_end), min(first + size, low_end + piece)
                    if a < b:
                        plan.append((core, x, source + a - low_end, k, a - first, b - a))
            plan.append((core, x, halves[0], 4, (2 * x + core) * dh, dh))
    vmem = pl.BlockSpec(memory_space=pltpu.VMEM)
    shapes = [(q.shape[2], 4 * q.shape[3]) for q in (c, e, o)] + [(n, LANES) for n in sizes[:3] + [HEADS * dh]]
    shapes += [(slots, LANES)] * 2 + [(LANES,)] * 5 + [(4 * LANES,)] + [(HEADS * dh * LANES // D,)] * 2
    return pl.pallas_call(
        functools.partial(emit_kernel, plan=tuple(plan), slots=slots),
        in_specs=[pl.BlockSpec(memory_space=pl.ANY)] * 4 + [vmem],
        out_specs=[vmem] * len(shapes),
        out_shape=[jax.ShapeDtypeStruct(shape, f32) for shape in shapes],
        scratch_shapes=[pltpu.VMEM(q.shape, q.dtype) for q in quarters]
        + [pltpu.VMEM((end - at_value, LANES), f32), pltpu.SemaphoreType.DMA((4,))],
        compiler_params=params(60),
        name="emit",
    )(c, e, o, tail, vec)


def mm(spec, left, right):
    return jnp.einsum(spec, left, right, preferred_element_type=jnp.float32)


def position_table(row_count, width_count):
    fine = 64
    inverse_freq = 10000.0 ** (-jnp.arange(0, width_count, 2).astype(jnp.float32) / width_count)
    high = (row_count // fine - 1 - jnp.arange(row_count // fine)) * fine
    low_part = fine - 1 - jnp.arange(fine)
    high_angle = high.astype(jnp.float32)[:, None, None] * inverse_freq
    low_angle = low_part.astype(jnp.float32)[None, :, None] * inverse_freq
    high_sin, high_cos = jnp.sin(high_angle), jnp.cos(high_angle)
    low_sin, low_cos = jnp.sin(low_angle), jnp.cos(low_angle)
    sines = high_sin * low_cos + high_cos * low_sin
    cosines = high_cos * low_cos - high_sin * low_sin
    return to_low(jnp.concatenate([sines, cosines], axis=2)).reshape(row_count, width_count)


def route_mask(routes, expert_count):
    return jnp.sum((routes[..., None] == jnp.arange(expert_count)).astype(jnp.float32), axis=-2)


def bit_of(axis, bit):
    return (lax.axis_index(axis) // bit) % 2


def swap(value, axis, bit):
    pairs = [(i, i ^ bit) for i in range(lax.axis_size(axis))]
    return lax.ppermute(value, axis, pairs)


def pick(value, index, axis):
    return lax.dynamic_index_in_dim(value, index, axis, keepdims=False)


def cut(value, index, axis):
    size = value.shape[axis] // 2
    return lax.dynamic_slice_in_dim(value, index * size, size, axis)


def axis_bits(axis):
    size = lax.axis_size(axis)
    return [1 << k for k in range(size.bit_length() - 1)]


def bits_tree(value, seg_size):
    count = len(axis_bits("seg"))
    return value.reshape((2,) * count + (value.shape[0] // seg_size, value.shape[1]))


class Share:
    def __init__(self, addends, bits):
        self.addends = addends
        self.bits = bits

    def total(self):
        out = to_wide(self.addends[0])
        for item in self.addends[1:]:
            out = out + to_wide(item)
        return to_low(out)

    def seg(self, number):
        if number >= len(axis_bits("seg")):
            return self
        bit = axis_bits("seg")[number]
        dim = len(self.bits) - 1 - self.bits.index(bit)
        mine = bit_of("seg", bit)
        sent = Share([pick(a, 1 - mine, dim) for a in self.addends], self.bits).total()
        come = swap(sent, "seg", bit)
        left = [b for b in self.bits if b != bit]
        return Share([pick(a, mine, dim) for a in self.addends] + [come], left)

    def rest(self):
        out = self
        for bit in self.bits:
            out = out.seg(axis_bits("seg").index(bit))
        return out

    def pos(self, number, dim):
        bit = axis_bits("pos")[number]
        mine = bit_of("pos", bit)
        at = len(self.bits) + dim
        sent = Share([cut(a, 1 - mine, at) for a in self.addends], self.bits).total()
        come = swap(sent, "pos", bit)
        return Share([cut(a, mine, at) for a in self.addends] + [come], self.bits)

    def pos_all(self, number):
        part = self.total()
        return Share([part, swap(part, "pos", axis_bits("pos")[number])], self.bits)


def together(stages):
    items, bits, swaps, lefts = [], [], [], []
    for item, axis, number in stages:
        bit = axis_bits(axis)[number]
        bits.append(bit_of(axis, bit))
        swaps.append((axis, bit))
        if axis == "seg":
            items.append((item.addends, len(item.bits) - 1 - item.bits.index(bit)))
            lefts.append([b for b in item.bits if b != bit])
        else:
            items.append((item.addends, "columns"))
            lefts.append(item.bits)
    pairs = fold(items, jnp.stack(bits).astype(jnp.int32))
    out = []
    for (sent, kept), (axis, bit), left in zip(pairs, swaps, lefts):
        out.append(Share([kept, swap(sent, axis, bit)], left))
    return out


def share(values, seg_size):
    return Share([bits_tree(v, seg_size) for v in values], axis_bits("seg"))


def widen(part, number, dim):
    bit = axis_bits("pos")[number]
    mine = bit_of("pos", bit)
    other = swap(part, "pos", bit)
    first = jnp.where(mine == 0, part, other)
    second = jnp.where(mine == 0, other, part)
    return jnp.concatenate([first, second], axis=dim)


def seg_blocks(value, seg_size):
    blocks, rows, lanes = value.shape
    inside = seg_size // blocks
    value = value.reshape(blocks, rows, inside, lanes // inside)
    value = jnp.transpose(value, (0, 2, 1, 3))
    count = len(axis_bits("seg"))
    return value.reshape((2,) * count + (rows, lanes // inside))


def vector_rows(vectors, seg_size):
    lanes = D // seg_size
    rows = jnp.concatenate([v.reshape(seg_size, -1, lanes) for v in vectors], axis=1)
    blocks = D // LANES
    rows = rows.reshape(blocks, seg_size // blocks, rows.shape[1], lanes)
    return jnp.transpose(rows, (0, 2, 1, 3)).reshape(blocks, -1, LANES)


def local(
    block_input,
    memory_rows,
    memory_length,
    value_routes,
    output_routes,
    first_gain,
    first_shift,
    query_weight,
    key_weight,
    position_weight,
    value_experts,
    value_router,
    content_bias,
    position_bias,
    output_experts,
    output_gate_matrix,
    second_gain,
    second_shift,
    up_projection_weight,
    expand_bias,
    down_projection_weight,
    contract_bias,
    output_cotangent,
):
    seg_count, local_rows, width = block_input.shape
    seg_size = lax.axis_size("seg")
    pos_index = lax.axis_index("pos")
    key_count = 2 * SEQ
    all_rows = seg_count * local_rows
    slots = HEADS * EXPERTS
    score_scale = DH ** (-0.5)
    line = lambda v: v.reshape(1, -1)

    value_pick = jnp.transpose(route_mask(value_routes, EXPERTS), (0, 1, 3, 4, 2))
    value_pick = value_pick.reshape(seg_count, 2, slots, local_rows)
    out_pick = jnp.transpose(route_mask(output_routes, EXPERTS), (0, 2, 3, 1))
    out_pick = out_pick.reshape(seg_count, slots, local_rows)
    pad = ((0, 0), (0, 32 - slots))
    gates = jnp.concatenate([jnp.pad(value_router, pad).T, jnp.pad(output_gate_matrix, pad).T], axis=0)

    def trade(value):
        return lax.all_to_all(value, "pos", split_axis=0, concat_axis=0, tiled=True)

    qk, normed, value_gate, out_gate = project(
        memory_rows,
        block_input,
        first_gain,
        first_shift,
        query_weight.T,
        key_weight.T,
        gates,
        value_pick,
        out_pick,
    )
    qk = trade(qk)
    values, value_all = experts(normed, value_experts.T, value_gate)
    values = trade(values)

    table_low = position_table(key_count, D)
    weight_local = pick(position_weight.reshape(D, HEADS, DH), pos_index, 1)
    positions = to_low(mm("nd,dc->cn", table_low, weight_local))

    head_content = pick(content_bias.reshape(HEADS, DH), pos_index, 0)
    head_position = pick(position_bias.reshape(HEADS, DH), pos_index, 0)
    probs = score(memory_length, qk, positions, head_content, head_position, score_scale)
    attended = attend(probs, values)

    core = bit_of("pos", 1).astype(jnp.int32).reshape(1)
    cotangent = output_cotangent.reshape(all_rows, width)
    (
        hidden,
        residual,
        grad_normed_two,
        down_sent,
        down_kept,
        up_sent,
        up_kept,
        expand_bias_grad,
    ) = middle(
        core,
        attended,
        out_gate,
        block_input.reshape(all_rows, width),
        cotangent,
        output_experts,
        second_gain,
        second_shift,
        up_projection_weight,
        line(expand_bias),
        down_projection_weight,
    )
    down_got = swap(down_sent, "pos", 1)
    up_got = swap(up_sent, "pos", 1)
    grad_residual, grad_attended, grad_out_logit, mix_sent, mix_kept, middle_sums = middle_back(
        core, residual, grad_normed_two, attended, out_gate, cotangent, output_experts, second_gain
    )
    grad_heads = trade(grad_attended)
    mix_got = swap(mix_sent, "pos", 1)
    down = share([down_kept, down_got], seg_size)
    up = share([up_kept, up_got], seg_size)
    mix = share([mix_kept, mix_got], seg_size)
    cube = seg_size * LANES == D and lax.axis_size("pos") == 4
    if cube:
        down, up = together([(down, "seg", 1), (up, "seg", 0)])
    else:
        down, up = down.seg(1), up.seg(0)

    grads, grad_rel, part_sums = attend_back(
        probs, grad_heads, qk, values, positions, head_content, head_position, score_scale
    )
    grads = trade(grads)
    part_sums, hidden = lax.optimization_barrier((part_sums, hidden))
    block_output = feed(hidden, down_projection_weight, residual, contract_bias)
    part_sums, block_output, down.addends, up.addends, mix.addends = lax.optimization_barrier(
        (part_sums, block_output, down.addends, up.addends, mix.addends)
    )
    if cube:
        down, up, mix = together([(down, "seg", 0), (up, "seg", 1), (mix, "pos", 1)])
    else:
        down, up, mix = down.seg(0), up.seg(1), mix.pos(1, 1)

    position_grad = to_low(mm("scn,nd->cd", grad_rel, table_low))
    position_grad = jnp.transpose(position_grad.reshape(DH, D // LANES, LANES), (1, 0, 2))
    head_hot = (jnp.arange(HEADS) == pos_index).astype(jnp.float32)[:, None]
    bias_sums = jnp.sum(part_sums, axis=0)
    biases = [(head_hot * bias_sums[k]).reshape(seg_size, -1) for k in range(2)]
    bias_row = jnp.concatenate(biases, axis=1)
    bias_row = jnp.pad(bias_row, ((0, 0), (0, D // seg_size - bias_row.shape[1])))
    extra = vector_rows(
        [middle_sums[0], middle_sums[1], middle_sums[2], expand_bias_grad[0], bias_row], seg_size
    )

    if cube:
        late, all_grads = lean(
            memory_rows,
            block_input,
            first_gain,
            first_shift,
            grads,
            grad_out_logit,
            value_gate,
            value_all,
            extra,
        )
    else:
        input_grad, late = back(
            memory_rows,
            block_input,
            first_gain,
            first_shift,
            grads,
            grad_out_logit,
            value_gate,
            value_all,
            value_experts.T,
            key_weight.T,
            query_weight.T,
            value_router.T,
            output_gate_matrix.T,
            grad_residual.reshape(seg_count, local_rows, width),
            extra,
        )
    late, position_grad, down.addends, up.addends, mix.addends = lax.optimization_barrier(
        (late, position_grad, down.addends, up.addends, mix.addends)
    )
    if cube:
        weights = (value_experts.T, key_weight.T, query_weight.T, value_router.T, output_gate_matrix.T)
        *quarters, vec, input_grad = finish(
            late,
            all_grads,
            weights,
            (memory_rows, block_input),
            grad_residual.reshape(seg_count, local_rows, width),
            first_gain,
            position_grad,
            down.addends,
            up.addends,
            mix.addends,
        )
        contract_weight_grad, expand_weight_grad, output_experts_grad, *rows_out = emit(quarters, vec, DH)
        experts_grad, keys_grad, queries_grad, positions_grad, value_grad, out_grad = rows_out[:6]
        vectors = rows_out[6:]
    else:
        late = Share([late], []).pos(0, 1).total()
        share_rows = late.shape[1] // 2
        one = Share([late[:, :share_rows]], []).pos(1, 1).total()
        piece_rows = one.shape[1]
        one = jnp.concatenate([one, position_grad], axis=1)
        one = Share([seg_blocks(one, seg_size)], axis_bits("seg")).rest().total()
        two = Share([seg_blocks(late[:, share_rows:], seg_size)], axis_bits("seg"))
        two = two.rest().pos(1, 0).total()
        tail = jnp.concatenate([one, two], axis=0)
        tail = to_wide(widen(widen(tail[None], 1, 0)[None], 0, 0))
        lanes = tail.shape[3]
        up = up.pos(1, 1).rest().total()
        expand_weight_grad = to_wide(widen(widen(up, 1, 1), 0, 1))
        down = down.pos(1, 1).rest().total()
        contract_weight_grad = to_wide(widen(widen(down, 1, 1), 0, 1))
        mix = mix.rest().total()
        output_experts_grad = to_wide(widen(widen(mix, 1, 1), 0, 1))
        parts = [tail[:, :, :piece_rows], tail[:, :, tail.shape[2] - piece_rows :]]
        main = jnp.concatenate([p.reshape(2, share_rows, lanes) for p in parts], axis=1).reshape(-1, lanes)
        heads = jnp.transpose(tail[:, :, piece_rows : tail.shape[2] - piece_rows], (1, 0, 2, 3))
        edges = (0,) + late_rows(DH)
        rows_out = [main[a:b] for a, b in zip(edges, edges[1:])] + [heads.reshape(HEADS * DH, lanes)]
        experts_grad, keys_grad, queries_grad, value_rows, out_rows, positions_grad = rows_out
        value_grad, out_grad = value_rows[:slots], out_rows[:slots]
        extra = out_rows[slots : slots + 8]
        piece = DH * HEADS // seg_size
        vectors = [value_rows[slots], value_rows[slots + 1], extra[0], extra[1], extra[2]]
        vectors += [extra[3:7].reshape(-1), extra[7, :piece], extra[7, piece : 2 * piece]]
    return (
        block_output.reshape(block_input.shape),
        input_grad,
        vectors[0],
        vectors[1],
        queries_grad.T,
        keys_grad.T,
        positions_grad.T,
        experts_grad.T,
        value_grad.T,
        vectors[6],
        vectors[7],
        output_experts_grad,
        out_grad.T,
        vectors[2],
        vectors[3],
        expand_weight_grad,
        vectors[5],
        contract_weight_grad,
        vectors[4],
    )


def solution(mesh):
    rows = P("seg", "pos", None)
    whole = P()
    placed = (
        rows,
        rows,
        P("seg"),
        P("seg", None, "pos", None, None),
        P("seg", "pos", None, None),
    )
    placed += (whole,) * 17 + (rows,)
    shares = [P("seg")] * 17
    for index in (2, 3, 4, 5, 6, 9, 10, 13, 15):
        shares[index] = P("seg", None)
    return jax.shard_map(
        local,
        mesh=mesh,
        in_specs=placed,
        out_specs=(rows, rows) + tuple(shares),
        check_vma=False,
    )
```

```python
import functools

import jax
import jax.numpy as jnp
from jax import lax
from jax.experimental import pallas as pl
from jax.experimental.pallas import tpu as pltpu
from jax.sharding import PartitionSpec as P

D = 1024
HEADS = 4
DH = 112
EXPERTS = 5
SEQ = 1024
norm_eps = 1e-05

NEG = -1e30
LANES = 128


def nn(left, right):
    return lax.dot_general(left, right, (((1,), (0,)), ((), ())), preferred_element_type=jnp.float32)


def nt(left, right):
    return lax.dot_general(left, right, (((1,), (1,)), ((), ())), preferred_element_type=jnp.float32)


def to_low(value):
    return value.astype(jnp.bfloat16)


def to_wide(value):
    return value.astype(jnp.float32)


def norm_parts(rows):
    center = rows - jnp.mean(rows, axis=1, keepdims=True)
    inv_std = lax.rsqrt(jnp.mean(center * center, axis=1, keepdims=True) + norm_eps)
    return center * inv_std, inv_std


def vector(value):
    return once(value.shape, lambda *_: (0,))


def once(shape, index_map):
    return pl.BlockSpec(shape, index_map, pipeline_mode=pl.Buffered(1))


def row(ref):
    return to_wide(ref[...]).reshape(1, -1)


def params(megabytes):
    return pltpu.CompilerParams(vmem_limit_bytes=megabytes << 20)


def project_kernel(
    mem_ref, blk_ref, gain_ref, shift_ref, wq_ref, wk_ref, gates_ref, pickv_ref, picko_ref,
    qk_ref, norm_ref, gatev_ref, gateo_ref,
):
    half = pl.program_id(1)
    rows = to_wide(jnp.where(half == 0, mem_ref[0], blk_ref[0]))
    unit, _ = norm_parts(rows)
    normed = to_low(unit * row(gain_ref) + row(shift_ref))
    norm_ref[0, 0] = normed
    turned = normed.T
    keys = to_low(nn(wk_ref[...], turned))
    dh = qk_ref.shape[3]
    logits = nn(gates_ref[...], turned)
    gatev_ref[0, 0] = jax.nn.sigmoid(logits[: pickv_ref.shape[2]]) * pickv_ref[0, 0]

    @pl.when(half == 0)
    def _():
        for h in range(qk_ref.shape[0]):
            qk_ref[h, 0, 1] = keys[h * dh : (h + 1) * dh]

    @pl.when(half == 1)
    def _():
        query = to_low(nn(wq_ref[...], turned))
        for h in range(qk_ref.shape[0]):
            qk_ref[h, 0, 0] = query[h * dh : (h + 1) * dh]
            qk_ref[h, 0, 2] = keys[h * dh : (h + 1) * dh]
        gateo_ref[0] = jax.nn.sigmoid(logits[logits.shape[0] // 2 :][: picko_ref.shape[1]]) * picko_ref[0]


def project(mem, blk, gain, shift, wqt, wkt, gates, pickv, picko):
    segs, rows, width = blk.shape
    inner = wqt.shape[0]
    slots = pickv.shape[2]
    low, f32 = jnp.bfloat16, jnp.float32
    dh = inner // HEADS
    flat = lambda s, r: (0, 0)
    row_spec = pl.BlockSpec((1, rows, width), lambda s, r: (s, 0, 0))
    return pl.pallas_call(
        project_kernel,
        grid=(segs, 2),
        in_specs=[
            row_spec,
            row_spec,
            vector(gain),
            vector(shift),
            once(wqt.shape, flat),
            once(wkt.shape, flat),
            once(gates.shape, flat),
            pl.BlockSpec((1, 1, slots, rows), lambda s, r: (s, r, 0, 0)),
            pl.BlockSpec((1, slots, rows), lambda s, r: (s, 0, 0)),
        ],
        out_specs=[
            pl.BlockSpec((HEADS, 1, 3, dh, rows), lambda s, r: (0, s, 0, 0, 0)),
            pl.BlockSpec((1, 1, rows, width), lambda s, r: (s, r, 0, 0)),
            pl.BlockSpec((1, 1, slots, rows), lambda s, r: (s, r, 0, 0)),
            pl.BlockSpec((1, slots, rows), lambda s, r: (s, 0, 0)),
        ],
        out_shape=[
            jax.ShapeDtypeStruct((HEADS, segs, 3, dh, rows), low),
            jax.ShapeDtypeStruct((segs, 2, rows, width), low),
            jax.ShapeDtypeStruct((segs, 2, slots, rows), f32),
            jax.ShapeDtypeStruct((segs, slots, rows), f32),
        ],
        compiler_params=params(60),
        cost_estimate=pl.CostEstimate(flops=3 * 10**9, bytes_accessed=8 * 10**6, transcendentals=0),
        name="project",
    )(mem, blk, gain, shift, wqt, wkt, gates, pickv, picko)


def experts_kernel(norm_ref, ve_ref, gate_ref, v_ref, all_ref):
    turned = norm_ref[0, 0].T
    heads, dh = v_ref.shape[0], v_ref.shape[3]
    group = nn(ve_ref[...], turned)
    all_ref[0, 0] = to_low(group)
    for h in range(heads):
        total = jnp.zeros((dh, turned.shape[1]), jnp.float32)
        for e in range(EXPERTS):
            slot = h * EXPERTS + e
            total = total + gate_ref[0, 0, slot : slot + 1] * group[slot * dh : (slot + 1) * dh]
        v_ref[h, 0, 0] = to_low(total)


def experts(normed, vet, gate):
    segs, _, rows, width = normed.shape
    inner = vet.shape[0]
    slots = gate.shape[2]
    dh = inner // (HEADS * EXPERTS)
    low = jnp.bfloat16
    return pl.pallas_call(
        experts_kernel,
        grid=(segs, 2),
        in_specs=[
            pl.BlockSpec((1, 1, rows, width), lambda s, r: (s, r, 0, 0)),
            once(vet.shape, lambda s, r: (0, 0)),
            pl.BlockSpec((1, 1, slots, rows), lambda s, r: (s, r, 0, 0)),
        ],
        out_specs=[
            pl.BlockSpec((HEADS, 1, 1, dh, rows), lambda s, r: (0, s, r, 0, 0)),
            pl.BlockSpec((1, 1, inner, rows), lambda s, r: (s, r, 0, 0)),
        ],
        out_shape=[
            jax.ShapeDtypeStruct((HEADS, segs, 2, dh, rows), low),
            jax.ShapeDtypeStruct((segs, 2, inner, rows), low),
        ],
        compiler_params=params(48),
        cost_estimate=pl.CostEstimate(flops=5 * 10**9, bytes_accessed=12 * 10**6, transcendentals=0),
        name="experts",
    )(normed, vet, gate)


def column(ref):
    value = row(ref)
    return jnp.broadcast_to(value, (LANES, value.shape[1])).T[:, :1]


def biased(query, bias, scale):
    return to_low((to_wide(query) + bias) * scale)


def score_kernel(len_ref, qk_ref, pos_ref, cb_ref, pb_ref, p_ref, kt_s, *, tiles, block, chunk, scale):
    seg = pl.program_id(0)
    start = tiles * block - len_ref[seg]
    for half in range(2):
        for t in range(tiles):
            c0 = (half * tiles + t) * block
            kt_s[:, c0 : c0 + block] = qk_ref[t, 0, 1 + half]
    mem = tiles * block
    cb, pb = column(cb_ref), column(pb_ref)
    for t in range(tiles):
        w = mem + (t + 1) * block
        base = (tiles - 1 - t) * block
        col = lax.broadcasted_iota(jnp.int32, (1, w), 1)
        bias = jnp.where(col >= start, 0.0, NEG)
        content = biased(qk_ref[t, 0, 0], cb, scale).T
        position = biased(qk_ref[t, 0, 0], pb, scale).T
        for r0 in range(0, block, chunk):
            raw = nn(position[r0 : r0 + chunk], pos_ref[:, base:])
            rel = pltpu.roll(raw, w - (block - 1) + r0, 1, stride=1, stride_axis=0)
            s = nn(content[r0 : r0 + chunk], kt_s[:, :w]) + rel
            row = lax.broadcasted_iota(jnp.int32, (chunk, w), 0) + (mem + t * block + r0)
            col_wide = lax.broadcasted_iota(jnp.int32, (chunk, w), 1)
            s = jnp.where(col_wide <= row, s + bias, NEG)
            e = jnp.exp(s - jnp.max(s, axis=1, keepdims=True))
            p = e * (1.0 / jnp.sum(e, axis=1, keepdims=True))
            p_ref[0, t * block + r0 : t * block + r0 + chunk, :w] = to_low(p)


def score(lengths, qk, post, cbias, pbias, scale):
    tiles, segs, _, dh, block = qk.shape
    keys = 2 * tiles * block
    return pl.pallas_call(
        functools.partial(score_kernel, tiles=tiles, block=block, chunk=256, scale=scale),
        grid_spec=pltpu.PrefetchScalarGridSpec(
            num_scalar_prefetch=1,
            grid=(segs,),
            in_specs=[
                pl.BlockSpec((tiles, 1, 3, dh, block), lambda s, _: (0, s, 0, 0, 0)),
                pl.BlockSpec((dh, keys), lambda s, _: (0, 0)),
                vector(cbias),
                vector(pbias),
            ],
            out_specs=pl.BlockSpec((1, tiles * block, keys), lambda s, _: (s, 0, 0)),
            scratch_shapes=[pltpu.VMEM((dh, keys), jnp.bfloat16)],
        ),
        out_shape=jax.ShapeDtypeStruct((segs, tiles * block, keys), jnp.bfloat16),
        compiler_params=params(48),
        cost_estimate=pl.CostEstimate(flops=12 * 10**9, bytes_accessed=10 * 10**6, transcendentals=4 * 10**6),
        name="score",
    )(lengths, qk, post, cbias, pbias)


def attend_kernel(p_ref, v_ref, out_ref, v_s, buf, sent, came, near, *, tiles, block):
    seg = pl.program_id(0)
    segs = buf.shape[1]
    me = lax.axis_index("pos")
    peers = [(me + d) % tiles for d in range(1, tiles)]

    @pl.when(seg == 0)
    def _():
        barrier = pltpu.get_barrier_semaphore()
        for peer in peers:
            pl.semaphore_signal(barrier, inc=1, device_id={"pos": peer}, device_id_type=pl.DeviceIdType.MESH)

    for half in range(2):
        for t in range(tiles):
            c0 = (half * tiles + t) * block
            v_s[c0 : c0 + block, :] = v_ref[t, 0, half].T
    for t in range(tiles):
        w = tiles * block + (t + 1) * block
        out = nn(p_ref[0, t * block : (t + 1) * block, :w], v_s[:w, :])
        buf[t, seg] = to_low(out).T

    @pl.when(seg == 0)
    def _():
        pl.semaphore_wait(pltpu.get_barrier_semaphore(), tiles - 1)

    def moves(s):
        away = [
            pltpu.make_async_remote_copy(
                src_ref=buf.at[peer, s],
                dst_ref=out_ref.at[me, s],
                send_sem=sent.at[d, s],
                recv_sem=came.at[d, s],
                device_id={"pos": peer},
                device_id_type=pl.DeviceIdType.MESH,
            )
            for d, peer in enumerate(peers)
        ]
        return away, pltpu.make_async_copy(buf.at[me, s], out_ref.at[me, s], near.at[s])

    away, here = moves(seg)
    for copy in away:
        copy.start()
    here.start()

    @pl.when(seg == segs - 1)
    def _():
        for s in range(segs):
            away, here = moves(s)
            for copy in away:
                copy.wait()
            here.wait()


def attend(p, v):
    tiles, segs, _, dh, block = v.shape
    keys = 2 * tiles * block
    return pl.pallas_call(
        functools.partial(attend_kernel, tiles=tiles, block=block),
        grid=(segs,),
        in_specs=[
            pl.BlockSpec((1, tiles * block, keys), lambda s: (s, 0, 0)),
            pl.BlockSpec((tiles, 1, 2, dh, block), lambda s: (0, s, 0, 0, 0)),
        ],
        out_specs=pl.BlockSpec(memory_space=pl.ANY),
        out_shape=jax.ShapeDtypeStruct((tiles, segs, dh, block), jnp.bfloat16),
        scratch_shapes=[
            pltpu.VMEM((keys, dh), jnp.bfloat16),
            pltpu.VMEM((tiles, segs, dh, block), jnp.bfloat16),
            pltpu.SemaphoreType.DMA((tiles - 1, segs)),
            pltpu.SemaphoreType.DMA((tiles - 1, segs)),
            pltpu.SemaphoreType.DMA((segs,)),
        ],
        compiler_params=pltpu.CompilerParams(vmem_limit_bytes=48 << 20, collective_id=1, has_side_effects=True),
        cost_estimate=pl.CostEstimate(flops=5 * 10**9, bytes_accessed=9 * 10**6, transcendentals=0),
        name="attend",
    )(p, v)


def attend_back_kernel(
    p_ref, g_ref, qk_ref, v_ref, pos_ref, cb_ref, pb_ref, d_ref, dpos_ref, sums_ref,
    k_s, vt_s, posr_s, dkt, dvt, dpt, ds_s, dr_s, *, tiles, block, chunk, scale,
):
    seg = pl.program_id(0)
    for half in range(2):
        for t in range(tiles):
            c0 = (half * tiles + t) * block
            k_s[c0 : c0 + block, :] = qk_ref[t, 0, 1 + half].T
            vt_s[:, c0 : c0 + block] = v_ref[t, 0, half]

    @pl.when(seg == 0)
    def _():
        posr_s[...] = pos_ref[...].T

    dkt[...] = jnp.zeros_like(dkt)
    dvt[...] = jnp.zeros_like(dvt)
    dpt[...] = jnp.zeros_like(dpt)
    mem = tiles * block
    dh = v_ref.shape[3]
    flip = (
        lax.broadcasted_iota(jnp.int32, (block, block), 0) + lax.broadcasted_iota(jnp.int32, (block, block), 1)
        == block - 1
    )
    flip_wide = jnp.where(flip, 1.0, 0.0)
    flip_low = to_low(flip_wide)
    cb, pb = column(cb_ref), column(pb_ref)
    content_sum = jnp.zeros((1, dh), jnp.float32)
    position_sum = jnp.zeros((1, dh), jnp.float32)
    for t in range(tiles):
        w = mem + (t + 1) * block
        base = (tiles - 1 - t) * block
        gt = g_ref[t, 0]
        g = gt.T
        for r0 in range(0, block, chunk):
            p = to_wide(p_ref[0, t * block + r0 : t * block + r0 + chunk, :w])
            prod = p * nn(g[r0 : r0 + chunk], vt_s[:, :w])
            delta = jnp.sum(prod, axis=1, keepdims=True)
            ds_s[r0 : r0 + chunk, :w] = to_low(prod - p * delta)
        ds = ds_s[:, :w]
        for r0 in range(0, block, chunk):
            turned = nn(flip_low[r0 : r0 + chunk], ds)
            dr_s[r0 : r0 + chunk, :w] = to_low(pltpu.roll(turned, r0, 1, stride=1, stride_axis=0))
        dr = dr_s[:, :w]
        dvt[:, :w] += nn(gt, p_ref[0, t * block : (t + 1) * block, :w])
        dkt[:, :w] += nn(biased(qk_ref[t, 0, 0], cb, scale), ds)
        position = to_low(nn(biased(qk_ref[t, 0, 0], pb, scale), flip_low))
        dpt[:, base:] += nn(position, dr)
        dc = nn(ds, k_s[:w, :])
        dp = nn(dr, posr_s[base:, :])
        content_sum = content_sum + jnp.sum(dc, axis=0, keepdims=True)
        position_sum = position_sum + jnp.sum(dp, axis=0, keepdims=True)
        dp = lax.dot_general(
            flip_wide,
            dp,
            (((1,), (0,)), ((), ())),
            precision=lax.Precision.HIGHEST,
            preferred_element_type=jnp.float32,
        )
        d_ref[t, 0, 0] = to_low((dc + dp) * scale).T
    sums_ref[0, 0:1] = content_sum * scale
    sums_ref[0, 1:2] = position_sum * scale
    dpos_ref[0] = to_low(dpt[...])
    for half in range(2):
        for t in range(tiles):
            c0 = (half * tiles + t) * block
            d_ref[t, 0, 1 + half] = to_low(dkt[:, c0 : c0 + block])
            d_ref[t, 0, 3 + half] = to_low(dvt[:, c0 : c0 + block])


def attend_back(p, g, qk, v, post, cbias, pbias, scale):
    tiles, segs, dh, block = g.shape
    keys = 2 * tiles * block
    low, f32 = jnp.bfloat16, jnp.float32

    def spec(parts):
        return pl.BlockSpec((tiles, 1, parts, dh, block), lambda s: (0, s, 0, 0, 0))

    return pl.pallas_call(
        functools.partial(attend_back_kernel, tiles=tiles, block=block, chunk=256, scale=scale),
        grid=(segs,),
        in_specs=[
            pl.BlockSpec((1, tiles * block, keys), lambda s: (s, 0, 0)),
            pl.BlockSpec((tiles, 1, dh, block), lambda s: (0, s, 0, 0)),
            spec(3),
            spec(2),
            pl.BlockSpec((dh, keys), lambda s: (0, 0)),
            vector(cbias),
            vector(pbias),
        ],
        out_specs=[
            spec(5),
            pl.BlockSpec((1, dh, keys), lambda s: (s, 0, 0)),
            pl.BlockSpec((1, 2, dh), lambda s: (s, 0, 0)),
        ],
        out_shape=[
            jax.ShapeDtypeStruct((tiles, segs, 5, dh, block), low),
            jax.ShapeDtypeStruct((segs, dh, keys), low),
            jax.ShapeDtypeStruct((segs, 2, dh), f32),
        ],
        scratch_shapes=[
            pltpu.VMEM((keys, dh), low),
            pltpu.VMEM((dh, keys), low),
            pltpu.VMEM((keys, dh), low),
            pltpu.VMEM((dh, keys), f32),
            pltpu.VMEM((dh, keys), f32),
            pltpu.VMEM((dh, keys), f32),
            pltpu.VMEM((block, keys), low),
            pltpu.VMEM((block, keys), low),
        ],
        compiler_params=params(56),
        cost_estimate=pl.CostEstimate(flops=25 * 10**9, bytes_accessed=14 * 10**6, transcendentals=0),
        name="attend_back",
    )(p, g, qk, v, post, cbias, pbias)


def mix_rows(mixed, att_ref, gate_ref):
    heads, segs, dh, rows = att_ref.shape
    for h in range(heads):
        for s in range(segs):
            att = to_wide(att_ref[h, s])
            for e in range(EXPERTS):
                slot = h * EXPERTS + e
                mixed[slot * dh : (slot + 1) * dh, s * rows : (s + 1) * rows] = to_low(
                    gate_ref[s, slot : slot + 1] * att
                )


def middle_kernel(
    core_ref, att_ref, gate_ref, x_ref, g_ref, oe_ref, gain_ref, shift_ref, wu_ref, bu_ref, wd_ref,
    hid_ref, res, gn, wds_ref, wdk_ref, wus_ref, wuk_ref, bu_out, mixed, n2, n2t, *, chunk,
):
    step = pl.program_id(0)
    steps = pl.num_programs(0)
    total, width = x_ref.shape
    half = width // 2
    mine = pl.multiple_of(core_ref[0] * half, half)
    other = pl.multiple_of((1 - core_ref[0]) * half, half)
    count = total // chunk

    @pl.when(step == 0)
    def _():
        mix_rows(mixed, att_ref, gate_ref)
        res[...] = to_wide(x_ref[...]) + nn(mixed[...].T, oe_ref[...])

        @pl.loop(0, count)
        def _(i):
            at = pl.ds(pl.multiple_of(i * chunk, chunk), chunk)
            unit, _ = norm_parts(res[at, :])
            n2[at, :] = to_low(unit * row(gain_ref) + row(shift_ref))

        n2t[...] = n2[...].T
        gn[...] = jnp.zeros_like(gn)

    wu = wu_ref[...]
    wd = wd_ref[...]
    v = nn(n2[...], wu) + to_wide(bu_ref[...])
    root = 0.7978845608028654
    square = v * v
    tanh = jnp.tanh(root * (v + 0.044715 * (square * v)))
    plus = 0.5 * (1.0 + tanh)
    hidden = to_low(v * plus)
    slope = plus + 0.5 * v * (1.0 - tanh * tanh) * (root * (1.0 + 0.134145 * square))
    gp = nt(g_ref[...], wd) * slope
    gp_low = to_low(gp)
    bu_out[...] = jnp.sum(to_wide(gp_low), axis=0, keepdims=True)
    hid_ref[...] = hidden
    gn[...] += nt(gp_low, wu)
    wu_grad = to_low(nn(n2t[...], gp_low))

    @pl.when(step < steps // 2)
    def _():
        wus_ref[...] = wu_grad

    @pl.when(step >= steps // 2)
    def _():
        wuk_ref[...] = wu_grad

    turned = hidden.T
    wds_ref[...] = to_low(nn(turned, g_ref[:, pl.ds(other, half)]))
    wdk_ref[...] = to_low(nn(turned, g_ref[:, pl.ds(mine, half)]))


def middle(core, att, gate, x, g, oe, gain, shift, wu, bu, wd, fc=512):
    heads, segs, dh, rows = att.shape
    total, width = x.shape
    ff = wu.shape[1]
    steps = ff // fc
    mid = steps // 2
    half = width // 2
    slots = gate.shape[1]
    inner = oe.shape[0]
    low, f32 = jnp.bfloat16, jnp.float32

    def fix(*shape):
        return pl.BlockSpec(shape, lambda i, c: (0,) * len(shape))

    def keep(*shape):
        return once(shape, lambda i, c: (0,) * len(shape))

    def unit(i, c):
        return (i + mid * (1 - c[0])) % steps

    return pl.pallas_call(
        functools.partial(middle_kernel, chunk=64),
        grid_spec=pltpu.PrefetchScalarGridSpec(
            num_scalar_prefetch=1,
            grid=(steps,),
            in_specs=[
                keep(heads, segs, dh, rows),
                keep(segs, slots, rows),
                keep(total, width),
                keep(total, width),
                keep(inner, width),
                vector(gain),
                vector(shift),
                pl.BlockSpec((width, fc), lambda i, c: (0, unit(i, c))),
                pl.BlockSpec((1, fc), lambda i, c: (0, unit(i, c))),
                pl.BlockSpec((fc, width), lambda i, c: (unit(i, c), 0)),
            ],
            out_specs=[
                pl.BlockSpec((total, fc), lambda i, c: (0, unit(i, c))),
                fix(total, width),
                fix(total, width),
                pl.BlockSpec((fc, half), lambda i, c: (unit(i, c), 0)),
                pl.BlockSpec((fc, half), lambda i, c: (unit(i, c), 0)),
                pl.BlockSpec((width, fc), lambda i, c: (0, jnp.minimum(i, mid - 1))),
                pl.BlockSpec((width, fc), lambda i, c: (0, jnp.maximum(i - mid, 0))),
                pl.BlockSpec((1, fc), lambda i, c: (0, unit(i, c))),
            ],
            scratch_shapes=[
                pltpu.VMEM((inner, total), low),
                pltpu.VMEM((total, width), low),
                pltpu.VMEM((width, total), low),
            ],
        ),
        out_shape=[
            jax.ShapeDtypeStruct((total, ff), low),
            jax.ShapeDtypeStruct((total, width), f32),
            jax.ShapeDtypeStruct((total, width), f32),
            jax.ShapeDtypeStruct((ff, half), low),
            jax.ShapeDtypeStruct((ff, half), low),
            jax.ShapeDtypeStruct((width, ff // 2), low),
            jax.ShapeDtypeStruct((width, ff // 2), low),
            jax.ShapeDtypeStruct((1, ff), f32),
        ],
        compiler_params=params(60),
        cost_estimate=pl.CostEstimate(flops=28 * 10**9, bytes_accessed=40 * 10**6, transcendentals=2 * 10**6),
        name="middle",
    )(core, att, gate, x, g, oe, gain, shift, wu, bu, wd)


def middle_back_kernel(
    core_ref, res, gn, att_ref, gate_ref, g_ref, oe_ref, gain_ref,
    gres_ref, gatt_ref, glog_ref, oes_ref, oek_ref, vec_ref, mixed, low_grad, turned, *, chunk,
):
    heads, segs, dh, rows = att_ref.shape
    total, width = g_ref.shape
    half = width // 2
    mine = pl.multiple_of(core_ref[0] * half, half)
    other = pl.multiple_of((1 - core_ref[0]) * half, half)
    mix_rows(mixed, att_ref, gate_ref)
    zero = jnp.zeros((1, width), jnp.float32)

    def rows_back(i, sums):
        at = pl.ds(pl.multiple_of(i * chunk, chunk), chunk)
        unit, inv_std = norm_parts(res[at, :])
        grad = gn[at, :]
        g = to_wide(g_ref[at, :])
        q = grad * row(gain_ref)
        back = q - jnp.mean(q, axis=1, keepdims=True) - unit * jnp.mean(q * unit, axis=1, keepdims=True)
        out = g + inv_std * back
        gres_ref[at, :] = out
        low_grad[at, :] = to_low(out)
        return (
            sums[0] + jnp.sum(grad * unit, axis=0, keepdims=True),
            sums[1] + jnp.sum(grad, axis=0, keepdims=True),
            sums[2] + jnp.sum(g, axis=0, keepdims=True),
        )

    sums = lax.fori_loop(0, total // chunk, rows_back, (zero, zero, zero))
    for k in range(3):
        vec_ref[k : k + 1] = sums[k]
    turned[...] = low_grad[...].T
    for h in range(heads):
        group = nn(oe_ref[h * EXPERTS * dh : (h + 1) * EXPERTS * dh], turned[...])
        for s in range(segs):
            att = to_wide(att_ref[h, s])
            grad = jnp.zeros((dh, rows), jnp.float32)
            for e in range(EXPERTS):
                slot = h * EXPERTS + e
                part = group[e * dh : (e + 1) * dh, s * rows : (s + 1) * rows]
                gate = gate_ref[s, slot : slot + 1]
                grad = grad + gate * part
                logit = jnp.sum(part * att, axis=0, keepdims=True) * (gate * (1.0 - gate))
                glog_ref[s, slot : slot + 1] = logit
            gatt_ref[h, s] = to_low(grad)
    oes_ref[...] = to_low(nn(mixed[...], low_grad[:, pl.ds(other, half)]))
    oek_ref[...] = to_low(nn(mixed[...], low_grad[:, pl.ds(mine, half)]))


def middle_back(core, res, gn, att, gate, g, oe, gain):
    inner, width = oe.shape
    total = g.shape[0]
    low, f32 = jnp.bfloat16, jnp.float32
    vmem = pl.BlockSpec(memory_space=pltpu.VMEM)
    return pl.pallas_call(
        functools.partial(middle_back_kernel, chunk=64),
        in_specs=[pl.BlockSpec(memory_space=pltpu.SMEM)] + [vmem] * 7,
        out_specs=[vmem] * 6,
        out_shape=[
            jax.ShapeDtypeStruct((total, width), f32),
            jax.ShapeDtypeStruct(att.shape, low),
            jax.ShapeDtypeStruct(gate.shape, f32),
            jax.ShapeDtypeStruct((inner, width // 2), low),
            jax.ShapeDtypeStruct((inner, width // 2), low),
            jax.ShapeDtypeStruct((3, width), f32),
        ],
        scratch_shapes=[
            pltpu.VMEM((inner, total), low),
            pltpu.VMEM((total, width), low),
            pltpu.VMEM((width, total), low),
        ],
        compiler_params=params(60),
        cost_estimate=pl.CostEstimate(flops=5 * 10**9, bytes_accessed=20 * 10**6, transcendentals=0),
        name="middle_back",
    )(core, res, gn, att, gate, g, oe, gain)


def feed_kernel(hid_ref, wd_ref, res_ref, bd_ref, y_ref, acc):
    step = pl.program_id(0)
    part = nn(hid_ref[...], wd_ref[...])

    @pl.when(step == 0)
    def _():
        acc[...] = res_ref[...] + part

    @pl.when(step > 0)
    def _():
        acc[...] += part

    @pl.when(step == pl.num_programs(0) - 1)
    def _():
        y_ref[...] = to_low(acc[...] + row(bd_ref))


def feed(hidden, wd, res, bd, fc=1024):
    total, ff = hidden.shape
    width = wd.shape[1]
    return pl.pallas_call(
        feed_kernel,
        grid=(ff // fc,),
        in_specs=[
            pl.BlockSpec((total, fc), lambda i: (0, i)),
            pl.BlockSpec((fc, width), lambda i: (i, 0)),
            once((total, width), lambda i: (0, 0)),
            vector(bd),
        ],
        out_specs=pl.BlockSpec((total, width), lambda i: (0, 0)),
        out_shape=jax.ShapeDtypeStruct((total, width), jnp.bfloat16),
        scratch_shapes=[pltpu.VMEM((total, width), jnp.float32)],
        compiler_params=params(60),
        cost_estimate=pl.CostEstimate(flops=1000, bytes_accessed=1000, transcendentals=0),
        name="feed",
    )(hidden, wd, res, bd)


def late_rows(dh):
    first = HEADS * EXPERTS * dh
    second = first + HEADS * dh
    third = second + HEADS * dh
    return first, second, third, third + 32, third + 64


def back_kernel(
    mem_ref, blk_ref, gain_ref, shift_ref, d_ref, glog_ref, gate_ref, all_ref, ve_ref, wk_ref, wq_ref,
    rv_ref, ro_ref, gres_ref, extra_ref, xg_ref, late_ref, vec, gt, every_gt, every_norm,
):
    half = pl.program_id(1)
    first_step = (pl.program_id(0) == 0) & (half == 0)
    heads, dh = d_ref.shape[0], d_ref.shape[3]
    slots = gate_ref.shape[2]
    at_key, at_query, at_value, at_out, end = late_rows(dh)

    @pl.when(first_step)
    def _():
        gt[at_value:end] = jnp.zeros((end - at_value, gt.shape[1]), jnp.bfloat16)
        vec[...] = jnp.zeros_like(vec)

    for h in range(heads):
        gv = to_wide(jnp.where(half == 0, d_ref[h, 0, 3], d_ref[h, 0, 4]))
        for e in range(EXPERTS):
            slot = h * EXPERTS + e
            gate = gate_ref[0, 0, slot : slot + 1]
            gt[slot * dh : (slot + 1) * dh] = to_low(gate * gv)
            logit = jnp.sum(to_wide(all_ref[0, 0, slot * dh : (slot + 1) * dh]) * gv, axis=0, keepdims=True)
            gt[at_value + slot : at_value + slot + 1] = to_low(logit * (gate * (1.0 - gate)))

    @pl.when(half == 0)
    def _():
        for h in range(heads):
            gt[at_key + h * dh : at_key + (h + 1) * dh] = d_ref[h, 0, 1]
        gt[at_query:at_value] = jnp.zeros((at_value - at_query, gt.shape[1]), jnp.bfloat16)
        gt[at_out : at_out + slots] = jnp.zeros((slots, gt.shape[1]), jnp.bfloat16)

    @pl.when(half == 1)
    def _():
        for h in range(heads):
            gt[at_key + h * dh : at_key + (h + 1) * dh] = d_ref[h, 0, 2]
            gt[at_query + h * dh : at_query + (h + 1) * dh] = d_ref[h, 0, 0]
        gt[at_out : at_out + slots] = to_low(glog_ref[0])

    rows = to_wide(jnp.where(half == 0, mem_ref[0], blk_ref[0]))
    unit, inv_std = norm_parts(rows)
    gain = row(gain_ref)
    normed = to_low(unit * gain + row(shift_ref))
    count = gt.shape[1]
    at = pl.multiple_of((pl.program_id(0) * 2 + half) * count, count)
    every_gt[:, pl.ds(at, count)] = gt[...]
    every_norm[pl.ds(at, count), :] = normed
    grad = nn(gt[:at_key].T, ve_ref[...]) + nn(gt[at_key:at_query].T, wk_ref[...])
    grad = grad + nn(gt[at_query:at_value].T, wq_ref[...])
    grad = grad + nn(gt[at_value : at_value + slots].T, rv_ref[...])
    grad = grad + nn(gt[at_out : at_out + slots].T, ro_ref[...])
    vec[0:1] += jnp.sum(grad * unit, axis=0, keepdims=True)
    vec[1:2] += jnp.sum(grad, axis=0, keepdims=True)

    @pl.when(half == 1)
    def _():
        q = grad * gain
        back = q - jnp.mean(q, axis=1, keepdims=True) - unit * jnp.mean(q * unit, axis=1, keepdims=True)
        xg_ref[0] = to_low(gres_ref[0] + inv_std * back)

    @pl.when((pl.program_id(0) == pl.num_programs(0) - 1) & (half == 1))
    def _():
        for k in range(0, late_ref.shape[0], 2):
            pair = to_low(nn(every_gt[...], every_norm[:, k * LANES : (k + 2) * LANES]))
            late_ref[k] = pair[:, :LANES]
            late_ref[k + 1] = pair[:, LANES:]
        for k in range(late_ref.shape[0]):
            both = vec[0:2, k * LANES : (k + 1) * LANES]
            late_ref[k, at_value + slots : at_value + slots + 2] = to_low(both)
            late_ref[k, at_out + slots : at_out + slots + 8] = to_low(extra_ref[k])


def back(mem, blk, gain, shift, grads, glog, gate, every, vet, wkt, wqt, rvt, rot, gres, extra):
    segs, rows, width = blk.shape
    heads, _, _, dh, _ = grads.shape
    slots = gate.shape[2]
    end = late_rows(dh)[-1]
    low, f32 = jnp.bfloat16, jnp.float32
    row_spec = pl.BlockSpec((1, rows, width), lambda s, r: (s, 0, 0))
    flat = lambda s, r: (0, 0)
    return pl.pallas_call(
        back_kernel,
        grid=(segs, 2),
        in_specs=[
            row_spec,
            row_spec,
            vector(gain),
            vector(shift),
            pl.BlockSpec((heads, 1, 5, dh, rows), lambda s, r: (0, s, 0, 0, 0)),
            pl.BlockSpec((1, slots, rows), lambda s, r: (s, 0, 0)),
            pl.BlockSpec((1, 1, slots, rows), lambda s, r: (s, r, 0, 0)),
            pl.BlockSpec((1, 1, every.shape[2], rows), lambda s, r: (s, r, 0, 0)),
            once(vet.shape, flat),
            once(wkt.shape, flat),
            once(wqt.shape, flat),
            once(rvt.shape, flat),
            once(rot.shape, flat),
            row_spec,
            once(extra.shape, lambda s, r: (0, 0, 0)),
        ],
        out_specs=[
            row_spec,
            pl.BlockSpec((width // LANES, end, LANES), lambda s, r: (0, 0, 0)),
        ],
        out_shape=[
            jax.ShapeDtypeStruct(blk.shape, low),
            jax.ShapeDtypeStruct((width // LANES, end, LANES), low),
        ],
        scratch_shapes=[
            pltpu.VMEM((8, width), f32),
            pltpu.VMEM((end, rows), low),
            pltpu.VMEM((end, 2 * segs * rows), low),
            pltpu.VMEM((2 * segs * rows, width), low),
        ],
        compiler_params=params(60),
        cost_estimate=pl.CostEstimate(flops=14 * 10**9, bytes_accessed=25 * 10**6, transcendentals=0),
        name="back",
    )(mem, blk, gain, shift, grads, glog, gate, every, vet, wkt, wqt, rvt, rot, gres, extra)


def lean_kernel(
    mem_ref, blk_ref, gain_ref, shift_ref, d_ref, glog_ref, gate_ref, all_ref, extra_ref, late_ref, gt, every_gt,
    every_norm,
):
    half = pl.program_id(1)
    first_step = (pl.program_id(0) == 0) & (half == 0)
    heads, dh = d_ref.shape[0], d_ref.shape[3]
    slots = gate_ref.shape[2]
    at_key, at_query, at_value, at_out, end = late_rows(dh)
    count = gt.shape[1]
    gt[at_value:end] = jnp.zeros((end - at_value, count), jnp.bfloat16)
    for h in range(heads):
        gv = to_wide(jnp.where(half == 0, d_ref[h, 0, 3], d_ref[h, 0, 4]))
        for e in range(EXPERTS):
            slot = h * EXPERTS + e
            gate = gate_ref[0, 0, slot : slot + 1]
            gt[slot * dh : (slot + 1) * dh] = to_low(gate * gv)
            logit = jnp.sum(to_wide(all_ref[0, 0, slot * dh : (slot + 1) * dh]) * gv, axis=0, keepdims=True)
            gt[at_value + slot : at_value + slot + 1] = to_low(logit * (gate * (1.0 - gate)))

    @pl.when(half == 0)
    def _():
        for h in range(heads):
            gt[at_key + h * dh : at_key + (h + 1) * dh] = d_ref[h, 0, 1]
        gt[at_query:at_value] = jnp.zeros((at_value - at_query, count), jnp.bfloat16)

    @pl.when(half == 1)
    def _():
        for h in range(heads):
            gt[at_key + h * dh : at_key + (h + 1) * dh] = d_ref[h, 0, 2]
            gt[at_query + h * dh : at_query + (h + 1) * dh] = d_ref[h, 0, 0]
        gt[at_out : at_out + slots] = to_low(glog_ref[0])

    unit, _ = norm_parts(to_wide(jnp.where(half == 0, mem_ref[0], blk_ref[0])))
    at = pl.multiple_of((pl.program_id(0) * 2 + half) * count, count)
    every_gt[:, pl.ds(at, count)] = gt[...]
    every_norm[pl.ds(at, count), :] = to_low(unit * row(gain_ref) + row(shift_ref))

    @pl.when((pl.program_id(0) == pl.num_programs(0) - 1) & (half == 1))
    def _():
        for k in range(0, late_ref.shape[0], 2):
            pair = to_low(nn(every_gt[...], every_norm[:, k * LANES : (k + 2) * LANES]))
            late_ref[k] = pair[:, :LANES]
            late_ref[k + 1] = pair[:, LANES:]
        for k in range(late_ref.shape[0]):
            late_ref[k, at_out + slots : at_out + slots + 8] = to_low(extra_ref[k])


def lean(mem, blk, gain, shift, grads, glog, gate, every, extra):
    segs, rows, width = blk.shape
    heads, _, _, dh, _ = grads.shape
    slots = gate.shape[2]
    end = late_rows(dh)[-1]
    low = jnp.bfloat16
    row_spec = pl.BlockSpec((1, rows, width), lambda s, r: (s, 0, 0))
    return pl.pallas_call(
        lean_kernel,
        grid=(segs, 2),
        in_specs=[
            row_spec,
            row_spec,
            vector(gain),
            vector(shift),
            pl.BlockSpec((heads, 1, 5, dh, rows), lambda s, r: (0, s, 0, 0, 0)),
            pl.BlockSpec((1, slots, rows), lambda s, r: (s, 0, 0)),
            pl.BlockSpec((1, 1, slots, rows), lambda s, r: (s, r, 0, 0)),
            pl.BlockSpec((1, 1, every.shape[2], rows), lambda s, r: (s, r, 0, 0)),
            once(extra.shape, lambda s, r: (0, 0, 0)),
        ],
        out_specs=[
            pl.BlockSpec((width // LANES, end, LANES), lambda s, r: (0, 0, 0)),
            pl.BlockSpec((end, rows), lambda s, r: (0, s * 2 + r)),
        ],
        out_shape=[
            jax.ShapeDtypeStruct((width // LANES, end, LANES), low),
            jax.ShapeDtypeStruct((end, 2 * segs * rows), low),
        ],
        scratch_shapes=[
            pltpu.VMEM((end, 2 * segs * rows), low),
            pltpu.VMEM((2 * segs * rows, width), low),
        ],
        compiler_params=params(60),
        cost_estimate=pl.CostEstimate(flops=7 * 10**9, bytes_accessed=25 * 10**6, transcendentals=0),
        name="lean",
    )(mem, blk, gain, shift, grads, glog, gate, every, extra)


def fold_kernel(bits_ref, *refs, counts):
    at = 0
    outs = sum(counts) * 2
    for k, count in enumerate(counts):
        for part in range(2):
            total = to_wide(refs[at][...])
            for extra in range(1, count):
                total = total + to_wide(refs[at + extra][...])
            refs[outs + 2 * k + part][...] = to_low(total).reshape(refs[outs + 2 * k + part].shape)
            at += count


def fold(items, bits):
    in_specs, arrays, out_specs, out_shape, counts = [], [], [], [], []
    steps = 4
    for k, (addends, dim) in enumerate(items):
        shape = addends[0].shape
        rows, cols = shape[-2:]
        lead = shape[:-2]
        if dim == "columns":
            left, width = lead, cols // 2
        else:
            left, width = lead[:dim] + lead[dim + 1 :], cols
        total = 1
        for size in left:
            total *= size
        group = min(total, steps)
        cut_rows = steps // group
        block_rows = rows // cut_rows
        span = total // group

        def where(i, c, side, k=k, dim=dim, left=left, lead=lead, span=span, cut_rows=cut_rows):
            half = c[k] if side else 1 - c[k]
            index = (i // cut_rows) * span
            coords = []
            for size in reversed(left):
                coords.append(index % size)
                index = index // size
            coords = coords[::-1]
            if dim == "columns":
                return tuple(coords) + (i % cut_rows, half)
            return tuple(coords[:dim]) + (half,) + tuple(coords[dim:]) + (i % cut_rows, 0)

        tail_axes, covered = [], 1
        for size in reversed(left):
            if covered < span:
                covered *= size
                tail_axes.append(size)
            else:
                tail_axes.append(1)
        tail_axes = tail_axes[::-1]
        assert covered == span
        if dim == "columns":
            block = tuple(tail_axes) + (block_rows, width)
        else:
            block = tuple(tail_axes[:dim]) + (1,) + tuple(tail_axes[dim:]) + (block_rows, cols)

        def spec_map(side, where=where, block=block):
            def index(i, c):
                coords = where(i, c, side)
                return tuple(x // b if n < len(block) - 2 else x for n, (x, b) in enumerate(zip(coords, block)))

            return index

        for side in range(2):
            for a in addends:
                arrays.append(a)
                in_specs.append(pl.BlockSpec(block, spec_map(side)))
        out_block = tuple(tail_axes) + (block_rows, width)

        def out_map(i, c, left=left, span=span, cut_rows=cut_rows, tail_axes=tail_axes):
            index = (i // cut_rows) * span
            coords = []
            for size in reversed(left):
                coords.append(index % size)
                index = index // size
            coords = coords[::-1]
            return tuple(x // b for x, b in zip(coords, tail_axes)) + (i % cut_rows, 0)

        for side in range(2):
            out_specs.append(pl.BlockSpec(out_block, out_map))
            out_shape.append(jax.ShapeDtypeStruct(tuple(left) + (rows, width), jnp.bfloat16))
        counts.append(len(addends))
    outs = pl.pallas_call(
        functools.partial(fold_kernel, counts=tuple(counts)),
        grid_spec=pltpu.PrefetchScalarGridSpec(
            num_scalar_prefetch=1, grid=(steps,), in_specs=in_specs, out_specs=out_specs
        ),
        out_shape=out_shape,
        compiler_params=params(48),
        cost_estimate=pl.CostEstimate(flops=10**7, bytes_accessed=30 * 10**6, transcendentals=0),
        name="fold",
    )(bits, *arrays)
    return [(outs[2 * k], outs[2 * k + 1]) for k in range(len(items))]


class Chain:
    def __init__(self, axes, stages, shape, halve):
        self.axes, self.stages, self.shape, self.halve = axes, stages, shape, halve

    def landing(self, extra=0):
        free, size, out = list(self.axes), list(self.shape), []
        for stage in self.stages:
            if stage in free:
                free.remove(stage)
            elif stage == "x":
                size[self.halve] //= 2
            elif stage != "c":
                break
            out.append((2,) * len(free) + tuple(size))
            if stage == "x":
                size[0] += extra
        return out


def plus(left, right):
    return to_low(to_wide(left) + to_wide(right))


LATE = ("L1", "L2", "L3")


def late_cut(share):
    return tuple(share // 50 * part for part in (13, 19, 18))


ORDER = (
    "L10 L20 L30 E0",
    "L21 L11 C0 B0",
    "O0 L22 L31 C1",
    "E1 L12 O1 L32",
    "B1 L13 L23 C2",
    "V0 O2 L33 C3",
    "E2 V1 L24 L14",
    "E3 V2 O3 L34",
    "L25 V3 O4 L15",
    "L26 V4 L35 L16",
    "L36",
)
STARTS = ("E", "C", "O")


def chains(c, e, o, share_rows):
    ends = ["GX", "GC"]
    return {
        "C": Chain(["w"], ["w", "x"] + ends, c, 1),
        "E": Chain(["w"], ["x", "w"] + ends, e, 1),
        "O": Chain(["w", "z", "y"], ["z", "y", "w"] + ends, o, 1),
    } | {
        name: Chain(["w", "z", "y"], ["c"] + list(stages) + ends, (rows, LANES), 0)
        for name, stages, rows in zip(LATE, ("xzyw", "yxwz", "yxzw"), late_cut(share_rows))
    }


def finish_kernel(
    late, gt_hbm, ve_hbm, wk_hbm, wq_hbm, mem_hbm, blk_hbm, gres_hbm, rv_ref, ro_ref, gain_ref, pos, c0, c1, e0, e1,
    o0, o1, outc, oute, outo, outl, outv, xg_ref, *scratch, table,
):
    def place(axis, bit):
        me = lax.axis_index(axis)
        mine = (me // bit) % 2
        return mine, {axis: me + bit * (1 - 2 * mine)}

    mine, who = {}, {}
    for name, axis, bit in (("c", "pos", 1), ("x", "pos", 2), ("y", "seg", 1), ("z", "seg", 2), ("w", "seg", 4)):
        mine[name], who[name] = place(axis, bit)
    barrier = pltpu.get_barrier_semaphore()
    for target in who.values():
        pl.semaphore_signal(barrier, inc=1, device_id=target, device_id_type=pl.DeviceIdType.MESH)
    pl.semaphore_wait(barrier, len(who))

    scratch = list(scratch)
    sent, came, near, loads = scratch[-4:]
    gt, ve, wk, wq, rows_in, gres, sums = scratch[-11:-4]
    vec = scratch[-19:-11]
    work = dict(zip(("C", "E", "O") + LATE + ("L1m",), scratch[:7]))
    landed, at = {}, 7
    for name, chain in table.items():
        stages = len(chain.landing())
        landed[name] = scratch[at : at + stages]
        at += stages
    both = {"C": (c0, c1), "E": (e0, e1), "O": (o0, o1)}
    lead_rows = pos.shape[3]
    late_half = table["L1"].shape[0] // 2
    outs = {"C": (outc, None), "E": (oute, None), "O": (outo, None)}
    first = 0
    for name in LATE:
        size = table[name].shape[0] // 2 + (lead_rows if name == "L1" else 0)
        outs[name] = (outl, (first, size))
        first += size
    started = {}
    copies = []

    def send(key, src, dst, target):
        copy = pltpu.make_async_remote_copy(
            src_ref=src,
            dst_ref=dst,
            send_sem=sent.at[len(copies)],
            recv_sem=came.at[len(copies)],
            device_id=who[target],
            device_id_type=pl.DeviceIdType.MESH,
        )
        copy.start()
        copies.append(copy)
        started[key] = copy

    free = {name: list(chain.axes) for name, chain in table.items()}
    span = {name: (None, chain.shape[chain.halve]) for name, chain in table.items()}

    def pieces(name, start, size):
        halve = table[name].halve
        if start is None:
            return (slice(None), slice(None))
        one = pl.ds(pl.multiple_of(start, 16 if halve == 0 else LANES), size)
        return (one, slice(None)) if halve == 0 else (slice(None), one)

    def part(name, axis, value):
        start, size = span[name]
        fixed = {a: mine[a] for a in table[name].axes if a not in free[name]}
        left = list(free[name])
        relative = None
        if axis == "x":
            size = size // 2
            relative = value * size
            start = relative if start is None else start + relative
        elif axis is not None:
            fixed[axis] = value
            left.remove(axis)
        return left, fixed, start, size, relative

    def total(name, stage, axis, value, store=None):
        left, fixed, start, size, relative = part(name, axis, value)
        chain = table[name]
        switch = name == "L1" and stage is not None and chain.stages[stage] == "x"
        buffer = work[name]

        def one(values):
            index = tuple(values[a] if a in values else fixed[a] for a in chain.axes)
            full = index + pieces(name, start, size)
            if stage is None:
                left_ref, right_ref = both[name]
                got = plus(left_ref[full], right_ref[full])
            else:
                lead = tuple(values[a] if a in values else fixed[a] for a in free[name])
                got = plus(buffer[full], landed[name][stage][lead + pieces(name, relative, size)])
            if store is not None:
                store(got)
            elif switch:
                work["L1m"][index + (slice(0, size), slice(None))] = got
                work["L1m"][index + (slice(size, None), slice(None))] = pos[index]
            else:
                buffer[full] = got

        count = 1 << len(left)
        if count == 1:
            one({})
        elif count == 2:
            for k in range(2):
                one({left[0]: k})
        else:

            @pl.loop(0, count)
            def _(i):
                one({a: (i // (1 << (len(left) - 1 - k))) % 2 for k, a in enumerate(left)})

    def advance(name, stage):
        chain = table[name]
        following = chain.stages[0 if stage is None else stage + 1]
        switch = name == "L1" and stage is not None and chain.stages[stage] == "x"
        number = 0 if stage is None else stage + 1
        out, rows = outs[name]
        place_out = (slice(None), slice(None)) if rows is None else (slice(rows[0], rows[0] + rows[1]), slice(None))
        if following == "GX":

            def store(got):
                out[(mine["c"], mine["x"]) + place_out] = got

            total(name, stage, None, None, store)
            at = out.at[(mine["c"], mine["x"]) + place_out]
            send((name, number), at, at, "x")
            return
        if following == "GC":
            at = out.at[(mine["c"], slice(None)) + place_out]
            send((name, number), at, at, "c")
            return
        other = 1 - mine[following]
        total(name, stage, following, other)
        if switch:
            left, fixed, _, _, _ = part(name, following, other)
            source = work["L1m"]
            index = tuple(slice(None) if a in left else fixed[a] for a in chain.axes) + (slice(None), slice(None))
        else:
            left, fixed, start, size, _ = part(name, following, other)
            source = work[name]
            index = tuple(slice(None) if a in left else fixed[a] for a in chain.axes) + pieces(name, start, size)
        send((name, number), source.at[index], landed[name][number], following)
        total(name, stage, following, mine[following])
        if switch:
            work["L1"] = work["L1m"]
            span["L1"] = (None, late_half + lead_rows)
        if following == "x":
            start, size = span[name]
            half = size // 2
            span[name] = (mine["x"] * half if start is None else start + mine["x"] * half, half)
        else:
            free[name].remove(following)

    share = sum(table[name].shape[0] for name in LATE)
    keep = {}
    first = 0
    for number, name in enumerate(LATE):
        size = table[name].shape[0]
        own = pl.multiple_of(mine["c"] * share + first, 16)
        theirs = pl.multiple_of((1 - mine["c"]) * share + first, 16)
        send((name, 0), late.at[:, :, :, pl.ds(theirs, size)], landed[name][0], "c")
        keep[name] = pltpu.make_async_copy(late.at[:, :, :, pl.ds(own, size)], work[name], near.at[number])
        keep[name].start()
        first += size
    for name in STARTS:
        advance(name, None)

    moves = [(gt_hbm, gt), (ve_hbm, ve), (wk_hbm, wk), (wq_hbm, wq), (gres_hbm, gres)]
    moves += [(mem_hbm, rows_in.at[:, 0]), (blk_hbm, rows_in.at[:, 1])]
    moves = [pltpu.make_async_copy(a, b, loads.at[k]) for k, (a, b) in enumerate(moves)]
    for move in moves:
        move.start()
    rows = rows_in.shape[2]
    slots = rv_ref.shape[0]
    at_key, at_query, at_value, at_out, _ = late_rows(pos.shape[3])

    def inputs(begin):
        @pl.loop(begin, begin + 2)
        def _(b):
            mine_gt = gt[:, pl.ds(pl.multiple_of(b * rows, rows), rows)]
            grad = nn(mine_gt[:at_key].T, ve[...]) + nn(mine_gt[at_key:at_query].T, wk[...])
            grad = grad + nn(mine_gt[at_query:at_value].T, wq[...])
            grad = grad + nn(mine_gt[at_value : at_value + slots].T, rv_ref[...])
            grad = grad + nn(mine_gt[at_out : at_out + slots].T, ro_ref[...])
            unit, inv_std = norm_parts(to_wide(rows_in[b // 2, b % 2]))
            sums[0:1] += jnp.sum(grad * unit, axis=0, keepdims=True)
            sums[1:2] += jnp.sum(grad, axis=0, keepdims=True)

            @pl.when(b % 2 == 1)
            def _():
                q = grad * row(gain_ref)
                back = q - jnp.mean(q, axis=1, keepdims=True) - unit * jnp.mean(q * unit, axis=1, keepdims=True)
                xg_ref[b // 2] = to_low(gres[b // 2] + inv_std * back)

    v0, v1, v2, vc, vx, vy, vz, vw = vec
    my, mz, mw = mine["y"], mine["z"], mine["w"]

    def vectors(stage):
        if stage < 0:
            for k in range(8):
                v0[k // 4, (k // 2) % 2, k % 2] = to_low(sums[:, k * LANES : (k + 1) * LANES])
            send(("V", 0), v0, vc, "c")
        elif stage == 0:
            v1[...] = plus(v0[...], vc[...])
            send(("V", 1), v1, vx, "x")
        elif stage == 1:
            v2[...] = plus(v1[...], vx[...])
            send(("V", 2), v2.at[:, :, 1 - my], vy, "y")
        elif stage == 2:
            for a in range(2):
                for b in range(2):
                    v2[a, b, my] = plus(v2[a, b, my], vy[a, b])
            send(("V", 3), v2.at[:, 1 - mz, my], vz, "z")
        elif stage == 3:
            for a in range(2):
                v2[a, mz, my] = plus(v2[a, mz, my], vz[a])
            send(("V", 4), v2.at[1 - mw, mz, my], vw, "w")
        else:
            outv[...] = to_wide(v2[mw, mz, my]) + to_wide(vw[...])

    for event in " ".join(ORDER).split():
        name, stage = event[:-1], int(event[-1])
        if name == "B":
            if stage == 0:
                for move in moves:
                    move.wait()
                sums[...] = jnp.zeros_like(sums)
            inputs(2 * stage)
            if stage == 1:
                vectors(-1)
            continue
        if name == "V":
            started[(name, stage)].wait_recv()
            vectors(stage)
            continue
        started[(name, stage)].wait_recv()
        if stage == 0 and name in keep:
            keep[name].wait()
        if stage + 1 < len(table[name].stages):
            advance(name, stage)
    for copy in copies:
        copy.wait_send()


def finish(late, gt, weights, rows, gres, gain, pos, c, e, o):
    low, f32 = jnp.bfloat16, jnp.float32
    cube = (2, 2, 2)
    share = late.shape[1] // 2
    table = chains(c[0].shape[1:], e[0].shape[1:], o[0].shape[3:], share)
    lead_rows = pos.shape[1]
    vmem = pl.BlockSpec(memory_space=pltpu.VMEM)
    hbm = pl.BlockSpec(memory_space=pl.ANY)
    shapes = [c[0].shape, e[0].shape, o[0].shape]
    shapes += [cube + table[name].shape for name in LATE]
    shapes += [cube + (table["L1"].shape[0] // 2 + lead_rows, LANES)]
    for name, chain in table.items():
        shapes += chain.landing(lead_rows if name == "L1" else 0)
    small = (16, LANES)
    shapes += [cube + small] * 5 + [(2, 2) + small, (2,) + small, small]
    segs, length, width = rows[0].shape
    shapes += [gt.shape] + [w.shape for w in weights[:3]] + [(segs, 2, length, width)]
    scratch = [pltpu.VMEM(shape, low) for shape in shapes]
    scratch += [pltpu.VMEM(gres.shape, f32), pltpu.VMEM((16, width), f32)]
    count = sum(len(chain.stages) for chain in table.values()) + 5
    scratch += [pltpu.SemaphoreType.DMA((count,)), pltpu.SemaphoreType.DMA((count,)), pltpu.SemaphoreType.DMA((3,))]
    scratch += [pltpu.SemaphoreType.DMA((7,))]
    out = [
        (c[0].shape[1], c[0].shape[2] // 2),
        (e[0].shape[1], e[0].shape[2] // 2),
        o[0].shape[3:],
        (share // 2 + lead_rows, LANES),
    ]
    out = [jax.ShapeDtypeStruct((2, 2) + shape, low) for shape in out]
    out += [jax.ShapeDtypeStruct(small, f32), jax.ShapeDtypeStruct(rows[0].shape, low)]
    return pl.pallas_call(
        functools.partial(finish_kernel, table=table),
        in_specs=[hbm] * 8 + [vmem] * 10,
        out_specs=[vmem] * 6,
        out_shape=out,
        scratch_shapes=scratch,
        compiler_params=pltpu.CompilerParams(vmem_limit_bytes=62 << 20, collective_id=0, has_side_effects=True),
        cost_estimate=pl.CostEstimate(flops=7 * 10**9, bytes_accessed=40 * 10**6, transcendentals=0),
        name="finish",
    )(
        late.reshape(cube + late.shape[1:]),
        gt,
        *weights[:3],
        *rows,
        gres,
        *weights[3:],
        gain,
        pos.reshape(cube + pos.shape[1:]),
        *c,
        *e,
        *o,
    )


def emit_kernel(c_hbm, e_hbm, o_hbm, l_hbm, vec_ref, *refs, plan, slots):
    outs, (c_ref, e_ref, o_ref, l_ref, vals, sems) = refs[:-6], refs[-6:]
    pairs = ((l_hbm, l_ref), (c_hbm, c_ref), (e_hbm, e_ref), (o_hbm, o_ref))
    copies = [pltpu.make_async_copy(a, b, sems.at[k]) for k, (a, b) in enumerate(pairs)]
    for copy in copies:
        copy.start()
    copies[0].wait()
    experts, keys, queries, positions, values, gates = outs[3:9]
    targets = (experts, keys, queries, vals, positions)
    for core, x, start, number, to, rows in plan:
        targets[number][to : to + rows] = to_wide(l_ref[core, x, start : start + rows])
    half = vals.shape[0] // 2
    values[...] = vals[:slots]
    gates[...] = vals[half : half + slots]
    first_gain, first_shift, second_gain, second_shift, contract, expand, content, position = outs[9:]
    first_gain[...] = vec_ref[0]
    first_shift[...] = vec_ref[1]
    lines = tuple((ref, half + slots + k) for k, ref in enumerate((second_gain, second_shift, contract)))
    for ref, number in lines:
        ref[...] = vals[number]
    for k in range(4):
        expand[k * LANES : (k + 1) * LANES] = vals[half + slots + 3 + k]
    size = content.shape[0]
    content[...] = vals[half + slots + 7, :size]
    position[...] = vals[half + slots + 7, size : 2 * size]
    for k, ref in enumerate((c_ref, e_ref, o_ref)):
        width = ref.shape[3]
        copies[k + 1].wait()
        for core in range(2):
            for x in range(2):
                at = (core * 2 + x) * width
                outs[k][:, at : at + width] = to_wide(ref[core, x])


def emit(quarters, vec, dh):
    c, e, o, tail = quarters
    f32 = jnp.float32
    slots = HEADS * EXPERTS
    at_key, at_query, at_value, _, end = late_rows(dh)
    halves = [rows // 2 for rows in late_cut(end // 2)]
    sizes = [at_key, at_query - at_key, at_value - at_query, end - at_value]
    starts = [0, at_key, at_query, at_value]
    plan = []
    for core in range(2):
        for x in range(2):
            for part, piece in enumerate(halves):
                source = sum(halves[:part]) + (dh if part else 0)
                low_end = core * (end // 2) + 2 * sum(halves[:part]) + x * piece
                for k, (first, size) in enumerate(zip(starts, sizes)):
                    a, b = max(first, low_end), min(first + size, low_end + piece)
                    if a < b:
                        plan.append((core, x, source + a - low_end, k, a - first, b - a))
            plan.append((core, x, halves[0], 4, (2 * x + core) * dh, dh))
    vmem = pl.BlockSpec(memory_space=pltpu.VMEM)
    shapes = [(q.shape[2], 4 * q.shape[3]) for q in (c, e, o)] + [(n, LANES) for n in sizes[:3] + [HEADS * dh]]
    shapes += [(slots, LANES)] * 2 + [(LANES,)] * 5 + [(4 * LANES,)] + [(HEADS * dh * LANES // D,)] * 2
    return pl.pallas_call(
        functools.partial(emit_kernel, plan=tuple(plan), slots=slots),
        in_specs=[pl.BlockSpec(memory_space=pl.ANY)] * 4 + [vmem],
        out_specs=[vmem] * len(shapes),
        out_shape=[jax.ShapeDtypeStruct(shape, f32) for shape in shapes],
        scratch_shapes=[pltpu.VMEM(q.shape, q.dtype) for q in quarters]
        + [pltpu.VMEM((end - at_value, LANES), f32), pltpu.SemaphoreType.DMA((4,))],
        compiler_params=params(60),
        name="emit",
    )(c, e, o, tail, vec)


def mm(spec, left, right):
    return jnp.einsum(spec, left, right, preferred_element_type=jnp.float32)


def position_table(row_count, width_count):
    fine = 64
    inverse_freq = 10000.0 ** (-jnp.arange(0, width_count, 2).astype(jnp.float32) / width_count)
    high = (row_count // fine - 1 - jnp.arange(row_count // fine)) * fine
    low_part = fine - 1 - jnp.arange(fine)
    high_angle = high.astype(jnp.float32)[:, None, None] * inverse_freq
    low_angle = low_part.astype(jnp.float32)[None, :, None] * inverse_freq
    high_sin, high_cos = jnp.sin(high_angle), jnp.cos(high_angle)
    low_sin, low_cos = jnp.sin(low_angle), jnp.cos(low_angle)
    sines = high_sin * low_cos + high_cos * low_sin
    cosines = high_cos * low_cos - high_sin * low_sin
    return to_low(jnp.concatenate([sines, cosines], axis=2)).reshape(row_count, width_count)


def route_mask(routes, expert_count):
    return jnp.sum((routes[..., None] == jnp.arange(expert_count)).astype(jnp.float32), axis=-2)


def bit_of(axis, bit):
    return (lax.axis_index(axis) // bit) % 2


def swap(value, axis, bit):
    pairs = [(i, i ^ bit) for i in range(lax.axis_size(axis))]
    return lax.ppermute(value, axis, pairs)


def pick(value, index, axis):
    return lax.dynamic_index_in_dim(value, index, axis, keepdims=False)


def cut(value, index, axis):
    size = value.shape[axis] // 2
    return lax.dynamic_slice_in_dim(value, index * size, size, axis)


def axis_bits(axis):
    size = lax.axis_size(axis)
    return [1 << k for k in range(size.bit_length() - 1)]


def bits_tree(value, seg_size):
    count = len(axis_bits("seg"))
    return value.reshape((2,) * count + (value.shape[0] // seg_size, value.shape[1]))


class Share:
    def __init__(self, addends, bits):
        self.addends = addends
        self.bits = bits

    def total(self):
        out = to_wide(self.addends[0])
        for item in self.addends[1:]:
            out = out + to_wide(item)
        return to_low(out)

    def seg(self, number):
        if number >= len(axis_bits("seg")):
            return self
        bit = axis_bits("seg")[number]
        dim = len(self.bits) - 1 - self.bits.index(bit)
        mine = bit_of("seg", bit)
        sent = Share([pick(a, 1 - mine, dim) for a in self.addends], self.bits).total()
        come = swap(sent, "seg", bit)
        left = [b for b in self.bits if b != bit]
        return Share([pick(a, mine, dim) for a in self.addends] + [come], left)

    def rest(self):
        out = self
        for bit in self.bits:
            out = out.seg(axis_bits("seg").index(bit))
        return out

    def pos(self, number, dim):
        bit = axis_bits("pos")[number]
        mine = bit_of("pos", bit)
        at = len(self.bits) + dim
        sent = Share([cut(a, 1 - mine, at) for a in self.addends], self.bits).total()
        come = swap(sent, "pos", bit)
        return Share([cut(a, mine, at) for a in self.addends] + [come], self.bits)

    def pos_all(self, number):
        part = self.total()
        return Share([part, swap(part, "pos", axis_bits("pos")[number])], self.bits)


def together(stages):
    items, bits, swaps, lefts = [], [], [], []
    for item, axis, number in stages:
        bit = axis_bits(axis)[number]
        bits.append(bit_of(axis, bit))
        swaps.append((axis, bit))
        if axis == "seg":
            items.append((item.addends, len(item.bits) - 1 - item.bits.index(bit)))
            lefts.append([b for b in item.bits if b != bit])
        else:
            items.append((item.addends, "columns"))
            lefts.append(item.bits)
    pairs = fold(items, jnp.stack(bits).astype(jnp.int32))
    out = []
    for (sent, kept), (axis, bit), left in zip(pairs, swaps, lefts):
        out.append(Share([kept, swap(sent, axis, bit)], left))
    return out


def share(values, seg_size):
    return Share([bits_tree(v, seg_size) for v in values], axis_bits("seg"))


def widen(part, number, dim):
    bit = axis_bits("pos")[number]
    mine = bit_of("pos", bit)
    other = swap(part, "pos", bit)
    first = jnp.where(mine == 0, part, other)
    second = jnp.where(mine == 0, other, part)
    return jnp.concatenate([first, second], axis=dim)


def seg_blocks(value, seg_size):
    blocks, rows, lanes = value.shape
    inside = seg_size // blocks
    value = value.reshape(blocks, rows, inside, lanes // inside)
    value = jnp.transpose(value, (0, 2, 1, 3))
    count = len(axis_bits("seg"))
    return value.reshape((2,) * count + (rows, lanes // inside))


def vector_rows(vectors, seg_size):
    lanes = D // seg_size
    rows = jnp.concatenate([v.reshape(seg_size, -1, lanes) for v in vectors], axis=1)
    blocks = D // LANES
    rows = rows.reshape(blocks, seg_size // blocks, rows.shape[1], lanes)
    return jnp.transpose(rows, (0, 2, 1, 3)).reshape(blocks, -1, LANES)


def local(
    block_input,
    memory_rows,
    memory_length,
    value_routes,
    output_routes,
    first_gain,
    first_shift,
    query_weight,
    key_weight,
    position_weight,
    value_experts,
    value_router,
    content_bias,
    position_bias,
    output_experts,
    output_gate_matrix,
    second_gain,
    second_shift,
    up_projection_weight,
    expand_bias,
    down_projection_weight,
    contract_bias,
    output_cotangent,
):
    seg_count, local_rows, width = block_input.shape
    seg_size = lax.axis_size("seg")
    pos_index = lax.axis_index("pos")
    key_count = 2 * SEQ
    all_rows = seg_count * local_rows
    slots = HEADS * EXPERTS
    score_scale = DH ** (-0.5)
    line = lambda v: v.reshape(1, -1)

    value_pick = jnp.transpose(route_mask(value_routes, EXPERTS), (0, 1, 3, 4, 2))
    value_pick = value_pick.reshape(seg_count, 2, slots, local_rows)
    out_pick = jnp.transpose(route_mask(output_routes, EXPERTS), (0, 2, 3, 1))
    out_pick = out_pick.reshape(seg_count, slots, local_rows)
    pad = ((0, 0), (0, 32 - slots))
    gates = jnp.concatenate([jnp.pad(value_router, pad).T, jnp.pad(output_gate_matrix, pad).T], axis=0)

    def trade(value):
        return lax.all_to_all(value, "pos", split_axis=0, concat_axis=0, tiled=True)

    qk, normed, value_gate, out_gate = project(
        memory_rows,
        block_input,
        first_gain,
        first_shift,
        query_weight.T,
        key_weight.T,
        gates,
        value_pick,
        out_pick,
    )
    qk = trade(qk)
    values, value_all = experts(normed, value_experts.T, value_gate)
    values = trade(values)

    table_low = position_table(key_count, D)
    weight_local = pick(position_weight.reshape(D, HEADS, DH), pos_index, 1)
    positions = to_low(mm("nd,dc->cn", table_low, weight_local))

    head_content = pick(content_bias.reshape(HEADS, DH), pos_index, 0)
    head_position = pick(position_bias.reshape(HEADS, DH), pos_index, 0)
    probs = score(memory_length, qk, positions, head_content, head_position, score_scale)
    attended = attend(probs, values)

    core = bit_of("pos", 1).astype(jnp.int32).reshape(1)
    cotangent = output_cotangent.reshape(all_rows, width)
    (
        hidden,
        residual,
        grad_normed_two,
        down_sent,
        down_kept,
        up_sent,
        up_kept,
        expand_bias_grad,
    ) = middle(
        core,
        attended,
        out_gate,
        block_input.reshape(all_rows, width),
        cotangent,
        output_experts,
        second_gain,
        second_shift,
        up_projection_weight,
        line(expand_bias),
        down_projection_weight,
    )
    down_got = swap(down_sent, "pos", 1)
    up_got = swap(up_sent, "pos", 1)
    grad_residual, grad_attended, grad_out_logit, mix_sent, mix_kept, middle_sums = middle_back(
        core, residual, grad_normed_two, attended, out_gate, cotangent, output_experts, second_gain
    )
    grad_heads = trade(grad_attended)
    mix_got = swap(mix_sent, "pos", 1)
    down = share([down_kept, down_got], seg_size)
    up = share([up_kept, up_got], seg_size)
    mix = share([mix_kept, mix_got], seg_size)
    cube = seg_size * LANES == D and lax.axis_size("pos") == 4
    if cube:
        down, up = together([(down, "seg", 1), (up, "seg", 0)])
    else:
        down, up = down.seg(1), up.seg(0)

    grads, grad_rel, part_sums = attend_back(
        probs, grad_heads, qk, values, positions, head_content, head_position, score_scale
    )
    grads = trade(grads)
    part_sums, hidden = lax.optimization_barrier((part_sums, hidden))
    block_output = feed(hidden, down_projection_weight, residual, contract_bias)
    part_sums, block_output, down.addends, up.addends, mix.addends = lax.optimization_barrier(
        (part_sums, block_output, down.addends, up.addends, mix.addends)
    )
    if cube:
        down, up, mix = together([(down, "seg", 0), (up, "seg", 1), (mix, "pos", 1)])
    else:
        down, up, mix = down.seg(0), up.seg(1), mix.pos(1, 1)

    position_grad = to_low(mm("scn,nd->cd", grad_rel, table_low))
    position_grad = jnp.transpose(position_grad.reshape(DH, D // LANES, LANES), (1, 0, 2))
    head_hot = (jnp.arange(HEADS) == pos_index).astype(jnp.float32)[:, None]
    bias_sums = jnp.sum(part_sums, axis=0)
    biases = [(head_hot * bias_sums[k]).reshape(seg_size, -1) for k in range(2)]
    bias_row = jnp.concatenate(biases, axis=1)
    bias_row = jnp.pad(bias_row, ((0, 0), (0, D // seg_size - bias_row.shape[1])))
    extra = vector_rows(
        [middle_sums[0], middle_sums[1], middle_sums[2], expand_bias_grad[0], bias_row], seg_size
    )

    if cube:
        late, all_grads = lean(
            memory_rows,
            block_input,
            first_gain,
            first_shift,
            grads,
            grad_out_logit,
            value_gate,
            value_all,
            extra,
        )
    else:
        input_grad, late = back(
            memory_rows,
            block_input,
            first_gain,
            first_shift,
            grads,
            grad_out_logit,
            value_gate,
            value_all,
            value_experts.T,
            key_weight.T,
            query_weight.T,
            value_router.T,
            output_gate_matrix.T,
            grad_residual.reshape(seg_count, local_rows, width),
            extra,
        )
    late, position_grad, down.addends, up.addends, mix.addends = lax.optimization_barrier(
        (late, position_grad, down.addends, up.addends, mix.addends)
    )
    if cube:
        weights = (value_experts.T, key_weight.T, query_weight.T, value_router.T, output_gate_matrix.T)
        *quarters, vec, input_grad = finish(
            late,
            all_grads,
            weights,
            (memory_rows, block_input),
            grad_residual.reshape(seg_count, local_rows, width),
            first_gain,
            position_grad,
            down.addends,
            up.addends,
            mix.addends,
        )
        contract_weight_grad, expand_weight_grad, output_experts_grad, *rows_out = emit(quarters, vec, DH)
        experts_grad, keys_grad, queries_grad, positions_grad, value_grad, out_grad = rows_out[:6]
        vectors = rows_out[6:]
    else:
        late = Share([late], []).pos(0, 1).total()
        share_rows = late.shape[1] // 2
        one = Share([late[:, :share_rows]], []).pos(1, 1).total()
        piece_rows = one.shape[1]
        one = jnp.concatenate([one, position_grad], axis=1)
        one = Share([seg_blocks(one, seg_size)], axis_bits("seg")).rest().total()
        two = Share([seg_blocks(late[:, share_rows:], seg_size)], axis_bits("seg"))
        two = two.rest().pos(1, 0).total()
        tail = jnp.concatenate([one, two], axis=0)
        tail = to_wide(widen(widen(tail[None], 1, 0)[None], 0, 0))
        lanes = tail.shape[3]
        up = up.pos(1, 1).rest().total()
        expand_weight_grad = to_wide(widen(widen(up, 1, 1), 0, 1))
        down = down.pos(1, 1).rest().total()
        contract_weight_grad = to_wide(widen(widen(down, 1, 1), 0, 1))
        mix = mix.rest().total()
        output_experts_grad = to_wide(widen(widen(mix, 1, 1), 0, 1))
        parts = [tail[:, :, :piece_rows], tail[:, :, tail.shape[2] - piece_rows :]]
        main = jnp.concatenate([p.reshape(2, share_rows, lanes) for p in parts], axis=1).reshape(-1, lanes)
        heads = jnp.transpose(tail[:, :, piece_rows : tail.shape[2] - piece_rows], (1, 0, 2, 3))
        edges = (0,) + late_rows(DH)
        rows_out = [main[a:b] for a, b in zip(edges, edges[1:])] + [heads.reshape(HEADS * DH, lanes)]
        experts_grad, keys_grad, queries_grad, value_rows, out_rows, positions_grad = rows_out
        value_grad, out_grad = value_rows[:slots], out_rows[:slots]
        extra = out_rows[slots : slots + 8]
        piece = DH * HEADS // seg_size
        vectors = [value_rows[slots], value_rows[slots + 1], extra[0], extra[1], extra[2]]
        vectors += [extra[3:7].reshape(-1), extra[7, :piece], extra[7, piece : 2 * piece]]
    return (
        block_output.reshape(block_input.shape),
        input_grad,
        vectors[0],
        vectors[1],
        queries_grad.T,
        keys_grad.T,
        positions_grad.T,
        experts_grad.T,
        value_grad.T,
        vectors[6],
        vectors[7],
        output_experts_grad,
        out_grad.T,
        vectors[2],
        vectors[3],
        expand_weight_grad,
        vectors[5],
        contract_weight_grad,
        vectors[4],
    )


def solution(mesh):
    rows = P("seg", "pos", None)
    whole = P()
    placed = (
        rows,
        rows,
        P("seg"),
        P("seg", None, "pos", None, None),
        P("seg", "pos", None, None),
    )
    placed += (whole,) * 17 + (rows,)
    shares = [P("seg")] * 17
    for index in (2, 3, 4, 5, 6, 9, 10, 13, 15):
        shares[index] = P("seg", None)
    return jax.shard_map(
        local,
        mesh=mesh,
        in_specs=placed,
        out_specs=(rows, rows) + tuple(shares),
        check_vma=False,
    )
```
